32 devices in a mesh: bin: 4 (over x, core), fsdp: 8 (over z, y).
Axes of the slice: x: 2, y: 2, z: 4, core: 2. Of those that a mesh axis runs over, the one named last changes fastest.
Arguments:
- latents: bfloat16 [4, 16, 256, 1152], P('bin', 'fsdp'), may hold values from -6 to 6
- cond: float32 [4, 1152], P('bin'), may hold values from -6 to 6
- live: int32 [4, 8], P('bin', 'fsdp'), may hold values from 1 to 2, 12 in all within a row
- w_ada: bfloat16 [1152, 6912], P(None, 'fsdp'), may hold values from -0.375 to 0.375
- b_ada: bfloat16 [6912], P('fsdp'), may hold values from -3 to 3
- w_qkv: bfloat16 [1152, 3456], P('fsdp'), may hold values from -0.1875 to 0.1875
- b_qv: bfloat16 [2304], P('fsdp'), may hold values from -3 to 3
- w_proj: bfloat16 [1152, 1152], P('fsdp'), may hold values from -0.5 to 0.5
- b_proj: bfloat16 [1152], P('fsdp'), may hold values from -3 to 3
- w_fc1: bfloat16 [1152, 4608], P('fsdp'), may hold values from -0.1875 to 0.1875
- b_fc1: bfloat16 [4608], P('fsdp'), may hold values from -3 to 3
- w_fc2: bfloat16 [4608, 1152], P('fsdp'), may hold values from -0.09375 to 0.09375
- b_fc2: bfloat16 [1152], P('fsdp'), may hold values from -3 to 3
- cotangent: bfloat16 [4, 16, 256, 1152], P('bin', 'fsdp'), may hold values from -6 to 6
Outputs:
- block_out: bfloat16 [4, 16, 256, 1152], P('bin', 'fsdp')
- latents_grad: float32 [4, 16, 256, 1152], P('bin', 'fsdp')
- cond_grad: float32 [4, 1152], P('bin')
- w_ada_grad: float32 [1152, 6912], P(None, 'fsdp')
- b_ada_grad: float32 [6912], P('fsdp')
- w_qkv_grad: float32 [1152, 3456], P('fsdp')
- b_qv_grad: float32 [2304], P('fsdp')
- w_proj_grad: float32 [1152, 1152], P('fsdp')
- b_proj_grad: float32 [1152], P('fsdp')
- w_fc1_grad: float32 [1152, 4608], P('fsdp')
- b_fc1_grad: float32 [4608], P('fsdp')
- w_fc2_grad: float32 [4608, 1152], P('fsdp')
- b_fc2_grad: float32 [1152], P('fsdp')
The draws below stay inside these ranges and needn't reach their ends.
Inputs may be any that keep to these rules, and one draw needn't show every extreme that they name: The counts of one bin's devices sum to 12; every bin has a device with 2 live images; a device's live images are its first slots.
All inputs are finite; a program needn't handle non-finite values.
Results may differ from the reference program's by a relative error of at most 0.015.
The reference program's roundings to bfloat16 on the way count: a program that leaves them out, or rounds other values in their place, can miss the bound.
Values may be sent and summed in bfloat16 or wider, within the bound.
A program may use at most 256 MiB of HBM per device.

```python
import math
import jax
import jax.numpy as jnp
import numpy as np
from jax import lax

D = 1152
HEADS = 16
HEAD_DIM = 72
MLP = 4608
SEQ = 256
IMG_DEV = 2
BINS = 4
IMAGES_BIN = 16
LIVE_BIN = 12
N_BIN = 4
N_FSDP = 8


def block_scale(key, dims, shards, low, high):
    factor_of, own = 1.0, jax.random.fold_in(key, 6)
    for axis_at, parts in shards:
        heights = jnp.exp(jax.random.uniform(jax.random.fold_in(own, axis_at), (parts,), jnp.float32, low / len(shards), high / len(shards)))
        factor_of = factor_of * jnp.repeat(heights, dims[axis_at] // parts).reshape([-1 if axis == axis_at else 1 for axis in range(len(dims))])
    return factor_of


def split_up(amount, total, most, lean):
    portions = [(1 << 20) // math.isqrt(grade ** lean) + 1 for grade in range(2, amount + 1)]
    surplus, holding = total - most - (amount - 1), [1] * (amount - 1)
    while surplus > 0:
        movable = [i for i in range(amount - 1) if holding[i] < most]
        whole, budget = sum([portions[i] for i in movable]), surplus
        for i in movable:
            more = min(most - holding[i], max(1, budget * portions[i] // whole), surplus)
            holding[i] = holding[i] + more
            surplus = surplus - more
    return np.array([most] + holding)


def ragged_sizes(rng, amount, total, most, skew):
    if amount == 2:
        one = jax.random.randint(rng, (), max(1, total - most), min(most, total - 1) + 1)
        return jnp.stack([one, total - one])
    tallies = jnp.asarray(split_up(amount, total, most, skew), jnp.int32)
    pairs = (amount - 1) // 2
    giver, receiver = tallies[1:1 + 2 * pairs:2], tallies[2:2 + 2 * pairs:2]
    room = jnp.minimum(giver - 1, most - receiver)
    moved = jax.random.randint(jax.random.fold_in(rng, 1), (pairs,), 0, 1 << 20) % (room + 1)
    tallies = tallies.at[1:1 + 2 * pairs:2].set(giver - moved).at[2:2 + 2 * pairs:2].set(receiver + moved)
    return tallies[jax.random.permutation(jax.random.fold_in(rng, 2), amount)]


def normal_values(rng, dims, width, bound, cuts=(), kind=jnp.bfloat16):
    drawn = jax.random.normal(rng, dims, jnp.float32) * width
    if len(cuts) > 0:
        drawn = block_scale(rng, dims, cuts, -0.22, 0.18) * drawn
    return jnp.clip(drawn, min=-bound, max=bound).astype(kind)


def setup_inputs(seed: int = 0) -> dict:
    splits = jax.random.split(jax.random.key(seed), 15)
    latents = normal_values(splits[0], (BINS, IMAGES_BIN, SEQ, D), 1.0, 6.0, ((0, 4), (1, 8)))
    cond = normal_values(splits[1], (BINS, D), 1.0, 6.0, ((0, 4),), jnp.float32)
    live = jax.vmap(lambda own: ragged_sizes(own, N_FSDP, LIVE_BIN, IMG_DEV, 2))(jax.random.split(splits[2], BINS)).reshape((BINS, N_FSDP)).astype(jnp.int32)
    w_ada = normal_values(splits[3], (D, 6 * D), (D // 4) ** -0.5, 0.375, ((1, 8),))
    b_ada = normal_values(splits[4], (6 * D,), 0.5, 3.0, ((0, 8),))
    w_qkv = normal_values(splits[5], (D, 3 * D), D ** -0.5, 0.1875, ((0, 8),))
    b_qv = normal_values(splits[6], (2 * D,), 0.5, 3.0, ((0, 8),))
    w_proj = normal_values(splits[7], (D, D), (D // 8) ** -0.5, 0.5, ((0, 8),))
    b_proj = normal_values(splits[8], (D,), 0.5, 3.0, ((0, 8),))
    w_fc1 = normal_values(splits[9], (D, MLP), D ** -0.5, 0.1875, ((0, 8),))
    b_fc1 = normal_values(splits[10], (MLP,), 0.5, 3.0, ((0, 8),))
    w_fc2 = normal_values(splits[11], (MLP, D), MLP ** -0.5, 0.09375, ((0, 8),))
    b_fc2 = normal_values(splits[12], (D,), 0.5, 3.0, ((0, 8),))
    cotangent = normal_values(splits[13], (BINS, IMAGES_BIN, SEQ, D), 1.0, 6.0, ((0, 4), (1, 8)))
    return dict(latents=latents, cond=cond, live=live, w_ada=w_ada, b_ada=b_ada, w_qkv=w_qkv, b_qv=b_qv, w_proj=w_proj, b_proj=b_proj, w_fc1=w_fc1, b_fc1=b_fc1, w_fc2=w_fc2, b_fc2=b_fc2, cotangent=cotangent)


@jax.custom_vjp
def low(v):
    return lax.optimization_barrier(v.astype(jnp.bfloat16)).astype(jnp.float32)

@jax.custom_vjp
def low_back(v):
    return v

def low_keep(v):
    return (low(v), None)

def low_pass(kept, grad):
    return (grad,)

def back_keep(v):
    return (v, None)

def back_low(kept, grad):
    return (low(grad),)
low.defvjp(low_keep, low_pass)
low_back.defvjp(back_keep, back_low)

def dot_high(left, right):
    return jnp.dot(left, right, precision=lax.Precision.HIGHEST)

def layer_norm(field):
    center = field - lax.optimization_barrier(jnp.mean(field, axis=-1, keepdims=True))
    return center * lax.rsqrt(lax.optimization_barrier(jnp.mean(center * center, axis=-1, keepdims=True)) + 1e-06)

def gelu_tanh(field):
    return 0.5 * field * (1.0 + jnp.tanh(0.7978845608028654 * (field + 0.044715 * field * field * field)))

def block_group(tokens, modulation, live_mask, weights):
    w_qkv, b_qv, w_proj, b_proj, w_fc1, b_fc1, w_fc2, b_fc2 = weights
    shift_one, scale_one, gate_one, shift_two, scale_two, gate_two = jnp.split(modulation, 6)
    group_size = tokens.shape[0]
    flat_rows = tokens.reshape(group_size * SEQ, D)
    h_first = low(layer_norm(flat_rows) * (1.0 + scale_one) + shift_one)
    qkv_bias = jnp.concatenate([b_qv[:D], jnp.zeros_like(b_qv[:D]), b_qv[D:]])
    qkv_rows = low(low_back(dot_high(h_first, w_qkv) + qkv_bias))
    qkv_rows = qkv_rows.reshape(group_size, SEQ, 3, HEADS, HEAD_DIM)
    queries = qkv_rows[:, :, 0]
    key_rows = qkv_rows[:, :, 1]
    value_rows = qkv_rows[:, :, 2]
    scores = low_back(jnp.einsum('gqhd,gkhd->ghqk', queries, key_rows, precision=lax.Precision.HIGHEST) * HEAD_DIM ** (-0.5))
    attn_probs = low(jax.nn.softmax(scores, axis=-1))
    attended = jnp.einsum('ghqk,gkhd->gqhd', attn_probs, value_rows, precision=lax.Precision.HIGHEST)
    attended = low(low_back(attended.reshape(group_size * SEQ, D)))
    branch = low_back(dot_high(attended, w_proj) + b_proj)
    middle = flat_rows + gate_one * branch
    h_second = low(layer_norm(middle) * (1.0 + scale_two) + shift_two)
    hidden = low(gelu_tanh(low_back(dot_high(h_second, w_fc1) + b_fc1)))
    mlp_out = low_back(dot_high(hidden, w_fc2) + b_fc2)
    result = (middle + gate_two * mlp_out).reshape(group_size, SEQ, D)
    return result * live_mask[:, None, None]

def forward(tokens, cond, w_ada, b_ada, w_qkv, b_qv, w_proj, b_proj, w_fc1, b_fc1, w_fc2, b_fc2, live):
    scaled = low(jax.nn.silu(cond))
    modulation = dot_high(scaled, w_ada) + b_ada
    groups = tokens.reshape(N_BIN * N_FSDP, IMG_DEV, SEQ, D)
    group_mod = jnp.repeat(modulation, N_FSDP, axis=0)
    slot_index = jnp.arange(IMG_DEV, dtype=jnp.int32)[None, :]
    live_mask = (slot_index < live.reshape(N_BIN * N_FSDP, 1).astype(jnp.int32)).astype(tokens.dtype)
    weights = (w_qkv, b_qv, w_proj, b_proj, w_fc1, b_fc1, w_fc2, b_fc2)
    group_step = jax.checkpoint(block_group)
    result = lax.map(lambda group_item: group_step(group_item[0], group_item[1], group_item[2], weights), (groups, group_mod, live_mask))
    return result.reshape(tokens.shape)

def reference(latents, cond, live, w_ada, b_ada, w_qkv, b_qv, w_proj, b_proj, w_fc1, b_fc1, w_fc2, b_fc2, cotangent):
    floats = [item.astype(jnp.float32) for item in (latents, cond, w_ada, b_ada, w_qkv, b_qv, w_proj, b_proj, w_fc1, b_fc1, w_fc2, b_fc2)]

    def run_forward(*inputs):
        return forward(*inputs, live)
    result, pull_back = jax.vjp(run_forward, *floats)
    gradients = pull_back(cotangent.astype(jnp.float32))
    return (result.astype(jnp.bfloat16), gradients[0], gradients[1], gradients[2], gradients[3], gradients[4], gradients[5], gradients[6], gradients[7], gradients[8], gradients[9], gradients[10], gradients[11])
```

```python
import functools

import jax
import jax.numpy as jnp
from jax import lax
from jax.experimental import pallas as pl
from jax.experimental.pallas import tpu as pltpu
from jax.sharding import PartitionSpec as P

HEAD_DIM = 72
MESH = pl.DeviceIdType.MESH
ROWS = 144
WID = 1152
NG = 3


def layer_norm(field):
    center = field - jnp.mean(field, axis=-1, keepdims=True)
    return center * lax.rsqrt(jnp.mean(center * center, axis=-1, keepdims=True) + 1e-06)


def gelu_tanh(field):
    return (
        0.5
        * field
        * (1.0 + jnp.tanh(0.7978845608028654 * (field + 0.044715 * field * field * field)))
    )


def modulate(field, shift_vec, scale_vec):
    return layer_norm(field) * (1.0 + scale_vec) + shift_vec


def pair_scores(query_block, key_block):
    return jnp.einsum(
        "gqhd,gkhd->ghqk", query_block, key_block, preferred_element_type=jnp.float32
    ) * HEAD_DIM ** (-0.5)


def attend_pair(group_item):
    query_block, key_block, value_block = group_item
    scores = pair_scores(query_block, key_block)
    highest = jnp.max(scores, axis=-1, keepdims=True)
    exp_scores = jnp.exp(scores - highest)
    totals = jnp.sum(exp_scores, axis=-1, keepdims=True)
    attn_probs = (exp_scores / totals).astype(jnp.bfloat16)
    attended = jnp.einsum(
        "ghqk,gkhd->gqhd", attn_probs, value_block, preferred_element_type=jnp.float32
    )
    return (attended, (highest + jnp.log(totals))[..., 0])


def attend_back(group_item):
    query_block, key_block, value_block, log_total, grad_att = group_item
    scores = pair_scores(query_block, key_block)
    attn_probs = jnp.exp(scores - log_total[..., None])
    grad_probs = jnp.einsum(
        "gqhd,gkhd->ghqk", grad_att, value_block, preferred_element_type=jnp.float32
    )
    row_terms = jnp.sum(attn_probs * grad_probs, axis=-1, keepdims=True)
    grad_scores = (attn_probs * (grad_probs - row_terms)).astype(jnp.bfloat16)
    grad_query = jnp.einsum(
        "ghqk,gkhd->gqhd", grad_scores, key_block, preferred_element_type=jnp.float32
    ) * HEAD_DIM ** (-0.5)
    grad_key = jnp.einsum(
        "ghqk,gqhd->gkhd", grad_scores, query_block, preferred_element_type=jnp.float32
    ) * HEAD_DIM ** (-0.5)
    grad_value = jnp.einsum(
        "ghqk,gqhd->gkhd",
        attn_probs.astype(jnp.bfloat16),
        grad_att,
        preferred_element_type=jnp.float32,
    )
    return jnp.stack([grad_query, grad_key, grad_value], axis=2)


def run_block(flat_rows, modulation, weights, images, length):
    full_qkv, full_proj, full_fc1, full_fc2, bias_qv, bias_proj, bias_fc1, bias_fc2 = weights
    width = flat_rows.shape[1]
    heads = width // HEAD_DIM
    pieces = jnp.split(modulation, 6)
    h_first = modulate(flat_rows, pieces[0], pieces[1]).astype(jnp.bfloat16)
    qkv_bias = jnp.concatenate(
        [bias_qv[:width], jnp.zeros((width,), jnp.bfloat16), bias_qv[width:]]
    ).astype(jnp.float32)
    qkv_rows = (jnp.dot(h_first, full_qkv, preferred_element_type=jnp.float32) + qkv_bias).astype(
        jnp.bfloat16
    )
    split_rows = qkv_rows.reshape(images // 2, 2, length, 3, heads, HEAD_DIM)
    attended, log_total = lax.map(
        attend_pair, (split_rows[:, :, :, 0], split_rows[:, :, :, 1], split_rows[:, :, :, 2])
    )
    attended = attended.reshape(images * length, width).astype(jnp.bfloat16)
    branch = jnp.dot(attended, full_proj, preferred_element_type=jnp.float32) + bias_proj.astype(
        jnp.float32
    )
    middle = flat_rows + pieces[2] * branch
    h_second = modulate(middle, pieces[3], pieces[4]).astype(jnp.bfloat16)
    pre_act = jnp.dot(h_second, full_fc1, preferred_element_type=jnp.float32) + bias_fc1.astype(
        jnp.float32
    )
    hidden = gelu_tanh(pre_act).astype(jnp.bfloat16)
    mlp_out = jnp.dot(hidden, full_fc2, preferred_element_type=jnp.float32) + bias_fc2.astype(
        jnp.float32
    )
    result = middle + pieces[5] * mlp_out
    return (
        h_first,
        split_rows,
        log_total,
        attended,
        branch,
        middle,
        h_second,
        pre_act,
        hidden,
        mlp_out,
        result,
    )


def on_device_generic(
    latents,
    cond,
    live,
    w_ada,
    b_ada,
    w_qkv,
    b_qv,
    w_proj,
    b_proj,
    w_fc1,
    b_fc1,
    w_fc2,
    b_fc2,
    cotangent,
):
    images = latents.shape[1]
    length = latents.shape[2]
    width = latents.shape[3]
    heads = width // HEAD_DIM
    scaled = jax.nn.silu(cond[0]).astype(jnp.bfloat16)
    mod_part = jnp.dot(scaled, w_ada, preferred_element_type=jnp.float32) + b_ada.astype(
        jnp.float32
    )
    modulation = lax.all_gather(mod_part, "fsdp", axis=0, tiled=True)
    gathered = (
        lax.all_gather(w_qkv, "fsdp", axis=0, tiled=True),
        lax.all_gather(w_proj, "fsdp", axis=0, tiled=True),
        lax.all_gather(w_fc1, "fsdp", axis=0, tiled=True),
        lax.all_gather(w_fc2, "fsdp", axis=0, tiled=True),
        lax.all_gather(b_qv, "fsdp", axis=0, tiled=True),
        lax.all_gather(b_proj, "fsdp", axis=0, tiled=True),
        lax.all_gather(b_fc1, "fsdp", axis=0, tiled=True),
        lax.all_gather(b_fc2, "fsdp", axis=0, tiled=True),
    )
    flat_rows = latents[0].reshape(images * length, width).astype(jnp.float32)
    live_mask = (lax.iota(jnp.int32, images) < live[0, 0]).astype(jnp.float32)
    row_mask = jnp.repeat(live_mask, length)[:, None]
    forward_run = run_block(flat_rows, modulation, gathered, images, length)
    block_out = (forward_run[10] * row_mask).astype(jnp.bfloat16).reshape(latents.shape)
    weights = (
        lax.all_gather(w_qkv, "fsdp", axis=0, tiled=True),
        lax.all_gather(w_proj, "fsdp", axis=0, tiled=True),
        lax.all_gather(w_fc1, "fsdp", axis=0, tiled=True),
        lax.all_gather(w_fc2, "fsdp", axis=0, tiled=True),
        lax.all_gather(b_qv, "fsdp", axis=0, tiled=True),
        lax.all_gather(b_proj, "fsdp", axis=0, tiled=True),
        lax.all_gather(b_fc1, "fsdp", axis=0, tiled=True),
        lax.all_gather(b_fc2, "fsdp", axis=0, tiled=True),
    )
    full_qkv, full_proj, full_fc1, full_fc2 = (weights[0], weights[1], weights[2], weights[3])
    saved = run_block(flat_rows, modulation, weights, images, length)
    (
        h_first,
        split_rows,
        log_total,
        attended,
        branch,
        middle,
        h_second,
        pre_act,
        hidden,
        mlp_out,
        result,
    ) = saved
    pieces = jnp.split(modulation, 6)
    grad_res = cotangent[0].reshape(images * length, width).astype(jnp.float32) * row_mask
    grad_out = (pieces[5] * grad_res).astype(jnp.bfloat16)
    grad_gate_two = jnp.sum(grad_res * mlp_out, axis=0)
    grad_fc2 = jnp.einsum("rf,rd->fd", hidden, grad_out, preferred_element_type=jnp.float32)
    grad_bfc2 = jnp.sum(grad_out.astype(jnp.float32), axis=0)
    grad_hidden = jnp.einsum("rd,fd->rf", grad_out, full_fc2, preferred_element_type=jnp.float32)
    gelu_pull = jax.vjp(gelu_tanh, pre_act)[1]
    grad_pre = gelu_pull(grad_hidden)[0].astype(jnp.bfloat16)
    grad_fc1 = jnp.einsum("rd,rf->df", h_second, grad_pre, preferred_element_type=jnp.float32)
    grad_bfc1 = jnp.sum(grad_pre.astype(jnp.float32), axis=0)
    grad_h2 = jnp.einsum("rf,df->rd", grad_pre, full_fc1, preferred_element_type=jnp.float32)
    second_pull = jax.vjp(modulate, middle, pieces[3], pieces[4])[1]
    grad_mid_norm, grad_shift_two, grad_scale_two = second_pull(grad_h2)
    grad_mid = grad_res + grad_mid_norm
    grad_branch = (pieces[2] * grad_mid).astype(jnp.bfloat16)
    grad_gate_one = jnp.sum(grad_mid * branch, axis=0)
    grad_proj = jnp.einsum("rd,re->de", attended, grad_branch, preferred_element_type=jnp.float32)
    grad_bproj = jnp.sum(grad_branch.astype(jnp.float32), axis=0)
    grad_att = jnp.einsum(
        "re,de->rd", grad_branch, full_proj, preferred_element_type=jnp.float32
    ).astype(jnp.bfloat16)
    grad_att = grad_att.reshape(images // 2, 2, length, heads, HEAD_DIM)
    grad_qkv = lax.map(
        attend_back,
        (
            split_rows[:, :, :, 0],
            split_rows[:, :, :, 1],
            split_rows[:, :, :, 2],
            log_total,
            grad_att,
        ),
    )
    grad_qkv = grad_qkv.reshape(images * length, 3 * width).astype(jnp.bfloat16)
    grad_wqkv = jnp.einsum("rd,re->de", h_first, grad_qkv, preferred_element_type=jnp.float32)
    qkv_sums = jnp.sum(grad_qkv.astype(jnp.float32), axis=0)
    grad_bqv = jnp.concatenate([qkv_sums[:width], qkv_sums[2 * width :]])
    grad_h1 = jnp.einsum("re,de->rd", grad_qkv, full_qkv, preferred_element_type=jnp.float32)
    first_pull = jax.vjp(modulate, flat_rows, pieces[0], pieces[1])[1]
    grad_rows_norm, grad_shift_one, grad_scale_one = first_pull(grad_h1)
    grad_rows = grad_mid + grad_rows_norm
    grad_mod = jnp.concatenate(
        [
            grad_shift_one,
            grad_scale_one,
            grad_gate_one,
            grad_shift_two,
            grad_scale_two,
            grad_gate_two,
        ]
    )
    shards = (
        lax.psum_scatter(grad_wqkv, "fsdp", scatter_dimension=0, tiled=True),
        lax.psum_scatter(grad_proj, "fsdp", scatter_dimension=0, tiled=True),
        lax.psum_scatter(grad_fc1, "fsdp", scatter_dimension=0, tiled=True),
        lax.psum_scatter(grad_fc2, "fsdp", scatter_dimension=0, tiled=True),
        lax.psum_scatter(grad_bqv, "fsdp", scatter_dimension=0, tiled=True),
        lax.psum_scatter(grad_bproj, "fsdp", scatter_dimension=0, tiled=True),
        lax.psum_scatter(grad_bfc1, "fsdp", scatter_dimension=0, tiled=True),
        lax.psum_scatter(grad_bfc2, "fsdp", scatter_dimension=0, tiled=True),
        lax.psum_scatter(grad_mod, "fsdp", scatter_dimension=0, tiled=True),
    )
    mod_mine = shards[8]
    grad_wada = scaled.astype(jnp.float32)[:, None] * mod_mine[None, :]
    grad_scaled = jnp.dot(w_ada.astype(jnp.float32), mod_mine, precision=lax.Precision.HIGHEST)
    grad_scaled = lax.psum(grad_scaled, "fsdp")
    silu_pull = jax.vjp(jax.nn.silu, cond[0])[1]
    grad_cond = silu_pull(grad_scaled)[0][None, :]
    totals = lax.psum(
        (
            shards[0],
            shards[1],
            shards[2],
            shards[3],
            shards[4],
            shards[5],
            shards[6],
            shards[7],
            grad_wada,
            mod_mine,
        ),
        "bin",
    )
    return (
        block_out,
        grad_rows.reshape(latents.shape),
        grad_cond,
        totals[8],
        totals[9],
        totals[0],
        totals[4],
        totals[1],
        totals[5],
        totals[2],
        totals[6],
        totals[3],
        totals[7],
    )


def coords():
    b=lax.axis_index("bin"); f=lax.axis_index("fsdp")
    x=b//2; c=lax.rem(b,2); z=f//2; y=lax.rem(f,2)
    return b,f,x,c,z,y

def gather_kernel(small_ref, la_ref, lb_ref, lc_ref, so_ref, wa_ref, wb_ref, wc_ref, loc_sem, sm_send, sm_recv, send_sem, recv_sem):
    b,f,x,c,z,y=coords()
    bx=lax.rem(b+2,4)
    bc=b+1-2*c
    bxc=lax.rem(bc+2,4)
    fy=f+1-2*y
    z1=z+1-2*lax.rem(z,2)
    mid=jnp.logical_or(z==1,z==2)
    zb=lax.rem(z+2,4)
    zc=3-z
    z2=jnp.where(mid,zc,zb); z3=jnp.where(mid,zb,zc)
    bar=pltpu.get_barrier_semaphore()
    for k in range(1,8):
        pl.semaphore_signal(bar,inc=1,device_id=(b,lax.rem(f+k,8)),device_id_type=MESH)
    pl.semaphore_signal(bar,inc=1,device_id=(bx,f),device_id_type=MESH)
    pl.semaphore_signal(bar,inc=1,device_id=(bc,f),device_id_type=MESH)
    pl.semaphore_wait(bar,9)
    W=(wa_ref,wb_ref,wc_ref); L=(la_ref,lb_ref,lc_ref)
    def blk(g,j,ff):
        return W[g].at[j,ff] if g<2 else W[g].at[ff,j]
    smalls=[]
    for k in range(1,8):
        cp=pltpu.make_async_remote_copy(src_ref=small_ref,dst_ref=so_ref.at[f],send_sem=sm_send.at[k],recv_sem=sm_recv.at[f],
            device_id=(b,lax.rem(f+k,8)),device_id_type=MESH)
        cp.start(); smalls.append(cp)
    own=pltpu.make_async_copy(small_ref,so_ref.at[f],sm_send.at[0]); own.start()
    locs=[]
    for g in range(NG):
        for j in range(4):
            cp=pltpu.make_async_copy(L[g].at[j],blk(g,j,f),loc_sem.at[g,j]); cp.start(); locs.append(cp)
    pend=[]
    cnt=[0,0,0]
    def send(g,j,ff,dev,cond=None,src=None):
        i=cnt[g]; cnt[g]+=1
        cp=pltpu.make_async_remote_copy(src_ref=blk(g,j,ff) if src is None else src,dst_ref=blk(g,j,ff),send_sem=send_sem.at[g,i],recv_sem=recv_sem.at[g,j,ff],device_id=dev,device_id_type=MESH)
        if cond is None: cp.start()
        else:
            @pl.when(cond)
            def _(): cp.start()
        pend.append((cp,cond))
    def arrive(g,j,ff):
        pltpu.make_async_copy(blk(g,j,ff),blk(g,j,ff),recv_sem.at[g,j,ff]).wait()
    up=(b,jnp.minimum(f+2,7)); dn=(b,jnp.maximum(f-2,0))
    fz1=z1*2+y
    def init(g):
        sb=L[g].at[b]; sx=L[g].at[bx]
        send(g,b,f,up,z<3,sb); send(g,b,f,dn,z>0,sb); send(g,b,f,(b,fy),None,sb); send(g,bx,f,(b,fz1),None,sx); send(g,bx,f,(b,fy),None,sx)
    def Z(g,zz,x_too):
        ff=zz*2+y
        arrive(g,b,ff)
        send(g,b,ff,up,jnp.logical_and(zz<z,z<3)); send(g,b,ff,dn,jnp.logical_and(zz>z,z>0))
        send(g,b,ff,(b,fy))
        if x_too: send(g,b,ff,(bx,f))
        send(g,b,ff,(bc,f))
    def Y(g,zz,x_too):
        ff=zz*2+1-y
        arrive(g,b,ff)
        if x_too: send(g,b,ff,(bx,f))
        send(g,b,ff,(bc,f))
    def X(g,j,ff):
        arrive(g,j,ff); send(g,j,ff,(bc,f))
    acts=[]
    for g in range(NG):
        a=[lambda g=g: Z(g,z1,False), lambda g=g: X(g,bx,fz1), lambda g=g: Y(g,z,False), lambda g=g: X(g,bx,fy),
           lambda g=g: Z(g,z2,True), lambda g=g: Y(g,z1,True), lambda g=g: Z(g,z3,True), lambda g=g: X(g,bx,z2*2+y), lambda g=g: Y(g,z2,True),
           lambda g=g: X(g,bx,z1*2+1-y), lambda g=g: X(g,bx,z3*2+y), lambda g=g: Y(g,z3,True), lambda g=g: X(g,bx,z2*2+1-y), lambda g=g: X(g,bx,z3*2+1-y)]
        acts.append(a)
    init(0)
    for g in range(NG):
        for i,a in enumerate(acts[g]):
            a()
            if i==7 and g<NG-1: init(g+1)
    for g in range(NG):
        for zz in range(4):
            for jj in (bc,bxc):
                @pl.when(zz!=z)
                def _(): arrive(g,jj,zz*2+y)
                arrive(g,jj,zz*2+1-y)
    for cp,cond in pend:
        if cond is None: cp.wait_send()
        else:
            @pl.when(cond)
            def _(cp=cp): cp.wait_send()
    own.wait()
    for cp in locs: cp.wait()
    for cp in smalls: cp.wait_send()
    for k in range(1,8):
        ff=lax.rem(f+k,8)
        pltpu.make_async_copy(so_ref.at[ff],so_ref.at[ff],sm_recv.at[ff]).wait()

def gather(small,la,lb,lc):
    A=pl.BlockSpec(memory_space=pl.ANY)
    return pl.pallas_call(gather_kernel,
        out_shape=(jax.ShapeDtypeStruct((8,8,256),jnp.float32),jax.ShapeDtypeStruct((4,8,ROWS,WID),jnp.bfloat16),jax.ShapeDtypeStruct((4,8,ROWS,WID),jnp.bfloat16),jax.ShapeDtypeStruct((8,4,ROWS,WID),jnp.bfloat16)),
        in_specs=[A]+[pl.BlockSpec(memory_space=pltpu.VMEM)]*3,out_specs=(A,)*4,
        scratch_shapes=[pltpu.SemaphoreType.DMA((3,4)),pltpu.SemaphoreType.DMA((8,)),pltpu.SemaphoreType.DMA((8,)),pltpu.SemaphoreType.DMA((3,40)),pltpu.SemaphoreType.DMA((3,4,8))],
        compiler_params=pltpu.CompilerParams(collective_id=1,has_side_effects=True),name="gather_weights")(small,la,lb,lc)


def reduce_kernel(small_ref, pa_ref, pb_ref, pc_ref, so_ref, oa_ref, ob_ref, oc_ref,
                  t, r0, rx4, ry4, ry3, rx2, rn, rz, rt, fin,
                  ld_sem, s0_send, s0_recv, send_sem, rx4_s, ry4_s, ry3_s, rx2_s, rn_s, rz_s, rt_s, o_loc, o_send, o_recv, sm_send, sm_recv):
    b,f,x,c,z,y=coords()
    bx=lax.rem(b+2,4); bc=b+1-2*c; bxc=lax.rem(bc+2,4)
    fy=f+1-2*y; yb=1-y
    z1=z+1-2*lax.rem(z,2)
    mid=jnp.logical_or(z==1,z==2)
    zb=lax.rem(z+2,4); zc=3-z
    z2=jnp.where(mid,zc,zb); z3=jnp.where(mid,zb,zc)
    fz1=z1*2+y
    bar=pltpu.get_barrier_semaphore()
    for k in range(1,32):
        d=lax.rem(b*8+f+k,32)
        pl.semaphore_signal(bar,inc=1,device_id=(d//8,lax.rem(d,8)),device_id_type=MESH)
    pl.semaphore_wait(bar,31)
    P=(pa_ref,pb_ref,pc_ref); O=(oa_ref,ob_ref,oc_ref)
    def blk(g,j,ff):
        return P[g].at[j,ff] if g<2 else P[g].at[ff,j]
    tw=[]
    order=[(1,z3,yb),(1,z2,yb),(1,z3,y),(1,z2,y),(1,z1,yb),(1,z,yb),(0,z3,yb),(0,z2,yb),(0,z1,yb),(0,z,yb),(0,z3,y),(0,z2,y),(1,z1,y),(0,z1,y),(0,z,y),(1,z,y)]
    mine=(b,bx); his=(bc,bxc)
    loads=[]
    for g in range(NG):
        for i,(jj,zz,yy) in enumerate(order):
            ff=zz*2+yy
            cp=pltpu.make_async_remote_copy(src_ref=blk(g,his[jj],ff),dst_ref=r0.at[g,i],send_sem=s0_send.at[g,i],recv_sem=s0_recv.at[g,i],device_id=(bc,f),device_id_type=MESH)
            cp.start(); tw.append((cp,None))
            ld=pltpu.make_async_copy(blk(g,mine[jj],ff),t.at[g,i],ld_sem.at[g,i]); ld.start(); loads.append(ld)
    sms=[]
    for k in range(1,32):
        d=lax.rem(b*8+f+k,32)
        cp=pltpu.make_async_remote_copy(src_ref=small_ref.at[lax.rem(d,8)],dst_ref=so_ref.at[b*8+f],send_sem=sm_send.at[k],recv_sem=sm_recv.at[b*8+f],device_id=(d//8,lax.rem(d,8)),device_id_type=MESH)
        cp.start(); sms.append(cp)
    own=pltpu.make_async_copy(small_ref.at[f],so_ref.at[b*8+f],sm_send.at[0]); own.start()
    def wait_on(ref,sem): pltpu.make_async_copy(ref,ref,sem).wait()
    def base(g,i):
        loads[g*16+i].wait(); wait_on(r0.at[g,i],s0_recv.at[g,i])
    def add(dst,srcs):
        @pl.loop(0,ROWS//16)
        def _(k):
            rows=pl.ds(pl.multiple_of(k*16,16),16)
            v=srcs[0][rows,:].astype(jnp.float32)
            for s in srcs[1:]: v=v+s[rows,:].astype(jnp.float32)
            dst[rows,:]=v.astype(dst.dtype)
    cnt=[0]*3
    def send(g,src,dst,rsem,dev,cond=None):
        i=cnt[g]; cnt[g]+=1
        cp=pltpu.make_async_remote_copy(src_ref=src,dst_ref=dst,send_sem=send_sem.at[g,i],recv_sem=rsem,device_id=dev,device_id_type=MESH)
        if cond is None: cp.start()
        else:
            @pl.when(cond)
            def _(): cp.start()
        tw.append((cp,cond))
    X=(bx,f); Y=(b,fy)
    def a4x(g,i,slot):
        base(g,i); add(t.at[g,i],[t.at[g,i],r0.at[g,i]]); send(g,t.at[g,i],rx4.at[g,slot],rx4_s.at[g,slot],X)
    def a2(g,i,slot):
        base(g,i); add(t.at[g,i],[t.at[g,i],r0.at[g,i]]); send(g,t.at[g,i],rx2.at[g,slot],rx2_s.at[g,slot],X)
    def a4y(g,i,slot):
        base(g,i); add(t.at[g,i],[t.at[g,i],r0.at[g,i]]); send(g,t.at[g,i],ry4.at[g,slot],ry4_s.at[g,slot],Y)
    def a3(g,i,slot,rslot):
        base(g,i)
        s=[t.at[g,i],r0.at[g,i]]
        if rslot is not None:
            wait_on(rx4.at[g,rslot],rx4_s.at[g,rslot]); s.append(rx4.at[g,rslot])
        add(t.at[g,i],s); send(g,t.at[g,i],ry3.at[g,slot],ry3_s.at[g,slot],Y)
    def m(g,i,zz,rslot,yslot):
        base(g,i)
        s=[t.at[g,i],r0.at[g,i]]
        if rslot is not None:
            wait_on(rx2.at[g,rslot],rx2_s.at[g,rslot]); s.append(rx2.at[g,rslot])
        wait_on(ry3.at[g,yslot],ry3_s.at[g,yslot]); s.append(ry3.at[g,yslot])
        behind=jnp.where(zz>z,z>0,z<3)
        add(t.at[g,i],s)
        @pl.when(behind)
        def _():
            wait_on(rz.at[g,zz],rz_s.at[g,zz]); add(t.at[g,i],[t.at[g,i],rz.at[g,zz]])
        nz=jnp.where(zz>z,z+1,z-1)
        slot=jnp.where(jnp.logical_and(zz==nz,zz<z),4,zz)
        send(g,t.at[g,i],rz.at[g,slot],rz_s.at[g,slot],(b,nz*2+y))
    def n(g,i):
        base(g,i); wait_on(ry4.at[g,1],ry4_s.at[g,1])
        add(t.at[g,i],[t.at[g,i],r0.at[g,i],ry4.at[g,1]]); send(g,t.at[g,i],rn.at[g],rn_s.at[g],(b,fz1))
    def t1(g,i):
        base(g,i); wait_on(ry3.at[g,0],ry3_s.at[g,0])
        add(t.at[g,i],[t.at[g,i],r0.at[g,i],ry3.at[g,0]])
        @pl.when(z>0)
        def _():
            wait_on(rz.at[g,z],rz_s.at[g,z]); add(t.at[g,i],[t.at[g,i],rz.at[g,z]])
        @pl.when(z<3)
        def _():
            wait_on(rz.at[g,4],rz_s.at[g,4]); add(t.at[g,i],[t.at[g,i],rz.at[g,4]])
        send(g,t.at[g,i],rt.at[g,0],rt_s.at[g,0],X)
    def t2(g,i):
        base(g,i); wait_on(ry4.at[g,0],ry4_s.at[g,0]); wait_on(rn.at[g],rn_s.at[g])
        add(t.at[g,i],[t.at[g,i],r0.at[g,i],ry4.at[g,0],rn.at[g]])
        send(g,t.at[g,i],rt.at[g,1],rt_s.at[g,1],X)
    def final(g):
        for q,(i,slot,j) in enumerate(((14,1,b),(15,0,bx))):
            wait_on(rt.at[g,slot],rt_s.at[g,slot])
            add(fin.at[g,q],[t.at[g,i],rt.at[g,slot]])
            cp=pltpu.make_async_copy(fin.at[g,q],O[g].at[j],o_loc.at[g,q]); cp.start()
            rc=pltpu.make_async_remote_copy(src_ref=fin.at[g,q],dst_ref=O[g].at[j],send_sem=o_send.at[g,q],recv_sem=o_recv.at[g,q],device_id=(bc,f),device_id_type=MESH)
            rc.start(); tw.append((rc,None)); loads2.append(cp)
    loads2=[]
    acts=[]
    for g in range(NG):
        a=[lambda g=g: a4x(g,0,0), lambda g=g: a4x(g,1,1), lambda g=g: a2(g,2,0), lambda g=g: a4y(g,4,1), lambda g=g: a2(g,3,1), lambda g=g: a4y(g,5,0),
           lambda g=g: a3(g,8,1,None), lambda g=g: a3(g,6,3,0), lambda g=g: a3(g,7,2,1), lambda g=g: a3(g,9,0,None)]
        e=[lambda g=g: m(g,10,z3,0,3), lambda g=g: m(g,11,z2,1,2), lambda g=g: n(g,12), lambda g=g: m(g,13,z1,None,1), lambda g=g: t2(g,15), lambda g=g: t1(g,14), lambda g=g: final(g)]
        acts.append((a,e))
    seq=list(acts[0][0])
    for g in range(NG):
        e=acts[g][1]; a=acts[g+1][0] if g+1<NG else []
        k=max(len(e),len(a))
        for i in range(k):
            if i<len(a): seq.append(a[i])
            if i<len(e): seq.append(e[i])
    for s in seq: s()
    for g in range(NG):
        for q,j in enumerate((bc,bxc)):
            wait_on(O[g].at[j],o_recv.at[g,q])
    for cp,cond in tw:
        if cond is None: cp.wait_send()
        else:
            @pl.when(cond)
            def _(cp=cp): cp.wait_send()
    for cp in loads2: cp.wait()
    own.wait()
    for cp in sms: cp.wait_send()
    for k in range(1,32):
        d=lax.rem(b*8+f+k,32)
        wait_on(so_ref.at[d],sm_recv.at[d])

def reduce(small,pa,pb,pc):
    A=pl.BlockSpec(memory_space=pl.ANY)
    D=pltpu.SemaphoreType.DMA
    B=jnp.bfloat16
    def V(*s,dt=B): return pltpu.VMEM(s+(ROWS,WID),dt)
    return pl.pallas_call(reduce_kernel,
        out_shape=(jax.ShapeDtypeStruct((32,8,256),jnp.float32),)+(jax.ShapeDtypeStruct((4,ROWS,WID),jnp.float32),)*3,
        in_specs=[A]*4,out_specs=(A,)*4,
        scratch_shapes=[V(3,16),V(3,16),V(3,2),V(3,2),V(3,4),V(3,2),V(3),V(3,5),V(3,2),V(3,2,dt=jnp.float32),
           D((3,16)),D((3,16)),D((3,16)),D((3,24)),D((3,2)),D((3,2)),D((3,4)),D((3,2)),D((3,)),D((3,5)),D((3,2)),D((3,2)),D((3,2)),D((3,2)),D((32,)),D((32,))],
        compiler_params=pltpu.CompilerParams(collective_id=2,has_side_effects=True,vmem_limit_bytes=63<<20),name="reduce_grads")(small,pa,pb,pc)


def head_window(h):
    start = HEAD_DIM * h
    low = start // 128 * 128
    width = 128 if start - low + HEAD_DIM <= 128 else 256
    return low, width, start - low


def attend_head(q, k, v, off, width):
    lanes = lax.broadcasted_iota(jnp.int32, (1, width), 1)
    keep = jnp.logical_and(lanes >= off, lanes < off + HEAD_DIM)
    q = jnp.where(keep, q, jnp.zeros_like(q))
    v = jnp.where(keep, v, jnp.zeros_like(v))
    scores = lax.dot_general(k, q, (((1,), (1,)), ((), ())), preferred_element_type=jnp.float32)
    scores = scores * HEAD_DIM ** (-0.5)
    e = jnp.exp(scores - jnp.max(scores, axis=0, keepdims=True))
    probs = e * (1.0 / jnp.sum(e, axis=0, keepdims=True))
    return lax.dot_general(
        probs.astype(jnp.bfloat16), v, (((0,), (0,)), ((), ())), preferred_element_type=jnp.float32
    )


def attend_kernel(q_ref, k_ref, v_ref, out_ref, acc):
    acc[...] = jnp.zeros_like(acc)
    for h in range(q_ref.shape[1] // HEAD_DIM):
        low, width, off = head_window(h)
        cols = slice(low, low + width)
        acc[:, cols] += attend_head(q_ref[:, cols], k_ref[:, cols], v_ref[:, cols], off, width)
    out_ref[...] = acc[...].astype(jnp.bfloat16)


def attend(q, k, v, length):
    rows, width = q.shape
    spec = pl.BlockSpec((length, width), lambda i: (i, 0))
    return pl.pallas_call(
        attend_kernel,
        grid=(rows // length,),
        out_shape=jax.ShapeDtypeStruct((rows, width), jnp.bfloat16),
        in_specs=[spec] * 3,
        out_specs=spec,
        scratch_shapes=[pltpu.VMEM((length, width), jnp.float32)],
        compiler_params=pltpu.CompilerParams(vmem_limit_bytes=40 << 20),
        name="attend",
    )(q, k, v)


def attend_head_back(q, k, v, g, off, width):
    lanes = lax.broadcasted_iota(jnp.int32, (1, width), 1)
    keep = jnp.logical_and(lanes >= off, lanes < off + HEAD_DIM)
    q = jnp.where(keep, q, jnp.zeros_like(q))
    g = jnp.where(keep, g, jnp.zeros_like(g))
    k_own = jnp.where(keep, k, jnp.zeros_like(k))
    nt = (((1,), (1,)), ((), ()))
    scores = lax.dot_general(k, q, nt, preferred_element_type=jnp.float32) * HEAD_DIM ** (-0.5)
    e = jnp.exp(scores - jnp.max(scores, axis=0, keepdims=True))
    probs = e * (1.0 / jnp.sum(e, axis=0, keepdims=True))
    grad_probs = lax.dot_general(v, g, nt, preferred_element_type=jnp.float32)
    row = jnp.sum(probs * grad_probs, axis=0, keepdims=True)
    grad_scores = (probs * (grad_probs - row)).astype(jnp.bfloat16)
    grad_v = jnp.dot(probs.astype(jnp.bfloat16), g, preferred_element_type=jnp.float32)
    grad_k = jnp.dot(grad_scores, q, preferred_element_type=jnp.float32) * HEAD_DIM ** (-0.5)
    grad_q = lax.dot_general(
        grad_scores, k_own, (((0,), (0,)), ((), ())), preferred_element_type=jnp.float32
    ) * HEAD_DIM ** (-0.5)
    return grad_q, grad_k, grad_v


def attend_back_kernel(q_ref, k_ref, v_ref, g_ref, dq_ref, dk_ref, dv_ref, aq, ak, av):
    for acc in (aq, ak, av):
        acc[...] = jnp.zeros_like(acc)
    for h in range(q_ref.shape[1] // HEAD_DIM):
        low, width, off = head_window(h)
        cols = slice(low, low + width)
        out = attend_head_back(q_ref[:, cols], k_ref[:, cols], v_ref[:, cols], g_ref[:, cols], off, width)
        for acc, part in zip((aq, ak, av), out):
            acc[:, cols] += part
    for ref, acc in zip((dq_ref, dk_ref, dv_ref), (aq, ak, av)):
        ref[...] = acc[...].astype(jnp.bfloat16)


def attend_grads(q, k, v, g, length):
    rows, width = q.shape
    spec = pl.BlockSpec((length, width), lambda i: (i, 0))
    return pl.pallas_call(
        attend_back_kernel,
        grid=(rows // length,),
        out_shape=(jax.ShapeDtypeStruct((rows, width), jnp.bfloat16),) * 3,
        in_specs=[spec] * 4,
        out_specs=(spec,) * 3,
        scratch_shapes=[pltpu.VMEM((length, width), jnp.float32)] * 3,
        compiler_params=pltpu.CompilerParams(vmem_limit_bytes=40 << 20),
        name="attend_grads",
    )(q, k, v, g)


def on_device_fast(
    latents, cond, live, w_ada, b_ada, w_qkv, b_qv, w_proj, b_proj, w_fc1, b_fc1, w_fc2, b_fc2, cotangent
):
    images, length, width = latents.shape[1:]
    rows = images * length
    f32 = jnp.float32
    scaled = jax.nn.silu(cond[0]).astype(jnp.bfloat16)
    mod_part = jnp.dot(scaled, w_ada, preferred_element_type=f32) + b_ada.astype(f32)
    biases = jnp.concatenate([b_qv, b_proj, b_fc1, b_fc2]).astype(f32)
    small = jnp.concatenate([mod_part, biases, jnp.zeros((32,), f32)]).reshape(8, 256)
    la = jnp.concatenate([jnp.transpose(w_qkv.reshape(ROWS, 3, WID), (1, 0, 2)), w_proj[None]])
    lb = jnp.transpose(w_fc1.reshape(ROWS, 4, WID), (1, 0, 2))
    lc = w_fc2.reshape(4, ROWS, WID)
    so, wa, wb, wc = gather(small, la, lb, lc)
    so = so.reshape(8, 2048)
    modulation = so[:, :864].reshape(6, width)
    bias_qv = so[:, 864:1152].reshape(2, width)
    bias_proj = so[:, 1152:1296].reshape(width)
    bias_fc1 = so[:, 1296:1872].reshape(4 * width)
    bias_fc2 = so[:, 1872:2016].reshape(width)
    wa = wa.reshape(4, width, width)
    wb = wb.reshape(4, width, width)
    wc = wc.reshape(4 * width, width)
    flat_rows = latents[0].reshape(rows, width).astype(f32)
    live_mask = (lax.iota(jnp.int32, images) < live[0, 0]).astype(f32)
    row_mask = jnp.repeat(live_mask, length)[:, None]
    h_first = modulate(flat_rows, modulation[0], modulation[1]).astype(jnp.bfloat16)

    def dense(left, right):
        return jnp.dot(left, right, preferred_element_type=f32)

    q = (dense(h_first, wa[0]) + bias_qv[0]).astype(jnp.bfloat16)
    k = dense(h_first, wa[1]).astype(jnp.bfloat16)
    v = (dense(h_first, wa[2]) + bias_qv[1]).astype(jnp.bfloat16)
    attended = attend(q, k, v, length)
    branch = dense(attended, wa[3]) + bias_proj
    middle = flat_rows + modulation[2] * branch
    h_second = modulate(middle, modulation[3], modulation[4]).astype(jnp.bfloat16)
    pre = [dense(h_second, wb[j]) + bias_fc1[j * width : (j + 1) * width] for j in range(4)]
    hidden = jnp.concatenate([gelu_tanh(p).astype(jnp.bfloat16) for p in pre], axis=1)
    mlp_out = dense(hidden, wc) + bias_fc2
    block_out = ((middle + modulation[5] * mlp_out) * row_mask).astype(jnp.bfloat16)
    grad_res = cotangent[0].reshape(rows, width).astype(f32) * row_mask
    grad_out = (modulation[5] * grad_res).astype(jnp.bfloat16)
    grad_gate_two = jnp.sum(grad_res * mlp_out, axis=0)

    def outer(left, right):
        return jnp.einsum("rd,re->de", left, right, preferred_element_type=f32)

    grad_fc2 = outer(hidden, grad_out).astype(jnp.bfloat16)
    grad_bfc2 = jnp.sum(grad_out.astype(f32), axis=0)
    grad_pre, grad_fc1 = [], []
    grad_h2 = 0.0
    for j in range(4):
        wcj = wc[j * width : (j + 1) * width]
        grad_hidden = jnp.einsum("rd,fd->rf", grad_out, wcj, preferred_element_type=f32)
        gp = jax.vjp(gelu_tanh, pre[j])[1](grad_hidden)[0].astype(jnp.bfloat16)
        grad_pre.append(gp)
        grad_fc1.append(outer(h_second, gp).astype(jnp.bfloat16))
        grad_h2 = grad_h2 + jnp.einsum("rf,df->rd", gp, wb[j], preferred_element_type=f32)
    grad_bfc1 = jnp.concatenate([jnp.sum(g.astype(f32), axis=0) for g in grad_pre])
    second_pull = jax.vjp(modulate, middle, modulation[3], modulation[4])[1]
    grad_mid_norm, grad_shift_two, grad_scale_two = second_pull(grad_h2)
    grad_mid = grad_res + grad_mid_norm
    grad_branch = (modulation[2] * grad_mid).astype(jnp.bfloat16)
    grad_gate_one = jnp.sum(grad_mid * branch, axis=0)
    grad_proj = outer(attended, grad_branch).astype(jnp.bfloat16)
    grad_bproj = jnp.sum(grad_branch.astype(f32), axis=0)
    grad_att = jnp.einsum("re,de->rd", grad_branch, wa[3], preferred_element_type=f32).astype(jnp.bfloat16)
    grads = attend_grads(q, k, v, grad_att, length)
    grad_bqv = [jnp.sum(grads[i].astype(f32), axis=0) for i in (0, 2)]
    grad_wa = [outer(h_first, g).astype(jnp.bfloat16) for g in grads] + [grad_proj]
    grad_h1 = sum(jnp.einsum("re,de->rd", g, wa[i], preferred_element_type=f32) for i, g in enumerate(grads))
    first_pull = jax.vjp(modulate, flat_rows, modulation[0], modulation[1])[1]
    grad_rows_norm, grad_shift_one, grad_scale_one = first_pull(grad_h1)
    grad_rows = grad_mid + grad_rows_norm
    grad_mod = jnp.concatenate(
        [grad_shift_one, grad_scale_one, grad_gate_one, grad_shift_two, grad_scale_two, grad_gate_two]
    )
    out_small = jnp.concatenate(
        [
            grad_mod.reshape(8, 864),
            jnp.concatenate(grad_bqv).reshape(8, 288),
            grad_bproj.reshape(8, ROWS),
            grad_bfc1.reshape(8, 576),
            grad_bfc2.reshape(8, ROWS),
            jnp.zeros((8, 32), f32),
        ],
        axis=1,
    ).reshape(8, 8, 256)
    so2, oa, ob, oc = reduce(
        out_small,
        jnp.stack(grad_wa).reshape(4, 8, ROWS, width),
        jnp.stack(grad_fc1).reshape(4, 8, ROWS, width),
        grad_fc2.reshape(8, 4, ROWS, width),
    )
    per_bin = jnp.sum(so2.reshape(4, 8, 2048), axis=1)
    sums = jnp.sum(per_bin, axis=0)
    mod_bins = per_bin[:, :864]
    scaled_bins = lax.all_gather(scaled, "bin", axis=0)
    grad_wada = jnp.einsum("bd,be->de", scaled_bins.astype(f32), mod_bins, precision=lax.Precision.HIGHEST)
    mod_mine = lax.dynamic_index_in_dim(mod_bins, lax.axis_index("bin"), 0, keepdims=False)
    grad_scaled = jnp.sum(w_ada.astype(f32) * mod_mine[None, :], axis=1)
    grad_scaled = lax.psum(grad_scaled, "fsdp")
    silu_pull = jax.vjp(jax.nn.silu, cond[0])[1]
    grad_cond = silu_pull(grad_scaled)[0][None, :]
    return (
        block_out.reshape(latents.shape),
        grad_rows.reshape(latents.shape),
        grad_cond,
        grad_wada,
        sums[:864],
        jnp.transpose(oa[:3], (1, 0, 2)).reshape(ROWS, 3 * width),
        sums[864:1152],
        oa[3],
        sums[1152:1296],
        jnp.transpose(ob, (1, 0, 2)).reshape(ROWS, 4 * width),
        sums[1296:1872],
        oc.reshape(4 * ROWS, width),
        sums[1872:2016],
    )


def solution(mesh):
    fast = mesh.shape["bin"] == 4 and mesh.shape["fsdp"] == 8
    return jax.shard_map(
        on_device_fast if fast else on_device_generic,
        mesh=mesh,
        in_specs=(
            P("bin", "fsdp", None, None),
            P("bin", None),
            P("bin", "fsdp"),
            P(None, "fsdp"),
            P("fsdp"),
            P("fsdp", None),
            P("fsdp"),
            P("fsdp", None),
            P("fsdp"),
            P("fsdp", None),
            P("fsdp"),
            P("fsdp", None),
            P("fsdp"),
            P("bin", "fsdp", None, None),
        ),
        out_specs=(
            P("bin", "fsdp", None, None),
            P("bin", "fsdp", None, None),
            P("bin", None),
            P(None, "fsdp"),
            P("fsdp"),
            P("fsdp", None),
            P("fsdp"),
            P("fsdp", None),
            P("fsdp"),
            P("fsdp", None),
            P("fsdp"),
            P("fsdp", None),
            P("fsdp"),
        ),
        check_vma=False,
    )
```

```python
import functools

import jax
import jax.numpy as jnp
from jax import lax
from jax.experimental import pallas as pl
from jax.experimental.pallas import tpu as pltpu
from jax.sharding import PartitionSpec as P

HEAD_DIM = 72
MESH = pl.DeviceIdType.MESH
ROWS = 144
WID = 1152
NG = 3


def layer_norm(field):
    center = field - jnp.mean(field, axis=-1, keepdims=True)
    return center * lax.rsqrt(jnp.mean(center * center, axis=-1, keepdims=True) + 1e-06)


def gelu_tanh(field):
    return (
        0.5
        * field
        * (1.0 + jnp.tanh(0.7978845608028654 * (field + 0.044715 * field * field * field)))
    )


def modulate(field, shift_vec, scale_vec):
    return layer_norm(field) * (1.0 + scale_vec) + shift_vec


def pair_scores(query_block, key_block):
    return jnp.einsum(
        "gqhd,gkhd->ghqk", query_block, key_block, preferred_element_type=jnp.float32
    ) * HEAD_DIM ** (-0.5)


def attend_pair(group_item):
    query_block, key_block, value_block = group_item
    scores = pair_scores(query_block, key_block)
    highest = jnp.max(scores, axis=-1, keepdims=True)
    exp_scores = jnp.exp(scores - highest)
    totals = jnp.sum(exp_scores, axis=-1, keepdims=True)
    attn_probs = (exp_scores / totals).astype(jnp.bfloat16)
    attended = jnp.einsum(
        "ghqk,gkhd->gqhd", attn_probs, value_block, preferred_element_type=jnp.float32
    )
    return (attended, (highest + jnp.log(totals))[..., 0])


def attend_back(group_item):
    query_block, key_block, value_block, log_total, grad_att = group_item
    scores = pair_scores(query_block, key_block)
    attn_probs = jnp.exp(scores - log_total[..., None])
    grad_probs = jnp.einsum(
        "gqhd,gkhd->ghqk", grad_att, value_block, preferred_element_type=jnp.float32
    )
    row_terms = jnp.sum(attn_probs * grad_probs, axis=-1, keepdims=True)
    grad_scores = (attn_probs * (grad_probs - row_terms)).astype(jnp.bfloat16)
    grad_query = jnp.einsum(
        "ghqk,gkhd->gqhd", grad_scores, key_block, preferred_element_type=jnp.float32
    ) * HEAD_DIM ** (-0.5)
    grad_key = jnp.einsum(
        "ghqk,gqhd->gkhd", grad_scores, query_block, preferred_element_type=jnp.float32
    ) * HEAD_DIM ** (-0.5)
    grad_value = jnp.einsum(
        "ghqk,gqhd->gkhd",
        attn_probs.astype(jnp.bfloat16),
        grad_att,
        preferred_element_type=jnp.float32,
    )
    return jnp.stack([grad_query, grad_key, grad_value], axis=2)


def run_block(flat_rows, modulation, weights, images, length):
    full_qkv, full_proj, full_fc1, full_fc2, bias_qv, bias_proj, bias_fc1, bias_fc2 = weights
    width = flat_rows.shape[1]
    heads = width // HEAD_DIM
    pieces = jnp.split(modulation, 6)
    h_first = modulate(flat_rows, pieces[0], pieces[1]).astype(jnp.bfloat16)
    qkv_bias = jnp.concatenate(
        [bias_qv[:width], jnp.zeros((width,), jnp.bfloat16), bias_qv[width:]]
    ).astype(jnp.float32)
    qkv_rows = (jnp.dot(h_first, full_qkv, preferred_element_type=jnp.float32) + qkv_bias).astype(
        jnp.bfloat16
    )
    split_rows = qkv_rows.reshape(images // 2, 2, length, 3, heads, HEAD_DIM)
    attended, log_total = lax.map(
        attend_pair, (split_rows[:, :, :, 0], split_rows[:, :, :, 1], split_rows[:, :, :, 2])
    )
    attended = attended.reshape(images * length, width).astype(jnp.bfloat16)
    branch = jnp.dot(attended, full_proj, preferred_element_type=jnp.float32) + bias_proj.astype(
        jnp.float32
    )
    middle = flat_rows + pieces[2] * branch
    h_second = modulate(middle, pieces[3], pieces[4]).astype(jnp.bfloat16)
    pre_act = jnp.dot(h_second, full_fc1, preferred_element_type=jnp.float32) + bias_fc1.astype(
        jnp.float32
    )
    hidden = gelu_tanh(pre_act).astype(jnp.bfloat16)
    mlp_out = jnp.dot(hidden, full_fc2, preferred_element_type=jnp.float32) + bias_fc2.astype(
        jnp.float32
    )
    result = middle + pieces[5] * mlp_out
    return (
        h_first,
        split_rows,
        log_total,
        attended,
        branch,
        middle,
        h_second,
        pre_act,
        hidden,
        mlp_out,
        result,
    )


def on_device_generic(
    latents,
    cond,
    live,
    w_ada,
    b_ada,
    w_qkv,
    b_qv,
    w_proj,
    b_proj,
    w_fc1,
    b_fc1,
    w_fc2,
    b_fc2,
    cotangent,
):
    images = latents.shape[1]
    length = latents.shape[2]
    width = latents.shape[3]
    heads = width // HEAD_DIM
    scaled = jax.nn.silu(cond[0]).astype(jnp.bfloat16)
    mod_part = jnp.dot(scaled, w_ada, preferred_element_type=jnp.float32) + b_ada.astype(
        jnp.float32
    )
    modulation = lax.all_gather(mod_part, "fsdp", axis=0, tiled=True)
    gathered = (
        lax.all_gather(w_qkv, "fsdp", axis=0, tiled=True),
        lax.all_gather(w_proj, "fsdp", axis=0, tiled=True),
        lax.all_gather(w_fc1, "fsdp", axis=0, tiled=True),
        lax.all_gather(w_fc2, "fsdp", axis=0, tiled=True),
        lax.all_gather(b_qv, "fsdp", axis=0, tiled=True),
        lax.all_gather(b_proj, "fsdp", axis=0, tiled=True),
        lax.all_gather(b_fc1, "fsdp", axis=0, tiled=True),
        lax.all_gather(b_fc2, "fsdp", axis=0, tiled=True),
    )
    flat_rows = latents[0].reshape(images * length, width).astype(jnp.float32)
    live_mask = (lax.iota(jnp.int32, images) < live[0, 0]).astype(jnp.float32)
    row_mask = jnp.repeat(live_mask, length)[:, None]
    forward_run = run_block(flat_rows, modulation, gathered, images, length)
    block_out = (forward_run[10] * row_mask).astype(jnp.bfloat16).reshape(latents.shape)
    weights = (
        lax.all_gather(w_qkv, "fsdp", axis=0, tiled=True),
        lax.all_gather(w_proj, "fsdp", axis=0, tiled=True),
        lax.all_gather(w_fc1, "fsdp", axis=0, tiled=True),
        lax.all_gather(w_fc2, "fsdp", axis=0, tiled=True),
        lax.all_gather(b_qv, "fsdp", axis=0, tiled=True),
        lax.all_gather(b_proj, "fsdp", axis=0, tiled=True),
        lax.all_gather(b_fc1, "fsdp", axis=0, tiled=True),
        lax.all_gather(b_fc2, "fsdp", axis=0, tiled=True),
    )
    full_qkv, full_proj, full_fc1, full_fc2 = (weights[0], weights[1], weights[2], weights[3])
    saved = run_block(flat_rows, modulation, weights, images, length)
    (
        h_first,
        split_rows,
        log_total,
        attended,
        branch,
        middle,
        h_second,
        pre_act,
        hidden,
        mlp_out,
        result,
    ) = saved
    pieces = jnp.split(modulation, 6)
    grad_res = cotangent[0].reshape(images * length, width).astype(jnp.float32) * row_mask
    grad_out = (pieces[5] * grad_res).astype(jnp.bfloat16)
    grad_gate_two = jnp.sum(grad_res * mlp_out, axis=0)
    grad_fc2 = jnp.einsum("rf,rd->fd", hidden, grad_out, preferred_element_type=jnp.float32)
    grad_bfc2 = jnp.sum(grad_out.astype(jnp.float32), axis=0)
    grad_hidden = jnp.einsum("rd,fd->rf", grad_out, full_fc2, preferred_element_type=jnp.float32)
    gelu_pull = jax.vjp(gelu_tanh, pre_act)[1]
    grad_pre = gelu_pull(grad_hidden)[0].astype(jnp.bfloat16)
    grad_fc1 = jnp.einsum("rd,rf->df", h_second, grad_pre, preferred_element_type=jnp.float32)
    grad_bfc1 = jnp.sum(grad_pre.astype(jnp.float32), axis=0)
    grad_h2 = jnp.einsum("rf,df->rd", grad_pre, full_fc1, preferred_element_type=jnp.float32)
    second_pull = jax.vjp(modulate, middle, pieces[3], pieces[4])[1]
    grad_mid_norm, grad_shift_two, grad_scale_two = second_pull(grad_h2)
    grad_mid = grad_res + grad_mid_norm
    grad_branch = (pieces[2] * grad_mid).astype(jnp.bfloat16)
    grad_gate_one = jnp.sum(grad_mid * branch, axis=0)
    grad_proj = jnp.einsum("rd,re->de", attended, grad_branch, preferred_element_type=jnp.float32)
    grad_bproj = jnp.sum(grad_branch.astype(jnp.float32), axis=0)
    grad_att = jnp.einsum(
        "re,de->rd", grad_branch, full_proj, preferred_element_type=jnp.float32
    ).astype(jnp.bfloat16)
    grad_att = grad_att.reshape(images // 2, 2, length, heads, HEAD_DIM)
    grad_qkv = lax.map(
        attend_back,
        (
            split_rows[:, :, :, 0],
            split_rows[:, :, :, 1],
            split_rows[:, :, :, 2],
            log_total,
            grad_att,
        ),
    )
    grad_qkv = grad_qkv.reshape(images * length, 3 * width).astype(jnp.bfloat16)
    grad_wqkv = jnp.einsum("rd,re->de", h_first, grad_qkv, preferred_element_type=jnp.float32)
    qkv_sums = jnp.sum(grad_qkv.astype(jnp.float32), axis=0)
    grad_bqv = jnp.concatenate([qkv_sums[:width], qkv_sums[2 * width :]])
    grad_h1 = jnp.einsum("re,de->rd", grad_qkv, full_qkv, preferred_element_type=jnp.float32)
    first_pull = jax.vjp(modulate, flat_rows, pieces[0], pieces[1])[1]
    grad_rows_norm, grad_shift_one, grad_scale_one = first_pull(grad_h1)
    grad_rows = grad_mid + grad_rows_norm
    grad_mod = jnp.concatenate(
        [
            grad_shift_one,
            grad_scale_one,
            grad_gate_one,
            grad_shift_two,
            grad_scale_two,
            grad_gate_two,
        ]
    )
    shards = (
        lax.psum_scatter(grad_wqkv, "fsdp", scatter_dimension=0, tiled=True),
        lax.psum_scatter(grad_proj, "fsdp", scatter_dimension=0, tiled=True),
        lax.psum_scatter(grad_fc1, "fsdp", scatter_dimension=0, tiled=True),
        lax.psum_scatter(grad_fc2, "fsdp", scatter_dimension=0, tiled=True),
        lax.psum_scatter(grad_bqv, "fsdp", scatter_dimension=0, tiled=True),
        lax.psum_scatter(grad_bproj, "fsdp", scatter_dimension=0, tiled=True),
        lax.psum_scatter(grad_bfc1, "fsdp", scatter_dimension=0, tiled=True),
        lax.psum_scatter(grad_bfc2, "fsdp", scatter_dimension=0, tiled=True),
        lax.psum_scatter(grad_mod, "fsdp", scatter_dimension=0, tiled=True),
    )
    mod_mine = shards[8]
    grad_wada = scaled.astype(jnp.float32)[:, None] * mod_mine[None, :]
    grad_scaled = jnp.dot(w_ada.astype(jnp.float32), mod_mine, precision=lax.Precision.HIGHEST)
    grad_scaled = lax.psum(grad_scaled, "fsdp")
    silu_pull = jax.vjp(jax.nn.silu, cond[0])[1]
    grad_cond = silu_pull(grad_scaled)[0][None, :]
    totals = lax.psum(
        (
            shards[0],
            shards[1],
            shards[2],
            shards[3],
            shards[4],
            shards[5],
            shards[6],
            shards[7],
            grad_wada,
            mod_mine,
        ),
        "bin",
    )
    return (
        block_out,
        grad_rows.reshape(latents.shape),
        grad_cond,
        totals[8],
        totals[9],
        totals[0],
        totals[4],
        totals[1],
        totals[5],
        totals[2],
        totals[6],
        totals[3],
        totals[7],
    )


TILE = 256
STRIP = 16


def coords():
    b = lax.axis_index("bin")
    f = lax.axis_index("fsdp")
    return b, f, b // 2, lax.rem(b, 2), f // 2, lax.rem(f, 2)


def strip_loop(rows, body):
    @pl.loop(0, rows // STRIP)
    def _(k):
        body(pl.ds(pl.multiple_of(k * STRIP, STRIP), STRIP))


def dense(left, right):
    return jnp.dot(left, right, preferred_element_type=jnp.float32)


def dense_nt(left, right):
    return lax.dot_general(left, right, (((1,), (1,)), ((), ())), preferred_element_type=jnp.float32)


def dense_tn(left, right):
    return lax.dot_general(left, right, (((0,), (0,)), ((), ())), preferred_element_type=jnp.float32)


def center_rows(v):
    v = v - jnp.mean(v, axis=-1, keepdims=True)
    inv = lax.rsqrt(jnp.mean(v * v, axis=-1, keepdims=True) + 1e-06)
    return v * inv, inv


def head_window(h):
    start = HEAD_DIM * h
    low = start // 128 * 128
    width = 128 if start - low + HEAD_DIM <= 128 else 256
    return low, width, start - low


def head_mask(off, width):
    lanes = lax.broadcasted_iota(jnp.int32, (1, width), 1)
    return jnp.logical_and(lanes >= off, lanes < off + HEAD_DIM)


def head_probs(q, k):
    scores = dense_nt(k, q) * HEAD_DIM ** (-0.5)
    e = jnp.exp(scores - jnp.max(scores, axis=0, keepdims=True))
    return e * (1.0 / jnp.sum(e, axis=0, keepdims=True))


def forward_kernel(
    vec_ref, la_ref, lb_ref, lc_ref, x_ref, res_ref,
    vec_out, wa_out, wb_out, wc_out, h1_out, qkv_out, att_out, branch_out, mid_out, h2_out, slope_out, hid_out, go_out, pc_out,
    wa, wb, wc, vecs, vec, xs, res, h1, qkv, att, mid, h2, hid, go, acc, slope, pst,
    loc_sem, sm_send, sm_recv, send_sem, recv_sem, in_sem, out_sem, wo_sem, co_sem, sl_sem, ps_sem,
):
    b, f, x, c, z, y = coords()
    bx = lax.rem(b + 2, 4)
    bc = b + 1 - 2 * c
    bxc = lax.rem(bc + 2, 4)
    fy = f + 1 - 2 * y
    yb = 1 - y
    z1 = z + 1 - 2 * lax.rem(z, 2)
    mid_z = jnp.logical_or(z == 1, z == 2)
    zb = lax.rem(z + 2, 4)
    zc = 3 - z
    z2 = jnp.where(mid_z, zc, zb)
    z3 = jnp.where(mid_z, zb, zc)
    fz1 = z1 * 2 + y
    bar = pltpu.get_barrier_semaphore()
    for k in range(1, 8):
        pl.semaphore_signal(bar, inc=1, device_id=(b, lax.rem(f + k, 8)), device_id_type=MESH)
    pl.semaphore_signal(bar, inc=1, device_id=(bx, f), device_id_type=MESH)
    pl.semaphore_signal(bar, inc=1, device_id=(bc, f), device_id_type=MESH)
    pl.semaphore_wait(bar, 9)

    W = (wa, wb, wc)
    L = (la_ref, lb_ref, lc_ref)

    def blk(g, j, ff):
        if g < 2:
            return W[g].at[j, pl.ds(pl.multiple_of(ff * ROWS, ROWS), ROWS)]
        return W[g].at[ff, j]

    smalls = []
    for k in range(1, 8):
        cp = pltpu.make_async_remote_copy(
            src_ref=vec_ref, dst_ref=vecs.at[f], send_sem=sm_send.at[k], recv_sem=sm_recv.at[f],
            device_id=(b, lax.rem(f + k, 8)), device_id_type=MESH,
        )
        cp.start()
        smalls.append(cp)
    own = pltpu.make_async_copy(vec_ref, vecs.at[f], sm_send.at[0])
    own.start()

    pend = []
    outs = []
    cnt = [0] * NG

    def send(g, j, ff, dev, cond=None, src=None):
        i = cnt[g]
        cnt[g] += 1
        cp = pltpu.make_async_remote_copy(
            src_ref=blk(g, j, ff) if src is None else src, dst_ref=blk(g, j, ff),
            send_sem=send_sem.at[g, i], recv_sem=recv_sem.at[g, j, ff], device_id=dev, device_id_type=MESH,
        )
        if cond is None:
            cp.start()
        else:
            @pl.when(cond)
            def _():
                cp.start()
        pend.append((cp, cond))

    def copy_out(src, dst, sem):
        cp = pltpu.make_async_copy(src, dst, sem)
        cp.start()
        return cp

    def arrive(g, j, ff, cond=None):
        def go_on():
            pltpu.make_async_copy(blk(g, j, ff), blk(g, j, ff), recv_sem.at[g, j, ff]).wait()
            if g == 2:
                copy_out(wc.at[ff, j], wc_out.at[ff, j], co_sem.at[j, ff])
        if cond is None:
            go_on()
        else:
            pl.when(cond)(go_on)

    up = (b, jnp.minimum(f + 2, 7))
    dn = (b, jnp.maximum(f - 2, 0))

    def init(g):
        sb = L[g].at[b]
        sx = L[g].at[bx]
        send(g, b, f, up, z < 3, sb)
        send(g, b, f, dn, z > 0, sb)
        send(g, b, f, (b, fy), None, sb)
        send(g, bx, f, (b, fz1), None, sx)
        send(g, bx, f, (b, fy), None, sx)

    locs = []

    def local(g):
        for j in range(4):
            locs.append(copy_out(L[g].at[j], blk(g, j, f), loc_sem.at[g, j]))

    def Z(g, zz, x_too):
        ff = zz * 2 + y
        arrive(g, b, ff)
        send(g, b, ff, up, jnp.logical_and(zz < z, z < 3))
        send(g, b, ff, dn, jnp.logical_and(zz > z, z > 0))
        send(g, b, ff, (b, fy))
        if x_too:
            send(g, b, ff, (bx, f))
        send(g, b, ff, (bc, f))

    def Y(g, zz, x_too):
        ff = zz * 2 + yb
        arrive(g, b, ff)
        if x_too:
            send(g, b, ff, (bx, f))
        send(g, b, ff, (bc, f))

    def X(g, ff):
        arrive(g, bx, ff)
        send(g, bx, ff, (bc, f))

    def actions(g):
        return [
            lambda: Z(g, z1, False), lambda: X(g, fz1), lambda: Y(g, z, False), lambda: X(g, fy),
            lambda: Z(g, z2, True), lambda: Y(g, z1, True), lambda: Z(g, z3, True), lambda: X(g, z2 * 2 + y),
            lambda: Y(g, z2, True), lambda: X(g, z1 * 2 + yb), lambda: X(g, z3 * 2 + y), lambda: Y(g, z3, True),
            lambda: X(g, z2 * 2 + yb), lambda: X(g, z3 * 2 + yb),
        ]

    def other_core(g):
        for zz in range(4):
            for jj in (bc, bxc):
                arrive(g, jj, zz * 2 + y, zz != z)
                arrive(g, jj, zz * 2 + yb)
        for cp in locs[g * 4 : g * 4 + 4]:
            cp.wait()

    def keep(src, dst, i):
        outs.append(copy_out(src, dst, out_sem.at[i]))

    def row(i):
        return vec[i : i + 1, :]

    def start_rows():
        own.wait()
        for k in range(1, 8):
            ff = lax.rem(f + k, 8)
            pltpu.make_async_copy(vecs.at[ff], vecs.at[ff], sm_recv.at[ff]).wait()
        total = vecs[0]
        for k in range(1, 8):
            total = total + vecs[k]
        vec[...] = total
        keep(vec, vec_out, 0)
        in_x.wait()

        def first(r):
            n, _ = center_rows(xs[r, :].astype(jnp.float32))
            h1[r, :] = (n * (1.0 + row(1)) + row(0)).astype(jnp.bfloat16)

        strip_loop(h1.shape[0], first)
        keep(h1, h1_out, 1)
        in_res.wait()

        def out_grad(r):
            go[r, :] = (res[r, :].astype(jnp.float32) * row(5)).astype(jnp.bfloat16)

        strip_loop(go.shape[0], out_grad)
        keep(go, go_out, 2)

    tiles = xs.shape[0] // TILE

    def tile(i):
        return pl.ds(pl.multiple_of(i * TILE, TILE), TILE)

    def project(j):
        @pl.loop(0, tiles)
        def _(i):
            v = dense(h1[tile(i), :], wa[j])
            if j != 1:
                v = v + row(6 + j // 2)
            qkv[j, tile(i), :] = v.astype(jnp.bfloat16)
        keep(qkv.at[j], qkv_out.at[j], 3 + j)

    def attention():
        @pl.loop(0, tiles)
        def _(i):
            acc[...] = jnp.zeros_like(acc)
            for h in range(WID // HEAD_DIM):
                low, width, off = head_window(h)
                cols = slice(low, low + width)
                mask = head_mask(off, width)
                q = qkv[0, tile(i), cols]
                v = qkv[2, tile(i), cols]
                probs = head_probs(jnp.where(mask, q, jnp.zeros_like(q)), qkv[1, tile(i), cols])
                acc[:, cols] += dense_tn(probs.astype(jnp.bfloat16), jnp.where(mask, v, jnp.zeros_like(v)))
            att[tile(i), :] = acc[...].astype(jnp.bfloat16)
        keep(att, att_out, 6)

    def branch():
        @pl.loop(0, tiles)
        def _(i):
            mid[tile(i), :] = dense(att[tile(i), :], wa[3]) + row(8)
        cp = copy_out(mid, branch_out, out_sem.at[7])
        cp.wait()

        def second(r):
            m = xs[r, :].astype(jnp.float32) + row(2) * mid[r, :]
            mid[r, :] = m
            n, _ = center_rows(m)
            h2[r, :] = (n * (1.0 + row(4)) + row(3)).astype(jnp.bfloat16)

        strip_loop(mid.shape[0], second)
        keep(mid, mid_out, 8)
        keep(h2, h2_out, 9)

    def hidden(j):
        cols = slice(j * WID, j * WID + WID)

        @pl.loop(0, tiles)
        def _(i):
            acc[...] = dense(h2[tile(i), :], wb[j]) + row(9 + j)

            @pl.when(j * tiles + i >= 1)
            def _():
                pltpu.make_async_copy(slope, slope_out.at[tile(0), :WID], sl_sem).wait()

            @pl.loop(0, TILE // STRIP)
            def _(k):
                r = pl.ds(pl.multiple_of(k * STRIP, STRIP), STRIP)
                v = acc[r, :]
                sq = v * v
                t = jnp.tanh(0.7978845608028654 * (v + 0.044715 * sq * v))
                half = 0.5 * (1.0 + t)
                slope[r, :] = half + 0.5 * v * (1.0 - t * t) * (0.7978845608028654 * (1.0 + 0.134145 * sq))
                hid[pl.ds(pl.multiple_of(i * TILE + k * STRIP, STRIP), STRIP), cols] = (v * half).astype(jnp.bfloat16)

            copy_out(slope, slope_out.at[tile(i), cols], sl_sem)
        if j == 3:
            pltpu.make_async_copy(slope, slope_out.at[tile(0), :WID], sl_sem).wait()
            keep(hid, hid_out, 10)

    part = pst.shape[1]

    def outer(j):
        @pl.loop(0, WID // part)
        def _(i):
            k = j * (WID // part) + i
            slot = lax.rem(k, 2)

            @pl.when(k >= 2)
            def _():
                pltpu.make_async_copy(pst.at[slot], pc_out.at[pl.ds(0, part)], ps_sem.at[slot]).wait()
            at = pl.multiple_of(k * part, part)
            pst[slot] = dense_tn(hid[:, pl.ds(at, part)], go[...]).astype(jnp.bfloat16)
            copy_out(pst.at[slot], pc_out.at[pl.ds(at, part)], ps_sem.at[slot])
        if j == 3:
            for slot in range(2):
                pltpu.make_async_copy(pst.at[slot], pc_out.at[pl.ds(0, part)], ps_sem.at[slot]).wait()

    def weights_out(g):
        outs.append(copy_out(W[g], (wa_out, wb_out)[g], wo_sem.at[g]))

    in_x = copy_out(x_ref, xs, in_sem.at[0])
    in_res = copy_out(res_ref, res, in_sem.at[1])
    acts = [actions(g) for g in range(NG)]
    run = lambda todo: [a() for a in todo]
    init(0)
    local(0)
    start_rows()
    run(acts[0][:8])
    init(1)
    local(1)
    run(acts[0][8:])
    run(acts[1][:5])
    other_core(0)
    weights_out(0)
    work = [lambda: project(0), lambda: project(1), lambda: project(2), attention, branch]
    ticks = [acts[1][5:6], acts[1][6:7], acts[1][7:8] + [lambda: init(2), lambda: local(2)], acts[1][8:11], acts[1][11:12]]
    for piece, tick in zip(work, ticks):
        piece()
        run(tick)
    run(acts[1][12:])
    run(acts[2][:5])
    other_core(1)
    weights_out(1)
    work = [functools.partial(hidden, j) for j in range(4)] + [functools.partial(outer, j) for j in range(4)]
    ticks = [acts[2][5 + i : 6 + i] for i in range(8)]
    for piece, tick in zip(work, ticks):
        piece()
        run(tick)
    run(acts[2][13:])
    for j in range(4):
        locs[8 + j].wait()
        copy_out(wc.at[f, j], wc_out.at[f, j], co_sem.at[j, f])
    other_core_c = 2
    for zz in range(4):
        for jj in (bc, bxc):
            arrive(other_core_c, jj, zz * 2 + y, zz != z)
            arrive(other_core_c, jj, zz * 2 + yb)
    for cp, cond in pend:
        if cond is None:
            cp.wait_send()
        else:
            @pl.when(cond)
            def _(cp=cp):
                cp.wait_send()
    for cp in smalls:
        cp.wait_send()
    for cp in outs:
        cp.wait()
    for ff in range(8):
        for j in range(4):
            pltpu.make_async_copy(wc.at[ff, j], wc_out.at[ff, j], co_sem.at[j, ff]).wait()


def forward(vec, la, lb, lc, x, res):
    any_space = pl.BlockSpec(memory_space=pl.ANY)
    f32, bf16 = jnp.float32, jnp.bfloat16
    rows = x.shape[0]
    sds = jax.ShapeDtypeStruct
    sem = pltpu.SemaphoreType.DMA
    mat = (rows, WID)
    outs = (
        sds((16, WID), f32), sds((4, WID, WID), bf16), sds((4, WID, WID), bf16), sds((8, 4, ROWS, WID), bf16),
        sds(mat, bf16), sds((3,) + mat, bf16), sds(mat, bf16), sds(mat, f32), sds(mat, f32), sds(mat, bf16),
        sds((rows, 4 * WID), f32), sds((rows, 4 * WID), bf16), sds(mat, bf16), sds((4 * WID, WID), bf16),
    )
    vm = pltpu.VMEM
    return pl.pallas_call(
        forward_kernel,
        out_shape=outs,
        in_specs=[any_space] * 6,
        out_specs=(any_space,) * len(outs),
        scratch_shapes=[
            vm((4, WID, WID), bf16), vm((4, WID, WID), bf16), vm((8, 4, ROWS, WID), bf16), vm((8, 16, WID), f32), vm((16, WID), f32),
            vm(mat, bf16), vm(mat, bf16), vm(mat, bf16), vm((3,) + mat, bf16), vm(mat, bf16), vm(mat, f32), vm(mat, bf16),
            vm((rows, 4 * WID), bf16), vm(mat, bf16), vm((TILE, WID), f32), vm((TILE, WID), f32), vm((2, 384, WID), bf16),
            sem((NG, 4)), sem((8,)), sem((8,)), sem((NG, 40)), sem((NG, 4, 8)), sem((2,)), sem((12,)), sem((2,)), sem((4, 8)), sem, sem((2,)),
        ],
        compiler_params=pltpu.CompilerParams(collective_id=1, has_side_effects=True, vmem_limit_bytes=63 << 20),
        name="forward",
    )(vec, la, lb, lc, x, res)


def reduce_kernel(small_ref, pa_ref, pb_ref, pc_ref, so_ref, oa_ref, ob_ref, oc_ref,
                  t, r0, rx4, ry4, ry3, rx2, rn, rz, rt, fin,
                  ld_sem, s0_send, s0_recv, send_sem, rx4_s, ry4_s, ry3_s, rx2_s, rn_s, rz_s, rt_s, o_loc, o_send, o_recv, sm_send, sm_recv):
    b,f,x,c,z,y=coords()
    bx=lax.rem(b+2,4); bc=b+1-2*c; bxc=lax.rem(bc+2,4)
    fy=f+1-2*y; yb=1-y
    z1=z+1-2*lax.rem(z,2)
    mid=jnp.logical_or(z==1,z==2)
    zb=lax.rem(z+2,4); zc=3-z
    z2=jnp.where(mid,zc,zb); z3=jnp.where(mid,zb,zc)
    fz1=z1*2+y
    bar=pltpu.get_barrier_semaphore()
    for k in range(1,32):
        d=lax.rem(b*8+f+k,32)
        pl.semaphore_signal(bar,inc=1,device_id=(d//8,lax.rem(d,8)),device_id_type=MESH)
    pl.semaphore_wait(bar,31)
    P=(pa_ref,pb_ref,pc_ref); O=(oa_ref,ob_ref,oc_ref)
    def blk(g,j,ff):
        return P[g].at[j,ff] if g<2 else P[g].at[ff,j]
    tw=[]
    order=[(1,z3,yb),(1,z2,yb),(1,z3,y),(1,z2,y),(1,z1,yb),(1,z,yb),(0,z3,yb),(0,z2,yb),(0,z1,yb),(0,z,yb),(0,z3,y),(0,z2,y),(1,z1,y),(0,z1,y),(0,z,y),(1,z,y)]
    mine=(b,bx); his=(bc,bxc)
    loads=[]
    for g in range(NG):
        for i,(jj,zz,yy) in enumerate(order):
            ff=zz*2+yy
            cp=pltpu.make_async_remote_copy(src_ref=blk(g,his[jj],ff),dst_ref=r0.at[g,i],send_sem=s0_send.at[g,i],recv_sem=s0_recv.at[g,i],device_id=(bc,f),device_id_type=MESH)
            cp.start(); tw.append((cp,None))
            ld=pltpu.make_async_copy(blk(g,mine[jj],ff),t.at[g,i],ld_sem.at[g,i]); ld.start(); loads.append(ld)
    sms=[]
    for k in range(1,32):
        d=lax.rem(b*8+f+k,32)
        cp=pltpu.make_async_remote_copy(src_ref=small_ref.at[lax.rem(d,8)],dst_ref=so_ref.at[b*8+f],send_sem=sm_send.at[k],recv_sem=sm_recv.at[b*8+f],device_id=(d//8,lax.rem(d,8)),device_id_type=MESH)
        cp.start(); sms.append(cp)
    own=pltpu.make_async_copy(small_ref.at[f],so_ref.at[b*8+f],sm_send.at[0]); own.start()
    def wait_on(ref,sem): pltpu.make_async_copy(ref,ref,sem).wait()
    def base(g,i):
        loads[g*16+i].wait(); wait_on(r0.at[g,i],s0_recv.at[g,i])
    def add(dst,srcs):
        @pl.loop(0,ROWS//16)
        def _(k):
            rows=pl.ds(pl.multiple_of(k*16,16),16)
            v=srcs[0][rows,:].astype(jnp.float32)
            for s in srcs[1:]: v=v+s[rows,:].astype(jnp.float32)
            dst[rows,:]=v.astype(dst.dtype)
    cnt=[0]*3
    def send(g,src,dst,rsem,dev,cond=None):
        i=cnt[g]; cnt[g]+=1
        cp=pltpu.make_async_remote_copy(src_ref=src,dst_ref=dst,send_sem=send_sem.at[g,i],recv_sem=rsem,device_id=dev,device_id_type=MESH)
        if cond is None: cp.start()
        else:
            @pl.when(cond)
            def _(): cp.start()
        tw.append((cp,cond))
    X=(bx,f); Y=(b,fy)
    def a4x(g,i,slot):
        base(g,i); add(t.at[g,i],[t.at[g,i],r0.at[g,i]]); send(g,t.at[g,i],rx4.at[g,slot],rx4_s.at[g,slot],X)
    def a2(g,i,slot):
        base(g,i); add(t.at[g,i],[t.at[g,i],r0.at[g,i]]); send(g,t.at[g,i],rx2.at[g,slot],rx2_s.at[g,slot],X)
    def a4y(g,i,slot):
        base(g,i); add(t.at[g,i],[t.at[g,i],r0.at[g,i]]); send(g,t.at[g,i],ry4.at[g,slot],ry4_s.at[g,slot],Y)
    def a3(g,i,slot,rslot):
        base(g,i)
        s=[t.at[g,i],r0.at[g,i]]
        if rslot is not None:
            wait_on(rx4.at[g,rslot],rx4_s.at[g,rslot]); s.append(rx4.at[g,rslot])
        add(t.at[g,i],s); send(g,t.at[g,i],ry3.at[g,slot],ry3_s.at[g,slot],Y)
    def m(g,i,zz,rslot,yslot):
        base(g,i)
        s=[t.at[g,i],r0.at[g,i]]
        if rslot is not None:
            wait_on(rx2.at[g,rslot],rx2_s.at[g,rslot]); s.append(rx2.at[g,rslot])
        wait_on(ry3.at[g,yslot],ry3_s.at[g,yslot]); s.append(ry3.at[g,yslot])
        behind=jnp.where(zz>z,z>0,z<3)
        add(t.at[g,i],s)
        @pl.when(behind)
        def _():
            wait_on(rz.at[g,zz],rz_s.at[g,zz]); add(t.at[g,i],[t.at[g,i],rz.at[g,zz]])
        nz=jnp.where(zz>z,z+1,z-1)
        slot=jnp.where(jnp.logical_and(zz==nz,zz<z),4,zz)
        send(g,t.at[g,i],rz.at[g,slot],rz_s.at[g,slot],(b,nz*2+y))
    def n(g,i):
        base(g,i); wait_on(ry4.at[g,1],ry4_s.at[g,1])
        add(t.at[g,i],[t.at[g,i],r0.at[g,i],ry4.at[g,1]]); send(g,t.at[g,i],rn.at[g],rn_s.at[g],(b,fz1))
    def t1(g,i):
        base(g,i); wait_on(ry3.at[g,0],ry3_s.at[g,0])
        add(t.at[g,i],[t.at[g,i],r0.at[g,i],ry3.at[g,0]])
        @pl.when(z>0)
        def _():
            wait_on(rz.at[g,z],rz_s.at[g,z]); add(t.at[g,i],[t.at[g,i],rz.at[g,z]])
        @pl.when(z<3)
        def _():
            wait_on(rz.at[g,4],rz_s.at[g,4]); add(t.at[g,i],[t.at[g,i],rz.at[g,4]])
        send(g,t.at[g,i],rt.at[g,0],rt_s.at[g,0],X)
    def t2(g,i):
        base(g,i); wait_on(ry4.at[g,0],ry4_s.at[g,0]); wait_on(rn.at[g],rn_s.at[g])
        add(t.at[g,i],[t.at[g,i],r0.at[g,i],ry4.at[g,0],rn.at[g]])
        send(g,t.at[g,i],rt.at[g,1],rt_s.at[g,1],X)
    def final(g):
        for q,(i,slot,j) in enumerate(((14,1,b),(15,0,bx))):
            wait_on(rt.at[g,slot],rt_s.at[g,slot])
            add(fin.at[g,q],[t.at[g,i],rt.at[g,slot]])
            cp=pltpu.make_async_copy(fin.at[g,q],O[g].at[j],o_loc.at[g,q]); cp.start()
            rc=pltpu.make_async_remote_copy(src_ref=fin.at[g,q],dst_ref=O[g].at[j],send_sem=o_send.at[g,q],recv_sem=o_recv.at[g,q],device_id=(bc,f),device_id_type=MESH)
            rc.start(); tw.append((rc,None)); loads2.append(cp)
    loads2=[]
    acts=[]
    for g in range(NG):
        a=[lambda g=g: a4x(g,0,0), lambda g=g: a4x(g,1,1), lambda g=g: a2(g,2,0), lambda g=g: a4y(g,4,1), lambda g=g: a2(g,3,1), lambda g=g: a4y(g,5,0),
           lambda g=g: a3(g,8,1,None), lambda g=g: a3(g,6,3,0), lambda g=g: a3(g,7,2,1), lambda g=g: a3(g,9,0,None)]
        e=[lambda g=g: m(g,10,z3,0,3), lambda g=g: m(g,11,z2,1,2), lambda g=g: n(g,12), lambda g=g: m(g,13,z1,None,1), lambda g=g: t2(g,15), lambda g=g: t1(g,14), lambda g=g: final(g)]
        acts.append((a,e))
    seq=list(acts[0][0])
    for g in range(NG):
        e=acts[g][1]; a=acts[g+1][0] if g+1<NG else []
        k=max(len(e),len(a))
        for i in range(k):
            if i<len(a): seq.append(a[i])
            if i<len(e): seq.append(e[i])
    for s in seq: s()
    for g in range(NG):
        for q,j in enumerate((bc,bxc)):
            wait_on(O[g].at[j],o_recv.at[g,q])
    for cp,cond in tw:
        if cond is None: cp.wait_send()
        else:
            @pl.when(cond)
            def _(cp=cp): cp.wait_send()
    for cp in loads2: cp.wait()
    own.wait()
    for cp in sms: cp.wait_send()
    for k in range(1,32):
        d=lax.rem(b*8+f+k,32)
        wait_on(so_ref.at[d],sm_recv.at[d])

def reduce(small,pa,pb,pc):
    A=pl.BlockSpec(memory_space=pl.ANY)
    D=pltpu.SemaphoreType.DMA
    B=jnp.bfloat16
    def V(*s,dt=B): return pltpu.VMEM(s+(ROWS,WID),dt)
    return pl.pallas_call(reduce_kernel,
        out_shape=(jax.ShapeDtypeStruct((32,8,256),jnp.float32),)+(jax.ShapeDtypeStruct((4,ROWS,WID),jnp.float32),)*3,
        in_specs=[A]*4,out_specs=(A,)*4,
        scratch_shapes=[V(3,16),V(3,16),V(3,2),V(3,2),V(3,4),V(3,2),V(3),V(3,5),V(3,2),V(3,2,dt=jnp.float32),
           D((3,16)),D((3,16)),D((3,16)),D((3,24)),D((3,2)),D((3,2)),D((3,4)),D((3,2)),D((3,)),D((3,5)),D((3,2)),D((3,2)),D((3,2)),D((3,2)),D((32,)),D((32,))],
        compiler_params=pltpu.CompilerParams(collective_id=2,has_side_effects=True,vmem_limit_bytes=63<<20),name="reduce_grads")(small,pa,pb,pc)


def attend_head_back(q, k, v, g, off, width):
    lanes = lax.broadcasted_iota(jnp.int32, (1, width), 1)
    keep = jnp.logical_and(lanes >= off, lanes < off + HEAD_DIM)
    q = jnp.where(keep, q, jnp.zeros_like(q))
    g = jnp.where(keep, g, jnp.zeros_like(g))
    k_own = jnp.where(keep, k, jnp.zeros_like(k))
    nt = (((1,), (1,)), ((), ()))
    scores = lax.dot_general(k, q, nt, preferred_element_type=jnp.float32) * HEAD_DIM ** (-0.5)
    e = jnp.exp(scores - jnp.max(scores, axis=0, keepdims=True))
    probs = e * (1.0 / jnp.sum(e, axis=0, keepdims=True))
    grad_probs = lax.dot_general(v, g, nt, preferred_element_type=jnp.float32)
    row = jnp.sum(probs * grad_probs, axis=0, keepdims=True)
    grad_scores = (probs * (grad_probs - row)).astype(jnp.bfloat16)
    grad_v = jnp.dot(probs.astype(jnp.bfloat16), g, preferred_element_type=jnp.float32)
    grad_k = jnp.dot(grad_scores, q, preferred_element_type=jnp.float32) * HEAD_DIM ** (-0.5)
    grad_q = lax.dot_general(
        grad_scores, k_own, (((0,), (0,)), ((), ())), preferred_element_type=jnp.float32
    ) * HEAD_DIM ** (-0.5)
    return grad_q, grad_k, grad_v


def attend_back_kernel(q_ref, k_ref, v_ref, g_ref, dq_ref, dk_ref, dv_ref, aq, ak, av):
    for acc in (aq, ak, av):
        acc[...] = jnp.zeros_like(acc)
    for h in range(q_ref.shape[1] // HEAD_DIM):
        low, width, off = head_window(h)
        cols = slice(low, low + width)
        out = attend_head_back(q_ref[:, cols], k_ref[:, cols], v_ref[:, cols], g_ref[:, cols], off, width)
        for acc, part in zip((aq, ak, av), out):
            acc[:, cols] += part
    for ref, acc in zip((dq_ref, dk_ref, dv_ref), (aq, ak, av)):
        ref[...] = acc[...].astype(jnp.bfloat16)


def attend_grads(q, k, v, g, length):
    rows, width = q.shape
    spec = pl.BlockSpec((length, width), lambda i: (i, 0))
    return pl.pallas_call(
        attend_back_kernel,
        grid=(rows // length,),
        out_shape=(jax.ShapeDtypeStruct((rows, width), jnp.bfloat16),) * 3,
        in_specs=[spec] * 4,
        out_specs=(spec,) * 3,
        scratch_shapes=[pltpu.VMEM((length, width), jnp.float32)] * 3,
        compiler_params=pltpu.CompilerParams(vmem_limit_bytes=40 << 20),
        name="attend_grads",
    )(q, k, v, g)


def on_device_fast(
    latents, cond, live, w_ada, b_ada, w_qkv, b_qv, w_proj, b_proj, w_fc1, b_fc1, w_fc2, b_fc2, cotangent
):
    images, length, width = latents.shape[1:]
    rows = images * length
    f32 = jnp.float32
    scaled = jax.nn.silu(cond[0]).astype(jnp.bfloat16)
    mod_part = jnp.dot(scaled, w_ada, preferred_element_type=f32) + b_ada.astype(f32)
    at = lax.axis_index("fsdp")

    def place(part, total):
        return lax.dynamic_update_slice(jnp.zeros((total,), f32), part, (at * part.shape[0],))

    parts = (mod_part, b_qv.astype(f32), b_proj.astype(f32), b_fc1.astype(f32), b_fc2.astype(f32))
    vec = jnp.concatenate([place(p, 8 * p.shape[0]) for p in parts] + [jnp.zeros((2 * width,), f32)]).reshape(16, width)
    la = jnp.concatenate([jnp.transpose(w_qkv.reshape(ROWS, 3, WID), (1, 0, 2)), w_proj[None]])
    lb = jnp.transpose(w_fc1.reshape(ROWS, 4, WID), (1, 0, 2))
    lc = w_fc2.reshape(4, ROWS, WID)
    live_mask = (lax.iota(jnp.int32, images) < live[0, 0]).astype(f32)
    row_mask = jnp.repeat(live_mask, length)[:, None]
    x_rows = latents[0].reshape(rows, width)
    res = cotangent[0].reshape(rows, width) * row_mask.astype(jnp.bfloat16)
    vec, wa, wb, wc, h_first, qkv, attended, branch, middle, h_second, slope, hidden, grad_out, grad_fc2 = forward(vec, la, lb, lc, x_rows, res)
    modulation = vec[:6]
    bias_fc2 = vec[13]
    wc = wc.reshape(4 * width, width)
    flat_rows = x_rows.astype(f32)

    def dense_x(left, right):
        return jnp.dot(left, right, preferred_element_type=f32)

    mlp_out = dense_x(hidden, wc) + bias_fc2
    block_out = ((middle + modulation[5] * mlp_out) * row_mask).astype(jnp.bfloat16)
    grad_res = res.astype(f32)
    grad_gate_two = jnp.sum(grad_res * mlp_out, axis=0)

    def outer(left, right):
        return jnp.einsum("rd,re->de", left, right, preferred_element_type=f32)

    grad_bfc2 = jnp.sum(grad_out.astype(f32), axis=0)
    grad_pre, grad_fc1 = [], []
    grad_h2 = 0.0
    for j in range(4):
        wcj = wc[j * width : (j + 1) * width]
        grad_hidden = jnp.einsum("rd,fd->rf", grad_out, wcj, preferred_element_type=f32)
        gp = (grad_hidden * slope[:, j * width : (j + 1) * width]).astype(jnp.bfloat16)
        grad_pre.append(gp)
        grad_fc1.append(outer(h_second, gp).astype(jnp.bfloat16))
        grad_h2 = grad_h2 + jnp.einsum("rf,df->rd", gp, wb[j], preferred_element_type=f32)
    grad_bfc1 = jnp.concatenate([jnp.sum(g.astype(f32), axis=0) for g in grad_pre])
    second_pull = jax.vjp(modulate, middle, modulation[3], modulation[4])[1]
    grad_mid_norm, grad_shift_two, grad_scale_two = second_pull(grad_h2)
    grad_mid = grad_res + grad_mid_norm
    grad_branch = (modulation[2] * grad_mid).astype(jnp.bfloat16)
    grad_gate_one = jnp.sum(grad_mid * branch, axis=0)
    grad_proj = outer(attended, grad_branch).astype(jnp.bfloat16)
    grad_bproj = jnp.sum(grad_branch.astype(f32), axis=0)
    grad_att = jnp.einsum("re,de->rd", grad_branch, wa[3], preferred_element_type=f32).astype(jnp.bfloat16)
    grads = attend_grads(qkv[0], qkv[1], qkv[2], grad_att, length)
    grad_bqv = [jnp.sum(grads[i].astype(f32), axis=0) for i in (0, 2)]
    grad_wa = [outer(h_first, g).astype(jnp.bfloat16) for g in grads] + [grad_proj]
    grad_h1 = sum(jnp.einsum("re,de->rd", g, wa[i], preferred_element_type=f32) for i, g in enumerate(grads))
    first_pull = jax.vjp(modulate, flat_rows, modulation[0], modulation[1])[1]
    grad_rows_norm, grad_shift_one, grad_scale_one = first_pull(grad_h1)
    grad_rows = grad_mid + grad_rows_norm
    grad_mod = jnp.concatenate(
        [grad_shift_one, grad_scale_one, grad_gate_one, grad_shift_two, grad_scale_two, grad_gate_two]
    )
    out_small = jnp.concatenate(
        [
            grad_mod.reshape(8, 864),
            jnp.concatenate(grad_bqv).reshape(8, 288),
            grad_bproj.reshape(8, ROWS),
            grad_bfc1.reshape(8, 576),
            grad_bfc2.reshape(8, ROWS),
            jnp.zeros((8, 32), f32),
        ],
        axis=1,
    ).reshape(8, 8, 256)
    so2, oa, ob, oc = reduce(
        out_small,
        jnp.stack(grad_wa).reshape(4, 8, ROWS, width),
        jnp.stack(grad_fc1).reshape(4, 8, ROWS, width),
        grad_fc2.reshape(8, 4, ROWS, width),
    )
    per_bin = jnp.sum(so2.reshape(4, 8, 2048), axis=1)
    sums = jnp.sum(per_bin, axis=0)
    mod_bins = per_bin[:, :864]
    scaled_bins = lax.all_gather(scaled, "bin", axis=0)
    grad_wada = jnp.einsum("bd,be->de", scaled_bins.astype(f32), mod_bins, precision=lax.Precision.HIGHEST)
    mod_mine = lax.dynamic_index_in_dim(mod_bins, lax.axis_index("bin"), 0, keepdims=False)
    grad_scaled = jnp.sum(w_ada.astype(f32) * mod_mine[None, :], axis=1)
    grad_scaled = lax.psum(grad_scaled, "fsdp")
    silu_pull = jax.vjp(jax.nn.silu, cond[0])[1]
    grad_cond = silu_pull(grad_scaled)[0][None, :]
    return (
        block_out.reshape(latents.shape),
        grad_rows.reshape(latents.shape),
        grad_cond,
        grad_wada,
        sums[:864],
        jnp.transpose(oa[:3], (1, 0, 2)).reshape(ROWS, 3 * width),
        sums[864:1152],
        oa[3],
        sums[1152:1296],
        jnp.transpose(ob, (1, 0, 2)).reshape(ROWS, 4 * width),
        sums[1296:1872],
        oc.reshape(4 * ROWS, width),
        sums[1872:2016],
    )


def solution(mesh):
    fast = mesh.shape["bin"] == 4 and mesh.shape["fsdp"] == 8
    return jax.shard_map(
        on_device_fast if fast else on_device_generic,
        mesh=mesh,
        in_specs=(
            P("bin", "fsdp", None, None),
            P("bin", None),
            P("bin", "fsdp"),
            P(None, "fsdp"),
            P("fsdp"),
            P("fsdp", None),
            P("fsdp"),
            P("fsdp", None),
            P("fsdp"),
            P("fsdp", None),
            P("fsdp"),
            P("fsdp", None),
            P("fsdp"),
            P("bin", "fsdp", None, None),
        ),
        out_specs=(
            P("bin", "fsdp", None, None),
            P("bin", "fsdp", None, None),
            P("bin", None),
            P(None, "fsdp"),
            P("fsdp"),
            P("fsdp", None),
            P("fsdp"),
            P("fsdp", None),
            P("fsdp"),
            P("fsdp", None),
            P("fsdp"),
            P("fsdp", None),
            P("fsdp"),
        ),
        check_vma=False,
    )
```

```python
import functools

import jax
import jax.numpy as jnp
from jax import lax
from jax.experimental import pallas as pl
from jax.experimental.pallas import tpu as pltpu
from jax.sharding import PartitionSpec as P

HEAD_DIM = 72
MESH = pl.DeviceIdType.MESH
ROWS = 144
WID = 1152
NG = 3


def layer_norm(field):
    center = field - jnp.mean(field, axis=-1, keepdims=True)
    return center * lax.rsqrt(jnp.mean(center * center, axis=-1, keepdims=True) + 1e-06)


def gelu_tanh(field):
    return (
        0.5
        * field
        * (1.0 + jnp.tanh(0.7978845608028654 * (field + 0.044715 * field * field * field)))
    )


def modulate(field, shift_vec, scale_vec):
    return layer_norm(field) * (1.0 + scale_vec) + shift_vec


def pair_scores(query_block, key_block):
    return jnp.einsum(
        "gqhd,gkhd->ghqk", query_block, key_block, preferred_element_type=jnp.float32
    ) * HEAD_DIM ** (-0.5)


def attend_pair(group_item):
    query_block, key_block, value_block = group_item
    scores = pair_scores(query_block, key_block)
    highest = jnp.max(scores, axis=-1, keepdims=True)
    exp_scores = jnp.exp(scores - highest)
    totals = jnp.sum(exp_scores, axis=-1, keepdims=True)
    attn_probs = (exp_scores / totals).astype(jnp.bfloat16)
    attended = jnp.einsum(
        "ghqk,gkhd->gqhd", attn_probs, value_block, preferred_element_type=jnp.float32
    )
    return (attended, (highest + jnp.log(totals))[..., 0])


def attend_back(group_item):
    query_block, key_block, value_block, log_total, grad_att = group_item
    scores = pair_scores(query_block, key_block)
    attn_probs = jnp.exp(scores - log_total[..., None])
    grad_probs = jnp.einsum(
        "gqhd,gkhd->ghqk", grad_att, value_block, preferred_element_type=jnp.float32
    )
    row_terms = jnp.sum(attn_probs * grad_probs, axis=-1, keepdims=True)
    grad_scores = (attn_probs * (grad_probs - row_terms)).astype(jnp.bfloat16)
    grad_query = jnp.einsum(
        "ghqk,gkhd->gqhd", grad_scores, key_block, preferred_element_type=jnp.float32
    ) * HEAD_DIM ** (-0.5)
    grad_key = jnp.einsum(
        "ghqk,gqhd->gkhd", grad_scores, query_block, preferred_element_type=jnp.float32
    ) * HEAD_DIM ** (-0.5)
    grad_value = jnp.einsum(
        "ghqk,gqhd->gkhd",
        attn_probs.astype(jnp.bfloat16),
        grad_att,
        preferred_element_type=jnp.float32,
    )
    return jnp.stack([grad_query, grad_key, grad_value], axis=2)


def run_block(flat_rows, modulation, weights, images, length):
    full_qkv, full_proj, full_fc1, full_fc2, bias_qv, bias_proj, bias_fc1, bias_fc2 = weights
    width = flat_rows.shape[1]
    heads = width // HEAD_DIM
    pieces = jnp.split(modulation, 6)
    h_first = modulate(flat_rows, pieces[0], pieces[1]).astype(jnp.bfloat16)
    qkv_bias = jnp.concatenate(
        [bias_qv[:width], jnp.zeros((width,), jnp.bfloat16), bias_qv[width:]]
    ).astype(jnp.float32)
    qkv_rows = (jnp.dot(h_first, full_qkv, preferred_element_type=jnp.float32) + qkv_bias).astype(
        jnp.bfloat16
    )
    split_rows = qkv_rows.reshape(images // 2, 2, length, 3, heads, HEAD_DIM)
    attended, log_total = lax.map(
        attend_pair, (split_rows[:, :, :, 0], split_rows[:, :, :, 1], split_rows[:, :, :, 2])
    )
    attended = attended.reshape(images * length, width).astype(jnp.bfloat16)
    branch = jnp.dot(attended, full_proj, preferred_element_type=jnp.float32) + bias_proj.astype(
        jnp.float32
    )
    middle = flat_rows + pieces[2] * branch
    h_second = modulate(middle, pieces[3], pieces[4]).astype(jnp.bfloat16)
    pre_act = jnp.dot(h_second, full_fc1, preferred_element_type=jnp.float32) + bias_fc1.astype(
        jnp.float32
    )
    hidden = gelu_tanh(pre_act).astype(jnp.bfloat16)
    mlp_out = jnp.dot(hidden, full_fc2, preferred_element_type=jnp.float32) + bias_fc2.astype(
        jnp.float32
    )
    result = middle + pieces[5] * mlp_out
    return (
        h_first,
        split_rows,
        log_total,
        attended,
        branch,
        middle,
        h_second,
        pre_act,
        hidden,
        mlp_out,
        result,
    )


def on_device_generic(
    latents,
    cond,
    live,
    w_ada,
    b_ada,
    w_qkv,
    b_qv,
    w_proj,
    b_proj,
    w_fc1,
    b_fc1,
    w_fc2,
    b_fc2,
    cotangent,
):
    images = latents.shape[1]
    length = latents.shape[2]
    width = latents.shape[3]
    heads = width // HEAD_DIM
    scaled = jax.nn.silu(cond[0]).astype(jnp.bfloat16)
    mod_part = jnp.dot(scaled, w_ada, preferred_element_type=jnp.float32) + b_ada.astype(
        jnp.float32
    )
    modulation = lax.all_gather(mod_part, "fsdp", axis=0, tiled=True)
    gathered = (
        lax.all_gather(w_qkv, "fsdp", axis=0, tiled=True),
        lax.all_gather(w_proj, "fsdp", axis=0, tiled=True),
        lax.all_gather(w_fc1, "fsdp", axis=0, tiled=True),
        lax.all_gather(w_fc2, "fsdp", axis=0, tiled=True),
        lax.all_gather(b_qv, "fsdp", axis=0, tiled=True),
        lax.all_gather(b_proj, "fsdp", axis=0, tiled=True),
        lax.all_gather(b_fc1, "fsdp", axis=0, tiled=True),
        lax.all_gather(b_fc2, "fsdp", axis=0, tiled=True),
    )
    flat_rows = latents[0].reshape(images * length, width).astype(jnp.float32)
    live_mask = (lax.iota(jnp.int32, images) < live[0, 0]).astype(jnp.float32)
    row_mask = jnp.repeat(live_mask, length)[:, None]
    forward_run = run_block(flat_rows, modulation, gathered, images, length)
    block_out = (forward_run[10] * row_mask).astype(jnp.bfloat16).reshape(latents.shape)
    weights = (
        lax.all_gather(w_qkv, "fsdp", axis=0, tiled=True),
        lax.all_gather(w_proj, "fsdp", axis=0, tiled=True),
        lax.all_gather(w_fc1, "fsdp", axis=0, tiled=True),
        lax.all_gather(w_fc2, "fsdp", axis=0, tiled=True),
        lax.all_gather(b_qv, "fsdp", axis=0, tiled=True),
        lax.all_gather(b_proj, "fsdp", axis=0, tiled=True),
        lax.all_gather(b_fc1, "fsdp", axis=0, tiled=True),
        lax.all_gather(b_fc2, "fsdp", axis=0, tiled=True),
    )
    full_qkv, full_proj, full_fc1, full_fc2 = (weights[0], weights[1], weights[2], weights[3])
    saved = run_block(flat_rows, modulation, weights, images, length)
    (
        h_first,
        split_rows,
        log_total,
        attended,
        branch,
        middle,
        h_second,
        pre_act,
        hidden,
        mlp_out,
        result,
    ) = saved
    pieces = jnp.split(modulation, 6)
    grad_res = cotangent[0].reshape(images * length, width).astype(jnp.float32) * row_mask
    grad_out = (pieces[5] * grad_res).astype(jnp.bfloat16)
    grad_gate_two = jnp.sum(grad_res * mlp_out, axis=0)
    grad_fc2 = jnp.einsum("rf,rd->fd", hidden, grad_out, preferred_element_type=jnp.float32)
    grad_bfc2 = jnp.sum(grad_out.astype(jnp.float32), axis=0)
    grad_hidden = jnp.einsum("rd,fd->rf", grad_out, full_fc2, preferred_element_type=jnp.float32)
    gelu_pull = jax.vjp(gelu_tanh, pre_act)[1]
    grad_pre = gelu_pull(grad_hidden)[0].astype(jnp.bfloat16)
    grad_fc1 = jnp.einsum("rd,rf->df", h_second, grad_pre, preferred_element_type=jnp.float32)
    grad_bfc1 = jnp.sum(grad_pre.astype(jnp.float32), axis=0)
    grad_h2 = jnp.einsum("rf,df->rd", grad_pre, full_fc1, preferred_element_type=jnp.float32)
    second_pull = jax.vjp(modulate, middle, pieces[3], pieces[4])[1]
    grad_mid_norm, grad_shift_two, grad_scale_two = second_pull(grad_h2)
    grad_mid = grad_res + grad_mid_norm
    grad_branch = (pieces[2] * grad_mid).astype(jnp.bfloat16)
    grad_gate_one = jnp.sum(grad_mid * branch, axis=0)
    grad_proj = jnp.einsum("rd,re->de", attended, grad_branch, preferred_element_type=jnp.float32)
    grad_bproj = jnp.sum(grad_branch.astype(jnp.float32), axis=0)
    grad_att = jnp.einsum(
        "re,de->rd", grad_branch, full_proj, preferred_element_type=jnp.float32
    ).astype(jnp.bfloat16)
    grad_att = grad_att.reshape(images // 2, 2, length, heads, HEAD_DIM)
    grad_qkv = lax.map(
        attend_back,
        (
            split_rows[:, :, :, 0],
            split_rows[:, :, :, 1],
            split_rows[:, :, :, 2],
            log_total,
            grad_att,
        ),
    )
    grad_qkv = grad_qkv.reshape(images * length, 3 * width).astype(jnp.bfloat16)
    grad_wqkv = jnp.einsum("rd,re->de", h_first, grad_qkv, preferred_element_type=jnp.float32)
    qkv_sums = jnp.sum(grad_qkv.astype(jnp.float32), axis=0)
    grad_bqv = jnp.concatenate([qkv_sums[:width], qkv_sums[2 * width :]])
    grad_h1 = jnp.einsum("re,de->rd", grad_qkv, full_qkv, preferred_element_type=jnp.float32)
    first_pull = jax.vjp(modulate, flat_rows, pieces[0], pieces[1])[1]
    grad_rows_norm, grad_shift_one, grad_scale_one = first_pull(grad_h1)
    grad_rows = grad_mid + grad_rows_norm
    grad_mod = jnp.concatenate(
        [
            grad_shift_one,
            grad_scale_one,
            grad_gate_one,
            grad_shift_two,
            grad_scale_two,
            grad_gate_two,
        ]
    )
    shards = (
        lax.psum_scatter(grad_wqkv, "fsdp", scatter_dimension=0, tiled=True),
        lax.psum_scatter(grad_proj, "fsdp", scatter_dimension=0, tiled=True),
        lax.psum_scatter(grad_fc1, "fsdp", scatter_dimension=0, tiled=True),
        lax.psum_scatter(grad_fc2, "fsdp", scatter_dimension=0, tiled=True),
        lax.psum_scatter(grad_bqv, "fsdp", scatter_dimension=0, tiled=True),
        lax.psum_scatter(grad_bproj, "fsdp", scatter_dimension=0, tiled=True),
        lax.psum_scatter(grad_bfc1, "fsdp", scatter_dimension=0, tiled=True),
        lax.psum_scatter(grad_bfc2, "fsdp", scatter_dimension=0, tiled=True),
        lax.psum_scatter(grad_mod, "fsdp", scatter_dimension=0, tiled=True),
    )
    mod_mine = shards[8]
    grad_wada = scaled.astype(jnp.float32)[:, None] * mod_mine[None, :]
    grad_scaled = jnp.dot(w_ada.astype(jnp.float32), mod_mine, precision=lax.Precision.HIGHEST)
    grad_scaled = lax.psum(grad_scaled, "fsdp")
    silu_pull = jax.vjp(jax.nn.silu, cond[0])[1]
    grad_cond = silu_pull(grad_scaled)[0][None, :]
    totals = lax.psum(
        (
            shards[0],
            shards[1],
            shards[2],
            shards[3],
            shards[4],
            shards[5],
            shards[6],
            shards[7],
            grad_wada,
            mod_mine,
        ),
        "bin",
    )
    return (
        block_out,
        grad_rows.reshape(latents.shape),
        grad_cond,
        totals[8],
        totals[9],
        totals[0],
        totals[4],
        totals[1],
        totals[5],
        totals[2],
        totals[6],
        totals[3],
        totals[7],
    )


TILE = 256
STRIP = 16


def coords():
    b = lax.axis_index("bin")
    f = lax.axis_index("fsdp")
    return b, f, b // 2, lax.rem(b, 2), f // 2, lax.rem(f, 2)


def strip_loop(rows, body):
    @pl.loop(0, rows // STRIP)
    def _(k):
        body(pl.ds(pl.multiple_of(k * STRIP, STRIP), STRIP))


def dense(left, right):
    return jnp.dot(left, right, preferred_element_type=jnp.float32)


def dense_nt(left, right):
    return lax.dot_general(left, right, (((1,), (1,)), ((), ())), preferred_element_type=jnp.float32)


def dense_tn(left, right):
    return lax.dot_general(left, right, (((0,), (0,)), ((), ())), preferred_element_type=jnp.float32)


def center_rows(v):
    v = v - jnp.mean(v, axis=-1, keepdims=True)
    inv = lax.rsqrt(jnp.mean(v * v, axis=-1, keepdims=True) + 1e-06)
    return v * inv, inv


def head_window(h):
    start = HEAD_DIM * h
    low = start // 128 * 128
    width = 128 if start - low + HEAD_DIM <= 128 else 256
    return low, width, start - low


def head_mask(off, width):
    lanes = lax.broadcasted_iota(jnp.int32, (1, width), 1)
    return jnp.logical_and(lanes >= off, lanes < off + HEAD_DIM)


def head_probs(q, k):
    scores = dense_nt(k, q) * HEAD_DIM ** (-0.5)
    e = jnp.exp(scores - jnp.max(scores, axis=0, keepdims=True))
    return e * (1.0 / jnp.sum(e, axis=0, keepdims=True))


def forward_kernel(
    vec_ref, la_ref, lb_ref, lc_ref, x_ref, res_ref,
    vec_out, wa_out, wb_out, wc_out, h1_out, qkv_out, att_out, branch_out, mid_out, h2_out, slope_out, hid_out, go_out, pc_out,
    wa, wb, wc, vecs, vec, xs, res, h1, qkv, att, mid, h2, hid, go, acc, slope, pst,
    loc_sem, sm_send, sm_recv, send_sem, recv_sem, in_sem, out_sem, wo_sem, co_sem, sl_sem, ps_sem,
):
    b, f, x, c, z, y = coords()
    bx = lax.rem(b + 2, 4)
    bc = b + 1 - 2 * c
    bxc = lax.rem(bc + 2, 4)
    fy = f + 1 - 2 * y
    yb = 1 - y
    z1 = z + 1 - 2 * lax.rem(z, 2)
    mid_z = jnp.logical_or(z == 1, z == 2)
    zb = lax.rem(z + 2, 4)
    zc = 3 - z
    z2 = jnp.where(mid_z, zc, zb)
    z3 = jnp.where(mid_z, zb, zc)
    fz1 = z1 * 2 + y
    bar = pltpu.get_barrier_semaphore()
    for k in range(1, 8):
        pl.semaphore_signal(bar, inc=1, device_id=(b, lax.rem(f + k, 8)), device_id_type=MESH)
    pl.semaphore_signal(bar, inc=1, device_id=(bx, f), device_id_type=MESH)
    pl.semaphore_signal(bar, inc=1, device_id=(bc, f), device_id_type=MESH)
    pl.semaphore_wait(bar, 9)

    W = (wa, wb, wc)
    L = (la_ref, lb_ref, lc_ref)

    def blk(g, j, ff):
        if g < 2:
            return W[g].at[j, pl.ds(pl.multiple_of(ff * ROWS, ROWS), ROWS)]
        return W[g].at[ff, j]

    smalls = []
    for k in range(1, 8):
        cp = pltpu.make_async_remote_copy(
            src_ref=vec_ref, dst_ref=vecs.at[f], send_sem=sm_send.at[k], recv_sem=sm_recv.at[f],
            device_id=(b, lax.rem(f + k, 8)), device_id_type=MESH,
        )
        cp.start()
        smalls.append(cp)
    own = pltpu.make_async_copy(vec_ref, vecs.at[f], sm_send.at[0])
    own.start()

    pend = []
    outs = []
    cnt = [0] * NG

    def send(g, j, ff, dev, cond=None, src=None):
        i = cnt[g]
        cnt[g] += 1
        cp = pltpu.make_async_remote_copy(
            src_ref=blk(g, j, ff) if src is None else src, dst_ref=blk(g, j, ff),
            send_sem=send_sem.at[g, i], recv_sem=recv_sem.at[g, j, ff], device_id=dev, device_id_type=MESH,
        )
        if cond is None:
            cp.start()
        else:
            @pl.when(cond)
            def _():
                cp.start()
        pend.append((cp, cond))

    def copy_out(src, dst, sem):
        cp = pltpu.make_async_copy(src, dst, sem)
        cp.start()
        return cp

    def arrive(g, j, ff, cond=None):
        def go_on():
            pltpu.make_async_copy(blk(g, j, ff), blk(g, j, ff), recv_sem.at[g, j, ff]).wait()
            if g == 2:
                copy_out(wc.at[ff, j], wc_out.at[ff, j], co_sem.at[j, ff])
        if cond is None:
            go_on()
        else:
            pl.when(cond)(go_on)

    up = (b, jnp.minimum(f + 2, 7))
    dn = (b, jnp.maximum(f - 2, 0))

    def init(g):
        sb = L[g].at[b]
        sx = L[g].at[bx]
        send(g, b, f, up, z < 3, sb)
        send(g, b, f, dn, z > 0, sb)
        send(g, b, f, (b, fy), None, sb)
        send(g, bx, f, (b, fz1), None, sx)
        send(g, bx, f, (b, fy), None, sx)

    locs = []

    def local(g):
        for j in range(4):
            locs.append(copy_out(L[g].at[j], blk(g, j, f), loc_sem.at[g, j]))

    def Z(g, zz, x_too):
        ff = zz * 2 + y
        arrive(g, b, ff)
        send(g, b, ff, up, jnp.logical_and(zz < z, z < 3))
        send(g, b, ff, dn, jnp.logical_and(zz > z, z > 0))
        send(g, b, ff, (b, fy))
        if x_too:
            send(g, b, ff, (bx, f))
        send(g, b, ff, (bc, f))

    def Y(g, zz, x_too):
        ff = zz * 2 + yb
        arrive(g, b, ff)
        if x_too:
            send(g, b, ff, (bx, f))
        send(g, b, ff, (bc, f))

    def X(g, ff):
        arrive(g, bx, ff)
        send(g, bx, ff, (bc, f))

    def actions(g):
        return [
            lambda: Z(g, z1, False), lambda: X(g, fz1), lambda: Y(g, z, False), lambda: X(g, fy),
            lambda: Z(g, z2, True), lambda: Y(g, z1, True), lambda: Z(g, z3, True), lambda: X(g, z2 * 2 + y),
            lambda: Y(g, z2, True), lambda: X(g, z1 * 2 + yb), lambda: X(g, z3 * 2 + y), lambda: Y(g, z3, True),
            lambda: X(g, z2 * 2 + yb), lambda: X(g, z3 * 2 + yb),
        ]

    def other_core(g):
        for zz in range(4):
            for jj in (bc, bxc):
                arrive(g, jj, zz * 2 + y, zz != z)
                arrive(g, jj, zz * 2 + yb)
        for cp in locs[g * 4 : g * 4 + 4]:
            cp.wait()

    def keep(src, dst, i):
        outs.append(copy_out(src, dst, out_sem.at[i]))

    def row(i):
        return vec[i : i + 1, :]

    def start_rows():
        own.wait()
        for k in range(1, 8):
            ff = lax.rem(f + k, 8)
            pltpu.make_async_copy(vecs.at[ff], vecs.at[ff], sm_recv.at[ff]).wait()
        total = vecs[0]
        for k in range(1, 8):
            total = total + vecs[k]
        vec[...] = total
        keep(vec, vec_out, 0)
        in_x.wait()

        def first(r):
            n, _ = center_rows(xs[r, :].astype(jnp.float32))
            h1[r, :] = (n * (1.0 + row(1)) + row(0)).astype(jnp.bfloat16)

        strip_loop(h1.shape[0], first)
        keep(h1, h1_out, 1)
        in_res.wait()

        def out_grad(r):
            go[r, :] = (res[r, :].astype(jnp.float32) * row(5)).astype(jnp.bfloat16)

        strip_loop(go.shape[0], out_grad)
        keep(go, go_out, 2)

    tiles = xs.shape[0] // TILE

    def tile(i):
        return pl.ds(pl.multiple_of(i * TILE, TILE), TILE)

    def project(j):
        @pl.loop(0, tiles)
        def _(i):
            v = dense(h1[tile(i), :], wa[j])
            if j != 1:
                v = v + row(6 + j // 2)
            qkv[j, tile(i), :] = v.astype(jnp.bfloat16)
        keep(qkv.at[j], qkv_out.at[j], 3 + j)

    def attention():
        @pl.loop(0, tiles)
        def _(i):
            acc[...] = jnp.zeros_like(acc)
            for h in range(WID // HEAD_DIM):
                low, width, off = head_window(h)
                cols = slice(low, low + width)
                mask = head_mask(off, width)
                q = qkv[0, tile(i), cols]
                v = qkv[2, tile(i), cols]
                probs = head_probs(jnp.where(mask, q, jnp.zeros_like(q)), qkv[1, tile(i), cols])
                acc[:, cols] += dense_tn(probs.astype(jnp.bfloat16), jnp.where(mask, v, jnp.zeros_like(v)))
            att[tile(i), :] = acc[...].astype(jnp.bfloat16)
        keep(att, att_out, 6)

    def branch():
        @pl.loop(0, tiles)
        def _(i):
            mid[tile(i), :] = dense(att[tile(i), :], wa[3]) + row(8)
        cp = copy_out(mid, branch_out, out_sem.at[7])
        cp.wait()

        def second(r):
            m = xs[r, :].astype(jnp.float32) + row(2) * mid[r, :]
            mid[r, :] = m
            n, _ = center_rows(m)
            h2[r, :] = (n * (1.0 + row(4)) + row(3)).astype(jnp.bfloat16)

        strip_loop(mid.shape[0], second)
        keep(mid, mid_out, 8)
        keep(h2, h2_out, 9)

    def hidden(j):
        cols = slice(j * WID, j * WID + WID)

        @pl.loop(0, tiles)
        def _(i):
            acc[...] = dense(h2[tile(i), :], wb[j]) + row(9 + j)

            @pl.when(j * tiles + i >= 1)
            def _():
                pltpu.make_async_copy(slope, slope_out.at[tile(0), :WID], sl_sem).wait()

            @pl.loop(0, TILE // STRIP)
            def _(k):
                r = pl.ds(pl.multiple_of(k * STRIP, STRIP), STRIP)
                v = acc[r, :]
                sq = v * v
                t = jnp.tanh(0.7978845608028654 * (v + 0.044715 * sq * v))
                half = 0.5 * (1.0 + t)
                slope[r, :] = half + 0.5 * v * (1.0 - t * t) * (0.7978845608028654 * (1.0 + 0.134145 * sq))
                hid[pl.ds(pl.multiple_of(i * TILE + k * STRIP, STRIP), STRIP), cols] = (v * half).astype(jnp.bfloat16)

            copy_out(slope, slope_out.at[tile(i), cols], sl_sem)
        if j == 3:
            pltpu.make_async_copy(slope, slope_out.at[tile(0), :WID], sl_sem).wait()
            keep(hid, hid_out, 10)

    part = pst.shape[1]

    def outer(j):
        @pl.loop(0, WID // part)
        def _(i):
            k = j * (WID // part) + i
            slot = lax.rem(k, 2)

            @pl.when(k >= 2)
            def _():
                pltpu.make_async_copy(pst.at[slot], pc_out.at[pl.ds(0, part)], ps_sem.at[slot]).wait()
            at = pl.multiple_of(k * part, part)
            pst[slot] = dense_tn(hid[:, pl.ds(at, part)], go[...]).astype(jnp.bfloat16)
            copy_out(pst.at[slot], pc_out.at[pl.ds(at, part)], ps_sem.at[slot])
        if j == 3:
            for slot in range(2):
                pltpu.make_async_copy(pst.at[slot], pc_out.at[pl.ds(0, part)], ps_sem.at[slot]).wait()

    def weights_out(g):
        outs.append(copy_out(W[g], (wa_out, wb_out)[g], wo_sem.at[g]))

    in_x = copy_out(x_ref, xs, in_sem.at[0])
    in_res = copy_out(res_ref, res, in_sem.at[1])
    acts = [actions(g) for g in range(NG)]
    run = lambda todo: [a() for a in todo]
    init(0)
    local(0)
    start_rows()
    run(acts[0][:8])
    init(1)
    local(1)
    run(acts[0][8:])
    run(acts[1][:5])
    other_core(0)
    weights_out(0)
    work = [lambda: project(0), lambda: project(1), lambda: project(2), attention, branch]
    ticks = [acts[1][5:6], acts[1][6:7], acts[1][7:8] + [lambda: init(2), lambda: local(2)], acts[1][8:11], acts[1][11:12]]
    for piece, tick in zip(work, ticks):
        piece()
        run(tick)
    run(acts[1][12:])
    run(acts[2][:5])
    other_core(1)
    weights_out(1)
    work = [functools.partial(hidden, j) for j in range(4)] + [functools.partial(outer, j) for j in range(4)]
    ticks = [acts[2][5 + i : 6 + i] for i in range(8)]
    for piece, tick in zip(work, ticks):
        piece()
        run(tick)
    run(acts[2][13:])
    for j in range(4):
        locs[8 + j].wait()
        copy_out(wc.at[f, j], wc_out.at[f, j], co_sem.at[j, f])
    other_core_c = 2
    for zz in range(4):
        for jj in (bc, bxc):
            arrive(other_core_c, jj, zz * 2 + y, zz != z)
            arrive(other_core_c, jj, zz * 2 + yb)
    for cp, cond in pend:
        if cond is None:
            cp.wait_send()
        else:
            @pl.when(cond)
            def _(cp=cp):
                cp.wait_send()
    for cp in smalls:
        cp.wait_send()
    for cp in outs:
        cp.wait()
    for ff in range(8):
        for j in range(4):
            pltpu.make_async_copy(wc.at[ff, j], wc_out.at[ff, j], co_sem.at[j, ff]).wait()


def forward(vec, la, lb, lc, x, res):
    any_space = pl.BlockSpec(memory_space=pl.ANY)
    f32, bf16 = jnp.float32, jnp.bfloat16
    rows = x.shape[0]
    sds = jax.ShapeDtypeStruct
    sem = pltpu.SemaphoreType.DMA
    mat = (rows, WID)
    outs = (
        sds((16, WID), f32), sds((4, WID, WID), bf16), sds((4, WID, WID), bf16), sds((8, 4, ROWS, WID), bf16),
        sds(mat, bf16), sds((3,) + mat, bf16), sds(mat, bf16), sds(mat, f32), sds(mat, f32), sds(mat, bf16),
        sds((rows, 4 * WID), f32), sds((rows, 4 * WID), bf16), sds(mat, bf16), sds((4 * WID, WID), bf16),
    )
    vm = pltpu.VMEM
    return pl.pallas_call(
        forward_kernel,
        out_shape=outs,
        in_specs=[any_space] * 6,
        out_specs=(any_space,) * len(outs),
        scratch_shapes=[
            vm((4, WID, WID), bf16), vm((4, WID, WID), bf16), vm((8, 4, ROWS, WID), bf16), vm((8, 16, WID), f32), vm((16, WID), f32),
            vm(mat, bf16), vm(mat, bf16), vm(mat, bf16), vm((3,) + mat, bf16), vm(mat, bf16), vm(mat, f32), vm(mat, bf16),
            vm((rows, 4 * WID), bf16), vm(mat, bf16), vm((TILE, WID), f32), vm((TILE, WID), f32), vm((2, 384, WID), bf16),
            sem((NG, 4)), sem((8,)), sem((8,)), sem((NG, 40)), sem((NG, 4, 8)), sem((2,)), sem((12,)), sem((2,)), sem((4, 8)), sem, sem((2,)),
        ],
        compiler_params=pltpu.CompilerParams(collective_id=1, has_side_effects=True, vmem_limit_bytes=63 << 20),
        name="forward",
    )(vec, la, lb, lc, x, res)


def backward_kernel(
    mask_ref, vec_ref, wa_ref, wb_ref, wc_ref, x_ref, res_ref, h1_ref, qkv_ref, att_ref, branch_ref, mid_ref, h2_ref, slope_ref,
    hid_ref, go_ref, pc_ref, ada_ref,
    sums_out, cond_out, oa_ref, ob_ref, oc_ref, block_out, lat_out, pa_ref, pb_ref,
    r0, ring, rx4, ry4, ry3, rx2, rn, rz, rt, fin, vec, wbuf, pst, mats, res, fl, sums8, smine, srecv, sall, ada, gvec, cmine, crecv,
    ring_sem, s0_send, s0_recv, send_sem, rx4_s, ry4_s, ry3_s, rx2_s, rn_s, rz_s, rt_s, o_loc, o_send, o_recv,
    w_sem, p_sem, m_sem, f_sem, sl_sem, out_sem, sm_send, sm_recv, ada_sem,
):
    f32, bf16 = jnp.float32, jnp.bfloat16
    b, f, x, c, z, y = coords()
    bx = lax.rem(b + 2, 4)
    bc = b + 1 - 2 * c
    bxc = lax.rem(bc + 2, 4)
    fy = f + 1 - 2 * y
    yb = 1 - y
    z1 = z + 1 - 2 * lax.rem(z, 2)
    mid_z = jnp.logical_or(z == 1, z == 2)
    zb = lax.rem(z + 2, 4)
    zc = 3 - z
    z2 = jnp.where(mid_z, zc, zb)
    z3 = jnp.where(mid_z, zb, zc)
    fz1 = z1 * 2 + y
    bar = pltpu.get_barrier_semaphore()
    for k in range(1, 8):
        pl.semaphore_signal(bar, inc=1, device_id=(b, lax.rem(f + k, 8)), device_id_type=MESH)
    pl.semaphore_signal(bar, inc=1, device_id=(bx, f), device_id_type=MESH)
    pl.semaphore_signal(bar, inc=1, device_id=(bc, f), device_id_type=MESH)
    pl.semaphore_wait(bar, 9)

    def start(src, dst, sem):
        cp = pltpu.make_async_copy(src, dst, sem)
        cp.start()
        return cp

    def wait_on(ref, sem):
        pltpu.make_async_copy(ref, ref, sem).wait()

    P = (pa_ref, pb_ref, pc_ref)
    O = (oa_ref, ob_ref, oc_ref)

    def blk(g, j, ff):
        if g < 2:
            return P[g].at[j, pl.ds(pl.multiple_of(ff * ROWS, ROWS), ROWS)]
        return P[g].at[ff, j]

    order = [
        (1, z3, yb), (1, z2, yb), (1, z3, y), (1, z2, y), (1, z1, yb), (1, z, yb), (0, z3, yb), (0, z2, yb),
        (0, z1, yb), (0, z, yb), (0, z3, y), (0, z2, y), (1, z1, y), (0, z1, y), (0, z, y), (1, z, y),
    ]
    mine = (b, bx)
    his = (bc, bxc)
    pend = []
    cnt = [0] * NG

    def open_group(g):
        for i, (jj, zz, yy) in enumerate(order):
            cp = pltpu.make_async_remote_copy(
                src_ref=blk(g, his[jj], zz * 2 + yy), dst_ref=r0.at[g, i], send_sem=s0_send.at[g, i],
                recv_sem=s0_recv.at[g, i], device_id=(bc, f), device_id_type=MESH,
            )
            cp.start()
            pend.append((cp, None))
        state["ready"].append(g)
        pump()

    state = {"ready": [], "issued": 0, "used": 0}
    depth = ring.shape[0]

    def pump():
        while state["issued"] < len(plan) and state["issued"] - state["used"] < depth:
            g, i = plan[state["issued"]]
            if g not in state["ready"]:
                return
            jj, zz, yy = order[i]
            slot = state["issued"] % depth
            start(blk(g, mine[jj], zz * 2 + yy), ring.at[slot], ring_sem.at[slot])
            state["issued"] += 1

    def add(dst, srcs):
        @pl.loop(0, ROWS // STRIP)
        def _(k):
            rows = pl.ds(pl.multiple_of(k * STRIP, STRIP), STRIP)
            v = srcs[0][rows, :].astype(f32)
            for s in srcs[1:]:
                v = v + s[rows, :].astype(f32)
            dst[rows, :] = v.astype(dst.dtype)

    def combine(g, i, more=(), cases=None):
        slot = state["used"] % depth
        assert plan[state["used"]] == (g, i)
        wait_on(ring.at[slot], ring_sem.at[slot])
        wait_on(r0.at[g, i], s0_recv.at[g, i])
        srcs = [r0.at[g, i], ring.at[slot]]
        for ref, sem in more:
            wait_on(ref, sem)
            srcs.append(ref)
        if cases is None:
            add(r0.at[g, i], srcs)
        else:
            for cond, extra in cases:
                @pl.when(cond)
                def _(extra=extra):
                    for ref, sem in extra:
                        wait_on(ref, sem)
                    add(r0.at[g, i], srcs + [ref for ref, _ in extra])
        state["used"] += 1
        pump()

    def send(g, src, dst, rsem, dev):
        i = cnt[g]
        cnt[g] += 1
        cp = pltpu.make_async_remote_copy(
            src_ref=src, dst_ref=dst, send_sem=send_sem.at[g, i], recv_sem=rsem, device_id=dev, device_id_type=MESH
        )
        cp.start()
        pend.append((cp, None))

    X = (bx, f)
    Y = (b, fy)

    def to_x4(g, i, slot):
        combine(g, i)
        send(g, r0.at[g, i], rx4.at[g, slot], rx4_s.at[g, slot], X)

    def to_x2(g, i, slot):
        combine(g, i)
        send(g, r0.at[g, i], rx2.at[g, slot], rx2_s.at[g, slot], X)

    def to_y4(g, i, slot):
        combine(g, i)
        send(g, r0.at[g, i], ry4.at[g, slot], ry4_s.at[g, slot], Y)

    def to_y3(g, i, slot, rslot):
        combine(g, i, () if rslot is None else ((rx4.at[g, rslot], rx4_s.at[g, rslot]),))
        send(g, r0.at[g, i], ry3.at[g, slot], ry3_s.at[g, slot], Y)

    def to_z(g, i, zz, rslot, yslot):
        more = [(ry3.at[g, yslot], ry3_s.at[g, yslot])]
        if rslot is not None:
            more.append((rx2.at[g, rslot], rx2_s.at[g, rslot]))
        behind = jnp.where(zz > z, z, 3 - z) > 0
        combine(g, i, more, [(behind, [(rz.at[g, zz], rz_s.at[g, zz])]), (jnp.logical_not(behind), [])])
        nz = jnp.where(zz > z, z + 1, z - 1)
        slot = jnp.where(jnp.logical_and(zz == nz, zz < z), 4, zz)
        send(g, r0.at[g, i], rz.at[g, slot], rz_s.at[g, slot], (b, nz * 2 + y))

    def to_near(g, i):
        combine(g, i, [(ry4.at[g, 1], ry4_s.at[g, 1])])
        send(g, r0.at[g, i], rn.at[g], rn_s.at[g], (b, fz1))

    def own_last(g, i):
        left = (rz.at[g, z], rz_s.at[g, z])
        right = (rz.at[g, 4], rz_s.at[g, 4])
        combine(g, i, [(ry3.at[g, 0], ry3_s.at[g, 0])], [(z == 0, [right]), (mid_z, [left, right]), (z == 3, [left])])
        send(g, r0.at[g, i], rt.at[g, 0], rt_s.at[g, 0], X)

    def other_last(g, i):
        combine(g, i, [(ry4.at[g, 0], ry4_s.at[g, 0]), (rn.at[g], rn_s.at[g])])
        send(g, r0.at[g, i], rt.at[g, 1], rt_s.at[g, 1], X)

    finals = []

    def final(g):
        if finals:
            for cp in finals[-2:]:
                cp[0].wait()
                cp[1].wait_send()
        for q, (i, slot, j) in enumerate(((14, 1, b), (15, 0, bx))):
            wait_on(rt.at[g, slot], rt_s.at[g, slot])
            add(fin.at[q], [r0.at[g, i], rt.at[g, slot]])
            loc = start(fin.at[q], O[g].at[j], o_loc.at[g, q])
            rc = pltpu.make_async_remote_copy(
                src_ref=fin.at[q], dst_ref=O[g].at[j], send_sem=o_send.at[g, q], recv_sem=o_recv.at[g, q],
                device_id=(bc, f), device_id_type=MESH,
            )
            rc.start()
            finals.append((loc, rc))

    def spread(g):
        return [
            (lambda: to_x4(g, 0, 0), 0), (lambda: to_x4(g, 1, 1), 1), (lambda: to_x2(g, 2, 0), 2), (lambda: to_y4(g, 4, 1), 4),
            (lambda: to_x2(g, 3, 1), 3), (lambda: to_y4(g, 5, 0), 5), (lambda: to_y3(g, 8, 1, None), 8),
            (lambda: to_y3(g, 6, 3, 0), 6), (lambda: to_y3(g, 7, 2, 1), 7), (lambda: to_y3(g, 9, 0, None), 9),
        ]

    def gather_up(g):
        return [
            (lambda: to_z(g, 10, z3, 0, 3), 10), (lambda: to_z(g, 11, z2, 1, 2), 11), (lambda: to_near(g, 12), 12),
            (lambda: to_z(g, 13, z1, None, 1), 13), (lambda: other_last(g, 15), 15), (lambda: own_last(g, 14), 14),
            (lambda: final(g), None),
        ]

    rows = res.shape[0]
    tiles = rows // TILE

    def tile(i):
        return pl.ds(pl.multiple_of(i * TILE, TILE), TILE)

    def row(i):
        return vec[i : i + 1, :]

    def load_mat(k, src):
        return start(src, mats.at[k], m_sem.at[k])

    def load_fl(k, src):
        return start(src, fl.at[k], f_sem.at[k])

    w_list = []
    for j in range(4):
        w_list += [wc_ref.at[j], wb_ref.at[j]]
    w_list += [wa_ref.at[3], wa_ref.at[0], wa_ref.at[1], wa_ref.at[2]] + [wc_ref.at[j] for j in range(4)]
    w_at = [0]

    def fetch(k):
        if k < len(w_list):
            start(w_list[k], wbuf.at[k % 2], w_sem.at[k % 2])

    def with_weight(body):
        k = w_at[0]
        w_at[0] += 1
        wait_on(wbuf.at[k % 2], w_sem.at[k % 2])
        body(wbuf.at[k % 2])
        fetch(k + 2)

    def colsum(i, v):
        sums8[i] += v[:8] + v[8:]

    p_cnt = [0]
    part = pst.shape[1]
    steps = WID // part

    def outer(left, right, dst):
        n = p_cnt[0]
        p_cnt[0] += 1

        @pl.loop(0, steps)
        def _(i):
            k = n * steps + i
            slot = lax.rem(k, 2)

            @pl.when(k >= 2)
            def _():
                wait_on(pst.at[slot], p_sem.at[slot])
            at = pl.multiple_of(i * part, part)
            pst[slot] = dense_tn(left[:, pl.ds(at, part)], right[...]).astype(bf16)
            start(pst.at[slot], dst.at[pl.ds(at, part)], p_sem.at[slot])

    def drain():
        for slot in range(2):
            wait_on(pst.at[slot], p_sem.at[slot])
        p_cnt[0] = 0

    GO, H2, GP, Q = 0, 1, 2, 3
    ATT, GB, GA, H1 = 0, 1, 2, 0

    def slope_load(k):
        if k < 4 * tiles:
            j, i = divmod(k, tiles)
            start(slope_ref.at[pl.ds(i * TILE, TILE), pl.ds(j * WID, WID)], fl.at[2, pl.ds((k % 2) * TILE, TILE)], sl_sem.at[k % 2])

    def mlp_back(j):
        def body(w):
            for i in range(tiles):
                k = j * tiles + i
                sl = fl.at[2, pl.ds((k % 2) * TILE, TILE)]
                fl[3, :TILE, :] = dense_nt(mats[GO, i * TILE : (i + 1) * TILE, :], w[...])
                wait_on(sl, sl_sem.at[k % 2])

                def strip(r):
                    v = (fl[3, r, :] * sl[r, :]).astype(bf16)
                    mats[GP, pl.ds(pl.multiple_of(i * TILE + r.start, STRIP), STRIP), :] = v
                    colsum(9 + j, v.astype(f32))

                strip_loop(TILE, strip)
                slope_load(k + 2)
        with_weight(body)

    def hidden_in(dst, j, left):
        def body(w):
            @pl.loop(0, tiles)
            def _(i):
                v = dense_nt(mats[left, tile(i), :], w[...])
                if j == 0:
                    fl[dst, tile(i), :] = v
                else:
                    fl[dst, tile(i), :] += v
        with_weight(body)

    def first_sums():
        def strip(r):
            colsum(13, mats[GO, r, :].astype(f32))
        strip_loop(rows, strip)

    def norm_two():
        wait_on(fl.at[1], f_sem.at[1])
        wait_on(fl.at[2], f_sem.at[2])

        def strip(r):
            n, inv = center_rows(fl[1, r, :])
            g = fl[0, r, :]
            colsum(4, g * n)
            colsum(3, g)
            dn = g * (1.0 + row(4))
            pull = dn - jnp.mean(dn, axis=-1, keepdims=True) - n * jnp.mean(dn * n, axis=-1, keepdims=True)
            gm = res[r, :].astype(f32) + inv * pull
            colsum(2, gm * fl[2, r, :])
            gb = (row(2) * gm).astype(bf16)
            colsum(8, gb.astype(f32))
            fl[1, r, :] = gm
            mats[GB, r, :] = gb

        strip_loop(rows, strip)

    def att_in():
        def body(w):
            @pl.loop(0, tiles)
            def _(i):
                mats[GA, tile(i), :] = dense_nt(mats[GB, tile(i), :], w[...]).astype(bf16)
        with_weight(body)

    def clear():
        def strip(r):
            for k in (0, 2, 3):
                fl[k, r, :] = jnp.zeros((STRIP, WID), f32)
        strip_loop(rows, strip)

    def att_back(heads):
        @pl.loop(0, tiles)
        def _(i):
            for h in heads:
                low, width, off = head_window(h)
                cols = slice(low, low + width)
                mask = head_mask(off, width)

                def pick(k):
                    v = mats[k, tile(i), cols]
                    return v, jnp.where(mask, v, jnp.zeros_like(v))

                _, q = pick(Q)
                k_all, k_own = pick(Q + 1)
                v_all = mats[Q + 2, tile(i), cols]
                _, g = pick(GA)
                probs = head_probs(q, k_all)
                grad_probs = dense_nt(v_all, g)
                total = jnp.sum(probs * grad_probs, axis=0, keepdims=True)
                gs = (probs * (grad_probs - total)).astype(bf16)
                fl[3, tile(i), cols] += dense(probs.astype(bf16), g)
                fl[2, tile(i), cols] += dense(gs, q) * HEAD_DIM ** (-0.5)
                fl[0, tile(i), cols] += dense_tn(gs, k_own) * HEAD_DIM ** (-0.5)

    def att_done():
        def strip(r):
            for k, a in enumerate((0, 2, 3)):
                v = fl[a, r, :].astype(bf16)
                mats[Q + k, r, :] = v
                if k != 1:
                    colsum(6 + k // 2, v.astype(f32))
        strip_loop(rows, strip)

    def norm_one():
        wait_on(mats.at[0], m_sem.at[0])

        def strip(r):
            n, inv = center_rows(mats[0, r, :].astype(f32))
            g = fl[0, r, :]
            colsum(1, g * n)
            colsum(0, g)
            dn = g * (1.0 + row(1))
            pull = dn - jnp.mean(dn, axis=-1, keepdims=True) - n * jnp.mean(dn * n, axis=-1, keepdims=True)
            fl[0, r, :] = fl[1, r, :] + inv * pull

        strip_loop(rows, strip)
        start(fl.at[0], lat_out, out_sem.at[0])

    def mlp_out(j):
        k = 1 + j
        wait_on(mats.at[k], m_sem.at[k])

        def body(w):
            @pl.loop(0, tiles)
            def _(i):
                v = dense(mats[k, tile(i), :], w[...])
                if j == 0:
                    fl[2, tile(i), :] = v
                else:
                    fl[2, tile(i), :] += v
        with_weight(body)

    def block_end():
        wait_on(fl.at[3], f_sem.at[3])
        for i in range(tiles):
            m = mask_ref[i]

            def strip(r):
                at = pl.ds(pl.multiple_of(i * TILE + r.start, STRIP), STRIP)
                v = fl[2, at, :] + row(13)
                colsum(5, v * res[at, :].astype(f32))
                mats[5, at, :] = ((fl[3, at, :] + row(5) * v) * m).astype(bf16)

            strip_loop(TILE, strip)
        start(mats.at[5], block_out, out_sem.at[1])

    def small_send(k, src, dst, dev):
        cp = pltpu.make_async_remote_copy(
            src_ref=src, dst_ref=dst, send_sem=sm_send.at[k], recv_sem=sm_recv.at[k], device_id=dev, device_id_type=MESH
        )
        cp.start()
        pend.append((cp, None))

    partners = [(b, fy), (b, fz1), (b, zb * 2 + y)]

    def small_first():
        for i in range(16):
            smine[0, i : i + 1, :] = jnp.sum(sums8[i], axis=0, keepdims=True)
        small_send(0, smine.at[0], srecv.at[0], partners[0])

    def small_step(k):
        wait_on(srecv.at[k], sm_recv.at[k])
        if k < 2:
            smine[k + 1] = smine[k] + srecv[k]
            small_send(k + 1, smine.at[k + 1], srecv.at[k + 1], partners[k + 1])
        else:
            sall[b] = smine[k] + srecv[k]
            sall[b, 14:15, :] = row(14).astype(bf16).astype(f32)
            small_send(3, sall.at[b], sall.at[b], X)
            small_send(4, sall.at[b], sall.at[b], (bc, f))

    def cond_first():
        at = 3 * f // 4
        for k in range(4):
            @pl.when(lax.rem(3 * f, 4) == k)
            def _(k=k):
                both = jnp.concatenate([sall[b, pl.ds(at, 1), :], sall[b, pl.ds(at + 1, 1), :]], axis=1)
                gvec[...] = both[:, 288 * k : 288 * k + gvec.shape[1]]
        wait_on(ada, ada_sem)
        v = gvec[...]
        high = v.astype(bf16)
        v = v - high.astype(f32)
        middle = v.astype(bf16)
        low = (v - middle.astype(f32)).astype(bf16)
        left = jnp.concatenate([high, middle, low, jnp.zeros((13, gvec.shape[1]), bf16)], axis=0)
        part_sum = dense(left, ada[...])
        cmine[0] = jnp.broadcast_to(jnp.sum(part_sum[:8], axis=0, keepdims=True), cmine.shape[1:])
        small_send(6, cmine.at[0], crecv.at[0], partners[0])

    def cond_step(k):
        wait_on(crecv.at[k], sm_recv.at[6 + k])
        cmine[k + 1] = cmine[k] + crecv[k]
        if k < 2:
            small_send(7 + k, cmine.at[k + 1], crecv.at[k + 1], partners[k + 1])
        else:
            start(cmine.at[3], cond_out, out_sem.at[5])

    def small_x():
        wait_on(sall.at[bx], sm_recv.at[3])
        small_send(5, sall.at[bx], sall.at[bx], (bc, f))

    def small_core():
        wait_on(sall.at[bc], sm_recv.at[4])
        wait_on(sall.at[bxc], sm_recv.at[5])
        start(sall, sums_out, out_sem.at[2])

    A, B, C = 0, 1, 2
    pieces1 = []
    for j in range(4):
        pieces1 += [
            functools.partial(mlp_back, j),
            functools.partial(outer, mats.at[H2], mats.at[GP], pb_ref.at[j]),
            functools.partial(hidden_in, 0, j, GP),
        ]

    def after_one():
        drain()
        open_group(B)
        load_mat(ATT, att_ref)
        load_fl(1, mid_ref)
        load_fl(2, branch_ref)

    def proj_outer():
        wait_on(mats.at[ATT], m_sem.at[ATT])
        outer(mats.at[ATT], mats.at[GB], pa_ref.at[3])

    def before_att():
        load_mat(H1, h1_ref)
        for k in range(3):
            wait_on(mats.at[Q + k], m_sem.at[Q + k])
        clear()

    heads = WID // HEAD_DIM
    pieces2 = [norm_two, proj_outer, att_in, before_att]
    pieces2 += [functools.partial(att_back, range(k, k + 4)) for k in range(0, heads, 4)] + [att_done]

    def a_outer(k):
        if k == 0:
            wait_on(mats.at[H1], m_sem.at[H1])
        outer(mats.at[H1], mats.at[Q + k], pa_ref.at[k])

    pieces2 += [functools.partial(a_outer, k) for k in range(3)]

    def after_two():
        drain()
        open_group(A)
        load_mat(0, x_ref)
        load_fl(3, mid_ref)
        for j in range(2):
            load_mat(1 + j, hid_ref.at[:, pl.ds(j * WID, WID)])

    def h1_in(k):
        hidden_in(0, k, Q + k)
        if k < 2:
            load_mat(Q + k, hid_ref.at[:, pl.ds((2 + k) * WID, WID)])

    pieces3 = [functools.partial(h1_in, k) for k in range(3)] + [norm_one]
    pieces3 += [functools.partial(mlp_out, j) for j in range(4)] + [block_end]
    tail = [small_first] + [functools.partial(small_step, k) for k in range(3)] + [cond_first, small_x] + [functools.partial(cond_step, k) for k in range(3)] + [small_core]

    def blend(*lists):
        out = []
        total = max(len(v) for v in lists)
        at = [0] * len(lists)
        for n in range(total):
            for k, v in enumerate(lists):
                upto = (n + 1) * len(v) // total
                out += v[at[k] : upto]
                at[k] = upto
        return out

    acts = {g: (spread(g), gather_up(g)) for g in range(NG)}
    seq = []
    seq += blend([(p, None) for p in pieces1], acts[C][0])
    seq += [(after_one, None)]
    seq += blend([(p, None) for p in pieces2], blend(acts[C][1], acts[B][0]))
    seq += [(after_two, None)]
    marks = {}

    def tag(g, part_list):
        return [(fn, (g, i) if i is not None else None) for fn, i in part_list]

    seq = blend([(p, None) for p in pieces1], tag(C, acts[C][0])) + [(after_one, None)]
    seq += blend([(p, None) for p in pieces2], blend(tag(C, acts[C][1]), tag(B, acts[B][0]))) + [(after_two, None)]
    seq += blend([(p, None) for p in pieces3 + tail], blend(tag(B, acts[B][1]), tag(A, acts[A][0])))
    seq += tag(A, acts[A][1])
    plan = [t for _, t in seq if t is not None]

    open_group(C)
    start(vec_ref, vec, out_sem.at[3])
    start(ada_ref, ada, ada_sem)
    load_mat(GO, go_ref)
    fetch(0)
    slope_load(0)
    load_mat(H2, h2_ref)
    fetch(1)
    slope_load(1)
    for k in range(3):
        load_mat(Q + k, qkv_ref.at[k])
    start(res_ref, res, out_sem.at[4])
    sums8[...] = jnp.zeros_like(sums8)
    wait_on(vec, out_sem.at[3])
    wait_on(mats.at[GO], m_sem.at[GO])
    wait_on(mats.at[H2], m_sem.at[H2])
    wait_on(res, out_sem.at[4])
    first_sums()
    for fn, _ in seq:
        fn()
    for loc, rc in finals[-2:]:
        loc.wait()
        rc.wait_send()
    for g in range(NG):
        for q, j in enumerate((bc, bxc)):
            wait_on(O[g].at[j], o_recv.at[g, q])
    for cp, _ in pend:
        cp.wait_send()
    wait_on(lat_out, out_sem.at[0])
    wait_on(block_out, out_sem.at[1])
    wait_on(sums_out, out_sem.at[2])
    wait_on(cond_out, out_sem.at[5])


def backward(mask, vec, wa, wb, wc, x, res, h1, qkv, att, branch, mid, h2, slope, hid, go, pc, w_ada):
    any_space = pl.BlockSpec(memory_space=pl.ANY)
    f32, bf16 = jnp.float32, jnp.bfloat16
    rows = x.shape[0]
    sds = jax.ShapeDtypeStruct
    sem = pltpu.SemaphoreType.DMA
    mat = (rows, WID)
    blkshape = (ROWS, WID)
    outs = (
        sds((4, 16, WID), f32), sds((8, WID), f32), sds((4,) + blkshape, f32), sds((4,) + blkshape, f32), sds((4,) + blkshape, f32),
        sds(mat, bf16), sds(mat, f32), sds((4, WID, WID), bf16), sds((4, WID, WID), bf16),
    )

    def vm(*shape, dt=bf16):
        return pltpu.VMEM(shape, dt)

    return pl.pallas_call(
        backward_kernel,
        out_shape=outs,
        in_specs=[pl.BlockSpec(memory_space=pltpu.SMEM)] + [any_space] * 17,
        out_specs=(any_space,) * len(outs),
        scratch_shapes=[
            vm(NG, 16, *blkshape), vm(4, *blkshape), vm(NG, 2, *blkshape), vm(NG, 2, *blkshape), vm(NG, 4, *blkshape), vm(NG, 2, *blkshape),
            vm(NG, *blkshape), vm(NG, 5, *blkshape), vm(NG, 2, *blkshape), vm(2, *blkshape, dt=f32),
            vm(16, WID, dt=f32), vm(2, WID, WID), vm(2, 384, WID), vm(6, *mat), vm(*mat), vm(4, *mat, dt=f32),
            vm(16, 8, WID, dt=f32), vm(3, 16, WID, dt=f32), vm(3, 16, WID, dt=f32), vm(4, 16, WID, dt=f32),
            vm(*w_ada.shape), vm(1, w_ada.shape[0], dt=f32), vm(4, 8, WID, dt=f32), vm(3, 8, WID, dt=f32),
            sem((4,)), sem((NG, 16)), sem((NG, 16)), sem((NG, 24)), sem((NG, 2)), sem((NG, 2)), sem((NG, 4)), sem((NG, 2)), sem((NG,)),
            sem((NG, 5)), sem((NG, 2)), sem((NG, 2)), sem((NG, 2)), sem((NG, 2)),
            sem((2,)), sem((2,)), sem((6,)), sem((4,)), sem((2,)), sem((6,)), sem((9,)), sem((9,)), sem,
        ],
        compiler_params=pltpu.CompilerParams(collective_id=2, has_side_effects=True, vmem_limit_bytes=64 << 20),
        name="backward",
    )(mask, vec, wa, wb, wc, x, res, h1, qkv, att, branch, mid, h2, slope, hid, go, pc, w_ada)


def on_device_fast(
    latents, cond, live, w_ada, b_ada, w_qkv, b_qv, w_proj, b_proj, w_fc1, b_fc1, w_fc2, b_fc2, cotangent
):
    images, length, width = latents.shape[1:]
    rows = images * length
    f32 = jnp.float32
    scaled = jax.nn.silu(cond[0]).astype(jnp.bfloat16)
    mod_part = jnp.dot(scaled, w_ada, preferred_element_type=f32) + b_ada.astype(f32)
    at = lax.axis_index("fsdp")

    def place(part, total):
        return lax.dynamic_update_slice(jnp.zeros((total,), f32), part, (at * part.shape[0],))

    parts = (mod_part, b_qv.astype(f32), b_proj.astype(f32), b_fc1.astype(f32), b_fc2.astype(f32))
    vec = jnp.concatenate([place(p, 8 * p.shape[0]) for p in parts] + [jnp.where(at == 0, scaled.astype(f32), 0.0), jnp.zeros((width,), f32)]).reshape(16, width)
    la = jnp.concatenate([jnp.transpose(w_qkv.reshape(ROWS, 3, WID), (1, 0, 2)), w_proj[None]])
    lb = jnp.transpose(w_fc1.reshape(ROWS, 4, WID), (1, 0, 2))
    lc = w_fc2.reshape(4, ROWS, WID)
    live_mask = (lax.iota(jnp.int32, images) < live[0, 0]).astype(f32)
    row_mask = jnp.repeat(live_mask, length)[:, None]
    x_rows = latents[0].reshape(rows, width)
    res = cotangent[0].reshape(rows, width) * row_mask.astype(jnp.bfloat16)
    vec, wa, wb, wc, h_first, qkv, attended, branch, middle, h_second, slope, hidden, grad_out, grad_fc2 = forward(vec, la, lb, lc, x_rows, res)
    sums, cond_sum, oa, ob, oc, block_out, grad_rows, _, _ = backward(
        live_mask, vec, wa, wb, wc.reshape(4, width, width), x_rows, res, h_first, qkv, attended, branch, middle, h_second, slope, hidden,
        grad_out, grad_fc2.reshape(8, 4, ROWS, width), jnp.transpose(w_ada),
    )
    flat = sums.reshape(4, 16 * width)
    total = jnp.sum(flat, axis=0)

    def mine(v, begin, size):
        return lax.dynamic_slice_in_dim(v, begin + at * size, size, axis=-1)

    mod_bins = mine(flat, 0, 6 * width // 8)
    grad_wada = jnp.einsum("bd,be->de", sums[:, 14], mod_bins, precision=lax.Precision.HIGHEST)
    silu_pull = jax.vjp(jax.nn.silu, cond[0])[1]
    grad_cond = silu_pull(cond_sum[0])[0][None, :]
    return (
        block_out.reshape(latents.shape),
        grad_rows.reshape(latents.shape),
        grad_cond,
        grad_wada,
        mine(total, 0, 6 * width // 8),
        jnp.transpose(oa[:3], (1, 0, 2)).reshape(ROWS, 3 * width),
        mine(total, 6 * width, 2 * width // 8),
        oa[3],
        mine(total, 8 * width, width // 8),
        jnp.transpose(ob, (1, 0, 2)).reshape(ROWS, 4 * width),
        mine(total, 9 * width, 4 * width // 8),
        oc.reshape(4 * ROWS, width),
        mine(total, 13 * width, width // 8),
    )


def solution(mesh):
    fast = mesh.shape["bin"] == 4 and mesh.shape["fsdp"] == 8
    return jax.shard_map(
        on_device_fast if fast else on_device_generic,
        mesh=mesh,
        in_specs=(
            P("bin", "fsdp", None, None),
            P("bin", None),
            P("bin", "fsdp"),
            P(None, "fsdp"),
            P("fsdp"),
            P("fsdp", None),
            P("fsdp"),
            P("fsdp", None),
            P("fsdp"),
            P("fsdp", None),
            P("fsdp"),
            P("fsdp", None),
            P("fsdp"),
            P("bin", "fsdp", None, None),
        ),
        out_specs=(
            P("bin", "fsdp", None, None),
            P("bin", "fsdp", None, None),
            P("bin", None),
            P(None, "fsdp"),
            P("fsdp"),
            P("fsdp", None),
            P("fsdp"),
            P("fsdp", None),
            P("fsdp"),
            P("fsdp", None),
            P("fsdp"),
            P("fsdp", None),
            P("fsdp"),
        ),
        check_vma=False,
    )
```

```python
import functools

import jax
import jax.numpy as jnp
from jax import lax
from jax.experimental import pallas as pl
from jax.experimental.pallas import tpu as pltpu
from jax.sharding import PartitionSpec as P

HEAD_DIM = 72
MESH = pl.DeviceIdType.MESH
ROWS = 144
WID = 1152
NG = 3


def layer_norm(field):
    center = field - jnp.mean(field, axis=-1, keepdims=True)
    return center * lax.rsqrt(jnp.mean(center * center, axis=-1, keepdims=True) + 1e-06)


def gelu_tanh(field):
    return (
        0.5
        * field
        * (1.0 + jnp.tanh(0.7978845608028654 * (field + 0.044715 * field * field * field)))
    )


def modulate(field, shift_vec, scale_vec):
    return layer_norm(field) * (1.0 + scale_vec) + shift_vec


def pair_scores(query_block, key_block):
    return jnp.einsum(
        "gqhd,gkhd->ghqk", query_block, key_block, preferred_element_type=jnp.float32
    ) * HEAD_DIM ** (-0.5)


def attend_pair(group_item):
    query_block, key_block, value_block = group_item
    scores = pair_scores(query_block, key_block)
    highest = jnp.max(scores, axis=-1, keepdims=True)
    exp_scores = jnp.exp(scores - highest)
    totals = jnp.sum(exp_scores, axis=-1, keepdims=True)
    attn_probs = (exp_scores / totals).astype(jnp.bfloat16)
    attended = jnp.einsum(
        "ghqk,gkhd->gqhd", attn_probs, value_block, preferred_element_type=jnp.float32
    )
    return (attended, (highest + jnp.log(totals))[..., 0])


def attend_back(group_item):
    query_block, key_block, value_block, log_total, grad_att = group_item
    scores = pair_scores(query_block, key_block)
    attn_probs = jnp.exp(scores - log_total[..., None])
    grad_probs = jnp.einsum(
        "gqhd,gkhd->ghqk", grad_att, value_block, preferred_element_type=jnp.float32
    )
    row_terms = jnp.sum(attn_probs * grad_probs, axis=-1, keepdims=True)
    grad_scores = (attn_probs * (grad_probs - row_terms)).astype(jnp.bfloat16)
    grad_query = jnp.einsum(
        "ghqk,gkhd->gqhd", grad_scores, key_block, preferred_element_type=jnp.float32
    ) * HEAD_DIM ** (-0.5)
    grad_key = jnp.einsum(
        "ghqk,gqhd->gkhd", grad_scores, query_block, preferred_element_type=jnp.float32
    ) * HEAD_DIM ** (-0.5)
    grad_value = jnp.einsum(
        "ghqk,gqhd->gkhd",
        attn_probs.astype(jnp.bfloat16),
        grad_att,
        preferred_element_type=jnp.float32,
    )
    return jnp.stack([grad_query, grad_key, grad_value], axis=2)


def run_block(flat_rows, modulation, weights, images, length):
    full_qkv, full_proj, full_fc1, full_fc2, bias_qv, bias_proj, bias_fc1, bias_fc2 = weights
    width = flat_rows.shape[1]
    heads = width // HEAD_DIM
    pieces = jnp.split(modulation, 6)
    h_first = modulate(flat_rows, pieces[0], pieces[1]).astype(jnp.bfloat16)
    qkv_bias = jnp.concatenate(
        [bias_qv[:width], jnp.zeros((width,), jnp.bfloat16), bias_qv[width:]]
    ).astype(jnp.float32)
    qkv_rows = (jnp.dot(h_first, full_qkv, preferred_element_type=jnp.float32) + qkv_bias).astype(
        jnp.bfloat16
    )
    split_rows = qkv_rows.reshape(images // 2, 2, length, 3, heads, HEAD_DIM)
    attended, log_total = lax.map(
        attend_pair, (split_rows[:, :, :, 0], split_rows[:, :, :, 1], split_rows[:, :, :, 2])
    )
    attended = attended.reshape(images * length, width).astype(jnp.bfloat16)
    branch = jnp.dot(attended, full_proj, preferred_element_type=jnp.float32) + bias_proj.astype(
        jnp.float32
    )
    middle = flat_rows + pieces[2] * branch
    h_second = modulate(middle, pieces[3], pieces[4]).astype(jnp.bfloat16)
    pre_act = jnp.dot(h_second, full_fc1, preferred_element_type=jnp.float32) + bias_fc1.astype(
        jnp.float32
    )
    hidden = gelu_tanh(pre_act).astype(jnp.bfloat16)
    mlp_out = jnp.dot(hidden, full_fc2, preferred_element_type=jnp.float32) + bias_fc2.astype(
        jnp.float32
    )
    result = middle + pieces[5] * mlp_out
    return (
        h_first,
        split_rows,
        log_total,
        attended,
        branch,
        middle,
        h_second,
        pre_act,
        hidden,
        mlp_out,
        result,
    )


def on_device_generic(
    latents,
    cond,
    live,
    w_ada,
    b_ada,
    w_qkv,
    b_qv,
    w_proj,
    b_proj,
    w_fc1,
    b_fc1,
    w_fc2,
    b_fc2,
    cotangent,
):
    images = latents.shape[1]
    length = latents.shape[2]
    width = latents.shape[3]
    heads = width // HEAD_DIM
    scaled = jax.nn.silu(cond[0]).astype(jnp.bfloat16)
    mod_part = jnp.dot(scaled, w_ada, preferred_element_type=jnp.float32) + b_ada.astype(
        jnp.float32
    )
    modulation = lax.all_gather(mod_part, "fsdp", axis=0, tiled=True)
    gathered = (
        lax.all_gather(w_qkv, "fsdp", axis=0, tiled=True),
        lax.all_gather(w_proj, "fsdp", axis=0, tiled=True),
        lax.all_gather(w_fc1, "fsdp", axis=0, tiled=True),
        lax.all_gather(w_fc2, "fsdp", axis=0, tiled=True),
        lax.all_gather(b_qv, "fsdp", axis=0, tiled=True),
        lax.all_gather(b_proj, "fsdp", axis=0, tiled=True),
        lax.all_gather(b_fc1, "fsdp", axis=0, tiled=True),
        lax.all_gather(b_fc2, "fsdp", axis=0, tiled=True),
    )
    flat_rows = latents[0].reshape(images * length, width).astype(jnp.float32)
    live_mask = (lax.iota(jnp.int32, images) < live[0, 0]).astype(jnp.float32)
    row_mask = jnp.repeat(live_mask, length)[:, None]
    forward_run = run_block(flat_rows, modulation, gathered, images, length)
    block_out = (forward_run[10] * row_mask).astype(jnp.bfloat16).reshape(latents.shape)
    weights = (
        lax.all_gather(w_qkv, "fsdp", axis=0, tiled=True),
        lax.all_gather(w_proj, "fsdp", axis=0, tiled=True),
        lax.all_gather(w_fc1, "fsdp", axis=0, tiled=True),
        lax.all_gather(w_fc2, "fsdp", axis=0, tiled=True),
        lax.all_gather(b_qv, "fsdp", axis=0, tiled=True),
        lax.all_gather(b_proj, "fsdp", axis=0, tiled=True),
        lax.all_gather(b_fc1, "fsdp", axis=0, tiled=True),
        lax.all_gather(b_fc2, "fsdp", axis=0, tiled=True),
    )
    full_qkv, full_proj, full_fc1, full_fc2 = (weights[0], weights[1], weights[2], weights[3])
    saved = run_block(flat_rows, modulation, weights, images, length)
    (
        h_first,
        split_rows,
        log_total,
        attended,
        branch,
        middle,
        h_second,
        pre_act,
        hidden,
        mlp_out,
        result,
    ) = saved
    pieces = jnp.split(modulation, 6)
    grad_res = cotangent[0].reshape(images * length, width).astype(jnp.float32) * row_mask
    grad_out = (pieces[5] * grad_res).astype(jnp.bfloat16)
    grad_gate_two = jnp.sum(grad_res * mlp_out, axis=0)
    grad_fc2 = jnp.einsum("rf,rd->fd", hidden, grad_out, preferred_element_type=jnp.float32)
    grad_bfc2 = jnp.sum(grad_out.astype(jnp.float32), axis=0)
    grad_hidden = jnp.einsum("rd,fd->rf", grad_out, full_fc2, preferred_element_type=jnp.float32)
    gelu_pull = jax.vjp(gelu_tanh, pre_act)[1]
    grad_pre = gelu_pull(grad_hidden)[0].astype(jnp.bfloat16)
    grad_fc1 = jnp.einsum("rd,rf->df", h_second, grad_pre, preferred_element_type=jnp.float32)
    grad_bfc1 = jnp.sum(grad_pre.astype(jnp.float32), axis=0)
    grad_h2 = jnp.einsum("rf,df->rd", grad_pre, full_fc1, preferred_element_type=jnp.float32)
    second_pull = jax.vjp(modulate, middle, pieces[3], pieces[4])[1]
    grad_mid_norm, grad_shift_two, grad_scale_two = second_pull(grad_h2)
    grad_mid = grad_res + grad_mid_norm
    grad_branch = (pieces[2] * grad_mid).astype(jnp.bfloat16)
    grad_gate_one = jnp.sum(grad_mid * branch, axis=0)
    grad_proj = jnp.einsum("rd,re->de", attended, grad_branch, preferred_element_type=jnp.float32)
    grad_bproj = jnp.sum(grad_branch.astype(jnp.float32), axis=0)
    grad_att = jnp.einsum(
        "re,de->rd", grad_branch, full_proj, preferred_element_type=jnp.float32
    ).astype(jnp.bfloat16)
    grad_att = grad_att.reshape(images // 2, 2, length, heads, HEAD_DIM)
    grad_qkv = lax.map(
        attend_back,
        (
            split_rows[:, :, :, 0],
            split_rows[:, :, :, 1],
            split_rows[:, :, :, 2],
            log_total,
            grad_att,
        ),
    )
    grad_qkv = grad_qkv.reshape(images * length, 3 * width).astype(jnp.bfloat16)
    grad_wqkv = jnp.einsum("rd,re->de", h_first, grad_qkv, preferred_element_type=jnp.float32)
    qkv_sums = jnp.sum(grad_qkv.astype(jnp.float32), axis=0)
    grad_bqv = jnp.concatenate([qkv_sums[:width], qkv_sums[2 * width :]])
    grad_h1 = jnp.einsum("re,de->rd", grad_qkv, full_qkv, preferred_element_type=jnp.float32)
    first_pull = jax.vjp(modulate, flat_rows, pieces[0], pieces[1])[1]
    grad_rows_norm, grad_shift_one, grad_scale_one = first_pull(grad_h1)
    grad_rows = grad_mid + grad_rows_norm
    grad_mod = jnp.concatenate(
        [
            grad_shift_one,
            grad_scale_one,
            grad_gate_one,
            grad_shift_two,
            grad_scale_two,
            grad_gate_two,
        ]
    )
    shards = (
        lax.psum_scatter(grad_wqkv, "fsdp", scatter_dimension=0, tiled=True),
        lax.psum_scatter(grad_proj, "fsdp", scatter_dimension=0, tiled=True),
        lax.psum_scatter(grad_fc1, "fsdp", scatter_dimension=0, tiled=True),
        lax.psum_scatter(grad_fc2, "fsdp", scatter_dimension=0, tiled=True),
        lax.psum_scatter(grad_bqv, "fsdp", scatter_dimension=0, tiled=True),
        lax.psum_scatter(grad_bproj, "fsdp", scatter_dimension=0, tiled=True),
        lax.psum_scatter(grad_bfc1, "fsdp", scatter_dimension=0, tiled=True),
        lax.psum_scatter(grad_bfc2, "fsdp", scatter_dimension=0, tiled=True),
        lax.psum_scatter(grad_mod, "fsdp", scatter_dimension=0, tiled=True),
    )
    mod_mine = shards[8]
    grad_wada = scaled.astype(jnp.float32)[:, None] * mod_mine[None, :]
    grad_scaled = jnp.dot(w_ada.astype(jnp.float32), mod_mine, precision=lax.Precision.HIGHEST)
    grad_scaled = lax.psum(grad_scaled, "fsdp")
    silu_pull = jax.vjp(jax.nn.silu, cond[0])[1]
    grad_cond = silu_pull(grad_scaled)[0][None, :]
    totals = lax.psum(
        (
            shards[0],
            shards[1],
            shards[2],
            shards[3],
            shards[4],
            shards[5],
            shards[6],
            shards[7],
            grad_wada,
            mod_mine,
        ),
        "bin",
    )
    return (
        block_out,
        grad_rows.reshape(latents.shape),
        grad_cond,
        totals[8],
        totals[9],
        totals[0],
        totals[4],
        totals[1],
        totals[5],
        totals[2],
        totals[6],
        totals[3],
        totals[7],
    )


TILE = 256
UN = 4
STRIP = 16


def coords():
    b = lax.axis_index("bin")
    f = lax.axis_index("fsdp")
    return b, f, b // 2, lax.rem(b, 2), f // 2, lax.rem(f, 2)


def strip_loop(rows, body, unroll=1):
    @pl.loop(0, rows // STRIP, unroll=unroll)
    def _(k):
        body(pl.ds(pl.multiple_of(k * STRIP, STRIP), STRIP))


def dense(left, right):
    return jnp.dot(left, right, preferred_element_type=jnp.float32)


def dense_nt(left, right):
    return lax.dot_general(left, right, (((1,), (1,)), ((), ())), preferred_element_type=jnp.float32)


def dense_tn(left, right):
    return lax.dot_general(left, right, (((0,), (0,)), ((), ())), preferred_element_type=jnp.float32)


def center_rows(v):
    v = v - jnp.mean(v, axis=-1, keepdims=True)
    inv = lax.rsqrt(jnp.mean(v * v, axis=-1, keepdims=True) + 1e-06)
    return v * inv, inv


def head_window(h):
    start = HEAD_DIM * h
    low = start // 128 * 128
    width = 128 if start - low + HEAD_DIM <= 128 else 256
    return low, width, start - low


def head_mask(off, width):
    lanes = lax.broadcasted_iota(jnp.int32, (1, width), 1)
    return jnp.logical_and(lanes >= off, lanes < off + HEAD_DIM)


def head_probs(q, k):
    scores = dense_nt(k, q) * HEAD_DIM ** (-0.5)
    e = jnp.exp(scores - jnp.max(scores, axis=0, keepdims=True))
    return e * (1.0 / jnp.sum(e, axis=0, keepdims=True))


def forward_kernel(
    vec_ref, la_ref, lb_ref, lc_ref, x_ref, res_ref,
    vec_out, wa_out, wb_out, wc_out, h1_out, qkv_out, att_out, branch_out, mid_out, h2_out, slope_out, hid_out, go_out, pc_out,
    wa, wb, wc, vecs, vec, xs, res, h1, qkv, att, mid, h2, hid, go, acc, slope, pst,
    loc_sem, sm_send, sm_recv, send_sem, recv_sem, in_sem, out_sem, wo_sem, co_sem, sl_sem, ps_sem,
):
    b, f, x, c, z, y = coords()
    bx = lax.rem(b + 2, 4)
    bc = b + 1 - 2 * c
    bxc = lax.rem(bc + 2, 4)
    fy = f + 1 - 2 * y
    yb = 1 - y
    z1 = z + 1 - 2 * lax.rem(z, 2)
    mid_z = jnp.logical_or(z == 1, z == 2)
    zb = lax.rem(z + 2, 4)
    zc = 3 - z
    z2 = jnp.where(mid_z, zc, zb)
    z3 = jnp.where(mid_z, zb, zc)
    fz1 = z1 * 2 + y
    bar = pltpu.get_barrier_semaphore()
    for k in range(1, 8):
        pl.semaphore_signal(bar, inc=1, device_id=(b, lax.rem(f + k, 8)), device_id_type=MESH)
    pl.semaphore_signal(bar, inc=1, device_id=(bx, f), device_id_type=MESH)
    pl.semaphore_signal(bar, inc=1, device_id=(bc, f), device_id_type=MESH)
    pl.semaphore_wait(bar, 9)

    W = (wa, wb, wc)
    L = (la_ref, lb_ref, lc_ref)

    def blk(g, j, ff):
        if g < 2:
            return W[g].at[j, pl.ds(pl.multiple_of(ff * ROWS, ROWS), ROWS)]
        return W[g].at[ff, j]

    smalls = []
    partners = ((b, fy), (b, fz1), (b, zb * 2 + y))

    def small_send(k):
        cp = pltpu.make_async_remote_copy(
            src_ref=vecs.at[k], dst_ref=vecs.at[3 + k], send_sem=sm_send.at[k], recv_sem=sm_recv.at[k],
            device_id=partners[k], device_id_type=MESH,
        )
        cp.start()
        smalls.append(cp)

    def small_step(k):
        pltpu.make_async_copy(vecs.at[3 + k], vecs.at[3 + k], sm_recv.at[k]).wait()
        total = vecs[k] + vecs[3 + k]
        if k < 2:
            vecs[k + 1] = total
            small_send(k + 1)
        else:
            vec[...] = total
            keep(vec, vec_out, 0)


    pend = []
    outs = []
    cnt = [0] * NG

    def send(g, j, ff, dev, cond=None, src=None):
        i = cnt[g]
        cnt[g] += 1
        cp = pltpu.make_async_remote_copy(
            src_ref=blk(g, j, ff) if src is None else src, dst_ref=blk(g, j, ff),
            send_sem=send_sem.at[g, i], recv_sem=recv_sem.at[g, j, ff], device_id=dev, device_id_type=MESH,
        )
        if cond is None:
            cp.start()
        else:
            @pl.when(cond)
            def _():
                cp.start()
        pend.append((cp, cond))

    def copy_out(src, dst, sem):
        cp = pltpu.make_async_copy(src, dst, sem)
        cp.start()
        return cp

    def arrive(g, j, ff, cond=None):
        def go_on():
            pltpu.make_async_copy(blk(g, j, ff), blk(g, j, ff), recv_sem.at[g, j, ff]).wait()
            if g == 2:
                copy_out(wc.at[ff, j], wc_out.at[ff, j], co_sem.at[j, ff])
        if cond is None:
            go_on()
        else:
            pl.when(cond)(go_on)

    up = (b, jnp.minimum(f + 2, 7))
    dn = (b, jnp.maximum(f - 2, 0))

    def init(g):
        sb = L[g].at[b]
        sx = L[g].at[bx]
        send(g, b, f, up, z < 3, sb)
        send(g, b, f, dn, z > 0, sb)
        send(g, b, f, (b, fy), None, sb)
        send(g, bx, f, (b, fz1), None, sx)
        send(g, bx, f, (b, fy), None, sx)

    locs = []

    def local(g):
        for j in range(4):
            locs.append(copy_out(L[g].at[j], blk(g, j, f), loc_sem.at[g, j]))

    def Z(g, zz, x_too):
        ff = zz * 2 + y
        arrive(g, b, ff)
        send(g, b, ff, up, jnp.logical_and(zz < z, z < 3))
        send(g, b, ff, dn, jnp.logical_and(zz > z, z > 0))
        send(g, b, ff, (b, fy))
        if x_too:
            send(g, b, ff, (bx, f))
        send(g, b, ff, (bc, f))

    def Y(g, zz, x_too):
        ff = zz * 2 + yb
        arrive(g, b, ff)
        if x_too:
            send(g, b, ff, (bx, f))
        send(g, b, ff, (bc, f))

    def X(g, ff):
        arrive(g, bx, ff)
        send(g, bx, ff, (bc, f))

    def actions(g):
        return [
            lambda: Z(g, z1, False), lambda: X(g, fz1), lambda: Y(g, z, False), lambda: X(g, fy),
            lambda: Z(g, z2, True), lambda: Y(g, z1, True), lambda: Z(g, z3, True), lambda: X(g, z2 * 2 + y),
            lambda: Y(g, z2, True), lambda: X(g, z1 * 2 + yb), lambda: X(g, z3 * 2 + y), lambda: Y(g, z3, True),
            lambda: X(g, z2 * 2 + yb), lambda: X(g, z3 * 2 + yb),
        ]

    def other_core(g):
        for zz in range(4):
            for jj in (bc, bxc):
                arrive(g, jj, zz * 2 + y, zz != z)
                arrive(g, jj, zz * 2 + yb)
        for cp in locs[g * 4 : g * 4 + 4]:
            cp.wait()

    def keep(src, dst, i):
        outs.append(copy_out(src, dst, out_sem.at[i]))

    def row(i):
        return vec[i : i + 1, :]

    def start_rows():
        in_x.wait()

        def first(r):
            n, _ = center_rows(xs[r, :].astype(jnp.float32))
            h1[r, :] = (n * (1.0 + row(1)) + row(0)).astype(jnp.bfloat16)

        strip_loop(h1.shape[0], first, UN)
        keep(h1, h1_out, 1)

    def start_grads():
        in_res.wait()

        def out_grad(r):
            go[r, :] = (res[r, :].astype(jnp.float32) * row(5)).astype(jnp.bfloat16)

        strip_loop(go.shape[0], out_grad)
        keep(go, go_out, 2)

    tiles = xs.shape[0] // TILE

    def tile(i):
        return pl.ds(pl.multiple_of(i * TILE, TILE), TILE)

    def project(j):
        @pl.loop(0, tiles)
        def _(i):
            v = dense(h1[tile(i), :], wa[j])
            if j != 1:
                v = v + row(6 + j // 2)
            qkv[j, tile(i), :] = v.astype(jnp.bfloat16)
        keep(qkv.at[j], qkv_out.at[j], 3 + j)

    def attention():
        @pl.loop(0, tiles)
        def _(i):
            acc[...] = jnp.zeros_like(acc)
            for h in range(WID // HEAD_DIM):
                low, width, off = head_window(h)
                cols = slice(low, low + width)
                mask = head_mask(off, width)
                q = qkv[0, tile(i), cols]
                v = qkv[2, tile(i), cols]
                probs = head_probs(jnp.where(mask, q, jnp.zeros_like(q)), qkv[1, tile(i), cols])
                acc[:, cols] += dense_tn(probs.astype(jnp.bfloat16), jnp.where(mask, v, jnp.zeros_like(v)))
            att[tile(i), :] = acc[...].astype(jnp.bfloat16)
        keep(att, att_out, 6)

    def branch():
        @pl.loop(0, tiles)
        def _(i):
            mid[tile(i), :] = dense(att[tile(i), :], wa[3]) + row(8)
        cp = copy_out(mid, branch_out, out_sem.at[7])
        cp.wait()

        def second(r):
            m = xs[r, :].astype(jnp.float32) + row(2) * mid[r, :]
            mid[r, :] = m
            n, _ = center_rows(m)
            h2[r, :] = (n * (1.0 + row(4)) + row(3)).astype(jnp.bfloat16)

        strip_loop(mid.shape[0], second, UN)
        keep(mid, mid_out, 8)
        keep(h2, h2_out, 9)

    def hidden(j):
        cols = slice(j * WID, j * WID + WID)

        @pl.loop(0, tiles)
        def _(i):
            acc[...] = dense(h2[tile(i), :], wb[j]) + row(9 + j)

            @pl.when(j * tiles + i >= 1)
            def _():
                pltpu.make_async_copy(slope, slope_out.at[tile(0), :WID], sl_sem).wait()

            @pl.loop(0, TILE // STRIP)
            def _(k):
                r = pl.ds(pl.multiple_of(k * STRIP, STRIP), STRIP)
                v = acc[r, :]
                sq = v * v
                t = jnp.tanh(0.7978845608028654 * (v + 0.044715 * sq * v))
                half = 0.5 * (1.0 + t)
                slope[r, :] = half + 0.5 * v * (1.0 - t * t) * (0.7978845608028654 * (1.0 + 0.134145 * sq))
                hid[pl.ds(pl.multiple_of(i * TILE + k * STRIP, STRIP), STRIP), cols] = (v * half).astype(jnp.bfloat16)

            copy_out(slope, slope_out.at[tile(i), cols], sl_sem)
        if j == 3:
            pltpu.make_async_copy(slope, slope_out.at[tile(0), :WID], sl_sem).wait()
            keep(hid, hid_out, 10)

    part = pst.shape[1]

    def outer(j):
        @pl.loop(0, WID // part)
        def _(i):
            k = j * (WID // part) + i
            slot = lax.rem(k, 2)

            @pl.when(k >= 2)
            def _():
                pltpu.make_async_copy(pst.at[slot], pc_out.at[pl.ds(0, part)], ps_sem.at[slot]).wait()
            at = pl.multiple_of(k * part, part)
            pst[slot] = dense_tn(hid[:, pl.ds(at, part)], go[...]).astype(jnp.bfloat16)
            copy_out(pst.at[slot], pc_out.at[pl.ds(at, part)], ps_sem.at[slot])
        if j == 3:
            for slot in range(2):
                pltpu.make_async_copy(pst.at[slot], pc_out.at[pl.ds(0, part)], ps_sem.at[slot]).wait()

    def weights_out(g):
        outs.append(copy_out(W[g], (wa_out, wb_out)[g], wo_sem.at[g]))

    in_x = copy_out(x_ref, xs, in_sem.at[0])
    in_res = copy_out(res_ref, res, in_sem.at[1])
    acts = [actions(g) for g in range(NG)]
    run = lambda todo: [a() for a in todo]
    own = pltpu.make_async_copy(vec_ref, vecs.at[0], sm_send.at[3])
    own.start()
    init(0)
    local(0)
    own.wait()
    small_send(0)
    run(acts[0][:1])
    small_step(0)
    run(acts[0][1:3])
    small_step(1)
    run(acts[0][3:5])
    small_step(2)
    run(acts[0][5:8])
    init(1)
    local(1)
    run(acts[0][8:11])
    start_rows()
    run(acts[0][11:])
    run(acts[1][:5])
    other_core(0)
    weights_out(0)
    work = [lambda: project(0), lambda: project(1), lambda: project(2), attention, branch, start_grads]
    ticks = [acts[1][5:6], acts[1][6:7], acts[1][7:8] + [lambda: init(2), lambda: local(2)], acts[1][8:11], acts[1][11:12], acts[1][12:13]]
    for piece, tick in zip(work, ticks):
        piece()
        run(tick)
    run(acts[1][13:])
    run(acts[2][:5])
    other_core(1)
    weights_out(1)
    work = [functools.partial(hidden, j) for j in range(4)] + [functools.partial(outer, j) for j in range(4)]
    ticks = [acts[2][5 + i : 6 + i] for i in range(8)]
    for piece, tick in zip(work, ticks):
        piece()
        run(tick)
    run(acts[2][13:])
    for j in range(4):
        locs[8 + j].wait()
        copy_out(wc.at[f, j], wc_out.at[f, j], co_sem.at[j, f])
    other_core_c = 2
    for zz in range(4):
        for jj in (bc, bxc):
            arrive(other_core_c, jj, zz * 2 + y, zz != z)
            arrive(other_core_c, jj, zz * 2 + yb)
    for cp, cond in pend:
        if cond is None:
            cp.wait_send()
        else:
            @pl.when(cond)
            def _(cp=cp):
                cp.wait_send()
    for cp in smalls:
        cp.wait_send()
    for cp in outs:
        cp.wait()
    for ff in range(8):
        for j in range(4):
            pltpu.make_async_copy(wc.at[ff, j], wc_out.at[ff, j], co_sem.at[j, ff]).wait()


def forward(vec, la, lb, lc, x, res):
    any_space = pl.BlockSpec(memory_space=pl.ANY)
    f32, bf16 = jnp.float32, jnp.bfloat16
    rows = x.shape[0]
    sds = jax.ShapeDtypeStruct
    sem = pltpu.SemaphoreType.DMA
    mat = (rows, WID)
    outs = (
        sds((16, WID), f32), sds((4, WID, WID), bf16), sds((4, WID, WID), bf16), sds((8, 4, ROWS, WID), bf16),
        sds(mat, bf16), sds((3,) + mat, bf16), sds(mat, bf16), sds(mat, f32), sds(mat, f32), sds(mat, bf16),
        sds((rows, 4 * WID), f32), sds((rows, 4 * WID), bf16), sds(mat, bf16), sds((4 * WID, WID), bf16),
    )
    vm = pltpu.VMEM
    return pl.pallas_call(
        forward_kernel,
        out_shape=outs,
        in_specs=[any_space] * 6,
        out_specs=(any_space,) * len(outs),
        scratch_shapes=[
            vm((4, WID, WID), bf16), vm((4, WID, WID), bf16), vm((8, 4, ROWS, WID), bf16), vm((6, 16, WID), f32), vm((16, WID), f32),
            vm(mat, bf16), vm(mat, bf16), vm(mat, bf16), vm((3,) + mat, bf16), vm(mat, bf16), vm(mat, f32), vm(mat, bf16),
            vm((rows, 4 * WID), bf16), vm(mat, bf16), vm((TILE, WID), f32), vm((TILE, WID), f32), vm((2, 384, WID), bf16),
            sem((NG, 4)), sem((8,)), sem((8,)), sem((NG, 40)), sem((NG, 4, 8)), sem((2,)), sem((12,)), sem((2,)), sem((4, 8)), sem, sem((2,)),
        ],
        compiler_params=pltpu.CompilerParams(collective_id=1, has_side_effects=True, vmem_limit_bytes=63 << 20),
        name="forward",
    )(vec, la, lb, lc, x, res)


PROGRAM = (
    -1, -1, 37, -1, 43, -1, 35, -1, 34, 39, -1, 38, -1, -1, -1, -1, 40, -1, -1, 44, 42, -1, 36, -1,
    41, 17, 45, 20, 19, 48, -1, -1, 25, 21, -1, 46, -1, 47, 23, -1, -1, -1, 26, 22, 49, 24, 28, -1,
    -1, -1, -1, -1, 18, -1, 30, 0, -1, 2, 4, 1, 31, -1, 27, 5, 6, -1, -1, -1, 7, 11, -1, 8,
    32, 10, -1, 50, -1, 3, 13, -1, 29, 9, -1, -1, -1, 14, -1, 12, -1, 15, -1, 33, -1, -1, -1, 16,
)


def backward_kernel(
    mask_ref, vec_ref, wa_ref, wb_ref, wc_ref, x_ref, res_ref, h1_ref, qkv_ref, att_ref, branch_ref, mid_ref, h2_ref, slope_ref,
    hid_ref, go_ref, pc_ref, ada_ref,
    sums_out, cond_out, oa_ref, ob_ref, oc_ref, block_out, lat_out, pa_ref, pb_ref,
    r0, ring, rx4, ry4, ry3, rx2, rn, rz, rt, fin, vec, wbuf, pst, mats, res, fl, sums8, smine, srecv, sall, ada, gvec, cmine, crecv,
    ring_sem, s0_send, s0_recv, send_sem, rx4_s, ry4_s, ry3_s, rx2_s, rn_s, rz_s, rt_s, o_loc, o_send, o_recv,
    w_sem, p_sem, m_sem, f_sem, sl_sem, out_sem, sm_send, sm_recv, ada_sem,
):
    f32, bf16 = jnp.float32, jnp.bfloat16
    b, f, x, c, z, y = coords()
    bx = lax.rem(b + 2, 4)
    bc = b + 1 - 2 * c
    bxc = lax.rem(bc + 2, 4)
    fy = f + 1 - 2 * y
    yb = 1 - y
    z1 = z + 1 - 2 * lax.rem(z, 2)
    mid_z = jnp.logical_or(z == 1, z == 2)
    zb = lax.rem(z + 2, 4)
    zc = 3 - z
    z2 = jnp.where(mid_z, zc, zb)
    z3 = jnp.where(mid_z, zb, zc)
    fz1 = z1 * 2 + y
    bar = pltpu.get_barrier_semaphore()
    for k in range(1, 8):
        pl.semaphore_signal(bar, inc=1, device_id=(b, lax.rem(f + k, 8)), device_id_type=MESH)
    pl.semaphore_signal(bar, inc=1, device_id=(bx, f), device_id_type=MESH)
    pl.semaphore_signal(bar, inc=1, device_id=(bc, f), device_id_type=MESH)
    pl.semaphore_wait(bar, 9)

    def start(src, dst, sem):
        cp = pltpu.make_async_copy(src, dst, sem)
        cp.start()
        return cp

    def wait_on(ref, sem):
        pltpu.make_async_copy(ref, ref, sem).wait()

    P = (pa_ref, pb_ref, pc_ref)
    O = (oa_ref, ob_ref, oc_ref)

    def blk(g, j, ff):
        if g < 2:
            return P[g].at[j, pl.ds(pl.multiple_of(ff * ROWS, ROWS), ROWS)]
        return P[g].at[ff, j]

    order = [
        (1, z3, yb), (1, z2, yb), (1, z3, y), (1, z2, y), (1, z1, yb), (1, z, yb), (0, z3, yb), (0, z2, yb),
        (0, z1, yb), (0, z, yb), (0, z3, y), (0, z2, y), (1, z1, y), (0, z1, y), (0, z, y), (1, z, y),
    ]
    mine = (b, bx)
    his = (bc, bxc)
    pend = []
    cnt = [0] * NG

    def open_group(g):
        for i, (jj, zz, yy) in enumerate(order):
            cp = pltpu.make_async_remote_copy(
                src_ref=blk(g, his[jj], zz * 2 + yy), dst_ref=r0.at[g, i], send_sem=s0_send.at[g, i],
                recv_sem=s0_recv.at[g, i], device_id=(bc, f), device_id_type=MESH,
            )
            cp.start()
            pend.append((cp, None))
        state["ready"].append(g)
        pump()

    state = {"ready": [], "issued": 0, "used": 0}
    depth = ring.shape[0]

    def pump():
        while state["issued"] < len(plan) and state["issued"] - state["used"] < depth:
            g, i = plan[state["issued"]]
            if g not in state["ready"]:
                return
            jj, zz, yy = order[i]
            slot = state["issued"] % depth
            start(blk(g, mine[jj], zz * 2 + yy), ring.at[slot], ring_sem.at[slot])
            state["issued"] += 1

    def add(dst, srcs):
        @pl.loop(0, ROWS // STRIP)
        def _(k):
            rows = pl.ds(pl.multiple_of(k * STRIP, STRIP), STRIP)
            v = srcs[0][rows, :].astype(f32)
            for s in srcs[1:]:
                v = v + s[rows, :].astype(f32)
            dst[rows, :] = v.astype(dst.dtype)

    def combine(g, i, more=()):
        slot = state["used"] % depth
        assert plan[state["used"]] == (g, i)
        wait_on(ring.at[slot], ring_sem.at[slot])
        wait_on(r0.at[g, i], s0_recv.at[g, i])
        srcs = [r0.at[g, i], ring.at[slot]]
        for ref, sem in more:
            wait_on(ref, sem)
            srcs.append(ref)
        add(r0.at[g, i], srcs)
        state["used"] += 1
        pump()

    def send(g, src, dst, rsem, dev):
        i = cnt[g]
        cnt[g] += 1
        cp = pltpu.make_async_remote_copy(
            src_ref=src, dst_ref=dst, send_sem=send_sem.at[g, i], recv_sem=rsem, device_id=dev, device_id_type=MESH
        )
        cp.start()
        pend.append((cp, None))

    X = (bx, f)
    Y = (b, fy)

    def to_x4(g, i, slot):
        combine(g, i)
        send(g, r0.at[g, i], rx4.at[g, slot], rx4_s.at[g, slot], X)

    def to_x2(g, i, slot):
        combine(g, i)
        send(g, r0.at[g, i], rx2.at[g, slot], rx2_s.at[g, slot], X)

    def to_y4(g, i, slot):
        combine(g, i)
        send(g, r0.at[g, i], ry4.at[g, slot], ry4_s.at[g, slot], Y)

    def to_y3(g, i, slot, rslot):
        combine(g, i, () if rslot is None else ((rx4.at[g, rslot], rx4_s.at[g, rslot]),))
        send(g, r0.at[g, i], ry3.at[g, slot], ry3_s.at[g, slot], Y)

    s2 = jnp.where(mid_z, 2, 1)
    s3 = jnp.where(mid_z, 1, 2)

    def to_z(g, i, zz, slot, rslot, yslot):
        more = [(ry3.at[g, yslot], ry3_s.at[g, yslot])]
        if rslot is not None:
            more.append((rx2.at[g, rslot], rx2_s.at[g, rslot]))
        combine(g, i, more)
        send(g, r0.at[g, i], rz.at[g, slot], rz_s.at[g, slot], (b, zz * 2 + y))

    def to_near(g, i):
        combine(g, i, [(ry4.at[g, 1], ry4_s.at[g, 1])])
        send(g, r0.at[g, i], rn.at[g], rn_s.at[g], (b, fz1))

    def own_last(g, i):
        combine(g, i, [(ry3.at[g, 0], ry3_s.at[g, 0])] + [(rz.at[g, k], rz_s.at[g, k]) for k in range(3)])
        send(g, r0.at[g, i], rt.at[g, 0], rt_s.at[g, 0], X)

    def other_last(g, i):
        combine(g, i, [(ry4.at[g, 0], ry4_s.at[g, 0]), (rn.at[g], rn_s.at[g])])
        send(g, r0.at[g, i], rt.at[g, 1], rt_s.at[g, 1], X)

    finals = []

    def final(g):
        if finals:
            for cp in finals[-2:]:
                cp[0].wait()
                cp[1].wait_send()
        for q, (i, slot, j) in enumerate(((14, 1, b), (15, 0, bx))):
            wait_on(rt.at[g, slot], rt_s.at[g, slot])
            add(fin.at[q], [r0.at[g, i], rt.at[g, slot]])
            loc = start(fin.at[q], O[g].at[j], o_loc.at[g, q])
            rc = pltpu.make_async_remote_copy(
                src_ref=fin.at[q], dst_ref=O[g].at[j], send_sem=o_send.at[g, q], recv_sem=o_recv.at[g, q],
                device_id=(bc, f), device_id_type=MESH,
            )
            rc.start()
            finals.append((loc, rc))

    def steps_of(g):
        return [
            (lambda: to_x4(g, 0, 0), 0), (lambda: to_y4(g, 4, 1), 4), (lambda: to_x4(g, 1, 1), 1), (lambda: to_y4(g, 5, 0), 5),
            (lambda: to_x2(g, 2, 0), 2), (lambda: to_x2(g, 3, 1), 3), (lambda: to_y3(g, 6, 3, 0), 6), (lambda: to_y3(g, 7, 2, 1), 7),
            (lambda: to_y3(g, 8, 1, None), 8), (lambda: to_y3(g, 9, 0, None), 9), (lambda: to_near(g, 12), 12),
            (lambda: to_z(g, 10, z3, s3, 0, 3), 10), (lambda: other_last(g, 15), 15), (lambda: to_z(g, 11, z2, s2, 1, 2), 11),
            (lambda: to_z(g, 13, z1, 0, None, 1), 13), (lambda: own_last(g, 14), 14), (lambda: final(g), None),
        ]

    rows = res.shape[0]
    tiles = rows // TILE

    def tile(i):
        return pl.ds(pl.multiple_of(i * TILE, TILE), TILE)

    def row(i):
        return vec[i : i + 1, :]

    def load_mat(k, src):
        return start(src, mats.at[k], m_sem.at[k])

    def load_fl(k, src):
        return start(src, fl.at[k], f_sem.at[k])

    w_list = []
    for j in range(4):
        w_list += [wc_ref.at[j], wb_ref.at[j]]
    w_list += [wa_ref.at[3], wa_ref.at[0], wa_ref.at[1], wa_ref.at[2]] + [wc_ref.at[j] for j in range(4)]
    w_at = [0]

    def fetch(k):
        if k < len(w_list):
            start(w_list[k], wbuf.at[k % 2], w_sem.at[k % 2])

    def with_weight(body):
        k = w_at[0]
        w_at[0] += 1
        wait_on(wbuf.at[k % 2], w_sem.at[k % 2])
        body(wbuf.at[k % 2])
        fetch(k + 2)

    def colsum(i, v):
        sums8[i] += v[:8] + v[8:]

    p_cnt = [0]
    part = pst.shape[1]
    steps = WID // part

    def outer(left, right, dst):
        n = p_cnt[0]
        p_cnt[0] += 1

        @pl.loop(0, steps)
        def _(i):
            k = n * steps + i
            slot = lax.rem(k, 2)

            @pl.when(k >= 2)
            def _():
                wait_on(pst.at[slot], p_sem.at[slot])
            at = pl.multiple_of(i * part, part)
            pst[slot] = dense_tn(left[:, pl.ds(at, part)], right[...]).astype(bf16)
            start(pst.at[slot], dst.at[pl.ds(at, part)], p_sem.at[slot])

    def drain():
        for slot in range(2):
            wait_on(pst.at[slot], p_sem.at[slot])
        p_cnt[0] = 0

    GO, H2, GP, Q = 0, 1, 2, 3
    ATT, GB, GA, H1 = 0, 1, 2, 0

    def slope_load(k):
        if k < 4 * tiles:
            j, i = divmod(k, tiles)
            start(slope_ref.at[pl.ds(i * TILE, TILE), pl.ds(j * WID, WID)], fl.at[2, pl.ds((k % 2) * TILE, TILE)], sl_sem.at[k % 2])

    def mlp_back(j):
        def body(w):
            for i in range(tiles):
                k = j * tiles + i
                sl = fl.at[2, pl.ds((k % 2) * TILE, TILE)]
                fl[3, :TILE, :] = dense_nt(mats[GO, i * TILE : (i + 1) * TILE, :], w[...])
                wait_on(sl, sl_sem.at[k % 2])

                def strip(r):
                    v = (fl[3, r, :] * sl[r, :]).astype(bf16)
                    mats[GP, pl.ds(pl.multiple_of(i * TILE + r.start, STRIP), STRIP), :] = v
                    colsum(9 + j, v.astype(f32))

                strip_loop(TILE, strip)
                slope_load(k + 2)
        with_weight(body)

    def hidden_in(dst, j, left):
        def body(w):
            @pl.loop(0, tiles)
            def _(i):
                v = dense_nt(mats[left, tile(i), :], w[...])
                if j == 0:
                    fl[dst, tile(i), :] = v
                else:
                    fl[dst, tile(i), :] += v
        with_weight(body)

    def first_sums():
        def strip(r):
            colsum(13, mats[GO, r, :].astype(f32))
        strip_loop(rows, strip)

    def norm_two():
        wait_on(fl.at[1], f_sem.at[1])
        wait_on(fl.at[2], f_sem.at[2])

        def strip(r):
            n, inv = center_rows(fl[1, r, :])
            g = fl[0, r, :]
            colsum(4, g * n)
            colsum(3, g)
            dn = g * (1.0 + row(4))
            pull = dn - jnp.mean(dn, axis=-1, keepdims=True) - n * jnp.mean(dn * n, axis=-1, keepdims=True)
            gm = res[r, :].astype(f32) + inv * pull
            colsum(2, gm * fl[2, r, :])
            gb = (row(2) * gm).astype(bf16)
            colsum(8, gb.astype(f32))
            fl[1, r, :] = gm
            mats[GB, r, :] = gb

        strip_loop(rows, strip, UN)

    def att_in():
        def body(w):
            @pl.loop(0, tiles)
            def _(i):
                mats[GA, tile(i), :] = dense_nt(mats[GB, tile(i), :], w[...]).astype(bf16)
        with_weight(body)

    def clear():
        def strip(r):
            for k in (0, 2, 3):
                fl[k, r, :] = jnp.zeros((STRIP, WID), f32)
        strip_loop(rows, strip)

    def att_back(heads):
        @pl.loop(0, tiles)
        def _(i):
            for h in heads:
                low, width, off = head_window(h)
                cols = slice(low, low + width)
                mask = head_mask(off, width)

                def pick(k):
                    v = mats[k, tile(i), cols]
                    return v, jnp.where(mask, v, jnp.zeros_like(v))

                _, q = pick(Q)
                k_all, k_own = pick(Q + 1)
                v_all = mats[Q + 2, tile(i), cols]
                _, g = pick(GA)
                probs = head_probs(q, k_all)
                grad_probs = dense_nt(v_all, g)
                total = jnp.sum(probs * grad_probs, axis=0, keepdims=True)
                gs = (probs * (grad_probs - total)).astype(bf16)
                fl[3, tile(i), cols] += dense(probs.astype(bf16), g)
                fl[2, tile(i), cols] += dense(gs, q) * HEAD_DIM ** (-0.5)
                fl[0, tile(i), cols] += dense_tn(gs, k_own) * HEAD_DIM ** (-0.5)

    def att_done():
        def strip(r):
            for k, a in enumerate((0, 2, 3)):
                v = fl[a, r, :].astype(bf16)
                mats[Q + k, r, :] = v
                if k != 1:
                    colsum(6 + k // 2, v.astype(f32))
        strip_loop(rows, strip)

    def norm_one():
        wait_on(mats.at[0], m_sem.at[0])

        def strip(r):
            n, inv = center_rows(mats[0, r, :].astype(f32))
            g = fl[0, r, :]
            colsum(1, g * n)
            colsum(0, g)
            dn = g * (1.0 + row(1))
            pull = dn - jnp.mean(dn, axis=-1, keepdims=True) - n * jnp.mean(dn * n, axis=-1, keepdims=True)
            fl[0, r, :] = fl[1, r, :] + inv * pull

        strip_loop(rows, strip, UN)
        start(fl.at[0], lat_out, out_sem.at[0])

    def mlp_out(j):
        k = 1 + j
        wait_on(mats.at[k], m_sem.at[k])

        def body(w):
            @pl.loop(0, tiles)
            def _(i):
                v = dense(mats[k, tile(i), :], w[...])
                if j == 0:
                    fl[2, tile(i), :] = v
                else:
                    fl[2, tile(i), :] += v
        with_weight(body)

    def block_end():
        wait_on(fl.at[3], f_sem.at[3])
        for i in range(tiles):
            m = mask_ref[i]

            def strip(r):
                at = pl.ds(pl.multiple_of(i * TILE + r.start, STRIP), STRIP)
                v = fl[2, at, :] + row(13)
                colsum(5, v * res[at, :].astype(f32))
                mats[5, at, :] = ((fl[3, at, :] + row(5) * v) * m).astype(bf16)

            strip_loop(TILE, strip)
        start(mats.at[5], block_out, out_sem.at[1])

    def small_send(k, src, dst, dev):
        cp = pltpu.make_async_remote_copy(
            src_ref=src, dst_ref=dst, send_sem=sm_send.at[k], recv_sem=sm_recv.at[k], device_id=dev, device_id_type=MESH
        )
        cp.start()
        pend.append((cp, None))

    partners = [(b, fy), (b, fz1), (b, zb * 2 + y)]

    def small_first():
        for i in range(16):
            smine[0, i : i + 1, :] = jnp.sum(sums8[i], axis=0, keepdims=True)
        small_send(0, smine.at[0], srecv.at[0], partners[0])

    def small_step(k):
        wait_on(srecv.at[k], sm_recv.at[k])
        if k < 2:
            smine[k + 1] = smine[k] + srecv[k]
            small_send(k + 1, smine.at[k + 1], srecv.at[k + 1], partners[k + 1])
        else:
            sall[b] = smine[k] + srecv[k]
            sall[b, 14:15, :] = row(14).astype(bf16).astype(f32)
            small_send(3, sall.at[b], sall.at[b], X)
            small_send(4, sall.at[b], sall.at[b], (bc, f))

    def cond_first():
        at = 3 * f // 4
        for k in range(4):
            @pl.when(lax.rem(3 * f, 4) == k)
            def _(k=k):
                both = jnp.concatenate([sall[b, pl.ds(at, 1), :], sall[b, pl.ds(at + 1, 1), :]], axis=1)
                gvec[...] = both[:, 288 * k : 288 * k + gvec.shape[1]]
        wait_on(ada, ada_sem)
        v = gvec[...]
        high = v.astype(bf16)
        v = v - high.astype(f32)
        middle = v.astype(bf16)
        low = (v - middle.astype(f32)).astype(bf16)
        left = jnp.concatenate([high, middle, low, jnp.zeros((13, gvec.shape[1]), bf16)], axis=0)
        part_sum = dense(left, ada[...])
        cmine[0] = jnp.broadcast_to(jnp.sum(part_sum[:8], axis=0, keepdims=True), cmine.shape[1:])
        small_send(6, cmine.at[0], crecv.at[0], partners[0])

    def cond_step(k):
        wait_on(crecv.at[k], sm_recv.at[6 + k])
        cmine[k + 1] = cmine[k] + crecv[k]
        if k < 2:
            small_send(7 + k, cmine.at[k + 1], crecv.at[k + 1], partners[k + 1])
        else:
            start(cmine.at[3], cond_out, out_sem.at[5])

    def small_x():
        wait_on(sall.at[bx], sm_recv.at[3])
        small_send(5, sall.at[bx], sall.at[bx], (bc, f))

    def small_core():
        wait_on(sall.at[bc], sm_recv.at[4])
        wait_on(sall.at[bxc], sm_recv.at[5])
        start(sall, sums_out, out_sem.at[2])

    A, B, C = 0, 1, 2
    pieces1 = []
    for j in range(4):
        pieces1 += [
            functools.partial(mlp_back, j),
            functools.partial(outer, mats.at[H2], mats.at[GP], pb_ref.at[j]),
            functools.partial(hidden_in, 0, j, GP),
        ]

    def after_one():
        drain()
        open_group(B)
        load_mat(ATT, att_ref)
        load_fl(1, mid_ref)
        load_fl(2, branch_ref)

    def proj_outer():
        wait_on(mats.at[ATT], m_sem.at[ATT])
        outer(mats.at[ATT], mats.at[GB], pa_ref.at[3])

    def before_att():
        load_mat(H1, h1_ref)
        for k in range(3):
            wait_on(mats.at[Q + k], m_sem.at[Q + k])
        clear()

    heads = WID // HEAD_DIM
    pieces2 = [norm_two, proj_outer, att_in, before_att]
    pieces2 += [functools.partial(att_back, range(k, k + 4)) for k in range(0, heads, 4)] + [att_done]

    def a_outer(k):
        if k == 0:
            wait_on(mats.at[H1], m_sem.at[H1])
        outer(mats.at[H1], mats.at[Q + k], pa_ref.at[k])

    pieces2 += [functools.partial(a_outer, k) for k in range(3)]

    def after_two():
        drain()
        open_group(A)
        load_mat(0, x_ref)
        load_fl(3, mid_ref)
        for j in range(2):
            load_mat(1 + j, hid_ref.at[:, pl.ds(j * WID, WID)])

    def h1_in(k):
        hidden_in(0, k, Q + k)
        if k < 2:
            load_mat(Q + k, hid_ref.at[:, pl.ds((2 + k) * WID, WID)])

    pieces3 = [functools.partial(h1_in, k) for k in range(3)] + [norm_one]
    pieces3 += [functools.partial(mlp_out, j) for j in range(4)] + [block_end]
    tail = [small_first] + [functools.partial(small_step, k) for k in range(3)] + [cond_first, small_x] + [functools.partial(cond_step, k) for k in range(3)] + [small_core]

    pieces = pieces1 + [after_one] + pieces2 + [after_two] + pieces3 + tail
    groups = [steps_of(g) for g in range(NG)]
    size = len(groups[0])
    seq = []
    for code in PROGRAM:
        if code < 0:
            seq.append((pieces.pop(0), None))
        else:
            g, n = divmod(code, size)
            fn, i = groups[g][n]
            seq.append((fn, None if i is None else (g, i)))
    assert not pieces
    plan = [t for _, t in seq if t is not None]

    open_group(C)
    start(vec_ref, vec, out_sem.at[3])
    start(ada_ref, ada, ada_sem)
    load_mat(GO, go_ref)
    fetch(0)
    slope_load(0)
    load_mat(H2, h2_ref)
    fetch(1)
    slope_load(1)
    for k in range(3):
        load_mat(Q + k, qkv_ref.at[k])
    start(res_ref, res, out_sem.at[4])
    sums8[...] = jnp.zeros_like(sums8)
    wait_on(vec, out_sem.at[3])
    wait_on(mats.at[GO], m_sem.at[GO])
    wait_on(mats.at[H2], m_sem.at[H2])
    wait_on(res, out_sem.at[4])
    first_sums()
    for fn, _ in seq:
        fn()
    for loc, rc in finals[-2:]:
        loc.wait()
        rc.wait_send()
    for g in range(NG):
        for q, j in enumerate((bc, bxc)):
            wait_on(O[g].at[j], o_recv.at[g, q])
    for cp, _ in pend:
        cp.wait_send()
    wait_on(lat_out, out_sem.at[0])
    wait_on(block_out, out_sem.at[1])
    wait_on(sums_out, out_sem.at[2])
    wait_on(cond_out, out_sem.at[5])


def backward(mask, vec, wa, wb, wc, x, res, h1, qkv, att, branch, mid, h2, slope, hid, go, pc, w_ada):
    any_space = pl.BlockSpec(memory_space=pl.ANY)
    f32, bf16 = jnp.float32, jnp.bfloat16
    rows = x.shape[0]
    sds = jax.ShapeDtypeStruct
    sem = pltpu.SemaphoreType.DMA
    mat = (rows, WID)
    blkshape = (ROWS, WID)
    outs = (
        sds((4, 16, WID), f32), sds((8, WID), f32), sds((4,) + blkshape, f32), sds((4,) + blkshape, f32), sds((4,) + blkshape, f32),
        sds(mat, bf16), sds(mat, f32), sds((4, WID, WID), bf16), sds((4, WID, WID), bf16),
    )

    def vm(*shape, dt=bf16):
        return pltpu.VMEM(shape, dt)

    return pl.pallas_call(
        backward_kernel,
        out_shape=outs,
        in_specs=[pl.BlockSpec(memory_space=pltpu.SMEM)] + [any_space] * 17,
        out_specs=(any_space,) * len(outs),
        scratch_shapes=[
            vm(NG, 16, *blkshape), vm(4, *blkshape), vm(NG, 2, *blkshape), vm(NG, 2, *blkshape), vm(NG, 4, *blkshape), vm(NG, 2, *blkshape),
            vm(NG, *blkshape), vm(NG, 3, *blkshape), vm(NG, 2, *blkshape), vm(2, *blkshape, dt=f32),
            vm(16, WID, dt=f32), vm(2, WID, WID), vm(2, 384, WID), vm(6, *mat), vm(*mat), vm(4, *mat, dt=f32),
            vm(16, 8, WID, dt=f32), vm(3, 16, WID, dt=f32), vm(3, 16, WID, dt=f32), vm(4, 16, WID, dt=f32),
            vm(*w_ada.shape), vm(1, w_ada.shape[0], dt=f32), vm(4, 8, WID, dt=f32), vm(3, 8, WID, dt=f32),
            sem((4,)), sem((NG, 16)), sem((NG, 16)), sem((NG, 24)), sem((NG, 2)), sem((NG, 2)), sem((NG, 4)), sem((NG, 2)), sem((NG,)),
            sem((NG, 3)), sem((NG, 2)), sem((NG, 2)), sem((NG, 2)), sem((NG, 2)),
            sem((2,)), sem((2,)), sem((6,)), sem((4,)), sem((2,)), sem((6,)), sem((9,)), sem((9,)), sem,
        ],
        compiler_params=pltpu.CompilerParams(collective_id=2, has_side_effects=True, vmem_limit_bytes=64 << 20),
        name="backward",
    )(mask, vec, wa, wb, wc, x, res, h1, qkv, att, branch, mid, h2, slope, hid, go, pc, w_ada)


def on_device_fast(
    latents, cond, live, w_ada, b_ada, w_qkv, b_qv, w_proj, b_proj, w_fc1, b_fc1, w_fc2, b_fc2, cotangent
):
    images, length, width = latents.shape[1:]
    rows = images * length
    f32 = jnp.float32
    scaled = jax.nn.silu(cond[0]).astype(jnp.bfloat16)
    mod_part = jnp.dot(scaled, w_ada, preferred_element_type=f32) + b_ada.astype(f32)
    at = lax.axis_index("fsdp")

    def place(part, total):
        return lax.dynamic_update_slice(jnp.zeros((total,), f32), part, (at * part.shape[0],))

    parts = (mod_part, b_qv.astype(f32), b_proj.astype(f32), b_fc1.astype(f32), b_fc2.astype(f32))
    vec = jnp.concatenate([place(p, 8 * p.shape[0]) for p in parts] + [jnp.where(at == 0, scaled.astype(f32), 0.0), jnp.zeros((width,), f32)]).reshape(16, width)
    la = jnp.concatenate([jnp.transpose(w_qkv.reshape(ROWS, 3, WID), (1, 0, 2)), w_proj[None]])
    lb = jnp.transpose(w_fc1.reshape(ROWS, 4, WID), (1, 0, 2))
    lc = w_fc2.reshape(4, ROWS, WID)
    live_mask = (lax.iota(jnp.int32, images) < live[0, 0]).astype(f32)
    row_mask = jnp.repeat(live_mask, length)[:, None]
    x_rows = latents[0].reshape(rows, width)
    res = cotangent[0].reshape(rows, width) * row_mask.astype(jnp.bfloat16)
    vec, wa, wb, wc, h_first, qkv, attended, branch, middle, h_second, slope, hidden, grad_out, grad_fc2 = forward(vec, la, lb, lc, x_rows, res)
    sums, cond_sum, oa, ob, oc, block_out, grad_rows, _, _ = backward(
        live_mask, vec, wa, wb, wc.reshape(4, width, width), x_rows, res, h_first, qkv, attended, branch, middle, h_second, slope, hidden,
        grad_out, grad_fc2.reshape(8, 4, ROWS, width), jnp.transpose(w_ada),
    )
    flat = sums.reshape(4, 16 * width)
    total = jnp.sum(flat, axis=0)

    def mine(v, begin, size):
        return lax.dynamic_slice_in_dim(v, begin + at * size, size, axis=-1)

    mod_bins = mine(flat, 0, 6 * width // 8)
    high = lax.reduce_precision(mod_bins, 8, 7)
    middle = lax.reduce_precision(mod_bins - high, 8, 7)
    low = lax.reduce_precision(mod_bins - high - middle, 8, 7)
    split = jnp.concatenate([high, middle, low]).astype(jnp.bfloat16)
    scaled_bins = jnp.tile(sums[:, 14].astype(jnp.bfloat16), (3, 1))
    grad_wada = jnp.einsum("bd,be->de", scaled_bins, split, preferred_element_type=f32)
    silu_pull = jax.vjp(jax.nn.silu, cond[0])[1]
    grad_cond = silu_pull(cond_sum[0])[0][None, :]
    return (
        block_out.reshape(latents.shape),
        grad_rows.reshape(latents.shape),
        grad_cond,
        grad_wada,
        mine(total, 0, 6 * width // 8),
        jnp.transpose(oa[:3], (1, 0, 2)).reshape(ROWS, 3 * width),
        mine(total, 6 * width, 2 * width // 8),
        oa[3],
        mine(total, 8 * width, width // 8),
        jnp.transpose(ob, (1, 0, 2)).reshape(ROWS, 4 * width),
        mine(total, 9 * width, 4 * width // 8),
        oc.reshape(4 * ROWS, width),
        mine(total, 13 * width, width // 8),
    )


def solution(mesh):
    fast = mesh.shape["bin"] == 4 and mesh.shape["fsdp"] == 8
    return jax.shard_map(
        on_device_fast if fast else on_device_generic,
        mesh=mesh,
        in_specs=(
            P("bin", "fsdp", None, None),
            P("bin", None),
            P("bin", "fsdp"),
            P(None, "fsdp"),
            P("fsdp"),
            P("fsdp", None),
            P("fsdp"),
            P("fsdp", None),
            P("fsdp"),
            P("fsdp", None),
            P("fsdp"),
            P("fsdp", None),
            P("fsdp"),
            P("bin", "fsdp", None, None),
        ),
        out_specs=(
            P("bin", "fsdp", None, None),
            P("bin", "fsdp", None, None),
            P("bin", None),
            P(None, "fsdp"),
            P("fsdp"),
            P("fsdp", None),
            P("fsdp"),
            P("fsdp", None),
            P("fsdp"),
            P("fsdp", None),
            P("fsdp"),
            P("fsdp", None),
            P("fsdp"),
        ),
        check_vma=False,
    )
```

```python
import functools

import jax
import jax.numpy as jnp
from jax import lax
from jax.experimental import pallas as pl
from jax.experimental.pallas import tpu as pltpu
from jax.sharding import PartitionSpec as P

HEAD_DIM = 72
MESH = pl.DeviceIdType.MESH
ROWS = 144
WID = 1152
NG = 3


def layer_norm(field):
    center = field - jnp.mean(field, axis=-1, keepdims=True)
    return center * lax.rsqrt(jnp.mean(center * center, axis=-1, keepdims=True) + 1e-06)


def gelu_tanh(field):
    return (
        0.5
        * field
        * (1.0 + jnp.tanh(0.7978845608028654 * (field + 0.044715 * field * field * field)))
    )


def modulate(field, shift_vec, scale_vec):
    return layer_norm(field) * (1.0 + scale_vec) + shift_vec


def pair_scores(query_block, key_block):
    return jnp.einsum(
        "gqhd,gkhd->ghqk", query_block, key_block, preferred_element_type=jnp.float32
    ) * HEAD_DIM ** (-0.5)


def attend_pair(group_item):
    query_block, key_block, value_block = group_item
    scores = pair_scores(query_block, key_block)
    highest = jnp.max(scores, axis=-1, keepdims=True)
    exp_scores = jnp.exp(scores - highest)
    totals = jnp.sum(exp_scores, axis=-1, keepdims=True)
    attn_probs = (exp_scores / totals).astype(jnp.bfloat16)
    attended = jnp.einsum(
        "ghqk,gkhd->gqhd", attn_probs, value_block, preferred_element_type=jnp.float32
    )
    return (attended, (highest + jnp.log(totals))[..., 0])


def attend_back(group_item):
    query_block, key_block, value_block, log_total, grad_att = group_item
    scores = pair_scores(query_block, key_block)
    attn_probs = jnp.exp(scores - log_total[..., None])
    grad_probs = jnp.einsum(
        "gqhd,gkhd->ghqk", grad_att, value_block, preferred_element_type=jnp.float32
    )
    row_terms = jnp.sum(attn_probs * grad_probs, axis=-1, keepdims=True)
    grad_scores = (attn_probs * (grad_probs - row_terms)).astype(jnp.bfloat16)
    grad_query = jnp.einsum(
        "ghqk,gkhd->gqhd", grad_scores, key_block, preferred_element_type=jnp.float32
    ) * HEAD_DIM ** (-0.5)
    grad_key = jnp.einsum(
        "ghqk,gqhd->gkhd", grad_scores, query_block, preferred_element_type=jnp.float32
    ) * HEAD_DIM ** (-0.5)
    grad_value = jnp.einsum(
        "ghqk,gqhd->gkhd",
        attn_probs.astype(jnp.bfloat16),
        grad_att,
        preferred_element_type=jnp.float32,
    )
    return jnp.stack([grad_query, grad_key, grad_value], axis=2)


def run_block(flat_rows, modulation, weights, images, length):
    full_qkv, full_proj, full_fc1, full_fc2, bias_qv, bias_proj, bias_fc1, bias_fc2 = weights
    width = flat_rows.shape[1]
    heads = width // HEAD_DIM
    pieces = jnp.split(modulation, 6)
    h_first = modulate(flat_rows, pieces[0], pieces[1]).astype(jnp.bfloat16)
    qkv_bias = jnp.concatenate(
        [bias_qv[:width], jnp.zeros((width,), jnp.bfloat16), bias_qv[width:]]
    ).astype(jnp.float32)
    qkv_rows = (jnp.dot(h_first, full_qkv, preferred_element_type=jnp.float32) + qkv_bias).astype(
        jnp.bfloat16
    )
    split_rows = qkv_rows.reshape(images // 2, 2, length, 3, heads, HEAD_DIM)
    attended, log_total = lax.map(
        attend_pair, (split_rows[:, :, :, 0], split_rows[:, :, :, 1], split_rows[:, :, :, 2])
    )
    attended = attended.reshape(images * length, width).astype(jnp.bfloat16)
    branch = jnp.dot(attended, full_proj, preferred_element_type=jnp.float32) + bias_proj.astype(
        jnp.float32
    )
    middle = flat_rows + pieces[2] * branch
    h_second = modulate(middle, pieces[3], pieces[4]).astype(jnp.bfloat16)
    pre_act = jnp.dot(h_second, full_fc1, preferred_element_type=jnp.float32) + bias_fc1.astype(
        jnp.float32
    )
    hidden = gelu_tanh(pre_act).astype(jnp.bfloat16)
    mlp_out = jnp.dot(hidden, full_fc2, preferred_element_type=jnp.float32) + bias_fc2.astype(
        jnp.float32
    )
    result = middle + pieces[5] * mlp_out
    return (
        h_first,
        split_rows,
        log_total,
        attended,
        branch,
        middle,
        h_second,
        pre_act,
        hidden,
        mlp_out,
        result,
    )


def on_device_generic(
    latents,
    cond,
    live,
    w_ada,
    b_ada,
    w_qkv,
    b_qv,
    w_proj,
    b_proj,
    w_fc1,
    b_fc1,
    w_fc2,
    b_fc2,
    cotangent,
):
    images = latents.shape[1]
    length = latents.shape[2]
    width = latents.shape[3]
    heads = width // HEAD_DIM
    scaled = jax.nn.silu(cond[0]).astype(jnp.bfloat16)
    mod_part = jnp.dot(scaled, w_ada, preferred_element_type=jnp.float32) + b_ada.astype(
        jnp.float32
    )
    modulation = lax.all_gather(mod_part, "fsdp", axis=0, tiled=True)
    gathered = (
        lax.all_gather(w_qkv, "fsdp", axis=0, tiled=True),
        lax.all_gather(w_proj, "fsdp", axis=0, tiled=True),
        lax.all_gather(w_fc1, "fsdp", axis=0, tiled=True),
        lax.all_gather(w_fc2, "fsdp", axis=0, tiled=True),
        lax.all_gather(b_qv, "fsdp", axis=0, tiled=True),
        lax.all_gather(b_proj, "fsdp", axis=0, tiled=True),
        lax.all_gather(b_fc1, "fsdp", axis=0, tiled=True),
        lax.all_gather(b_fc2, "fsdp", axis=0, tiled=True),
    )
    flat_rows = latents[0].reshape(images * length, width).astype(jnp.float32)
    live_mask = (lax.iota(jnp.int32, images) < live[0, 0]).astype(jnp.float32)
    row_mask = jnp.repeat(live_mask, length)[:, None]
    forward_run = run_block(flat_rows, modulation, gathered, images, length)
    block_out = (forward_run[10] * row_mask).astype(jnp.bfloat16).reshape(latents.shape)
    weights = (
        lax.all_gather(w_qkv, "fsdp", axis=0, tiled=True),
        lax.all_gather(w_proj, "fsdp", axis=0, tiled=True),
        lax.all_gather(w_fc1, "fsdp", axis=0, tiled=True),
        lax.all_gather(w_fc2, "fsdp", axis=0, tiled=True),
        lax.all_gather(b_qv, "fsdp", axis=0, tiled=True),
        lax.all_gather(b_proj, "fsdp", axis=0, tiled=True),
        lax.all_gather(b_fc1, "fsdp", axis=0, tiled=True),
        lax.all_gather(b_fc2, "fsdp", axis=0, tiled=True),
    )
    full_qkv, full_proj, full_fc1, full_fc2 = (weights[0], weights[1], weights[2], weights[3])
    saved = run_block(flat_rows, modulation, weights, images, length)
    (
        h_first,
        split_rows,
        log_total,
        attended,
        branch,
        middle,
        h_second,
        pre_act,
        hidden,
        mlp_out,
        result,
    ) = saved
    pieces = jnp.split(modulation, 6)
    grad_res = cotangent[0].reshape(images * length, width).astype(jnp.float32) * row_mask
    grad_out = (pieces[5] * grad_res).astype(jnp.bfloat16)
    grad_gate_two = jnp.sum(grad_res * mlp_out, axis=0)
    grad_fc2 = jnp.einsum("rf,rd->fd", hidden, grad_out, preferred_element_type=jnp.float32)
    grad_bfc2 = jnp.sum(grad_out.astype(jnp.float32), axis=0)
    grad_hidden = jnp.einsum("rd,fd->rf", grad_out, full_fc2, preferred_element_type=jnp.float32)
    gelu_pull = jax.vjp(gelu_tanh, pre_act)[1]
    grad_pre = gelu_pull(grad_hidden)[0].astype(jnp.bfloat16)
    grad_fc1 = jnp.einsum("rd,rf->df", h_second, grad_pre, preferred_element_type=jnp.float32)
    grad_bfc1 = jnp.sum(grad_pre.astype(jnp.float32), axis=0)
    grad_h2 = jnp.einsum("rf,df->rd", grad_pre, full_fc1, preferred_element_type=jnp.float32)
    second_pull = jax.vjp(modulate, middle, pieces[3], pieces[4])[1]
    grad_mid_norm, grad_shift_two, grad_scale_two = second_pull(grad_h2)
    grad_mid = grad_res + grad_mid_norm
    grad_branch = (pieces[2] * grad_mid).astype(jnp.bfloat16)
    grad_gate_one = jnp.sum(grad_mid * branch, axis=0)
    grad_proj = jnp.einsum("rd,re->de", attended, grad_branch, preferred_element_type=jnp.float32)
    grad_bproj = jnp.sum(grad_branch.astype(jnp.float32), axis=0)
    grad_att = jnp.einsum(
        "re,de->rd", grad_branch, full_proj, preferred_element_type=jnp.float32
    ).astype(jnp.bfloat16)
    grad_att = grad_att.reshape(images // 2, 2, length, heads, HEAD_DIM)
    grad_qkv = lax.map(
        attend_back,
        (
            split_rows[:, :, :, 0],
            split_rows[:, :, :, 1],
            split_rows[:, :, :, 2],
            log_total,
            grad_att,
        ),
    )
    grad_qkv = grad_qkv.reshape(images * length, 3 * width).astype(jnp.bfloat16)
    grad_wqkv = jnp.einsum("rd,re->de", h_first, grad_qkv, preferred_element_type=jnp.float32)
    qkv_sums = jnp.sum(grad_qkv.astype(jnp.float32), axis=0)
    grad_bqv = jnp.concatenate([qkv_sums[:width], qkv_sums[2 * width :]])
    grad_h1 = jnp.einsum("re,de->rd", grad_qkv, full_qkv, preferred_element_type=jnp.float32)
    first_pull = jax.vjp(modulate, flat_rows, pieces[0], pieces[1])[1]
    grad_rows_norm, grad_shift_one, grad_scale_one = first_pull(grad_h1)
    grad_rows = grad_mid + grad_rows_norm
    grad_mod = jnp.concatenate(
        [
            grad_shift_one,
            grad_scale_one,
            grad_gate_one,
            grad_shift_two,
            grad_scale_two,
            grad_gate_two,
        ]
    )
    shards = (
        lax.psum_scatter(grad_wqkv, "fsdp", scatter_dimension=0, tiled=True),
        lax.psum_scatter(grad_proj, "fsdp", scatter_dimension=0, tiled=True),
        lax.psum_scatter(grad_fc1, "fsdp", scatter_dimension=0, tiled=True),
        lax.psum_scatter(grad_fc2, "fsdp", scatter_dimension=0, tiled=True),
        lax.psum_scatter(grad_bqv, "fsdp", scatter_dimension=0, tiled=True),
        lax.psum_scatter(grad_bproj, "fsdp", scatter_dimension=0, tiled=True),
        lax.psum_scatter(grad_bfc1, "fsdp", scatter_dimension=0, tiled=True),
        lax.psum_scatter(grad_bfc2, "fsdp", scatter_dimension=0, tiled=True),
        lax.psum_scatter(grad_mod, "fsdp", scatter_dimension=0, tiled=True),
    )
    mod_mine = shards[8]
    grad_wada = scaled.astype(jnp.float32)[:, None] * mod_mine[None, :]
    grad_scaled = jnp.dot(w_ada.astype(jnp.float32), mod_mine, precision=lax.Precision.HIGHEST)
    grad_scaled = lax.psum(grad_scaled, "fsdp")
    silu_pull = jax.vjp(jax.nn.silu, cond[0])[1]
    grad_cond = silu_pull(grad_scaled)[0][None, :]
    totals = lax.psum(
        (
            shards[0],
            shards[1],
            shards[2],
            shards[3],
            shards[4],
            shards[5],
            shards[6],
            shards[7],
            grad_wada,
            mod_mine,
        ),
        "bin",
    )
    return (
        block_out,
        grad_rows.reshape(latents.shape),
        grad_cond,
        totals[8],
        totals[9],
        totals[0],
        totals[4],
        totals[1],
        totals[5],
        totals[2],
        totals[6],
        totals[3],
        totals[7],
    )


TILE = 256
UN = 4
GATHER_PROGRAM = (
    0, 1, 2, 5, -1, 9, 4, 20, 7, -1, 19, 10, 13, -1, 11, 3, -1, 24, 16, 14, 17, 15, 30, 12,
    21, 8, 29, 6, 18, 28, -1, 38, 42, 23, 39, -1, 41, 22, 35, -1, -1, -1, 43, 26, 32, -1, 47, 33,
    -1, 34, 25, 27, 31, 36, 37, 44, 49, -1, -1, 48, -1, 40, 51, -1, 54, 53, -1, 46, 45, 50, 52, 55,
    -1, -1, -1, 56, -1, -1,
)
STRIP = 16


def coords():
    b = lax.axis_index("bin")
    f = lax.axis_index("fsdp")
    return b, f, b // 2, lax.rem(b, 2), f // 2, lax.rem(f, 2)


def strip_loop(rows, body, unroll=1):
    @pl.loop(0, rows // STRIP, unroll=unroll)
    def _(k):
        body(pl.ds(pl.multiple_of(k * STRIP, STRIP), STRIP))


def dense(left, right):
    return jnp.dot(left, right, preferred_element_type=jnp.float32)


def dense_nt(left, right):
    return lax.dot_general(left, right, (((1,), (1,)), ((), ())), preferred_element_type=jnp.float32)


def dense_tn(left, right):
    return lax.dot_general(left, right, (((0,), (0,)), ((), ())), preferred_element_type=jnp.float32)


def center_rows(v):
    v = v - jnp.mean(v, axis=-1, keepdims=True)
    inv = lax.rsqrt(jnp.mean(v * v, axis=-1, keepdims=True) + 1e-06)
    return v * inv, inv


def head_window(h):
    start = HEAD_DIM * h
    low = start // 128 * 128
    width = 128 if start - low + HEAD_DIM <= 128 else 256
    return low, width, start - low


def head_mask(off, width):
    lanes = lax.broadcasted_iota(jnp.int32, (1, width), 1)
    return jnp.logical_and(lanes >= off, lanes < off + HEAD_DIM)


def head_probs(q, k):
    scores = dense_nt(k, q) * HEAD_DIM ** (-0.5)
    high = jnp.max(scores, axis=0, keepdims=True)
    e = jnp.exp(scores - high)
    total = jnp.sum(e, axis=0, keepdims=True)
    return e * (1.0 / total), high + jnp.log(total)


def forward_kernel(
    vec_ref, la_ref, lb_ref, lc_ref, x_ref, res_ref,
    vec_out, wa_out, wb_out, wc_out, h1_out, qkv_out, att_out, branch_out, mid_out, h2_out, slope_out, hid_out, go_out, pc_out, lse_out, norm_out, inv_out,
    wa, wb, wc, vecs, vec, xs, res, h1, qkv, att, mid, h2, hid, go, acc, slope, pst, lse, norm, inv,
    loc_sem, sm_send, sm_recv, send_sem, recv_sem, in_sem, out_sem, wo_sem, co_sem, sl_sem, ps_sem,
):
    b, f, x, c, z, y = coords()
    bx = lax.rem(b + 2, 4)
    bc = b + 1 - 2 * c
    bxc = lax.rem(bc + 2, 4)
    fy = f + 1 - 2 * y
    yb = 1 - y
    z1 = z + 1 - 2 * lax.rem(z, 2)
    mid_z = jnp.logical_or(z == 1, z == 2)
    zb = lax.rem(z + 2, 4)
    zc = 3 - z
    z2 = jnp.where(mid_z, zc, zb)
    z3 = jnp.where(mid_z, zb, zc)
    fz1 = z1 * 2 + y
    bar = pltpu.get_barrier_semaphore()
    for k in range(1, 8):
        pl.semaphore_signal(bar, inc=1, device_id=(b, lax.rem(f + k, 8)), device_id_type=MESH)
    pl.semaphore_signal(bar, inc=1, device_id=(bx, f), device_id_type=MESH)
    pl.semaphore_signal(bar, inc=1, device_id=(bc, f), device_id_type=MESH)
    pl.semaphore_wait(bar, 9)

    W = (wa, wb, wc)
    L = (la_ref, lb_ref, lc_ref)

    def blk(g, j, ff):
        if g < 2:
            return W[g].at[j, pl.ds(pl.multiple_of(ff * ROWS, ROWS), ROWS)]
        return W[g].at[ff, j]

    smalls = []
    partners = ((b, fy), (b, fz1), (b, zb * 2 + y))

    def small_send(k):
        cp = pltpu.make_async_remote_copy(
            src_ref=vecs.at[k], dst_ref=vecs.at[3 + k], send_sem=sm_send.at[k], recv_sem=sm_recv.at[k],
            device_id=partners[k], device_id_type=MESH,
        )
        cp.start()
        smalls.append(cp)

    def small_step(k):
        pltpu.make_async_copy(vecs.at[3 + k], vecs.at[3 + k], sm_recv.at[k]).wait()
        total = vecs[k] + vecs[3 + k]
        if k < 2:
            vecs[k + 1] = total
            small_send(k + 1)
        else:
            vec[...] = total
            keep(vec, vec_out, 0)


    pend = []
    outs = []
    cnt = [0] * NG

    def send(g, j, ff, dev, cond=None, src=None):
        i = cnt[g]
        cnt[g] += 1
        cp = pltpu.make_async_remote_copy(
            src_ref=blk(g, j, ff) if src is None else src, dst_ref=blk(g, j, ff),
            send_sem=send_sem.at[g, i], recv_sem=recv_sem.at[g, j, ff], device_id=dev, device_id_type=MESH,
        )
        if cond is None:
            cp.start()
        else:
            @pl.when(cond)
            def _():
                cp.start()
        pend.append((cp, cond))

    def copy_out(src, dst, sem):
        cp = pltpu.make_async_copy(src, dst, sem)
        cp.start()
        return cp

    def arrive(g, j, ff, cond=None):
        def go_on():
            pltpu.make_async_copy(blk(g, j, ff), blk(g, j, ff), recv_sem.at[g, j, ff]).wait()
            if g == 2:
                copy_out(wc.at[ff, j], wc_out.at[ff, j], co_sem.at[j, ff])
        if cond is None:
            go_on()
        else:
            pl.when(cond)(go_on)

    up = (b, jnp.minimum(f + 2, 7))
    dn = (b, jnp.maximum(f - 2, 0))

    def piece(g, j):
        if g != 1:
            return L[g].at[j]
        return lb_ref.at[:, pl.ds(pl.multiple_of(j * WID, WID), WID)]

    def start_sends(g):
        sb = piece(g, b)
        sx = piece(g, bx)
        return [
            lambda: send(g, b, f, up, z < 3, sb), lambda: send(g, b, f, dn, z > 0, sb), lambda: send(g, b, f, (b, fy), None, sb),
            lambda: send(g, bx, f, (b, fz1), None, sx), lambda: send(g, bx, f, (b, fy), None, sx),
        ]

    locs = []

    def local(g):
        for j in range(4):
            locs.append(copy_out(piece(g, j), blk(g, j, f), loc_sem.at[g, j]))

    def Z(g, zz, x_too):
        ff = zz * 2 + y
        arrive(g, b, ff)
        send(g, b, ff, up, jnp.logical_and(zz < z, z < 3))
        send(g, b, ff, dn, jnp.logical_and(zz > z, z > 0))
        send(g, b, ff, (b, fy))
        if x_too:
            send(g, b, ff, (bx, f))
        send(g, b, ff, (bc, f))

    def Y(g, zz, x_too):
        ff = zz * 2 + yb
        arrive(g, b, ff)
        if x_too:
            send(g, b, ff, (bx, f))
        send(g, b, ff, (bc, f))

    def X(g, ff):
        arrive(g, bx, ff)
        send(g, bx, ff, (bc, f))

    def actions(g):
        return [
            lambda: Z(g, z1, False), lambda: X(g, fz1), lambda: Y(g, z, False), lambda: X(g, fy),
            lambda: Z(g, z2, True), lambda: Y(g, z1, True), lambda: Z(g, z3, True), lambda: X(g, z2 * 2 + y),
            lambda: Y(g, z2, True), lambda: X(g, z1 * 2 + yb), lambda: X(g, z3 * 2 + y), lambda: Y(g, z3, True),
            lambda: X(g, z2 * 2 + yb), lambda: X(g, z3 * 2 + yb),
        ]

    def other_core(g):
        for zz in range(4):
            for jj in (bc, bxc):
                arrive(g, jj, zz * 2 + y, zz != z)
                arrive(g, jj, zz * 2 + yb)
        for cp in locs[g * 4 : g * 4 + 4]:
            cp.wait()

    def keep(src, dst, i):
        outs.append(copy_out(src, dst, out_sem.at[i]))

    def row(i):
        return vec[i : i + 1, :]

    def start_rows():
        in_x.wait()

        def first(r):
            n, _ = center_rows(xs[r, :].astype(jnp.float32))
            h1[r, :] = (n * (1.0 + row(1)) + row(0)).astype(jnp.bfloat16)

        strip_loop(h1.shape[0], first, UN)
        keep(h1, h1_out, 1)

    def start_grads():
        in_res.wait()

        def out_grad(r):
            go[r, :] = (res[r, :].astype(jnp.float32) * row(5)).astype(jnp.bfloat16)

        strip_loop(go.shape[0], out_grad)
        keep(go, go_out, 2)

    tiles = xs.shape[0] // TILE

    def tile(i):
        return pl.ds(pl.multiple_of(i * TILE, TILE), TILE)

    def project(j):
        @pl.loop(0, tiles)
        def _(i):
            v = dense(h1[tile(i), :], wa[j])
            if j != 1:
                v = v + row(6 + j // 2)
            qkv[j, tile(i), :] = v.astype(jnp.bfloat16)
        keep(qkv.at[j], qkv_out.at[j], 3 + j)

    def attention():
        @pl.loop(0, tiles)
        def _(i):
            acc[...] = jnp.zeros_like(acc)
            for h in range(WID // HEAD_DIM):
                low, width, off = head_window(h)
                cols = slice(low, low + width)
                mask = head_mask(off, width)
                q = qkv[0, tile(i), cols]
                v = qkv[2, tile(i), cols]
                probs, lse[i, h : h + 1, :] = head_probs(jnp.where(mask, q, jnp.zeros_like(q)), qkv[1, tile(i), cols])
                acc[:, cols] += dense_tn(probs.astype(jnp.bfloat16), jnp.where(mask, v, jnp.zeros_like(v)))
            att[tile(i), :] = acc[...].astype(jnp.bfloat16)
        keep(att, att_out, 6)
        keep(lse, lse_out, 11)

    def branch():
        @pl.loop(0, tiles)
        def _(i):
            mid[tile(i), :] = dense(att[tile(i), :], wa[3]) + row(8)
        cp = copy_out(mid, branch_out, out_sem.at[7])
        cp.wait()

        def second(r):
            m = xs[r, :].astype(jnp.float32) + row(2) * mid[r, :]
            mid[r, :] = m
            n, inverse = center_rows(m)
            norm[r, :] = n
            inv[r, :] = jnp.broadcast_to(inverse, (STRIP, 128))
            h2[r, :] = (n * (1.0 + row(4)) + row(3)).astype(jnp.bfloat16)

        strip_loop(mid.shape[0], second, UN)
        keep(mid, mid_out, 8)
        keep(h2, h2_out, 9)
        keep(norm, norm_out, 12)
        keep(inv, inv_out, 13)

    def hidden(j):
        cols = slice(j * WID, j * WID + WID)

        @pl.loop(0, tiles)
        def _(i):
            acc[...] = dense(h2[tile(i), :], wb[j]) + row(9 + j)

            @pl.when(j * tiles + i >= 1)
            def _():
                pltpu.make_async_copy(slope, slope_out.at[tile(0), :WID], sl_sem).wait()

            @pl.loop(0, TILE // STRIP)
            def _(k):
                r = pl.ds(pl.multiple_of(k * STRIP, STRIP), STRIP)
                v = acc[r, :]
                sq = v * v
                t = jnp.tanh(0.7978845608028654 * (v + 0.044715 * sq * v))
                half = 0.5 * (1.0 + t)
                slope[r, :] = half + 0.5 * v * (1.0 - t * t) * (0.7978845608028654 * (1.0 + 0.134145 * sq))
                hid[pl.ds(pl.multiple_of(i * TILE + k * STRIP, STRIP), STRIP), cols] = (v * half).astype(jnp.bfloat16)

            copy_out(slope, slope_out.at[tile(i), cols], sl_sem)
        if j == 3:
            pltpu.make_async_copy(slope, slope_out.at[tile(0), :WID], sl_sem).wait()
            keep(hid, hid_out, 10)

    part = pst.shape[1]

    def outer(j):
        @pl.loop(0, WID // part)
        def _(i):
            k = j * (WID // part) + i
            slot = lax.rem(k, 2)

            @pl.when(k >= 2)
            def _():
                pltpu.make_async_copy(pst.at[slot], pc_out.at[pl.ds(0, part)], ps_sem.at[slot]).wait()
            at = pl.multiple_of(k * part, part)
            pst[slot] = dense_tn(hid[:, pl.ds(at, part)], go[...]).astype(jnp.bfloat16)
            copy_out(pst.at[slot], pc_out.at[pl.ds(at, part)], ps_sem.at[slot])
        if j == 3:
            for slot in range(2):
                pltpu.make_async_copy(pst.at[slot], pc_out.at[pl.ds(0, part)], ps_sem.at[slot]).wait()

    def weights_out(g):
        outs.append(copy_out(W[g], (wa_out, wb_out)[g], wo_sem.at[g]))

    in_x = copy_out(x_ref, xs, in_sem.at[0])
    in_res = copy_out(res_ref, res, in_sem.at[1])
    def ready(g):
        other_core(g)
        weights_out(g)

    pieces = [functools.partial(small_step, k) for k in range(3)] + [start_rows, functools.partial(ready, 0)]
    pieces += [functools.partial(project, j) for j in range(3)] + [attention, branch, start_grads, functools.partial(ready, 1)]
    pieces += [functools.partial(hidden, j) for j in range(4)] + [functools.partial(outer, j) for j in range(4)]
    groups = [start_sends(g) + actions(g) for g in range(NG)]
    size = len(groups[0])
    own = pltpu.make_async_copy(vec_ref, vecs.at[0], sm_send.at[3])
    own.start()
    for g in range(NG):
        local(g)
    begun = False
    for code in GATHER_PROGRAM[:-1]:
        if code < 0:
            pieces.pop(0)()
        else:
            g, n = divmod(code, size)
            if n >= 5 and not begun:
                begun = True
                own.wait()
                small_send(0)
            groups[g][n]()
    assert not pieces
    for j in range(4):
        locs[8 + j].wait()
        copy_out(wc.at[f, j], wc_out.at[f, j], co_sem.at[j, f])
    other_core_c = 2
    for zz in range(4):
        for jj in (bc, bxc):
            arrive(other_core_c, jj, zz * 2 + y, zz != z)
            arrive(other_core_c, jj, zz * 2 + yb)
    for cp, cond in pend:
        if cond is None:
            cp.wait_send()
        else:
            @pl.when(cond)
            def _(cp=cp):
                cp.wait_send()
    for cp in smalls:
        cp.wait_send()
    for cp in outs:
        cp.wait()
    for ff in range(8):
        for j in range(4):
            pltpu.make_async_copy(wc.at[ff, j], wc_out.at[ff, j], co_sem.at[j, ff]).wait()


def forward(vec, la, lb, lc, x, res):
    any_space = pl.BlockSpec(memory_space=pl.ANY)
    f32, bf16 = jnp.float32, jnp.bfloat16
    rows = x.shape[0]
    sds = jax.ShapeDtypeStruct
    sem = pltpu.SemaphoreType.DMA
    mat = (rows, WID)
    outs = (
        sds((16, WID), f32), sds((4, WID, WID), bf16), sds((4, WID, WID), bf16), sds((8, 4, ROWS, WID), bf16),
        sds(mat, bf16), sds((3,) + mat, bf16), sds(mat, bf16), sds(mat, f32), sds(mat, f32), sds(mat, bf16),
        sds((rows, 4 * WID), f32), sds((rows, 4 * WID), bf16), sds(mat, bf16), sds((4 * WID, WID), bf16),
        sds((rows // TILE, 16, TILE), f32), sds(mat, f32), sds((rows, 128), f32),
    )
    vm = pltpu.VMEM
    return pl.pallas_call(
        forward_kernel,
        out_shape=outs,
        in_specs=[any_space] * 6,
        out_specs=(any_space,) * len(outs),
        scratch_shapes=[
            vm((4, WID, WID), bf16), vm((4, WID, WID), bf16), vm((8, 4, ROWS, WID), bf16), vm((6, 16, WID), f32), vm((16, WID), f32),
            vm(mat, bf16), vm(mat, bf16), vm(mat, bf16), vm((3,) + mat, bf16), vm(mat, bf16), vm(mat, f32), vm(mat, bf16),
            vm((rows, 4 * WID), bf16), vm(mat, bf16), vm((TILE, WID), f32), vm((TILE, WID), f32), vm((2, 384, WID), bf16),
            vm((rows // TILE, 16, TILE), f32), vm(mat, f32), vm((rows, 128), f32),
            sem((NG, 4)), sem((8,)), sem((8,)), sem((NG, 40)), sem((NG, 4, 8)), sem((2,)), sem((14,)), sem((2,)), sem((4, 8)), sem, sem((2,)),
        ],
        compiler_params=pltpu.CompilerParams(collective_id=1, has_side_effects=True, vmem_limit_bytes=63 << 20),
        name="forward",
    )(vec, la, lb, lc, x, res)


PROGRAM = (
    36, 34, -1, 37, -1, 35, -1, -1, -1, 38, 42, -1, -1, -1, 39, -1, 41, -1, -1, 43, -1, 40, -1, -1,
    19, 44, -1, 26, -1, -1, 25, 47, 48, 17, -1, 46, 24, 21, -1, 45, 22, -1, 23, -1, -1, -1, 18, 28,
    -1, 49, -1, -1, 20, 31, 0, 30, 4, -1, 1, 27, -1, -1, 6, 2, 5, 8, -1, 11, -1, 7, 10, 29,
    3, 32, -1, -1, -1, 13, -1, 14, 9, -1, -1, 12, -1, -1, -1, -1, 15, -1, 50, 33, -1, -1, -1, 16,
)


def backward_kernel(
    mask_ref, vec_ref, wa_ref, wb_ref, wc_ref, x_ref, res_ref, h1_ref, qkv_ref, att_ref, branch_ref, mid_ref, h2_ref, slope_ref,
    hid_ref, go_ref, pc_ref, ada_ref, lse_ref, norm_ref, inv_ref,
    sums_out, cond_out, oa_ref, ob_ref, oc_ref, block_out, lat_out, pa_ref, pb_ref,
    r0, ring, rx4, ry4, ry3, rx2, rn, rz, rt, fin, vec, wbuf, pst, mats, res, fl, sums8, smine, srecv, sall, ada, gvec, cmine, crecv, lse, inv2,
    ring_sem, s0_send, s0_recv, send_sem, rx4_s, ry4_s, ry3_s, rx2_s, rn_s, rz_s, rt_s, o_loc, o_send, o_recv,
    w_sem, p_sem, m_sem, f_sem, sl_sem, out_sem, sm_send, sm_recv, ada_sem, lse_sem, inv_sem,
):
    f32, bf16 = jnp.float32, jnp.bfloat16
    b, f, x, c, z, y = coords()
    bx = lax.rem(b + 2, 4)
    bc = b + 1 - 2 * c
    bxc = lax.rem(bc + 2, 4)
    fy = f + 1 - 2 * y
    yb = 1 - y
    z1 = z + 1 - 2 * lax.rem(z, 2)
    mid_z = jnp.logical_or(z == 1, z == 2)
    zb = lax.rem(z + 2, 4)
    zc = 3 - z
    z2 = jnp.where(mid_z, zc, zb)
    z3 = jnp.where(mid_z, zb, zc)
    fz1 = z1 * 2 + y
    bar = pltpu.get_barrier_semaphore()
    for k in range(1, 8):
        pl.semaphore_signal(bar, inc=1, device_id=(b, lax.rem(f + k, 8)), device_id_type=MESH)
    pl.semaphore_signal(bar, inc=1, device_id=(bx, f), device_id_type=MESH)
    pl.semaphore_signal(bar, inc=1, device_id=(bc, f), device_id_type=MESH)
    pl.semaphore_wait(bar, 9)

    def start(src, dst, sem):
        cp = pltpu.make_async_copy(src, dst, sem)
        cp.start()
        return cp

    def wait_on(ref, sem):
        pltpu.make_async_copy(ref, ref, sem).wait()

    P = (pa_ref, pb_ref, pc_ref)
    O = (oa_ref, ob_ref, oc_ref)

    def blk(g, j, ff):
        if g < 2:
            return P[g].at[j, pl.ds(pl.multiple_of(ff * ROWS, ROWS), ROWS)]
        return P[g].at[ff, j]

    order = [
        (1, z3, yb), (1, z2, yb), (1, z3, y), (1, z2, y), (1, z1, yb), (1, z, yb), (0, z3, yb), (0, z2, yb),
        (0, z1, yb), (0, z, yb), (0, z3, y), (0, z2, y), (1, z1, y), (0, z1, y), (0, z, y), (1, z, y),
    ]
    mine = (b, bx)
    his = (bc, bxc)
    pend = []
    cnt = [0] * NG

    def open_group(g):
        for i, (jj, zz, yy) in enumerate(order):
            cp = pltpu.make_async_remote_copy(
                src_ref=blk(g, his[jj], zz * 2 + yy), dst_ref=r0.at[g, i], send_sem=s0_send.at[g, i],
                recv_sem=s0_recv.at[g, i], device_id=(bc, f), device_id_type=MESH,
            )
            cp.start()
            pend.append((cp, None))
        state["ready"].append(g)
        pump()

    state = {"ready": [], "issued": 0, "used": 0}
    depth = ring.shape[0]

    def pump():
        while state["issued"] < len(plan) and state["issued"] - state["used"] < depth:
            g, i = plan[state["issued"]]
            if g not in state["ready"]:
                return
            jj, zz, yy = order[i]
            slot = state["issued"] % depth
            start(blk(g, mine[jj], zz * 2 + yy), ring.at[slot], ring_sem.at[slot])
            state["issued"] += 1

    def add(dst, srcs):
        @pl.loop(0, ROWS // STRIP, unroll=1)
        def _(k):
            rows = pl.ds(pl.multiple_of(k * STRIP, STRIP), STRIP)
            if len(srcs) == 2 and dst.dtype == bf16:
                dst[rows, :] = srcs[0][rows, :] + srcs[1][rows, :]
                return
            v = srcs[0][rows, :].astype(f32)
            for s in srcs[1:]:
                v = v + s[rows, :].astype(f32)
            dst[rows, :] = v.astype(dst.dtype)

    def combine(g, i, more=()):
        slot = state["used"] % depth
        assert plan[state["used"]] == (g, i)
        wait_on(ring.at[slot], ring_sem.at[slot])
        wait_on(r0.at[g, i], s0_recv.at[g, i])
        srcs = [r0.at[g, i], ring.at[slot]]
        for ref, sem in more:
            wait_on(ref, sem)
            srcs.append(ref)
        add(r0.at[g, i], srcs)
        state["used"] += 1
        pump()

    def send(g, src, dst, rsem, dev):
        i = cnt[g]
        cnt[g] += 1
        cp = pltpu.make_async_remote_copy(
            src_ref=src, dst_ref=dst, send_sem=send_sem.at[g, i], recv_sem=rsem, device_id=dev, device_id_type=MESH
        )
        cp.start()
        pend.append((cp, None))

    X = (bx, f)
    Y = (b, fy)

    def to_x4(g, i, slot):
        combine(g, i)
        send(g, r0.at[g, i], rx4.at[g, slot], rx4_s.at[g, slot], X)

    def to_x2(g, i, slot):
        combine(g, i)
        send(g, r0.at[g, i], rx2.at[g, slot], rx2_s.at[g, slot], X)

    def to_y4(g, i, slot):
        combine(g, i)
        send(g, r0.at[g, i], ry4.at[g, slot], ry4_s.at[g, slot], Y)

    def to_y3(g, i, slot, rslot):
        combine(g, i, () if rslot is None else ((rx4.at[g, rslot], rx4_s.at[g, rslot]),))
        send(g, r0.at[g, i], ry3.at[g, slot], ry3_s.at[g, slot], Y)

    s2 = jnp.where(mid_z, 2, 1)
    s3 = jnp.where(mid_z, 1, 2)

    def to_z(g, i, zz, slot, rslot, yslot):
        more = [(ry3.at[g, yslot], ry3_s.at[g, yslot])]
        if rslot is not None:
            more.append((rx2.at[g, rslot], rx2_s.at[g, rslot]))
        combine(g, i, more)
        send(g, r0.at[g, i], rz.at[g, slot], rz_s.at[g, slot], (b, zz * 2 + y))

    def to_near(g, i):
        combine(g, i, [(ry4.at[g, 1], ry4_s.at[g, 1])])
        send(g, r0.at[g, i], rn.at[g], rn_s.at[g], (b, fz1))

    def own_last(g, i):
        combine(g, i, [(ry3.at[g, 0], ry3_s.at[g, 0])] + [(rz.at[g, k], rz_s.at[g, k]) for k in range(3)])
        send(g, r0.at[g, i], rt.at[g, 0], rt_s.at[g, 0], X)

    def other_last(g, i):
        combine(g, i, [(ry4.at[g, 0], ry4_s.at[g, 0]), (rn.at[g], rn_s.at[g])])
        send(g, r0.at[g, i], rt.at[g, 1], rt_s.at[g, 1], X)

    finals = []

    def final(g):
        if finals:
            for cp in finals[-2:]:
                cp[0].wait()
                cp[1].wait_send()
        for q, (i, slot, j) in enumerate(((14, 1, b), (15, 0, bx))):
            wait_on(rt.at[g, slot], rt_s.at[g, slot])
            add(fin.at[q], [r0.at[g, i], rt.at[g, slot]])
            loc = start(fin.at[q], O[g].at[j], o_loc.at[g, q])
            rc = pltpu.make_async_remote_copy(
                src_ref=fin.at[q], dst_ref=O[g].at[j], send_sem=o_send.at[g, q], recv_sem=o_recv.at[g, q],
                device_id=(bc, f), device_id_type=MESH,
            )
            rc.start()
            finals.append((loc, rc))

    def steps_of(g):
        return [
            (lambda: to_x4(g, 0, 0), 0), (lambda: to_y4(g, 4, 1), 4), (lambda: to_x4(g, 1, 1), 1), (lambda: to_y4(g, 5, 0), 5),
            (lambda: to_x2(g, 2, 0), 2), (lambda: to_x2(g, 3, 1), 3), (lambda: to_y3(g, 6, 3, 0), 6), (lambda: to_y3(g, 7, 2, 1), 7),
            (lambda: to_y3(g, 8, 1, None), 8), (lambda: to_y3(g, 9, 0, None), 9), (lambda: to_near(g, 12), 12),
            (lambda: to_z(g, 10, z3, s3, 0, 3), 10), (lambda: other_last(g, 15), 15), (lambda: to_z(g, 11, z2, s2, 1, 2), 11),
            (lambda: to_z(g, 13, z1, 0, None, 1), 13), (lambda: own_last(g, 14), 14), (lambda: final(g), None),
        ]

    rows = res.shape[0]
    tiles = rows // TILE

    def tile(i):
        return pl.ds(pl.multiple_of(i * TILE, TILE), TILE)

    def row(i):
        return vec[i : i + 1, :]

    def load_mat(k, src):
        return start(src, mats.at[k], m_sem.at[k])

    def load_fl(k, src):
        return start(src, fl.at[k], f_sem.at[k])

    w_list = []
    for j in range(4):
        w_list += [wc_ref.at[j], wb_ref.at[j]]
    w_list += [wa_ref.at[3], wa_ref.at[0], wa_ref.at[1], wa_ref.at[2]] + [wc_ref.at[j] for j in range(4)]
    w_at = [0]

    def fetch(k):
        if k < len(w_list):
            start(w_list[k], wbuf.at[k % 2], w_sem.at[k % 2])

    def with_weight(body):
        k = w_at[0]
        w_at[0] += 1
        wait_on(wbuf.at[k % 2], w_sem.at[k % 2])
        body(wbuf.at[k % 2])
        fetch(k + 2)

    def colsum(i, v):
        sums8[i] += v[:8] + v[8:]

    p_cnt = [0]
    part = pst.shape[1]
    steps = WID // part

    def outer(left, right, dst):
        n = p_cnt[0]
        p_cnt[0] += 1

        @pl.loop(0, steps)
        def _(i):
            k = n * steps + i
            slot = lax.rem(k, 2)

            @pl.when(k >= 2)
            def _():
                wait_on(pst.at[slot], p_sem.at[slot])
            at = pl.multiple_of(i * part, part)
            pst[slot] = dense_tn(left[:, pl.ds(at, part)], right[...]).astype(bf16)
            start(pst.at[slot], dst.at[pl.ds(at, part)], p_sem.at[slot])

    def drain():
        for slot in range(2):
            wait_on(pst.at[slot], p_sem.at[slot])
        p_cnt[0] = 0

    GO, H2, GP, Q = 0, 1, 2, 3
    ATT, GB, GA, H1 = 0, 1, 2, 0

    def slope_load(k):
        if k < 4 * tiles:
            j, i = divmod(k, tiles)
            start(slope_ref.at[pl.ds(i * TILE, TILE), pl.ds(j * WID, WID)], fl.at[2, pl.ds((k % 2) * TILE, TILE)], sl_sem.at[k % 2])

    def mlp_back(j):
        def body(w):
            for i in range(tiles):
                k = j * tiles + i
                sl = fl.at[2, pl.ds((k % 2) * TILE, TILE)]
                fl[3, :TILE, :] = dense_nt(mats[GO, i * TILE : (i + 1) * TILE, :], w[...])
                wait_on(sl, sl_sem.at[k % 2])

                def strip(r):
                    v = (fl[3, r, :] * sl[r, :]).astype(bf16)
                    mats[GP, pl.ds(pl.multiple_of(i * TILE + r.start, STRIP), STRIP), :] = v
                    colsum(9 + j, v.astype(f32))

                strip_loop(TILE, strip)
                slope_load(k + 2)
        with_weight(body)

    def hidden_in(dst, j, left):
        def body(w):
            @pl.loop(0, tiles)
            def _(i):
                v = dense_nt(mats[left, tile(i), :], w[...])
                if j == 0:
                    fl[dst, tile(i), :] = v
                else:
                    fl[dst, tile(i), :] += v
        with_weight(body)

    def first_sums():
        def strip(r):
            colsum(13, mats[GO, r, :].astype(f32))
        strip_loop(rows, strip)

    def norm_two():
        wait_on(fl.at[1], f_sem.at[1])
        wait_on(fl.at[2], f_sem.at[2])

        def strip(r):
            n = fl[1, r, :]
            inv = inv2[r, 0:1]
            g = fl[0, r, :]
            colsum(4, g * n)
            colsum(3, g)
            dn = g * (1.0 + row(4))
            pull = dn - jnp.mean(dn, axis=-1, keepdims=True) - n * jnp.mean(dn * n, axis=-1, keepdims=True)
            gm = res[r, :].astype(f32) + inv * pull
            colsum(2, gm * fl[2, r, :])
            gb = (row(2) * gm).astype(bf16)
            colsum(8, gb.astype(f32))
            fl[1, r, :] = gm
            mats[GB, r, :] = gb

        strip_loop(rows, strip, UN)

    def att_in():
        def body(w):
            @pl.loop(0, tiles)
            def _(i):
                mats[GA, tile(i), :] = dense_nt(mats[GB, tile(i), :], w[...]).astype(bf16)
        with_weight(body)

    def clear():
        def strip(r):
            for k in (0, 2, 3):
                fl[k, r, :] = jnp.zeros((STRIP, WID), f32)
        strip_loop(rows, strip)

    def att_back(heads):
        @pl.loop(0, tiles)
        def _(i):
            for h in heads:
                low, width, off = head_window(h)
                cols = slice(low, low + width)
                mask = head_mask(off, width)

                def pick(k):
                    v = mats[k, tile(i), cols]
                    return v, jnp.where(mask, v, jnp.zeros_like(v))

                _, q = pick(Q)
                k_all, k_own = pick(Q + 1)
                v_all = mats[Q + 2, tile(i), cols]
                _, g = pick(GA)
                scores = dense_nt(k_all, q) * HEAD_DIM ** (-0.5)
                probs = jnp.exp(scores - lse[i, h : h + 1, :])
                grad_probs = dense_nt(v_all, g)
                total = jnp.sum(probs * grad_probs, axis=0, keepdims=True)
                gs = (probs * (grad_probs - total)).astype(bf16)
                fl[3, tile(i), cols] += dense(probs.astype(bf16), g)
                fl[2, tile(i), cols] += dense(gs, q) * HEAD_DIM ** (-0.5)
                fl[0, tile(i), cols] += dense_tn(gs, k_own) * HEAD_DIM ** (-0.5)

    def att_done():
        def strip(r):
            for k, a in enumerate((0, 2, 3)):
                v = fl[a, r, :].astype(bf16)
                mats[Q + k, r, :] = v
                if k != 1:
                    colsum(6 + k // 2, v.astype(f32))
        strip_loop(rows, strip)

    def norm_one():
        wait_on(mats.at[0], m_sem.at[0])

        def strip(r):
            n, inv = center_rows(mats[0, r, :].astype(f32))
            g = fl[0, r, :]
            colsum(1, g * n)
            colsum(0, g)
            dn = g * (1.0 + row(1))
            pull = dn - jnp.mean(dn, axis=-1, keepdims=True) - n * jnp.mean(dn * n, axis=-1, keepdims=True)
            fl[0, r, :] = fl[1, r, :] + inv * pull

        strip_loop(rows, strip, UN)
        start(fl.at[0], lat_out, out_sem.at[0])

    def mlp_out(j):
        k = 1 + j
        wait_on(mats.at[k], m_sem.at[k])

        def body(w):
            @pl.loop(0, tiles)
            def _(i):
                v = dense(mats[k, tile(i), :], w[...])
                if j == 0:
                    fl[2, tile(i), :] = v
                else:
                    fl[2, tile(i), :] += v
        with_weight(body)

    def block_end():
        wait_on(fl.at[3], f_sem.at[3])
        for i in range(tiles):
            m = mask_ref[i]

            def strip(r):
                at = pl.ds(pl.multiple_of(i * TILE + r.start, STRIP), STRIP)
                v = fl[2, at, :] + row(13)
                colsum(5, v * res[at, :].astype(f32))
                mats[5, at, :] = ((fl[3, at, :] + row(5) * v) * m).astype(bf16)

            strip_loop(TILE, strip)
        start(mats.at[5], block_out, out_sem.at[1])

    def small_send(k, src, dst, dev):
        cp = pltpu.make_async_remote_copy(
            src_ref=src, dst_ref=dst, send_sem=sm_send.at[k], recv_sem=sm_recv.at[k], device_id=dev, device_id_type=MESH
        )
        cp.start()
        pend.append((cp, None))

    partners = [(b, fy), (b, fz1), (b, zb * 2 + y)]

    def small_first():
        for i in range(16):
            smine[0, i : i + 1, :] = jnp.sum(sums8[i], axis=0, keepdims=True)
        small_send(0, smine.at[0], srecv.at[0], partners[0])

    def small_step(k):
        wait_on(srecv.at[k], sm_recv.at[k])
        if k < 2:
            smine[k + 1] = smine[k] + srecv[k]
            small_send(k + 1, smine.at[k + 1], srecv.at[k + 1], partners[k + 1])
        else:
            sall[b] = smine[k] + srecv[k]
            sall[b, 14:15, :] = row(14).astype(bf16).astype(f32)
            small_send(3, sall.at[b], sall.at[b], X)
            small_send(4, sall.at[b], sall.at[b], (bc, f))

    def cond_first():
        at = 3 * f // 4
        for k in range(4):
            @pl.when(lax.rem(3 * f, 4) == k)
            def _(k=k):
                both = jnp.concatenate([sall[b, pl.ds(at, 1), :], sall[b, pl.ds(at + 1, 1), :]], axis=1)
                gvec[...] = both[:, 288 * k : 288 * k + gvec.shape[1]]
        wait_on(ada, ada_sem)
        v = gvec[...]
        high = v.astype(bf16)
        v = v - high.astype(f32)
        middle = v.astype(bf16)
        low = (v - middle.astype(f32)).astype(bf16)
        left = jnp.concatenate([high, middle, low, jnp.zeros((13, gvec.shape[1]), bf16)], axis=0)
        part_sum = dense(left, ada[...])
        cmine[0] = jnp.broadcast_to(jnp.sum(part_sum[:8], axis=0, keepdims=True), cmine.shape[1:])
        small_send(6, cmine.at[0], crecv.at[0], partners[0])

    def cond_step(k):
        wait_on(crecv.at[k], sm_recv.at[6 + k])
        cmine[k + 1] = cmine[k] + crecv[k]
        if k < 2:
            small_send(7 + k, cmine.at[k + 1], crecv.at[k + 1], partners[k + 1])
        else:
            start(cmine.at[3], cond_out, out_sem.at[5])

    def small_x():
        wait_on(sall.at[bx], sm_recv.at[3])
        small_send(5, sall.at[bx], sall.at[bx], (bc, f))

    def small_core():
        wait_on(sall.at[bc], sm_recv.at[4])
        wait_on(sall.at[bxc], sm_recv.at[5])
        start(sall, sums_out, out_sem.at[2])

    A, B, C = 0, 1, 2
    pieces1 = []
    for j in range(4):
        pieces1 += [
            functools.partial(mlp_back, j),
            functools.partial(outer, mats.at[H2], mats.at[GP], pb_ref.at[j]),
            functools.partial(hidden_in, 0, j, GP),
        ]

    def after_one():
        drain()
        open_group(B)
        load_mat(ATT, att_ref)
        load_fl(1, norm_ref)
        load_fl(2, branch_ref)

    def proj_outer():
        wait_on(mats.at[ATT], m_sem.at[ATT])
        outer(mats.at[ATT], mats.at[GB], pa_ref.at[3])

    def before_att():
        load_mat(H1, h1_ref)
        for k in range(3):
            wait_on(mats.at[Q + k], m_sem.at[Q + k])
        clear()

    heads = WID // HEAD_DIM
    pieces2 = [norm_two, proj_outer, att_in, before_att]
    pieces2 += [functools.partial(att_back, range(k, k + 4)) for k in range(0, heads, 4)] + [att_done]

    def a_outer(k):
        if k == 0:
            wait_on(mats.at[H1], m_sem.at[H1])
        outer(mats.at[H1], mats.at[Q + k], pa_ref.at[k])

    pieces2 += [functools.partial(a_outer, k) for k in range(3)]

    def after_two():
        drain()
        open_group(A)
        load_mat(0, x_ref)
        load_fl(3, mid_ref)
        for j in range(2):
            load_mat(1 + j, hid_ref.at[:, pl.ds(j * WID, WID)])

    def h1_in(k):
        hidden_in(0, k, Q + k)
        if k < 2:
            load_mat(Q + k, hid_ref.at[:, pl.ds((2 + k) * WID, WID)])

    pieces3 = [functools.partial(h1_in, k) for k in range(3)] + [norm_one]
    pieces3 += [functools.partial(mlp_out, j) for j in range(4)] + [block_end]
    tail = [small_first] + [functools.partial(small_step, k) for k in range(3)] + [cond_first, small_x] + [functools.partial(cond_step, k) for k in range(3)] + [small_core]

    pieces = pieces1 + [after_one] + pieces2 + [after_two] + pieces3 + tail
    groups = [steps_of(g) for g in range(NG)]
    size = len(groups[0])
    seq = []
    for code in PROGRAM:
        if code < 0:
            seq.append((pieces.pop(0), None))
        else:
            g, n = divmod(code, size)
            fn, i = groups[g][n]
            seq.append((fn, None if i is None else (g, i)))
    assert not pieces
    plan = [t for _, t in seq if t is not None]

    open_group(C)
    start(vec_ref, vec, out_sem.at[3])
    start(ada_ref, ada, ada_sem)
    start(lse_ref, lse, lse_sem)
    start(inv_ref, inv2, inv_sem)
    load_mat(GO, go_ref)
    fetch(0)
    slope_load(0)
    load_mat(H2, h2_ref)
    fetch(1)
    slope_load(1)
    for k in range(3):
        load_mat(Q + k, qkv_ref.at[k])
    start(res_ref, res, out_sem.at[4])
    sums8[...] = jnp.zeros_like(sums8)
    wait_on(vec, out_sem.at[3])
    wait_on(mats.at[GO], m_sem.at[GO])
    wait_on(mats.at[H2], m_sem.at[H2])
    wait_on(res, out_sem.at[4])
    wait_on(lse, lse_sem)
    wait_on(inv2, inv_sem)
    first_sums()
    for fn, _ in seq:
        fn()
    for loc, rc in finals[-2:]:
        loc.wait()
        rc.wait_send()
    for g in range(NG):
        for q, j in enumerate((bc, bxc)):
            wait_on(O[g].at[j], o_recv.at[g, q])
    for cp, _ in pend:
        cp.wait_send()
    wait_on(lat_out, out_sem.at[0])
    wait_on(block_out, out_sem.at[1])
    wait_on(sums_out, out_sem.at[2])
    wait_on(cond_out, out_sem.at[5])


def backward(mask, vec, wa, wb, wc, x, res, h1, qkv, att, branch, mid, h2, slope, hid, go, pc, w_ada, lse, norm, inv):
    any_space = pl.BlockSpec(memory_space=pl.ANY)
    f32, bf16 = jnp.float32, jnp.bfloat16
    rows = x.shape[0]
    sds = jax.ShapeDtypeStruct
    sem = pltpu.SemaphoreType.DMA
    mat = (rows, WID)
    blkshape = (ROWS, WID)
    outs = (
        sds((4, 16, WID), f32), sds((8, WID), f32), sds((4,) + blkshape, f32), sds((4,) + blkshape, f32), sds((4,) + blkshape, f32),
        sds(mat, bf16), sds(mat, f32), sds((4, WID, WID), bf16), sds((4, WID, WID), bf16),
    )

    def vm(*shape, dt=bf16):
        return pltpu.VMEM(shape, dt)

    return pl.pallas_call(
        backward_kernel,
        out_shape=outs,
        in_specs=[pl.BlockSpec(memory_space=pltpu.SMEM)] + [any_space] * 20,
        out_specs=(any_space,) * len(outs),
        scratch_shapes=[
            vm(NG, 16, *blkshape), vm(4, *blkshape), vm(NG, 2, *blkshape), vm(NG, 2, *blkshape), vm(NG, 4, *blkshape), vm(NG, 2, *blkshape),
            vm(NG, *blkshape), vm(NG, 3, *blkshape), vm(NG, 2, *blkshape), vm(2, *blkshape, dt=f32),
            vm(16, WID, dt=f32), vm(2, WID, WID), vm(2, 384, WID), vm(6, *mat), vm(*mat), vm(4, *mat, dt=f32),
            vm(16, 8, WID, dt=f32), vm(3, 16, WID, dt=f32), vm(3, 16, WID, dt=f32), vm(4, 16, WID, dt=f32),
            vm(*w_ada.shape), vm(1, w_ada.shape[0], dt=f32), vm(4, 8, WID, dt=f32), vm(3, 8, WID, dt=f32), vm(*lse.shape, dt=f32), vm(rows, 128, dt=f32),
            sem((4,)), sem((NG, 16)), sem((NG, 16)), sem((NG, 24)), sem((NG, 2)), sem((NG, 2)), sem((NG, 4)), sem((NG, 2)), sem((NG,)),
            sem((NG, 3)), sem((NG, 2)), sem((NG, 2)), sem((NG, 2)), sem((NG, 2)),
            sem((2,)), sem((2,)), sem((6,)), sem((4,)), sem((2,)), sem((6,)), sem((9,)), sem((9,)), sem, sem, sem,
        ],
        compiler_params=pltpu.CompilerParams(collective_id=2, has_side_effects=True, vmem_limit_bytes=64 << 20),
        name="backward",
    )(mask, vec, wa, wb, wc, x, res, h1, qkv, att, branch, mid, h2, slope, hid, go, pc, w_ada, lse, norm, inv)


def on_device_fast(
    latents, cond, live, w_ada, b_ada, w_qkv, b_qv, w_proj, b_proj, w_fc1, b_fc1, w_fc2, b_fc2, cotangent
):
    images, length, width = latents.shape[1:]
    rows = images * length
    f32 = jnp.float32
    scaled = jax.nn.silu(cond[0]).astype(jnp.bfloat16)
    mod_part = jnp.dot(scaled, w_ada, preferred_element_type=f32) + b_ada.astype(f32)
    at = lax.axis_index("fsdp")

    def place(part, total):
        return lax.dynamic_update_slice(jnp.zeros((total,), f32), part, (at * part.shape[0],))

    parts = (mod_part, b_qv.astype(f32), b_proj.astype(f32), b_fc1.astype(f32), b_fc2.astype(f32))
    vec = jnp.concatenate([place(p, 8 * p.shape[0]) for p in parts] + [jnp.where(at == 0, scaled.astype(f32), 0.0), jnp.zeros((width,), f32)]).reshape(16, width)
    la = jnp.concatenate([jnp.transpose(w_qkv.reshape(ROWS, 3, WID), (1, 0, 2)), w_proj[None]])
    lc = w_fc2.reshape(4, ROWS, WID)
    live_mask = (lax.iota(jnp.int32, images) < live[0, 0]).astype(f32)
    row_mask = jnp.repeat(live_mask, length)[:, None]
    x_rows = latents[0].reshape(rows, width)
    res = cotangent[0].reshape(rows, width) * row_mask.astype(jnp.bfloat16)
    vec, wa, wb, wc, h_first, qkv, attended, branch, middle, h_second, slope, hidden, grad_out, grad_fc2, lse, norm, inv = forward(vec, la, w_fc1, lc, x_rows, res)
    sums, cond_sum, oa, ob, oc, block_out, grad_rows, _, _ = backward(
        live_mask, vec, wa, wb, wc.reshape(4, width, width), x_rows, res, h_first, qkv, attended, branch, middle, h_second, slope, hidden,
        grad_out, grad_fc2.reshape(8, 4, ROWS, width), jnp.transpose(w_ada), lse, norm, inv,
    )
    flat = sums.reshape(4, 16 * width)
    total = jnp.sum(flat, axis=0)

    def mine(v, begin, size):
        return lax.dynamic_slice_in_dim(v, begin + at * size, size, axis=-1)

    mod_bins = mine(flat, 0, 6 * width // 8)
    high = lax.reduce_precision(mod_bins, 8, 7)
    middle = lax.reduce_precision(mod_bins - high, 8, 7)
    low = lax.reduce_precision(mod_bins - high - middle, 8, 7)
    split = jnp.concatenate([high, middle, low]).astype(jnp.bfloat16)
    scaled_bins = jnp.tile(sums[:, 14].astype(jnp.bfloat16), (3, 1))
    grad_wada = jnp.einsum("bd,be->de", scaled_bins, split, preferred_element_type=f32)
    silu_pull = jax.vjp(jax.nn.silu, cond[0])[1]
    grad_cond = silu_pull(cond_sum[0])[0][None, :]
    return (
        block_out.reshape(latents.shape),
        grad_rows.reshape(latents.shape),
        grad_cond,
        grad_wada,
        mine(total, 0, 6 * width // 8),
        jnp.transpose(oa[:3], (1, 0, 2)).reshape(ROWS, 3 * width),
        mine(total, 6 * width, 2 * width // 8),
        oa[3],
        mine(total, 8 * width, width // 8),
        jnp.transpose(ob, (1, 0, 2)).reshape(ROWS, 4 * width),
        mine(total, 9 * width, 4 * width // 8),
        oc.reshape(4 * ROWS, width),
        mine(total, 13 * width, width // 8),
    )


def solution(mesh):
    fast = mesh.shape["bin"] == 4 and mesh.shape["fsdp"] == 8
    return jax.shard_map(
        on_device_fast if fast else on_device_generic,
        mesh=mesh,
        in_specs=(
            P("bin", "fsdp", None, None),
            P("bin", None),
            P("bin", "fsdp"),
            P(None, "fsdp"),
            P("fsdp"),
            P("fsdp", None),
            P("fsdp"),
            P("fsdp", None),
            P("fsdp"),
            P("fsdp", None),
            P("fsdp"),
            P("fsdp", None),
            P("fsdp"),
            P("bin", "fsdp", None, None),
        ),
        out_specs=(
            P("bin", "fsdp", None, None),
            P("bin", "fsdp", None, None),
            P("bin", None),
            P(None, "fsdp"),
            P("fsdp"),
            P("fsdp", None),
            P("fsdp"),
            P("fsdp", None),
            P("fsdp"),
            P("fsdp", None),
            P("fsdp"),
            P("fsdp", None),
            P("fsdp"),
        ),
        check_vma=False,
    )
```

```python
import functools

import jax
import jax.numpy as jnp
from jax import lax
from jax.experimental import pallas as pl
from jax.experimental.pallas import tpu as pltpu
from jax.sharding import PartitionSpec as P

HEAD_DIM = 72
MESH = pl.DeviceIdType.MESH
ROWS = 144
WID = 1152
NG = 3


def layer_norm(field):
    center = field - jnp.mean(field, axis=-1, keepdims=True)
    return center * lax.rsqrt(jnp.mean(center * center, axis=-1, keepdims=True) + 1e-06)


def gelu_tanh(field):
    return (
        0.5
        * field
        * (1.0 + jnp.tanh(0.7978845608028654 * (field + 0.044715 * field * field * field)))
    )


def modulate(field, shift_vec, scale_vec):
    return layer_norm(field) * (1.0 + scale_vec) + shift_vec


def pair_scores(query_block, key_block):
    return jnp.einsum(
        "gqhd,gkhd->ghqk", query_block, key_block, preferred_element_type=jnp.float32
    ) * HEAD_DIM ** (-0.5)


def attend_pair(group_item):
    query_block, key_block, value_block = group_item
    scores = pair_scores(query_block, key_block)
    highest = jnp.max(scores, axis=-1, keepdims=True)
    exp_scores = jnp.exp(scores - highest)
    totals = jnp.sum(exp_scores, axis=-1, keepdims=True)
    attn_probs = (exp_scores / totals).astype(jnp.bfloat16)
    attended = jnp.einsum(
        "ghqk,gkhd->gqhd", attn_probs, value_block, preferred_element_type=jnp.float32
    )
    return (attended, (highest + jnp.log(totals))[..., 0])


def attend_back(group_item):
    query_block, key_block, value_block, log_total, grad_att = group_item
    scores = pair_scores(query_block, key_block)
    attn_probs = jnp.exp(scores - log_total[..., None])
    grad_probs = jnp.einsum(
        "gqhd,gkhd->ghqk", grad_att, value_block, preferred_element_type=jnp.float32
    )
    row_terms = jnp.sum(attn_probs * grad_probs, axis=-1, keepdims=True)
    grad_scores = (attn_probs * (grad_probs - row_terms)).astype(jnp.bfloat16)
    grad_query = jnp.einsum(
        "ghqk,gkhd->gqhd", grad_scores, key_block, preferred_element_type=jnp.float32
    ) * HEAD_DIM ** (-0.5)
    grad_key = jnp.einsum(
        "ghqk,gqhd->gkhd", grad_scores, query_block, preferred_element_type=jnp.float32
    ) * HEAD_DIM ** (-0.5)
    grad_value = jnp.einsum(
        "ghqk,gqhd->gkhd",
        attn_probs.astype(jnp.bfloat16),
        grad_att,
        preferred_element_type=jnp.float32,
    )
    return jnp.stack([grad_query, grad_key, grad_value], axis=2)


def run_block(flat_rows, modulation, weights, images, length):
    full_qkv, full_proj, full_fc1, full_fc2, bias_qv, bias_proj, bias_fc1, bias_fc2 = weights
    width = flat_rows.shape[1]
    heads = width // HEAD_DIM
    pieces = jnp.split(modulation, 6)
    h_first = modulate(flat_rows, pieces[0], pieces[1]).astype(jnp.bfloat16)
    qkv_bias = jnp.concatenate(
        [bias_qv[:width], jnp.zeros((width,), jnp.bfloat16), bias_qv[width:]]
    ).astype(jnp.float32)
    qkv_rows = (jnp.dot(h_first, full_qkv, preferred_element_type=jnp.float32) + qkv_bias).astype(
        jnp.bfloat16
    )
    split_rows = qkv_rows.reshape(images // 2, 2, length, 3, heads, HEAD_DIM)
    attended, log_total = lax.map(
        attend_pair, (split_rows[:, :, :, 0], split_rows[:, :, :, 1], split_rows[:, :, :, 2])
    )
    attended = attended.reshape(images * length, width).astype(jnp.bfloat16)
    branch = jnp.dot(attended, full_proj, preferred_element_type=jnp.float32) + bias_proj.astype(
        jnp.float32
    )
    middle = flat_rows + pieces[2] * branch
    h_second = modulate(middle, pieces[3], pieces[4]).astype(jnp.bfloat16)
    pre_act = jnp.dot(h_second, full_fc1, preferred_element_type=jnp.float32) + bias_fc1.astype(
        jnp.float32
    )
    hidden = gelu_tanh(pre_act).astype(jnp.bfloat16)
    mlp_out = jnp.dot(hidden, full_fc2, preferred_element_type=jnp.float32) + bias_fc2.astype(
        jnp.float32
    )
    result = middle + pieces[5] * mlp_out
    return (
        h_first,
        split_rows,
        log_total,
        attended,
        branch,
        middle,
        h_second,
        pre_act,
        hidden,
        mlp_out,
        result,
    )


def on_device_generic(
    latents,
    cond,
    live,
    w_ada,
    b_ada,
    w_qkv,
    b_qv,
    w_proj,
    b_proj,
    w_fc1,
    b_fc1,
    w_fc2,
    b_fc2,
    cotangent,
):
    images = latents.shape[1]
    length = latents.shape[2]
    width = latents.shape[3]
    heads = width // HEAD_DIM
    scaled = jax.nn.silu(cond[0]).astype(jnp.bfloat16)
    mod_part = jnp.dot(scaled, w_ada, preferred_element_type=jnp.float32) + b_ada.astype(
        jnp.float32
    )
    modulation = lax.all_gather(mod_part, "fsdp", axis=0, tiled=True)
    gathered = (
        lax.all_gather(w_qkv, "fsdp", axis=0, tiled=True),
        lax.all_gather(w_proj, "fsdp", axis=0, tiled=True),
        lax.all_gather(w_fc1, "fsdp", axis=0, tiled=True),
        lax.all_gather(w_fc2, "fsdp", axis=0, tiled=True),
        lax.all_gather(b_qv, "fsdp", axis=0, tiled=True),
        lax.all_gather(b_proj, "fsdp", axis=0, tiled=True),
        lax.all_gather(b_fc1, "fsdp", axis=0, tiled=True),
        lax.all_gather(b_fc2, "fsdp", axis=0, tiled=True),
    )
    flat_rows = latents[0].reshape(images * length, width).astype(jnp.float32)
    live_mask = (lax.iota(jnp.int32, images) < live[0, 0]).astype(jnp.float32)
    row_mask = jnp.repeat(live_mask, length)[:, None]
    forward_run = run_block(flat_rows, modulation, gathered, images, length)
    block_out = (forward_run[10] * row_mask).astype(jnp.bfloat16).reshape(latents.shape)
    weights = (
        lax.all_gather(w_qkv, "fsdp", axis=0, tiled=True),
        lax.all_gather(w_proj, "fsdp", axis=0, tiled=True),
        lax.all_gather(w_fc1, "fsdp", axis=0, tiled=True),
        lax.all_gather(w_fc2, "fsdp", axis=0, tiled=True),
        lax.all_gather(b_qv, "fsdp", axis=0, tiled=True),
        lax.all_gather(b_proj, "fsdp", axis=0, tiled=True),
        lax.all_gather(b_fc1, "fsdp", axis=0, tiled=True),
        lax.all_gather(b_fc2, "fsdp", axis=0, tiled=True),
    )
    full_qkv, full_proj, full_fc1, full_fc2 = (weights[0], weights[1], weights[2], weights[3])
    saved = run_block(flat_rows, modulation, weights, images, length)
    (
        h_first,
        split_rows,
        log_total,
        attended,
        branch,
        middle,
        h_second,
        pre_act,
        hidden,
        mlp_out,
        result,
    ) = saved
    pieces = jnp.split(modulation, 6)
    grad_res = cotangent[0].reshape(images * length, width).astype(jnp.float32) * row_mask
    grad_out = (pieces[5] * grad_res).astype(jnp.bfloat16)
    grad_gate_two = jnp.sum(grad_res * mlp_out, axis=0)
    grad_fc2 = jnp.einsum("rf,rd->fd", hidden, grad_out, preferred_element_type=jnp.float32)
    grad_bfc2 = jnp.sum(grad_out.astype(jnp.float32), axis=0)
    grad_hidden = jnp.einsum("rd,fd->rf", grad_out, full_fc2, preferred_element_type=jnp.float32)
    gelu_pull = jax.vjp(gelu_tanh, pre_act)[1]
    grad_pre = gelu_pull(grad_hidden)[0].astype(jnp.bfloat16)
    grad_fc1 = jnp.einsum("rd,rf->df", h_second, grad_pre, preferred_element_type=jnp.float32)
    grad_bfc1 = jnp.sum(grad_pre.astype(jnp.float32), axis=0)
    grad_h2 = jnp.einsum("rf,df->rd", grad_pre, full_fc1, preferred_element_type=jnp.float32)
    second_pull = jax.vjp(modulate, middle, pieces[3], pieces[4])[1]
    grad_mid_norm, grad_shift_two, grad_scale_two = second_pull(grad_h2)
    grad_mid = grad_res + grad_mid_norm
    grad_branch = (pieces[2] * grad_mid).astype(jnp.bfloat16)
    grad_gate_one = jnp.sum(grad_mid * branch, axis=0)
    grad_proj = jnp.einsum("rd,re->de", attended, grad_branch, preferred_element_type=jnp.float32)
    grad_bproj = jnp.sum(grad_branch.astype(jnp.float32), axis=0)
    grad_att = jnp.einsum(
        "re,de->rd", grad_branch, full_proj, preferred_element_type=jnp.float32
    ).astype(jnp.bfloat16)
    grad_att = grad_att.reshape(images // 2, 2, length, heads, HEAD_DIM)
    grad_qkv = lax.map(
        attend_back,
        (
            split_rows[:, :, :, 0],
            split_rows[:, :, :, 1],
            split_rows[:, :, :, 2],
            log_total,
            grad_att,
        ),
    )
    grad_qkv = grad_qkv.reshape(images * length, 3 * width).astype(jnp.bfloat16)
    grad_wqkv = jnp.einsum("rd,re->de", h_first, grad_qkv, preferred_element_type=jnp.float32)
    qkv_sums = jnp.sum(grad_qkv.astype(jnp.float32), axis=0)
    grad_bqv = jnp.concatenate([qkv_sums[:width], qkv_sums[2 * width :]])
    grad_h1 = jnp.einsum("re,de->rd", grad_qkv, full_qkv, preferred_element_type=jnp.float32)
    first_pull = jax.vjp(modulate, flat_rows, pieces[0], pieces[1])[1]
    grad_rows_norm, grad_shift_one, grad_scale_one = first_pull(grad_h1)
    grad_rows = grad_mid + grad_rows_norm
    grad_mod = jnp.concatenate(
        [
            grad_shift_one,
            grad_scale_one,
            grad_gate_one,
            grad_shift_two,
            grad_scale_two,
            grad_gate_two,
        ]
    )
    shards = (
        lax.psum_scatter(grad_wqkv, "fsdp", scatter_dimension=0, tiled=True),
        lax.psum_scatter(grad_proj, "fsdp", scatter_dimension=0, tiled=True),
        lax.psum_scatter(grad_fc1, "fsdp", scatter_dimension=0, tiled=True),
        lax.psum_scatter(grad_fc2, "fsdp", scatter_dimension=0, tiled=True),
        lax.psum_scatter(grad_bqv, "fsdp", scatter_dimension=0, tiled=True),
        lax.psum_scatter(grad_bproj, "fsdp", scatter_dimension=0, tiled=True),
        lax.psum_scatter(grad_bfc1, "fsdp", scatter_dimension=0, tiled=True),
        lax.psum_scatter(grad_bfc2, "fsdp", scatter_dimension=0, tiled=True),
        lax.psum_scatter(grad_mod, "fsdp", scatter_dimension=0, tiled=True),
    )
    mod_mine = shards[8]
    grad_wada = scaled.astype(jnp.float32)[:, None] * mod_mine[None, :]
    grad_scaled = jnp.dot(w_ada.astype(jnp.float32), mod_mine, precision=lax.Precision.HIGHEST)
    grad_scaled = lax.psum(grad_scaled, "fsdp")
    silu_pull = jax.vjp(jax.nn.silu, cond[0])[1]
    grad_cond = silu_pull(grad_scaled)[0][None, :]
    totals = lax.psum(
        (
            shards[0],
            shards[1],
            shards[2],
            shards[3],
            shards[4],
            shards[5],
            shards[6],
            shards[7],
            grad_wada,
            mod_mine,
        ),
        "bin",
    )
    return (
        block_out,
        grad_rows.reshape(latents.shape),
        grad_cond,
        totals[8],
        totals[9],
        totals[0],
        totals[4],
        totals[1],
        totals[5],
        totals[2],
        totals[6],
        totals[3],
        totals[7],
    )


TILE = 256
UN = 4
GATHER_PROGRAM = (
    0, 1, 4, 5, -1, 9, 19, 20, 10, -1, 2, 11, 13, -1, 24, 12, 22, 8, -1, 42, 3, 16, 17, 14,
    15, 30, 6, 28, 23, 7, 18, 39, 38, 29, 25, 21, 34, -1, -1, 35, -1, 32, 47, 43, -1, 33, 49, 26,
    37, 41, 27, 40, 36, 31, -1, 46, -1, -1, 44, 48, -1, 50, 51, -1, 53, 54, -1, 45, 52, -1, 55, 56,
    -1,
)
STRIP = 16


def coords():
    b = lax.axis_index("bin")
    f = lax.axis_index("fsdp")
    return b, f, b // 2, lax.rem(b, 2), f // 2, lax.rem(f, 2)


def strip_loop(rows, body, unroll=1):
    @pl.loop(0, rows // STRIP, unroll=unroll)
    def _(k):
        body(pl.ds(pl.multiple_of(k * STRIP, STRIP), STRIP))


def dense(left, right):
    return jnp.dot(left, right, preferred_element_type=jnp.float32)


def dense_nt(left, right):
    return lax.dot_general(left, right, (((1,), (1,)), ((), ())), preferred_element_type=jnp.float32)


def dense_tn(left, right):
    return lax.dot_general(left, right, (((0,), (0,)), ((), ())), preferred_element_type=jnp.float32)


def center_rows(v):
    v = v - jnp.mean(v, axis=-1, keepdims=True)
    inv = lax.rsqrt(jnp.mean(v * v, axis=-1, keepdims=True) + 1e-06)
    return v * inv, inv


def head_window(h):
    start = HEAD_DIM * h
    low = start // 128 * 128
    width = 128 if start - low + HEAD_DIM <= 128 else 256
    return low, width, start - low


def head_mask(off, width):
    lanes = lax.broadcasted_iota(jnp.int32, (1, width), 1)
    return jnp.logical_and(lanes >= off, lanes < off + HEAD_DIM)


def head_probs(q, k):
    scores = dense_nt(k, q) * HEAD_DIM ** (-0.5)
    high = jnp.max(scores, axis=0, keepdims=True)
    e = jnp.exp(scores - high)
    total = jnp.sum(e, axis=0, keepdims=True)
    return e * (1.0 / total), high + jnp.log(total)


def forward_kernel(
    vec_ref, la_ref, lb_ref, lc_ref, x_ref, res_ref,
    vec_out, wa_out, wb_out, wc_out, h1_out, qkv_out, att_out, branch_out, mid_out, h2_out, slope_out, hid_out, go_out, pc_out, lse_out, norm_out, inv_out,
    wa, wb, wc, vecs, vec, xs, res, h1, qkv, att, mid, h2, hid, go, acc, slope, pst, lse, norm, inv,
    loc_sem, sm_send, sm_recv, send_sem, recv_sem, in_sem, out_sem, wo_sem, co_sem, sl_sem, ps_sem,
):
    b, f, x, c, z, y = coords()
    bx = lax.rem(b + 2, 4)
    bc = b + 1 - 2 * c
    bxc = lax.rem(bc + 2, 4)
    fy = f + 1 - 2 * y
    yb = 1 - y
    z1 = z + 1 - 2 * lax.rem(z, 2)
    mid_z = jnp.logical_or(z == 1, z == 2)
    zb = lax.rem(z + 2, 4)
    zc = 3 - z
    z2 = jnp.where(mid_z, zc, zb)
    z3 = jnp.where(mid_z, zb, zc)
    fz1 = z1 * 2 + y
    bar = pltpu.get_barrier_semaphore()
    for k in range(1, 8):
        pl.semaphore_signal(bar, inc=1, device_id=(b, lax.rem(f + k, 8)), device_id_type=MESH)
    pl.semaphore_signal(bar, inc=1, device_id=(bx, f), device_id_type=MESH)
    pl.semaphore_signal(bar, inc=1, device_id=(bc, f), device_id_type=MESH)
    pl.semaphore_wait(bar, 9)

    W = (wa, wb, wc)
    L = (la_ref, lb_ref, lc_ref)

    def blk(g, j, ff):
        if g < 2:
            return W[g].at[j, pl.ds(pl.multiple_of(ff * ROWS, ROWS), ROWS)]
        return W[g].at[ff, j]

    smalls = []
    partners = ((b, fy), (b, fz1), (b, zb * 2 + y))

    def small_send(k):
        cp = pltpu.make_async_remote_copy(
            src_ref=vecs.at[k], dst_ref=vecs.at[3 + k], send_sem=sm_send.at[k], recv_sem=sm_recv.at[k],
            device_id=partners[k], device_id_type=MESH,
        )
        cp.start()
        smalls.append(cp)

    def small_step(k):
        pltpu.make_async_copy(vecs.at[3 + k], vecs.at[3 + k], sm_recv.at[k]).wait()
        total = vecs[k] + vecs[3 + k]
        if k < 2:
            vecs[k + 1] = total
            small_send(k + 1)
        else:
            vec[...] = total
            keep(vec, vec_out, 0)


    pend = []
    outs = []
    cnt = [0] * NG

    def send(g, j, ff, dev, cond=None, src=None):
        i = cnt[g]
        cnt[g] += 1
        cp = pltpu.make_async_remote_copy(
            src_ref=blk(g, j, ff) if src is None else src, dst_ref=blk(g, j, ff),
            send_sem=send_sem.at[g, i], recv_sem=recv_sem.at[g, j, ff], device_id=dev, device_id_type=MESH,
        )
        if cond is None:
            cp.start()
        else:
            @pl.when(cond)
            def _():
                cp.start()
        pend.append((cp, cond))

    def copy_out(src, dst, sem):
        cp = pltpu.make_async_copy(src, dst, sem)
        cp.start()
        return cp

    def arrive(g, j, ff, cond=None):
        def go_on():
            pltpu.make_async_copy(blk(g, j, ff), blk(g, j, ff), recv_sem.at[g, j, ff]).wait()
            if g == 2:
                copy_out(wc.at[ff, j], wc_out.at[ff, j], co_sem.at[j, ff])
        if cond is None:
            go_on()
        else:
            pl.when(cond)(go_on)

    up = (b, jnp.minimum(f + 2, 7))
    dn = (b, jnp.maximum(f - 2, 0))

    def piece(g, j):
        if g != 1:
            return L[g].at[j]
        return lb_ref.at[:, pl.ds(pl.multiple_of(j * WID, WID), WID)]

    def start_sends(g):
        sb = piece(g, b)
        sx = piece(g, bx)
        return [
            lambda: send(g, b, f, up, z < 3, sb), lambda: send(g, b, f, dn, z > 0, sb), lambda: send(g, b, f, (b, fy), None, sb),
            lambda: send(g, bx, f, (b, fz1), None, sx), lambda: send(g, bx, f, (b, fy), None, sx),
        ]

    locs = []

    def local(g):
        for j in range(4):
            locs.append(copy_out(piece(g, j), blk(g, j, f), loc_sem.at[g, j]))

    def Z(g, zz, x_too):
        ff = zz * 2 + y
        arrive(g, b, ff)
        send(g, b, ff, up, jnp.logical_and(zz < z, z < 3))
        send(g, b, ff, dn, jnp.logical_and(zz > z, z > 0))
        send(g, b, ff, (b, fy))
        if x_too:
            send(g, b, ff, (bx, f))
        send(g, b, ff, (bc, f))

    def Y(g, zz, x_too):
        ff = zz * 2 + yb
        arrive(g, b, ff)
        if x_too:
            send(g, b, ff, (bx, f))
        send(g, b, ff, (bc, f))

    def X(g, ff):
        arrive(g, bx, ff)
        send(g, bx, ff, (bc, f))

    def actions(g):
        return [
            lambda: Z(g, z1, False), lambda: X(g, fz1), lambda: Y(g, z, False), lambda: X(g, fy),
            lambda: Z(g, z2, True), lambda: Y(g, z1, True), lambda: Z(g, z3, True), lambda: X(g, z2 * 2 + y),
            lambda: Y(g, z2, True), lambda: X(g, z1 * 2 + yb), lambda: X(g, z3 * 2 + y), lambda: Y(g, z3, True),
            lambda: X(g, z2 * 2 + yb), lambda: X(g, z3 * 2 + yb),
        ]

    def other_core(g):
        for zz in range(4):
            for jj in (bc, bxc):
                arrive(g, jj, zz * 2 + y, zz != z)
                arrive(g, jj, zz * 2 + yb)
        for cp in locs[g * 4 : g * 4 + 4]:
            cp.wait()

    def keep(src, dst, i):
        outs.append(copy_out(src, dst, out_sem.at[i]))

    def row(i):
        return vec[i : i + 1, :]

    def start_rows():
        in_x.wait()

        def first(r):
            n, _ = center_rows(xs[r, :].astype(jnp.float32))
            h1[r, :] = (n * (1.0 + row(1)) + row(0)).astype(jnp.bfloat16)

        strip_loop(h1.shape[0], first, UN)
        keep(h1, h1_out, 1)

    def start_grads():
        in_res.wait()

        def out_grad(r):
            go[r, :] = (res[r, :].astype(jnp.float32) * row(5)).astype(jnp.bfloat16)

        strip_loop(go.shape[0], out_grad)
        keep(go, go_out, 2)

    tiles = xs.shape[0] // TILE

    def tile(i):
        return pl.ds(pl.multiple_of(i * TILE, TILE), TILE)

    def project():
        @pl.loop(0, 3 * tiles)
        def _(k):
            j = k // tiles
            at = tile(lax.rem(k, tiles))
            bias = jnp.where(j == 1, 0.0, vec[pl.ds(6 + j // 2, 1), :])
            qkv[j, at, :] = (dense(h1[at, :], wa[j]) + bias).astype(jnp.bfloat16)
        keep(qkv, qkv_out, 3)

    def attention():
        @pl.loop(0, tiles)
        def _(i):
            acc[...] = jnp.zeros_like(acc)
            for h in range(WID // HEAD_DIM):
                low, width, off = head_window(h)
                cols = slice(low, low + width)
                mask = head_mask(off, width)
                q = qkv[0, tile(i), cols]
                v = qkv[2, tile(i), cols]
                probs, lse[i, h : h + 1, :] = head_probs(jnp.where(mask, q, jnp.zeros_like(q)), qkv[1, tile(i), cols])
                acc[:, cols] += dense_tn(probs.astype(jnp.bfloat16), jnp.where(mask, v, jnp.zeros_like(v)))
            att[tile(i), :] = acc[...].astype(jnp.bfloat16)
        keep(att, att_out, 6)
        keep(lse, lse_out, 11)

    def branch():
        @pl.loop(0, tiles)
        def _(i):
            mid[tile(i), :] = dense(att[tile(i), :], wa[3]) + row(8)
        cp = copy_out(mid, branch_out, out_sem.at[7])
        cp.wait()

        def second(r):
            m = xs[r, :].astype(jnp.float32) + row(2) * mid[r, :]
            mid[r, :] = m
            n, inverse = center_rows(m)
            norm[r, :] = n
            inv[r, :] = jnp.broadcast_to(inverse, (STRIP, 128))
            h2[r, :] = (n * (1.0 + row(4)) + row(3)).astype(jnp.bfloat16)

        strip_loop(mid.shape[0], second, UN)
        keep(mid, mid_out, 8)
        keep(h2, h2_out, 9)
        keep(norm, norm_out, 12)
        keep(inv, inv_out, 13)

    def hidden(j):
        cols = slice(j * WID, j * WID + WID)

        @pl.loop(0, tiles)
        def _(i):
            acc[...] = dense(h2[tile(i), :], wb[j]) + row(9 + j)

            @pl.when(j * tiles + i >= 1)
            def _():
                pltpu.make_async_copy(slope, slope_out.at[tile(0), :WID], sl_sem).wait()

            @pl.loop(0, TILE // STRIP)
            def _(k):
                r = pl.ds(pl.multiple_of(k * STRIP, STRIP), STRIP)
                v = acc[r, :]
                sq = v * v
                t = jnp.tanh(0.7978845608028654 * (v + 0.044715 * sq * v))
                half = 0.5 * (1.0 + t)
                slope[r, :] = half + 0.5 * v * (1.0 - t * t) * (0.7978845608028654 * (1.0 + 0.134145 * sq))
                hid[pl.ds(pl.multiple_of(i * TILE + k * STRIP, STRIP), STRIP), cols] = (v * half).astype(jnp.bfloat16)

            copy_out(slope, slope_out.at[tile(i), cols], sl_sem)
        if j == 3:
            pltpu.make_async_copy(slope, slope_out.at[tile(0), :WID], sl_sem).wait()
            keep(hid, hid_out, 10)

    part = pst.shape[1]

    def outer():
        @pl.loop(0, 4 * WID // part)
        def _(k):
            slot = lax.rem(k, 2)

            @pl.when(k >= 2)
            def _():
                pltpu.make_async_copy(pst.at[slot], pc_out.at[pl.ds(0, part)], ps_sem.at[slot]).wait()
            at = pl.multiple_of(k * part, part)
            pst[slot] = dense_tn(hid[:, pl.ds(at, part)], go[...]).astype(jnp.bfloat16)
            copy_out(pst.at[slot], pc_out.at[pl.ds(at, part)], ps_sem.at[slot])
        for slot in range(2):
            pltpu.make_async_copy(pst.at[slot], pc_out.at[pl.ds(0, part)], ps_sem.at[slot]).wait()

    def weights_out(g):
        outs.append(copy_out(W[g], (wa_out, wb_out)[g], wo_sem.at[g]))

    in_x = copy_out(x_ref, xs, in_sem.at[0])
    in_res = copy_out(res_ref, res, in_sem.at[1])
    def ready(g):
        other_core(g)
        weights_out(g)

    pieces = [functools.partial(small_step, k) for k in range(3)] + [start_rows, functools.partial(ready, 0)]
    pieces += [project, attention, branch, start_grads, functools.partial(ready, 1)]
    pieces += [functools.partial(hidden, j) for j in range(4)] + [outer]
    groups = [start_sends(g) + actions(g) for g in range(NG)]
    size = len(groups[0])
    own = pltpu.make_async_copy(vec_ref, vecs.at[0], sm_send.at[3])
    own.start()
    for g in range(NG):
        local(g)
    begun = False
    for code in GATHER_PROGRAM[:-1]:
        if code < 0:
            pieces.pop(0)()
        else:
            g, n = divmod(code, size)
            if n >= 5 and not begun:
                begun = True
                own.wait()
                small_send(0)
            groups[g][n]()
    assert not pieces
    for j in range(4):
        locs[8 + j].wait()
        copy_out(wc.at[f, j], wc_out.at[f, j], co_sem.at[j, f])
    other_core_c = 2
    for zz in range(4):
        for jj in (bc, bxc):
            arrive(other_core_c, jj, zz * 2 + y, zz != z)
            arrive(other_core_c, jj, zz * 2 + yb)
    for cp, cond in pend:
        if cond is None:
            cp.wait_send()
        else:
            @pl.when(cond)
            def _(cp=cp):
                cp.wait_send()
    for cp in smalls:
        cp.wait_send()
    for cp in outs:
        cp.wait()
    for ff in range(8):
        for j in range(4):
            pltpu.make_async_copy(wc.at[ff, j], wc_out.at[ff, j], co_sem.at[j, ff]).wait()


def forward(vec, la, lb, lc, x, res):
    any_space = pl.BlockSpec(memory_space=pl.ANY)
    f32, bf16 = jnp.float32, jnp.bfloat16
    rows = x.shape[0]
    sds = jax.ShapeDtypeStruct
    sem = pltpu.SemaphoreType.DMA
    mat = (rows, WID)
    outs = (
        sds((16, WID), f32), sds((4, WID, WID), bf16), sds((4, WID, WID), bf16), sds((8, 4, ROWS, WID), bf16),
        sds(mat, bf16), sds((3,) + mat, bf16), sds(mat, bf16), sds(mat, f32), sds(mat, f32), sds(mat, bf16),
        sds((rows, 4 * WID), f32), sds((rows, 4 * WID), bf16), sds(mat, bf16), sds((4 * WID, WID), bf16),
        sds((rows // TILE, 16, TILE), f32), sds(mat, f32), sds((rows, 128), f32),
    )
    vm = pltpu.VMEM
    return pl.pallas_call(
        forward_kernel,
        out_shape=outs,
        in_specs=[any_space] * 6,
        out_specs=(any_space,) * len(outs),
        scratch_shapes=[
            vm((4, WID, WID), bf16), vm((4, WID, WID), bf16), vm((8, 4, ROWS, WID), bf16), vm((6, 16, WID), f32), vm((16, WID), f32),
            vm(mat, bf16), vm(mat, bf16), vm(mat, bf16), vm((3,) + mat, bf16), vm(mat, bf16), vm(mat, f32), vm(mat, bf16),
            vm((rows, 4 * WID), bf16), vm(mat, bf16), vm((TILE, WID), f32), vm((TILE, WID), f32), vm((2, 384, WID), bf16),
            vm((rows // TILE, 16, TILE), f32), vm(mat, f32), vm((rows, 128), f32),
            sem((NG, 4)), sem((8,)), sem((8,)), sem((NG, 40)), sem((NG, 4, 8)), sem((2,)), sem((14,)), sem((2,)), sem((4, 8)), sem, sem((2,)),
        ],
        compiler_params=pltpu.CompilerParams(collective_id=1, has_side_effects=True, vmem_limit_bytes=63 << 20),
        name="forward",
    )(vec, la, lb, lc, x, res)


PROGRAM = (
    36, 35, 34, -1, 43, -1, -1, -1, -1, 37, -1, -1, -1, 38, 41, -1, 39, -1, -1, -1, 40, -1, 42, -1,
    17, 45, -1, -1, 18, -1, 19, 44, -1, 26, 47, 22, 23, 48, 21, 24, -1, -1, 25, 46, -1, -1, 28, 49,
    -1, -1, 20, 30, -1, 0, 4, 27, 2, 1, -1, 31, -1, 6, -1, 5, 8, 11, 7, 50, 3, 32, 10, -1,
    -1, 29, -1, 13, 9, -1, 14, -1, 12, -1, -1, -1, -1, -1, 15, -1, -1, -1, 33, -1, -1, 16,
)


def backward_kernel(
    mask_ref, vec_ref, wa_ref, wb_ref, wc_ref, x_ref, res_ref, h1_ref, qkv_ref, att_ref, branch_ref, mid_ref, h2_ref, slope_ref,
    hid_ref, go_ref, pc_ref, ada_ref, lse_ref, norm_ref, inv_ref,
    sums_out, cond_out, oa_ref, ob_ref, oc_ref, block_out, lat_out, pa_ref, pb_ref,
    r0, ring, rx4, ry4, ry3, rx2, rn, rz, rt, fin, vec, wbuf, pst, mats, res, fl, sums8, smine, srecv, sall, ada, gvec, cmine, crecv, lse, inv2,
    ring_sem, s0_send, s0_recv, send_sem, rx4_s, ry4_s, ry3_s, rx2_s, rn_s, rz_s, rt_s, o_loc, o_send, o_recv,
    w_sem, p_sem, m_sem, f_sem, sl_sem, out_sem, sm_send, sm_recv, ada_sem, lse_sem, inv_sem,
):
    f32, bf16 = jnp.float32, jnp.bfloat16
    b, f, x, c, z, y = coords()
    bx = lax.rem(b + 2, 4)
    bc = b + 1 - 2 * c
    bxc = lax.rem(bc + 2, 4)
    fy = f + 1 - 2 * y
    yb = 1 - y
    z1 = z + 1 - 2 * lax.rem(z, 2)
    mid_z = jnp.logical_or(z == 1, z == 2)
    zb = lax.rem(z + 2, 4)
    zc = 3 - z
    z2 = jnp.where(mid_z, zc, zb)
    z3 = jnp.where(mid_z, zb, zc)
    fz1 = z1 * 2 + y
    bar = pltpu.get_barrier_semaphore()
    for k in range(1, 8):
        pl.semaphore_signal(bar, inc=1, device_id=(b, lax.rem(f + k, 8)), device_id_type=MESH)
    pl.semaphore_signal(bar, inc=1, device_id=(bx, f), device_id_type=MESH)
    pl.semaphore_signal(bar, inc=1, device_id=(bc, f), device_id_type=MESH)
    pl.semaphore_wait(bar, 9)

    def start(src, dst, sem):
        cp = pltpu.make_async_copy(src, dst, sem)
        cp.start()
        return cp

    def wait_on(ref, sem):
        pltpu.make_async_copy(ref, ref, sem).wait()

    P = (pa_ref, pb_ref, pc_ref)
    O = (oa_ref, ob_ref, oc_ref)

    def blk(g, j, ff):
        if g < 2:
            return P[g].at[j, pl.ds(pl.multiple_of(ff * ROWS, ROWS), ROWS)]
        return P[g].at[ff, j]

    order = [
        (1, z3, yb), (1, z2, yb), (1, z3, y), (1, z2, y), (1, z1, yb), (1, z, yb), (0, z3, yb), (0, z2, yb),
        (0, z1, yb), (0, z, yb), (0, z3, y), (0, z2, y), (1, z1, y), (0, z1, y), (0, z, y), (1, z, y),
    ]
    mine = (b, bx)
    his = (bc, bxc)
    pend = []
    cnt = [0] * NG

    def open_group(g):
        for i, (jj, zz, yy) in enumerate(order):
            cp = pltpu.make_async_remote_copy(
                src_ref=blk(g, his[jj], zz * 2 + yy), dst_ref=r0.at[g, i], send_sem=s0_send.at[g, i],
                recv_sem=s0_recv.at[g, i], device_id=(bc, f), device_id_type=MESH,
            )
            cp.start()
            pend.append((cp, None))
        state["ready"].append(g)
        pump()

    state = {"ready": [], "issued": 0, "used": 0}
    depth = ring.shape[0]

    def pump():
        while state["issued"] < len(plan) and state["issued"] - state["used"] < depth:
            g, i = plan[state["issued"]]
            if g not in state["ready"]:
                return
            jj, zz, yy = order[i]
            slot = state["issued"] % depth
            start(blk(g, mine[jj], zz * 2 + yy), ring.at[slot], ring_sem.at[slot])
            state["issued"] += 1

    def add(dst, srcs):
        @pl.loop(0, ROWS // STRIP, unroll=1)
        def _(k):
            rows = pl.ds(pl.multiple_of(k * STRIP, STRIP), STRIP)
            if len(srcs) == 2 and dst.dtype == bf16:
                dst[rows, :] = srcs[0][rows, :] + srcs[1][rows, :]
                return
            v = srcs[0][rows, :].astype(f32)
            for s in srcs[1:]:
                v = v + s[rows, :].astype(f32)
            dst[rows, :] = v.astype(dst.dtype)

    def combine(g, i, more=()):
        slot = state["used"] % depth
        assert plan[state["used"]] == (g, i)
        wait_on(ring.at[slot], ring_sem.at[slot])
        wait_on(r0.at[g, i], s0_recv.at[g, i])
        srcs = [r0.at[g, i], ring.at[slot]]
        for ref, sem in more:
            wait_on(ref, sem)
            srcs.append(ref)
        add(r0.at[g, i], srcs)
        state["used"] += 1
        pump()

    def send(g, src, dst, rsem, dev):
        i = cnt[g]
        cnt[g] += 1
        cp = pltpu.make_async_remote_copy(
            src_ref=src, dst_ref=dst, send_sem=send_sem.at[g, i], recv_sem=rsem, device_id=dev, device_id_type=MESH
        )
        cp.start()
        pend.append((cp, None))

    X = (bx, f)
    Y = (b, fy)

    def to_x4(g, i, slot):
        combine(g, i)
        send(g, r0.at[g, i], rx4.at[g, slot], rx4_s.at[g, slot], X)

    def to_x2(g, i, slot):
        combine(g, i)
        send(g, r0.at[g, i], rx2.at[g, slot], rx2_s.at[g, slot], X)

    def to_y4(g, i, slot):
        combine(g, i)
        send(g, r0.at[g, i], ry4.at[g, slot], ry4_s.at[g, slot], Y)

    def to_y3(g, i, slot, rslot):
        combine(g, i, () if rslot is None else ((rx4.at[g, rslot], rx4_s.at[g, rslot]),))
        send(g, r0.at[g, i], ry3.at[g, slot], ry3_s.at[g, slot], Y)

    s2 = jnp.where(mid_z, 2, 1)
    s3 = jnp.where(mid_z, 1, 2)

    def to_z(g, i, zz, slot, rslot, yslot):
        more = [(ry3.at[g, yslot], ry3_s.at[g, yslot])]
        if rslot is not None:
            more.append((rx2.at[g, rslot], rx2_s.at[g, rslot]))
        combine(g, i, more)
        send(g, r0.at[g, i], rz.at[g, slot], rz_s.at[g, slot], (b, zz * 2 + y))

    def to_near(g, i):
        combine(g, i, [(ry4.at[g, 1], ry4_s.at[g, 1])])
        send(g, r0.at[g, i], rn.at[g], rn_s.at[g], (b, fz1))

    def own_last(g, i):
        combine(g, i, [(ry3.at[g, 0], ry3_s.at[g, 0])] + [(rz.at[g, k], rz_s.at[g, k]) for k in range(3)])
        send(g, r0.at[g, i], rt.at[g, 0], rt_s.at[g, 0], X)

    def other_last(g, i):
        combine(g, i, [(ry4.at[g, 0], ry4_s.at[g, 0]), (rn.at[g], rn_s.at[g])])
        send(g, r0.at[g, i], rt.at[g, 1], rt_s.at[g, 1], X)

    finals = []

    def final(g):
        if finals:
            for cp in finals[-2:]:
                cp[0].wait()
                cp[1].wait_send()
        for q, (i, slot, j) in enumerate(((14, 1, b), (15, 0, bx))):
            wait_on(rt.at[g, slot], rt_s.at[g, slot])
            add(fin.at[q], [r0.at[g, i], rt.at[g, slot]])
            loc = start(fin.at[q], O[g].at[j], o_loc.at[g, q])
            rc = pltpu.make_async_remote_copy(
                src_ref=fin.at[q], dst_ref=O[g].at[j], send_sem=o_send.at[g, q], recv_sem=o_recv.at[g, q],
                device_id=(bc, f), device_id_type=MESH,
            )
            rc.start()
            finals.append((loc, rc))

    def steps_of(g):
        return [
            (lambda: to_x4(g, 0, 0), 0), (lambda: to_y4(g, 4, 1), 4), (lambda: to_x4(g, 1, 1), 1), (lambda: to_y4(g, 5, 0), 5),
            (lambda: to_x2(g, 2, 0), 2), (lambda: to_x2(g, 3, 1), 3), (lambda: to_y3(g, 6, 3, 0), 6), (lambda: to_y3(g, 7, 2, 1), 7),
            (lambda: to_y3(g, 8, 1, None), 8), (lambda: to_y3(g, 9, 0, None), 9), (lambda: to_near(g, 12), 12),
            (lambda: to_z(g, 10, z3, s3, 0, 3), 10), (lambda: other_last(g, 15), 15), (lambda: to_z(g, 11, z2, s2, 1, 2), 11),
            (lambda: to_z(g, 13, z1, 0, None, 1), 13), (lambda: own_last(g, 14), 14), (lambda: final(g), None),
        ]

    rows = res.shape[0]
    tiles = rows // TILE

    def tile(i):
        return pl.ds(pl.multiple_of(i * TILE, TILE), TILE)

    def row(i):
        return vec[i : i + 1, :]

    def load_mat(k, src):
        return start(src, mats.at[k], m_sem.at[k])

    def load_fl(k, src):
        return start(src, fl.at[k], f_sem.at[k])

    w_list = []
    for j in range(4):
        w_list += [wc_ref.at[j], wb_ref.at[j]]
    w_list += [wa_ref.at[3], wa_ref.at[0], wa_ref.at[1], wa_ref.at[2]] + [wc_ref.at[j] for j in range(4)]
    w_at = [0]

    def fetch(k):
        if k < len(w_list):
            start(w_list[k], wbuf.at[k % 2], w_sem.at[k % 2])

    def with_weight(body):
        k = w_at[0]
        w_at[0] += 1
        wait_on(wbuf.at[k % 2], w_sem.at[k % 2])
        body(wbuf.at[k % 2])
        fetch(k + 2)

    def colsum(i, v):
        sums8[i] += v[:8] + v[8:]

    p_cnt = [0]
    part = pst.shape[1]
    steps = WID // part

    def outer(left, right, dst, many=1):
        n = p_cnt[0]
        p_cnt[0] += many

        @pl.loop(0, steps * many)
        def _(i):
            k = n * steps + i
            slot = lax.rem(k, 2)

            @pl.when(k >= 2)
            def _():
                wait_on(pst.at[slot], p_sem.at[slot])
            at = pl.multiple_of(lax.rem(i, steps) * part, part)
            other = right[...] if many == 1 else right[i // steps]
            pst[slot] = dense_tn(left[:, pl.ds(at, part)], other).astype(bf16)
            to = dst if many == 1 else dst.at[i // steps]
            start(pst.at[slot], to.at[pl.ds(at, part)], p_sem.at[slot])

    def drain():
        for slot in range(2):
            wait_on(pst.at[slot], p_sem.at[slot])
        p_cnt[0] = 0

    GO, H2, GP, Q = 0, 1, 2, 3
    ATT, GB, GA, H1 = 0, 1, 2, 0

    def slope_load(j, i):
        at = tile(i)
        start(slope_ref.at[at, pl.ds(j * WID, WID)], fl.at[2, at], sl_sem.at[i])

    def mlp_back(j):
        def body(w):
            @pl.loop(0, tiles)
            def _(i):
                sl = fl.at[2, tile(i)]
                fl[3, :TILE, :] = dense_nt(mats[GO, tile(i), :], w[...])
                wait_on(sl, sl_sem.at[i])

                def strip(r):
                    v = (fl[3, r, :] * sl[r, :]).astype(bf16)
                    mats[GP, pl.ds(pl.multiple_of(i * TILE + r.start, STRIP), STRIP), :] = v
                    colsum(9 + j, v.astype(f32))

                strip_loop(TILE, strip, 2)
                if j < 3:
                    slope_load(j + 1, i)
        with_weight(body)

    def hidden_in(dst, j, left):
        def body(w):
            @pl.loop(0, tiles)
            def _(i):
                v = dense_nt(mats[left, tile(i), :], w[...])
                if j == 0:
                    fl[dst, tile(i), :] = v
                else:
                    fl[dst, tile(i), :] += v
        with_weight(body)

    def first_sums():
        def strip(r):
            colsum(13, mats[GO, r, :].astype(f32))
        strip_loop(rows, strip)

    def norm_two():
        wait_on(fl.at[1], f_sem.at[1])
        wait_on(fl.at[2], f_sem.at[2])

        def strip(r):
            n = fl[1, r, :]
            inv = inv2[r, 0:1]
            g = fl[0, r, :]
            colsum(4, g * n)
            colsum(3, g)
            dn = g * (1.0 + row(4))
            pull = dn - jnp.mean(dn, axis=-1, keepdims=True) - n * jnp.mean(dn * n, axis=-1, keepdims=True)
            gm = res[r, :].astype(f32) + inv * pull
            colsum(2, gm * fl[2, r, :])
            gb = (row(2) * gm).astype(bf16)
            colsum(8, gb.astype(f32))
            fl[1, r, :] = gm
            mats[GB, r, :] = gb

        strip_loop(rows, strip, UN)

    def att_in():
        def body(w):
            @pl.loop(0, tiles)
            def _(i):
                mats[GA, tile(i), :] = dense_nt(mats[GB, tile(i), :], w[...]).astype(bf16)
        with_weight(body)

    def clear():
        def strip(r):
            for k in (0, 2, 3):
                fl[k, r, :] = jnp.zeros((STRIP, WID), f32)
        strip_loop(rows, strip)

    def att_back(heads):
        @pl.loop(0, tiles)
        def _(i):
            for h in heads:
                low, width, off = head_window(h)
                cols = slice(low, low + width)
                mask = head_mask(off, width)

                def pick(k):
                    v = mats[k, tile(i), cols]
                    return v, jnp.where(mask, v, jnp.zeros_like(v))

                _, q = pick(Q)
                k_all, k_own = pick(Q + 1)
                v_all = mats[Q + 2, tile(i), cols]
                _, g = pick(GA)
                scores = dense_nt(k_all, q) * HEAD_DIM ** (-0.5)
                probs = jnp.exp(scores - lse[i, h : h + 1, :])
                grad_probs = dense_nt(v_all, g)
                total = jnp.sum(probs * grad_probs, axis=0, keepdims=True)
                gs = (probs * (grad_probs - total)).astype(bf16)
                fl[3, tile(i), cols] += dense(probs.astype(bf16), g)
                fl[2, tile(i), cols] += dense(gs, q) * HEAD_DIM ** (-0.5)
                fl[0, tile(i), cols] += dense_tn(gs, k_own) * HEAD_DIM ** (-0.5)

    def att_done():
        def strip(r):
            for k, a in enumerate((0, 2, 3)):
                v = fl[a, r, :].astype(bf16)
                mats[Q + k, r, :] = v
                if k != 1:
                    colsum(6 + k // 2, v.astype(f32))
        strip_loop(rows, strip)

    def norm_one():
        wait_on(mats.at[0], m_sem.at[0])

        def strip(r):
            n, inv = center_rows(mats[0, r, :].astype(f32))
            g = fl[0, r, :]
            colsum(1, g * n)
            colsum(0, g)
            dn = g * (1.0 + row(1))
            pull = dn - jnp.mean(dn, axis=-1, keepdims=True) - n * jnp.mean(dn * n, axis=-1, keepdims=True)
            fl[0, r, :] = fl[1, r, :] + inv * pull

        strip_loop(rows, strip, UN)
        start(fl.at[0], lat_out, out_sem.at[0])

    def mlp_out(j):
        k = 1 + j
        wait_on(mats.at[k], m_sem.at[k])

        def body(w):
            @pl.loop(0, tiles)
            def _(i):
                v = dense(mats[k, tile(i), :], w[...])
                if j == 0:
                    fl[2, tile(i), :] = v
                else:
                    fl[2, tile(i), :] += v
        with_weight(body)

    def block_end():
        wait_on(fl.at[3], f_sem.at[3])
        for i in range(tiles):
            m = mask_ref[i]

            def strip(r):
                at = pl.ds(pl.multiple_of(i * TILE + r.start, STRIP), STRIP)
                v = fl[2, at, :] + row(13)
                colsum(5, v * res[at, :].astype(f32))
                mats[5, at, :] = ((fl[3, at, :] + row(5) * v) * m).astype(bf16)

            strip_loop(TILE, strip)
        start(mats.at[5], block_out, out_sem.at[1])

    def small_send(k, src, dst, dev):
        cp = pltpu.make_async_remote_copy(
            src_ref=src, dst_ref=dst, send_sem=sm_send.at[k], recv_sem=sm_recv.at[k], device_id=dev, device_id_type=MESH
        )
        cp.start()
        pend.append((cp, None))

    partners = [(b, fy), (b, fz1), (b, zb * 2 + y)]

    def small_first():
        for i in range(16):
            smine[0, i : i + 1, :] = jnp.sum(sums8[i], axis=0, keepdims=True)
        small_send(0, smine.at[0], srecv.at[0], partners[0])

    def small_step(k):
        wait_on(srecv.at[k], sm_recv.at[k])
        if k < 2:
            smine[k + 1] = smine[k] + srecv[k]
            small_send(k + 1, smine.at[k + 1], srecv.at[k + 1], partners[k + 1])
        else:
            sall[b] = smine[k] + srecv[k]
            sall[b, 14:15, :] = row(14).astype(bf16).astype(f32)
            small_send(3, sall.at[b], sall.at[b], X)
            small_send(4, sall.at[b], sall.at[b], (bc, f))

    def cond_first():
        at = 3 * f // 4
        for k in range(4):
            @pl.when(lax.rem(3 * f, 4) == k)
            def _(k=k):
                both = jnp.concatenate([sall[b, pl.ds(at, 1), :], sall[b, pl.ds(at + 1, 1), :]], axis=1)
                gvec[...] = both[:, 288 * k : 288 * k + gvec.shape[1]]
        wait_on(ada, ada_sem)
        v = gvec[...]
        high = v.astype(bf16)
        v = v - high.astype(f32)
        middle = v.astype(bf16)
        low = (v - middle.astype(f32)).astype(bf16)
        left = jnp.concatenate([high, middle, low, jnp.zeros((13, gvec.shape[1]), bf16)], axis=0)
        part_sum = dense(left, ada[...])
        cmine[0] = jnp.broadcast_to(jnp.sum(part_sum[:8], axis=0, keepdims=True), cmine.shape[1:])
        small_send(6, cmine.at[0], crecv.at[0], partners[0])

    def cond_step(k):
        wait_on(crecv.at[k], sm_recv.at[6 + k])
        cmine[k + 1] = cmine[k] + crecv[k]
        if k < 2:
            small_send(7 + k, cmine.at[k + 1], crecv.at[k + 1], partners[k + 1])
        else:
            start(cmine.at[3], cond_out, out_sem.at[5])

    def small_x():
        wait_on(sall.at[bx], sm_recv.at[3])
        small_send(5, sall.at[bx], sall.at[bx], (bc, f))

    def small_core():
        wait_on(sall.at[bc], sm_recv.at[4])
        wait_on(sall.at[bxc], sm_recv.at[5])
        start(sall, sums_out, out_sem.at[2])

    A, B, C = 0, 1, 2
    pieces1 = []
    for j in range(4):
        pieces1 += [
            functools.partial(mlp_back, j),
            functools.partial(outer, mats.at[H2], mats.at[GP], pb_ref.at[j]),
            functools.partial(hidden_in, 0, j, GP),
        ]

    def after_one():
        drain()
        open_group(B)
        load_mat(ATT, att_ref)
        load_fl(1, norm_ref)
        load_fl(2, branch_ref)

    def proj_outer():
        wait_on(mats.at[ATT], m_sem.at[ATT])
        outer(mats.at[ATT], mats.at[GB], pa_ref.at[3])

    def before_att():
        load_mat(H1, h1_ref)
        for k in range(3):
            wait_on(mats.at[Q + k], m_sem.at[Q + k])
        clear()

    heads = WID // HEAD_DIM
    pieces2 = [norm_two, proj_outer, att_in, before_att]
    pieces2 += [functools.partial(att_back, range(k, k + 4)) for k in range(0, heads, 4)] + [att_done]

    def a_outer():
        wait_on(mats.at[H1], m_sem.at[H1])
        outer(mats.at[H1], mats.at[pl.ds(Q, 3)], pa_ref, 3)

    pieces2 += [a_outer]

    def after_two():
        drain()
        open_group(A)
        load_mat(0, x_ref)
        load_fl(3, mid_ref)
        for j in range(2):
            load_mat(1 + j, hid_ref.at[:, pl.ds(j * WID, WID)])

    def h1_in(k):
        hidden_in(0, k, Q + k)
        if k < 2:
            load_mat(Q + k, hid_ref.at[:, pl.ds((2 + k) * WID, WID)])

    pieces3 = [functools.partial(h1_in, k) for k in range(3)] + [norm_one]
    pieces3 += [functools.partial(mlp_out, j) for j in range(4)] + [block_end]
    tail = [small_first] + [functools.partial(small_step, k) for k in range(3)] + [cond_first, small_x] + [functools.partial(cond_step, k) for k in range(3)] + [small_core]

    pieces = pieces1 + [after_one] + pieces2 + [after_two] + pieces3 + tail
    groups = [steps_of(g) for g in range(NG)]
    size = len(groups[0])
    seq = []
    for code in PROGRAM:
        if code < 0:
            seq.append((pieces.pop(0), None))
        else:
            g, n = divmod(code, size)
            fn, i = groups[g][n]
            seq.append((fn, None if i is None else (g, i)))
    assert not pieces
    plan = [t for _, t in seq if t is not None]

    open_group(C)
    start(vec_ref, vec, out_sem.at[3])
    start(ada_ref, ada, ada_sem)
    start(lse_ref, lse, lse_sem)
    start(inv_ref, inv2, inv_sem)
    load_mat(GO, go_ref)
    fetch(0)
    for i in range(tiles):
        slope_load(0, i)
    load_mat(H2, h2_ref)
    fetch(1)
    for k in range(3):
        load_mat(Q + k, qkv_ref.at[k])
    start(res_ref, res, out_sem.at[4])
    sums8[...] = jnp.zeros_like(sums8)
    wait_on(vec, out_sem.at[3])
    wait_on(mats.at[GO], m_sem.at[GO])
    wait_on(mats.at[H2], m_sem.at[H2])
    wait_on(res, out_sem.at[4])
    wait_on(lse, lse_sem)
    wait_on(inv2, inv_sem)
    first_sums()
    for fn, _ in seq:
        fn()
    for loc, rc in finals[-2:]:
        loc.wait()
        rc.wait_send()
    for g in range(NG):
        for q, j in enumerate((bc, bxc)):
            wait_on(O[g].at[j], o_recv.at[g, q])
    for cp, _ in pend:
        cp.wait_send()
    wait_on(lat_out, out_sem.at[0])
    wait_on(block_out, out_sem.at[1])
    wait_on(sums_out, out_sem.at[2])
    wait_on(cond_out, out_sem.at[5])


def backward(mask, vec, wa, wb, wc, x, res, h1, qkv, att, branch, mid, h2, slope, hid, go, pc, w_ada, lse, norm, inv):
    any_space = pl.BlockSpec(memory_space=pl.ANY)
    f32, bf16 = jnp.float32, jnp.bfloat16
    rows = x.shape[0]
    sds = jax.ShapeDtypeStruct
    sem = pltpu.SemaphoreType.DMA
    mat = (rows, WID)
    blkshape = (ROWS, WID)
    outs = (
        sds((4, 16, WID), f32), sds((8, WID), f32), sds((4,) + blkshape, f32), sds((4,) + blkshape, f32), sds((4,) + blkshape, f32),
        sds(mat, bf16), sds(mat, f32), sds((4, WID, WID), bf16), sds((4, WID, WID), bf16),
    )

    def vm(*shape, dt=bf16):
        return pltpu.VMEM(shape, dt)

    return pl.pallas_call(
        backward_kernel,
        out_shape=outs,
        in_specs=[pl.BlockSpec(memory_space=pltpu.SMEM)] + [any_space] * 20,
        out_specs=(any_space,) * len(outs),
        scratch_shapes=[
            vm(NG, 16, *blkshape), vm(4, *blkshape), vm(NG, 2, *blkshape), vm(NG, 2, *blkshape), vm(NG, 4, *blkshape), vm(NG, 2, *blkshape),
            vm(NG, *blkshape), vm(NG, 3, *blkshape), vm(NG, 2, *blkshape), vm(2, *blkshape, dt=f32),
            vm(16, WID, dt=f32), vm(2, WID, WID), vm(2, 384, WID), vm(6, *mat), vm(*mat), vm(4, *mat, dt=f32),
            vm(16, 8, WID, dt=f32), vm(3, 16, WID, dt=f32), vm(3, 16, WID, dt=f32), vm(4, 16, WID, dt=f32),
            vm(*w_ada.shape), vm(1, w_ada.shape[0], dt=f32), vm(4, 8, WID, dt=f32), vm(3, 8, WID, dt=f32), vm(*lse.shape, dt=f32), vm(rows, 128, dt=f32),
            sem((4,)), sem((NG, 16)), sem((NG, 16)), sem((NG, 24)), sem((NG, 2)), sem((NG, 2)), sem((NG, 4)), sem((NG, 2)), sem((NG,)),
            sem((NG, 3)), sem((NG, 2)), sem((NG, 2)), sem((NG, 2)), sem((NG, 2)),
            sem((2,)), sem((2,)), sem((6,)), sem((4,)), sem((2,)), sem((6,)), sem((9,)), sem((9,)), sem, sem, sem,
        ],
        compiler_params=pltpu.CompilerParams(collective_id=2, has_side_effects=True, vmem_limit_bytes=64 << 20),
        name="backward",
    )(mask, vec, wa, wb, wc, x, res, h1, qkv, att, branch, mid, h2, slope, hid, go, pc, w_ada, lse, norm, inv)


def on_device_fast(
    latents, cond, live, w_ada, b_ada, w_qkv, b_qv, w_proj, b_proj, w_fc1, b_fc1, w_fc2, b_fc2, cotangent
):
    images, length, width = latents.shape[1:]
    rows = images * length
    f32 = jnp.float32
    scaled = jax.nn.silu(cond[0]).astype(jnp.bfloat16)
    mod_part = jnp.dot(scaled, w_ada, preferred_element_type=f32) + b_ada.astype(f32)
    at = lax.axis_index("fsdp")

    def place(part, total):
        return lax.dynamic_update_slice(jnp.zeros((total,), f32), part, (at * part.shape[0],))

    parts = (mod_part, b_qv.astype(f32), b_proj.astype(f32), b_fc1.astype(f32), b_fc2.astype(f32))
    vec = jnp.concatenate([place(p, 8 * p.shape[0]) for p in parts] + [jnp.where(at == 0, scaled.astype(f32), 0.0), jnp.zeros((width,), f32)]).reshape(16, width)
    la = jnp.concatenate([jnp.transpose(w_qkv.reshape(ROWS, 3, WID), (1, 0, 2)), w_proj[None]])
    lc = w_fc2.reshape(4, ROWS, WID)
    live_mask = (lax.iota(jnp.int32, images) < live[0, 0]).astype(f32)
    row_mask = jnp.repeat(live_mask, length)[:, None]
    x_rows = latents[0].reshape(rows, width)
    res = cotangent[0].reshape(rows, width) * row_mask.astype(jnp.bfloat16)
    vec, wa, wb, wc, h_first, qkv, attended, branch, middle, h_second, slope, hidden, grad_out, grad_fc2, lse, norm, inv = forward(vec, la, w_fc1, lc, x_rows, res)
    sums, cond_sum, oa, ob, oc, block_out, grad_rows, _, _ = backward(
        live_mask, vec, wa, wb, wc.reshape(4, width, width), x_rows, res, h_first, qkv, attended, branch, middle, h_second, slope, hidden,
        grad_out, grad_fc2.reshape(8, 4, ROWS, width), jnp.transpose(w_ada), lse, norm, inv,
    )
    flat = sums.reshape(4, 16 * width)
    total = jnp.sum(flat, axis=0)

    def mine(v, begin, size):
        return lax.dynamic_slice_in_dim(v, begin + at * size, size, axis=-1)

    mod_bins = mine(flat, 0, 6 * width // 8)
    high = lax.reduce_precision(mod_bins, 8, 7)
    middle = lax.reduce_precision(mod_bins - high, 8, 7)
    low = lax.reduce_precision(mod_bins - high - middle, 8, 7)
    split = jnp.concatenate([high, middle, low]).astype(jnp.bfloat16)
    scaled_bins = jnp.tile(sums[:, 14].astype(jnp.bfloat16), (3, 1))
    grad_wada = jnp.einsum("bd,be->de", scaled_bins, split, preferred_element_type=f32)
    silu_pull = jax.vjp(jax.nn.silu, cond[0])[1]
    grad_cond = silu_pull(cond_sum[0])[0][None, :]
    return (
        block_out.reshape(latents.shape),
        grad_rows.reshape(latents.shape),
        grad_cond,
        grad_wada,
        mine(total, 0, 6 * width // 8),
        jnp.transpose(oa[:3], (1, 0, 2)).reshape(ROWS, 3 * width),
        mine(total, 6 * width, 2 * width // 8),
        oa[3],
        mine(total, 8 * width, width // 8),
        jnp.transpose(ob, (1, 0, 2)).reshape(ROWS, 4 * width),
        mine(total, 9 * width, 4 * width // 8),
        oc.reshape(4 * ROWS, width),
        mine(total, 13 * width, width // 8),
    )


def solution(mesh):
    fast = mesh.shape["bin"] == 4 and mesh.shape["fsdp"] == 8
    return jax.shard_map(
        on_device_fast if fast else on_device_generic,
        mesh=mesh,
        in_specs=(
            P("bin", "fsdp", None, None),
            P("bin", None),
            P("bin", "fsdp"),
            P(None, "fsdp"),
            P("fsdp"),
            P("fsdp", None),
            P("fsdp"),
            P("fsdp", None),
            P("fsdp"),
            P("fsdp", None),
            P("fsdp"),
            P("fsdp", None),
            P("fsdp"),
            P("bin", "fsdp", None, None),
        ),
        out_specs=(
            P("bin", "fsdp", None, None),
            P("bin", "fsdp", None, None),
            P("bin", None),
            P(None, "fsdp"),
            P("fsdp"),
            P("fsdp", None),
            P("fsdp"),
            P("fsdp", None),
            P("fsdp"),
            P("fsdp", None),
            P("fsdp"),
            P("fsdp", None),
            P("fsdp"),
        ),
        check_vma=False,
    )
```

```python
import functools

import jax
import jax.numpy as jnp
from jax import lax
from jax.experimental import pallas as pl
from jax.experimental.pallas import tpu as pltpu
from jax.sharding import PartitionSpec as P

HEAD_DIM = 72
MESH = pl.DeviceIdType.MESH
ROWS = 144
WID = 1152
NG = 3


def layer_norm(field):
    center = field - jnp.mean(field, axis=-1, keepdims=True)
    return center * lax.rsqrt(jnp.mean(center * center, axis=-1, keepdims=True) + 1e-06)


def gelu_tanh(field):
    return (
        0.5
        * field
        * (1.0 + jnp.tanh(0.7978845608028654 * (field + 0.044715 * field * field * field)))
    )


def modulate(field, shift_vec, scale_vec):
    return layer_norm(field) * (1.0 + scale_vec) + shift_vec


def pair_scores(query_block, key_block):
    return jnp.einsum(
        "gqhd,gkhd->ghqk", query_block, key_block, preferred_element_type=jnp.float32
    ) * HEAD_DIM ** (-0.5)


def attend_pair(group_item):
    query_block, key_block, value_block = group_item
    scores = pair_scores(query_block, key_block)
    highest = jnp.max(scores, axis=-1, keepdims=True)
    exp_scores = jnp.exp(scores - highest)
    totals = jnp.sum(exp_scores, axis=-1, keepdims=True)
    attn_probs = (exp_scores / totals).astype(jnp.bfloat16)
    attended = jnp.einsum(
        "ghqk,gkhd->gqhd", attn_probs, value_block, preferred_element_type=jnp.float32
    )
    return (attended, (highest + jnp.log(totals))[..., 0])


def attend_back(group_item):
    query_block, key_block, value_block, log_total, grad_att = group_item
    scores = pair_scores(query_block, key_block)
    attn_probs = jnp.exp(scores - log_total[..., None])
    grad_probs = jnp.einsum(
        "gqhd,gkhd->ghqk", grad_att, value_block, preferred_element_type=jnp.float32
    )
    row_terms = jnp.sum(attn_probs * grad_probs, axis=-1, keepdims=True)
    grad_scores = (attn_probs * (grad_probs - row_terms)).astype(jnp.bfloat16)
    grad_query = jnp.einsum(
        "ghqk,gkhd->gqhd", grad_scores, key_block, preferred_element_type=jnp.float32
    ) * HEAD_DIM ** (-0.5)
    grad_key = jnp.einsum(
        "ghqk,gqhd->gkhd", grad_scores, query_block, preferred_element_type=jnp.float32
    ) * HEAD_DIM ** (-0.5)
    grad_value = jnp.einsum(
        "ghqk,gqhd->gkhd",
        attn_probs.astype(jnp.bfloat16),
        grad_att,
        preferred_element_type=jnp.float32,
    )
    return jnp.stack([grad_query, grad_key, grad_value], axis=2)


def run_block(flat_rows, modulation, weights, images, length):
    full_qkv, full_proj, full_fc1, full_fc2, bias_qv, bias_proj, bias_fc1, bias_fc2 = weights
    width = flat_rows.shape[1]
    heads = width // HEAD_DIM
    pieces = jnp.split(modulation, 6)
    h_first = modulate(flat_rows, pieces[0], pieces[1]).astype(jnp.bfloat16)
    qkv_bias = jnp.concatenate(
        [bias_qv[:width], jnp.zeros((width,), jnp.bfloat16), bias_qv[width:]]
    ).astype(jnp.float32)
    qkv_rows = (jnp.dot(h_first, full_qkv, preferred_element_type=jnp.float32) + qkv_bias).astype(
        jnp.bfloat16
    )
    split_rows = qkv_rows.reshape(images // 2, 2, length, 3, heads, HEAD_DIM)
    attended, log_total = lax.map(
        attend_pair, (split_rows[:, :, :, 0], split_rows[:, :, :, 1], split_rows[:, :, :, 2])
    )
    attended = attended.reshape(images * length, width).astype(jnp.bfloat16)
    branch = jnp.dot(attended, full_proj, preferred_element_type=jnp.float32) + bias_proj.astype(
        jnp.float32
    )
    middle = flat_rows + pieces[2] * branch
    h_second = modulate(middle, pieces[3], pieces[4]).astype(jnp.bfloat16)
    pre_act = jnp.dot(h_second, full_fc1, preferred_element_type=jnp.float32) + bias_fc1.astype(
        jnp.float32
    )
    hidden = gelu_tanh(pre_act).astype(jnp.bfloat16)
    mlp_out = jnp.dot(hidden, full_fc2, preferred_element_type=jnp.float32) + bias_fc2.astype(
        jnp.float32
    )
    result = middle + pieces[5] * mlp_out
    return (
        h_first,
        split_rows,
        log_total,
        attended,
        branch,
        middle,
        h_second,
        pre_act,
        hidden,
        mlp_out,
        result,
    )


def on_device_generic(
    latents,
    cond,
    live,
    w_ada,
    b_ada,
    w_qkv,
    b_qv,
    w_proj,
    b_proj,
    w_fc1,
    b_fc1,
    w_fc2,
    b_fc2,
    cotangent,
):
    images = latents.shape[1]
    length = latents.shape[2]
    width = latents.shape[3]
    heads = width // HEAD_DIM
    scaled = jax.nn.silu(cond[0]).astype(jnp.bfloat16)
    mod_part = jnp.dot(scaled, w_ada, preferred_element_type=jnp.float32) + b_ada.astype(
        jnp.float32
    )
    modulation = lax.all_gather(mod_part, "fsdp", axis=0, tiled=True)
    gathered = (
        lax.all_gather(w_qkv, "fsdp", axis=0, tiled=True),
        lax.all_gather(w_proj, "fsdp", axis=0, tiled=True),
        lax.all_gather(w_fc1, "fsdp", axis=0, tiled=True),
        lax.all_gather(w_fc2, "fsdp", axis=0, tiled=True),
        lax.all_gather(b_qv, "fsdp", axis=0, tiled=True),
        lax.all_gather(b_proj, "fsdp", axis=0, tiled=True),
        lax.all_gather(b_fc1, "fsdp", axis=0, tiled=True),
        lax.all_gather(b_fc2, "fsdp", axis=0, tiled=True),
    )
    flat_rows = latents[0].reshape(images * length, width).astype(jnp.float32)
    live_mask = (lax.iota(jnp.int32, images) < live[0, 0]).astype(jnp.float32)
    row_mask = jnp.repeat(live_mask, length)[:, None]
    forward_run = run_block(flat_rows, modulation, gathered, images, length)
    block_out = (forward_run[10] * row_mask).astype(jnp.bfloat16).reshape(latents.shape)
    weights = (
        lax.all_gather(w_qkv, "fsdp", axis=0, tiled=True),
        lax.all_gather(w_proj, "fsdp", axis=0, tiled=True),
        lax.all_gather(w_fc1, "fsdp", axis=0, tiled=True),
        lax.all_gather(w_fc2, "fsdp", axis=0, tiled=True),
        lax.all_gather(b_qv, "fsdp", axis=0, tiled=True),
        lax.all_gather(b_proj, "fsdp", axis=0, tiled=True),
        lax.all_gather(b_fc1, "fsdp", axis=0, tiled=True),
        lax.all_gather(b_fc2, "fsdp", axis=0, tiled=True),
    )
    full_qkv, full_proj, full_fc1, full_fc2 = (weights[0], weights[1], weights[2], weights[3])
    saved = run_block(flat_rows, modulation, weights, images, length)
    (
        h_first,
        split_rows,
        log_total,
        attended,
        branch,
        middle,
        h_second,
        pre_act,
        hidden,
        mlp_out,
        result,
    ) = saved
    pieces = jnp.split(modulation, 6)
    grad_res = cotangent[0].reshape(images * length, width).astype(jnp.float32) * row_mask
    grad_out = (pieces[5] * grad_res).astype(jnp.bfloat16)
    grad_gate_two = jnp.sum(grad_res * mlp_out, axis=0)
    grad_fc2 = jnp.einsum("rf,rd->fd", hidden, grad_out, preferred_element_type=jnp.float32)
    grad_bfc2 = jnp.sum(grad_out.astype(jnp.float32), axis=0)
    grad_hidden = jnp.einsum("rd,fd->rf", grad_out, full_fc2, preferred_element_type=jnp.float32)
    gelu_pull = jax.vjp(gelu_tanh, pre_act)[1]
    grad_pre = gelu_pull(grad_hidden)[0].astype(jnp.bfloat16)
    grad_fc1 = jnp.einsum("rd,rf->df", h_second, grad_pre, preferred_element_type=jnp.float32)
    grad_bfc1 = jnp.sum(grad_pre.astype(jnp.float32), axis=0)
    grad_h2 = jnp.einsum("rf,df->rd", grad_pre, full_fc1, preferred_element_type=jnp.float32)
    second_pull = jax.vjp(modulate, middle, pieces[3], pieces[4])[1]
    grad_mid_norm, grad_shift_two, grad_scale_two = second_pull(grad_h2)
    grad_mid = grad_res + grad_mid_norm
    grad_branch = (pieces[2] * grad_mid).astype(jnp.bfloat16)
    grad_gate_one = jnp.sum(grad_mid * branch, axis=0)
    grad_proj = jnp.einsum("rd,re->de", attended, grad_branch, preferred_element_type=jnp.float32)
    grad_bproj = jnp.sum(grad_branch.astype(jnp.float32), axis=0)
    grad_att = jnp.einsum(
        "re,de->rd", grad_branch, full_proj, preferred_element_type=jnp.float32
    ).astype(jnp.bfloat16)
    grad_att = grad_att.reshape(images // 2, 2, length, heads, HEAD_DIM)
    grad_qkv = lax.map(
        attend_back,
        (
            split_rows[:, :, :, 0],
            split_rows[:, :, :, 1],
            split_rows[:, :, :, 2],
            log_total,
            grad_att,
        ),
    )
    grad_qkv = grad_qkv.reshape(images * length, 3 * width).astype(jnp.bfloat16)
    grad_wqkv = jnp.einsum("rd,re->de", h_first, grad_qkv, preferred_element_type=jnp.float32)
    qkv_sums = jnp.sum(grad_qkv.astype(jnp.float32), axis=0)
    grad_bqv = jnp.concatenate([qkv_sums[:width], qkv_sums[2 * width :]])
    grad_h1 = jnp.einsum("re,de->rd", grad_qkv, full_qkv, preferred_element_type=jnp.float32)
    first_pull = jax.vjp(modulate, flat_rows, pieces[0], pieces[1])[1]
    grad_rows_norm, grad_shift_one, grad_scale_one = first_pull(grad_h1)
    grad_rows = grad_mid + grad_rows_norm
    grad_mod = jnp.concatenate(
        [
            grad_shift_one,
            grad_scale_one,
            grad_gate_one,
            grad_shift_two,
            grad_scale_two,
            grad_gate_two,
        ]
    )
    shards = (
        lax.psum_scatter(grad_wqkv, "fsdp", scatter_dimension=0, tiled=True),
        lax.psum_scatter(grad_proj, "fsdp", scatter_dimension=0, tiled=True),
        lax.psum_scatter(grad_fc1, "fsdp", scatter_dimension=0, tiled=True),
        lax.psum_scatter(grad_fc2, "fsdp", scatter_dimension=0, tiled=True),
        lax.psum_scatter(grad_bqv, "fsdp", scatter_dimension=0, tiled=True),
        lax.psum_scatter(grad_bproj, "fsdp", scatter_dimension=0, tiled=True),
        lax.psum_scatter(grad_bfc1, "fsdp", scatter_dimension=0, tiled=True),
        lax.psum_scatter(grad_bfc2, "fsdp", scatter_dimension=0, tiled=True),
        lax.psum_scatter(grad_mod, "fsdp", scatter_dimension=0, tiled=True),
    )
    mod_mine = shards[8]
    grad_wada = scaled.astype(jnp.float32)[:, None] * mod_mine[None, :]
    grad_scaled = jnp.dot(w_ada.astype(jnp.float32), mod_mine, precision=lax.Precision.HIGHEST)
    grad_scaled = lax.psum(grad_scaled, "fsdp")
    silu_pull = jax.vjp(jax.nn.silu, cond[0])[1]
    grad_cond = silu_pull(grad_scaled)[0][None, :]
    totals = lax.psum(
        (
            shards[0],
            shards[1],
            shards[2],
            shards[3],
            shards[4],
            shards[5],
            shards[6],
            shards[7],
            grad_wada,
            mod_mine,
        ),
        "bin",
    )
    return (
        block_out,
        grad_rows.reshape(latents.shape),
        grad_cond,
        totals[8],
        totals[9],
        totals[0],
        totals[4],
        totals[1],
        totals[5],
        totals[2],
        totals[6],
        totals[3],
        totals[7],
    )


TILE = 256
UN = 4
GATHER_PROGRAM = (
    0, 1, 4, 5, -1, 9, 19, 20, 10, -1, 2, 11, 13, -1, 24, 12, 22, 8, -1, 42, 3, 16, 17, 14,
    15, 30, 6, 28, 23, 7, 18, 39, 38, 29, 25, 21, 34, -1, -1, 35, -1, 32, 47, 43, -1, 33, 49, 26,
    37, 41, 27, 40, 36, 31, -1, 46, -1, -1, 44, 48, -1, 50, 51, -1, 53, 54, -1, 45, 52, -1, 55, 56,
    -1,
)
STRIP = 16


def coords():
    b = lax.axis_index("bin")
    f = lax.axis_index("fsdp")
    return b, f, b // 2, lax.rem(b, 2), f // 2, lax.rem(f, 2)


def strip_loop(rows, body, unroll=1):
    @pl.loop(0, rows // STRIP, unroll=unroll)
    def _(k):
        body(pl.ds(pl.multiple_of(k * STRIP, STRIP), STRIP))


def dense(left, right):
    return jnp.dot(left, right, preferred_element_type=jnp.float32)


def dense_nt(left, right):
    return lax.dot_general(left, right, (((1,), (1,)), ((), ())), preferred_element_type=jnp.float32)


def dense_tn(left, right):
    return lax.dot_general(left, right, (((0,), (0,)), ((), ())), preferred_element_type=jnp.float32)


def center_rows(v):
    v = v - jnp.mean(v, axis=-1, keepdims=True)
    inv = lax.rsqrt(jnp.mean(v * v, axis=-1, keepdims=True) + 1e-06)
    return v * inv, inv


def head_window(h):
    start = HEAD_DIM * h
    low = start // 128 * 128
    width = 128 if start - low + HEAD_DIM <= 128 else 256
    return low, width, start - low


def head_mask(off, width):
    lanes = lax.broadcasted_iota(jnp.int32, (1, width), 1)
    return jnp.logical_and(lanes >= off, lanes < off + HEAD_DIM)


def head_probs(q, k):
    scores = dense_nt(k, q) * HEAD_DIM ** (-0.5)
    high = jnp.max(scores, axis=0, keepdims=True)
    e = jnp.exp(scores - high)
    total = jnp.sum(e, axis=0, keepdims=True)
    return e * (1.0 / total), high + jnp.log(total)


def forward_kernel(
    vec_ref, la_ref, lb_ref, lc_ref, x_ref, res_ref,
    vec_out, wa_out, wb_out, wc_out, h1_out, qkv_out, att_out, branch_out, mid_out, h2_out, slope_out, hid_out, go_out, pc_out, lse_out, norm_out, inv_out,
    wa, wb, wc, vecs, vec, xs, res, h1, qkv, att, mid, h2, hid, go, acc, slope, pst, lse, norm, inv,
    loc_sem, sm_send, sm_recv, send_sem, recv_sem, in_sem, out_sem, wo_sem, co_sem, sl_sem, ps_sem,
):
    b, f, x, c, z, y = coords()
    bx = lax.rem(b + 2, 4)
    bc = b + 1 - 2 * c
    bxc = lax.rem(bc + 2, 4)
    fy = f + 1 - 2 * y
    yb = 1 - y
    z1 = z + 1 - 2 * lax.rem(z, 2)
    mid_z = jnp.logical_or(z == 1, z == 2)
    zb = lax.rem(z + 2, 4)
    zc = 3 - z
    z2 = jnp.where(mid_z, zc, zb)
    z3 = jnp.where(mid_z, zb, zc)
    fz1 = z1 * 2 + y
    bar = pltpu.get_barrier_semaphore()
    for k in range(1, 8):
        pl.semaphore_signal(bar, inc=1, device_id=(b, lax.rem(f + k, 8)), device_id_type=MESH)
    pl.semaphore_signal(bar, inc=1, device_id=(bx, f), device_id_type=MESH)
    pl.semaphore_signal(bar, inc=1, device_id=(bc, f), device_id_type=MESH)
    pl.semaphore_wait(bar, 9)

    W = (wa, wb, wc)
    L = (la_ref, lb_ref, lc_ref)

    def blk(g, j, ff):
        if g < 2:
            return W[g].at[j, pl.ds(pl.multiple_of(ff * ROWS, ROWS), ROWS)]
        return W[g].at[ff, j]

    smalls = []
    partners = ((b, fy), (b, fz1), (b, zb * 2 + y))

    def small_send(k):
        cp = pltpu.make_async_remote_copy(
            src_ref=vecs.at[k], dst_ref=vecs.at[3 + k], send_sem=sm_send.at[k], recv_sem=sm_recv.at[k],
            device_id=partners[k], device_id_type=MESH,
        )
        cp.start()
        smalls.append(cp)

    def small_step(k):
        pltpu.make_async_copy(vecs.at[3 + k], vecs.at[3 + k], sm_recv.at[k]).wait()
        total = vecs[k] + vecs[3 + k]
        if k < 2:
            vecs[k + 1] = total
            small_send(k + 1)
        else:
            vec[...] = total
            keep(vec, vec_out, 0)


    pend = []
    outs = []
    cnt = [0] * NG

    def send(g, j, ff, dev, cond=None, src=None):
        i = cnt[g]
        cnt[g] += 1
        cp = pltpu.make_async_remote_copy(
            src_ref=blk(g, j, ff) if src is None else src, dst_ref=blk(g, j, ff),
            send_sem=send_sem.at[g, i], recv_sem=recv_sem.at[g, j, ff], device_id=dev, device_id_type=MESH,
        )
        if cond is None:
            cp.start()
        else:
            @pl.when(cond)
            def _():
                cp.start()
        pend.append((cp, cond))

    def copy_out(src, dst, sem):
        cp = pltpu.make_async_copy(src, dst, sem)
        cp.start()
        return cp

    def arrive(g, j, ff, cond=None):
        def go_on():
            pltpu.make_async_copy(blk(g, j, ff), blk(g, j, ff), recv_sem.at[g, j, ff]).wait()
            if g == 2:
                copy_out(wc.at[ff, j], wc_out.at[ff, j], co_sem.at[j, ff])
        if cond is None:
            go_on()
        else:
            pl.when(cond)(go_on)

    up = (b, jnp.minimum(f + 2, 7))
    dn = (b, jnp.maximum(f - 2, 0))

    def piece(g, j):
        if g != 1:
            return L[g].at[j]
        return lb_ref.at[:, pl.ds(pl.multiple_of(j * WID, WID), WID)]

    def start_sends(g):
        sb = piece(g, b)
        sx = piece(g, bx)
        return [
            lambda: send(g, b, f, up, z < 3, sb), lambda: send(g, b, f, dn, z > 0, sb), lambda: send(g, b, f, (b, fy), None, sb),
            lambda: send(g, bx, f, (b, fz1), None, sx), lambda: send(g, bx, f, (b, fy), None, sx),
        ]

    locs = []

    def local(g):
        for j in range(4):
            locs.append(copy_out(piece(g, j), blk(g, j, f), loc_sem.at[g, j]))

    def Z(g, zz, x_too):
        ff = zz * 2 + y
        arrive(g, b, ff)
        send(g, b, ff, up, jnp.logical_and(zz < z, z < 3))
        send(g, b, ff, dn, jnp.logical_and(zz > z, z > 0))
        send(g, b, ff, (b, fy))
        if x_too:
            send(g, b, ff, (bx, f))
        send(g, b, ff, (bc, f))

    def Y(g, zz, x_too):
        ff = zz * 2 + yb
        arrive(g, b, ff)
        if x_too:
            send(g, b, ff, (bx, f))
        send(g, b, ff, (bc, f))

    def X(g, ff):
        arrive(g, bx, ff)
        send(g, bx, ff, (bc, f))

    def actions(g):
        return [
            lambda: Z(g, z1, False), lambda: X(g, fz1), lambda: Y(g, z, False), lambda: X(g, fy),
            lambda: Z(g, z2, True), lambda: Y(g, z1, True), lambda: Z(g, z3, True), lambda: X(g, z2 * 2 + y),
            lambda: Y(g, z2, True), lambda: X(g, z1 * 2 + yb), lambda: X(g, z3 * 2 + y), lambda: Y(g, z3, True),
            lambda: X(g, z2 * 2 + yb), lambda: X(g, z3 * 2 + yb),
        ]

    def other_core(g):
        for zz in range(4):
            for jj in (bc, bxc):
                arrive(g, jj, zz * 2 + y, zz != z)
                arrive(g, jj, zz * 2 + yb)
        for cp in locs[g * 4 : g * 4 + 4]:
            cp.wait()

    def keep(src, dst, i):
        outs.append(copy_out(src, dst, out_sem.at[i]))

    def row(i):
        return vec[i : i + 1, :]

    def start_rows():
        in_x.wait()

        def first(r):
            n, _ = center_rows(xs[r, :].astype(jnp.float32))
            h1[r, :] = (n * (1.0 + row(1)) + row(0)).astype(jnp.bfloat16)

        strip_loop(h1.shape[0], first, UN)
        keep(h1, h1_out, 1)

    def start_grads():
        in_res.wait()

        def out_grad(r):
            go[r, :] = (res[r, :].astype(jnp.float32) * row(5)).astype(jnp.bfloat16)

        strip_loop(go.shape[0], out_grad)
        keep(go, go_out, 2)

    tiles = xs.shape[0] // TILE

    def tile(i):
        return pl.ds(pl.multiple_of(i * TILE, TILE), TILE)

    def project():
        @pl.loop(0, 3 * tiles)
        def _(k):
            j = k // tiles
            at = tile(lax.rem(k, tiles))
            bias = jnp.where(j == 1, 0.0, vec[pl.ds(6 + j // 2, 1), :])
            qkv[j, at, :] = (dense(h1[at, :], wa[j]) + bias).astype(jnp.bfloat16)
        keep(qkv, qkv_out, 3)

    def attention():
        @pl.loop(0, tiles)
        def _(i):
            acc[...] = jnp.zeros_like(acc)
            for h in range(WID // HEAD_DIM):
                low, width, off = head_window(h)
                cols = slice(low, low + width)
                mask = head_mask(off, width)
                q = qkv[0, tile(i), cols]
                v = qkv[2, tile(i), cols]
                probs, lse[i, h : h + 1, :] = head_probs(jnp.where(mask, q, jnp.zeros_like(q)), qkv[1, tile(i), cols])
                acc[:, cols] += dense_tn(probs.astype(jnp.bfloat16), jnp.where(mask, v, jnp.zeros_like(v)))
            att[tile(i), :] = acc[...].astype(jnp.bfloat16)
        keep(att, att_out, 6)
        keep(lse, lse_out, 11)

    def branch():
        @pl.loop(0, tiles)
        def _(i):
            mid[tile(i), :] = dense(att[tile(i), :], wa[3]) + row(8)
        cp = copy_out(mid, branch_out, out_sem.at[7])
        cp.wait()

        def second(r):
            m = xs[r, :].astype(jnp.float32) + row(2) * mid[r, :]
            mid[r, :] = m
            n, inverse = center_rows(m)
            norm[r, :] = n
            inv[r, :] = jnp.broadcast_to(inverse, (STRIP, 128))
            h2[r, :] = (n * (1.0 + row(4)) + row(3)).astype(jnp.bfloat16)

        strip_loop(mid.shape[0], second, UN)
        keep(mid, mid_out, 8)
        keep(h2, h2_out, 9)
        keep(norm, norm_out, 12)
        keep(inv, inv_out, 13)

    def hidden(j):
        cols = slice(j * WID, j * WID + WID)

        @pl.loop(0, tiles)
        def _(i):
            acc[...] = dense(h2[tile(i), :], wb[j]) + row(9 + j)

            @pl.when(j * tiles + i >= 1)
            def _():
                pltpu.make_async_copy(slope, slope_out.at[tile(0), :WID], sl_sem).wait()

            @pl.loop(0, TILE // STRIP, unroll=2)
            def _(k):
                r = pl.ds(pl.multiple_of(k * STRIP, STRIP), STRIP)
                v = acc[r, :]
                sq = v * v
                t = jnp.tanh(0.7978845608028654 * (v + 0.044715 * sq * v))
                half = 0.5 * (1.0 + t)
                slope[r, :] = half + 0.5 * v * (1.0 - t * t) * (0.7978845608028654 * (1.0 + 0.134145 * sq))
                hid[pl.ds(pl.multiple_of(i * TILE + k * STRIP, STRIP), STRIP), cols] = (v * half).astype(jnp.bfloat16)

            copy_out(slope, slope_out.at[tile(i), cols], sl_sem)
        if j == 3:
            pltpu.make_async_copy(slope, slope_out.at[tile(0), :WID], sl_sem).wait()
            keep(hid, hid_out, 10)

    part = pst.shape[1]

    def outer():
        @pl.loop(0, 4 * WID // part)
        def _(k):
            slot = lax.rem(k, 2)

            @pl.when(k >= 2)
            def _():
                pltpu.make_async_copy(pst.at[slot], pc_out.at[pl.ds(0, part)], ps_sem.at[slot]).wait()
            at = pl.multiple_of(k * part, part)
            pst[slot] = dense_tn(hid[:, pl.ds(at, part)], go[...]).astype(jnp.bfloat16)
            copy_out(pst.at[slot], pc_out.at[pl.ds(at, part)], ps_sem.at[slot])
        for slot in range(2):
            pltpu.make_async_copy(pst.at[slot], pc_out.at[pl.ds(0, part)], ps_sem.at[slot]).wait()

    def weights_out(g):
        outs.append(copy_out(W[g], (wa_out, wb_out)[g], wo_sem.at[g]))

    in_x = copy_out(x_ref, xs, in_sem.at[0])
    in_res = copy_out(res_ref, res, in_sem.at[1])
    def ready(g):
        other_core(g)
        weights_out(g)

    pieces = [functools.partial(small_step, k) for k in range(3)] + [start_rows, functools.partial(ready, 0)]
    pieces += [project, attention, branch, start_grads, functools.partial(ready, 1)]
    pieces += [functools.partial(hidden, j) for j in range(4)] + [outer]
    groups = [start_sends(g) + actions(g) for g in range(NG)]
    size = len(groups[0])
    own = pltpu.make_async_copy(vec_ref, vecs.at[0], sm_send.at[3])
    own.start()
    for g in range(NG):
        local(g)
    begun = False
    for code in GATHER_PROGRAM[:-1]:
        if code < 0:
            pieces.pop(0)()
        else:
            g, n = divmod(code, size)
            if n >= 5 and not begun:
                begun = True
                own.wait()
                small_send(0)
            groups[g][n]()
    assert not pieces
    for j in range(4):
        locs[8 + j].wait()
        copy_out(wc.at[f, j], wc_out.at[f, j], co_sem.at[j, f])
    other_core_c = 2
    for zz in range(4):
        for jj in (bc, bxc):
            arrive(other_core_c, jj, zz * 2 + y, zz != z)
            arrive(other_core_c, jj, zz * 2 + yb)
    for cp, cond in pend:
        if cond is None:
            cp.wait_send()
        else:
            @pl.when(cond)
            def _(cp=cp):
                cp.wait_send()
    for cp in smalls:
        cp.wait_send()
    for cp in outs:
        cp.wait()
    for ff in range(8):
        for j in range(4):
            pltpu.make_async_copy(wc.at[ff, j], wc_out.at[ff, j], co_sem.at[j, ff]).wait()


def forward(vec, la, lb, lc, x, res):
    any_space = pl.BlockSpec(memory_space=pl.ANY)
    f32, bf16 = jnp.float32, jnp.bfloat16
    rows = x.shape[0]
    sds = jax.ShapeDtypeStruct
    sem = pltpu.SemaphoreType.DMA
    mat = (rows, WID)
    outs = (
        sds((16, WID), f32), sds((4, WID, WID), bf16), sds((4, WID, WID), bf16), sds((8, 4, ROWS, WID), bf16),
        sds(mat, bf16), sds((3,) + mat, bf16), sds(mat, bf16), sds(mat, f32), sds(mat, f32), sds(mat, bf16),
        sds((rows, 4 * WID), f32), sds((rows, 4 * WID), bf16), sds(mat, bf16), sds((4 * WID, WID), bf16),
        sds((rows // TILE, 16, TILE), f32), sds(mat, f32), sds((rows, 128), f32),
    )
    vm = pltpu.VMEM
    return pl.pallas_call(
        forward_kernel,
        out_shape=outs,
        in_specs=[any_space] * 6,
        out_specs=(any_space,) * len(outs),
        scratch_shapes=[
            vm((4, WID, WID), bf16), vm((4, WID, WID), bf16), vm((8, 4, ROWS, WID), bf16), vm((6, 16, WID), f32), vm((16, WID), f32),
            vm(mat, bf16), vm(mat, bf16), vm(mat, bf16), vm((3,) + mat, bf16), vm(mat, bf16), vm(mat, f32), vm(mat, bf16),
            vm((rows, 4 * WID), bf16), vm(mat, bf16), vm((TILE, WID), f32), vm((TILE, WID), f32), vm((2, 384, WID), bf16),
            vm((rows // TILE, 16, TILE), f32), vm(mat, f32), vm((rows, 128), f32),
            sem((NG, 4)), sem((8,)), sem((8,)), sem((NG, 40)), sem((NG, 4, 8)), sem((2,)), sem((14,)), sem((2,)), sem((4, 8)), sem, sem((2,)),
        ],
        compiler_params=pltpu.CompilerParams(collective_id=1, has_side_effects=True, vmem_limit_bytes=63 << 20),
        name="forward",
    )(vec, la, lb, lc, x, res)


PROGRAM = (
    36, 35, 34, -1, 43, -1, -1, -1, -1, 37, -1, -1, -1, 38, 41, -1, 39, -1, -1, -1, 40, -1, 42, -1,
    17, 45, -1, -1, 18, -1, 19, 44, -1, 26, 47, 22, 23, 48, 21, 24, -1, -1, 25, 46, -1, -1, 28, 49,
    -1, -1, 20, 30, -1, 0, 4, 27, 2, 1, -1, 31, -1, 6, -1, 5, 8, 11, 7, 50, 3, 32, 10, -1,
    -1, 29, -1, 13, 9, -1, 14, -1, 12, -1, -1, -1, -1, -1, 15, -1, -1, -1, 33, -1, -1, 16,
)


def backward_kernel(
    mask_ref, vec_ref, wa_ref, wb_ref, wc_ref, x_ref, res_ref, h1_ref, qkv_ref, att_ref, branch_ref, mid_ref, h2_ref, slope_ref,
    hid_ref, go_ref, pc_ref, ada_ref, lse_ref, norm_ref, inv_ref,
    sums_out, cond_out, oa_ref, ob_ref, oc_ref, block_out, lat_out, pa_ref, pb_ref,
    r0, ring, rx4, ry4, ry3, rx2, rn, rz, rt, fin, vec, wbuf, pst, mats, res, fl, sums8, smine, srecv, sall, ada, gvec, cmine, crecv, lse, inv2,
    ring_sem, s0_send, s0_recv, send_sem, rx4_s, ry4_s, ry3_s, rx2_s, rn_s, rz_s, rt_s, o_loc, o_send, o_recv,
    w_sem, p_sem, m_sem, f_sem, sl_sem, out_sem, sm_send, sm_recv, ada_sem, lse_sem, inv_sem,
):
    f32, bf16 = jnp.float32, jnp.bfloat16
    b, f, x, c, z, y = coords()
    bx = lax.rem(b + 2, 4)
    bc = b + 1 - 2 * c
    bxc = lax.rem(bc + 2, 4)
    fy = f + 1 - 2 * y
    yb = 1 - y
    z1 = z + 1 - 2 * lax.rem(z, 2)
    mid_z = jnp.logical_or(z == 1, z == 2)
    zb = lax.rem(z + 2, 4)
    zc = 3 - z
    z2 = jnp.where(mid_z, zc, zb)
    z3 = jnp.where(mid_z, zb, zc)
    fz1 = z1 * 2 + y
    bar = pltpu.get_barrier_semaphore()
    for k in range(1, 8):
        pl.semaphore_signal(bar, inc=1, device_id=(b, lax.rem(f + k, 8)), device_id_type=MESH)
    pl.semaphore_signal(bar, inc=1, device_id=(bx, f), device_id_type=MESH)
    pl.semaphore_signal(bar, inc=1, device_id=(bc, f), device_id_type=MESH)
    pl.semaphore_wait(bar, 9)

    def start(src, dst, sem):
        cp = pltpu.make_async_copy(src, dst, sem)
        cp.start()
        return cp

    def wait_on(ref, sem):
        pltpu.make_async_copy(ref, ref, sem).wait()

    P = (pa_ref, pb_ref, pc_ref)
    O = (oa_ref, ob_ref, oc_ref)

    def blk(g, j, ff):
        if g < 2:
            return P[g].at[j, pl.ds(pl.multiple_of(ff * ROWS, ROWS), ROWS)]
        return P[g].at[ff, j]

    order = [
        (1, z3, yb), (1, z2, yb), (1, z3, y), (1, z2, y), (1, z1, yb), (1, z, yb), (0, z3, yb), (0, z2, yb),
        (0, z1, yb), (0, z, yb), (0, z3, y), (0, z2, y), (1, z1, y), (0, z1, y), (0, z, y), (1, z, y),
    ]
    mine = (b, bx)
    his = (bc, bxc)
    pend = []
    cnt = [0] * NG

    def open_group(g):
        for i, (jj, zz, yy) in enumerate(order):
            cp = pltpu.make_async_remote_copy(
                src_ref=blk(g, his[jj], zz * 2 + yy), dst_ref=r0.at[g, i], send_sem=s0_send.at[g, i],
                recv_sem=s0_recv.at[g, i], device_id=(bc, f), device_id_type=MESH,
            )
            cp.start()
            pend.append((cp, None))
        state["ready"].append(g)
        pump()

    state = {"ready": [], "issued": 0, "used": 0}
    depth = ring.shape[0]

    def pump():
        while state["issued"] < len(plan) and state["issued"] - state["used"] < depth:
            g, i = plan[state["issued"]]
            if g not in state["ready"]:
                return
            jj, zz, yy = order[i]
            slot = state["issued"] % depth
            start(blk(g, mine[jj], zz * 2 + yy), ring.at[slot], ring_sem.at[slot])
            state["issued"] += 1

    def add(dst, srcs):
        @pl.loop(0, ROWS // STRIP, unroll=3)
        def _(k):
            rows = pl.ds(pl.multiple_of(k * STRIP, STRIP), STRIP)
            if len(srcs) == 2 and dst.dtype == bf16:
                dst[rows, :] = srcs[0][rows, :] + srcs[1][rows, :]
                return
            v = srcs[0][rows, :].astype(f32)
            for s in srcs[1:]:
                v = v + s[rows, :].astype(f32)
            dst[rows, :] = v.astype(dst.dtype)

    def combine(g, i, more=()):
        slot = state["used"] % depth
        assert plan[state["used"]] == (g, i)
        wait_on(ring.at[slot], ring_sem.at[slot])
        wait_on(r0.at[g, i], s0_recv.at[g, i])
        srcs = [r0.at[g, i], ring.at[slot]]
        for ref, sem in more:
            wait_on(ref, sem)
            srcs.append(ref)
        add(r0.at[g, i], srcs)
        state["used"] += 1
        pump()

    def send(g, src, dst, rsem, dev):
        i = cnt[g]
        cnt[g] += 1
        cp = pltpu.make_async_remote_copy(
            src_ref=src, dst_ref=dst, send_sem=send_sem.at[g, i], recv_sem=rsem, device_id=dev, device_id_type=MESH
        )
        cp.start()
        pend.append((cp, None))

    X = (bx, f)
    Y = (b, fy)

    def to_x4(g, i, slot):
        combine(g, i)
        send(g, r0.at[g, i], rx4.at[g, slot], rx4_s.at[g, slot], X)

    def to_x2(g, i, slot):
        combine(g, i)
        send(g, r0.at[g, i], rx2.at[g, slot], rx2_s.at[g, slot], X)

    def to_y4(g, i, slot):
        combine(g, i)
        send(g, r0.at[g, i], ry4.at[g, slot], ry4_s.at[g, slot], Y)

    def to_y3(g, i, slot, rslot):
        combine(g, i, () if rslot is None else ((rx4.at[g, rslot], rx4_s.at[g, rslot]),))
        send(g, r0.at[g, i], ry3.at[g, slot], ry3_s.at[g, slot], Y)

    s2 = jnp.where(mid_z, 2, 1)
    s3 = jnp.where(mid_z, 1, 2)

    def to_z(g, i, zz, slot, rslot, yslot):
        more = [(ry3.at[g, yslot], ry3_s.at[g, yslot])]
        if rslot is not None:
            more.append((rx2.at[g, rslot], rx2_s.at[g, rslot]))
        combine(g, i, more)
        send(g, r0.at[g, i], rz.at[g, slot], rz_s.at[g, slot], (b, zz * 2 + y))

    def to_near(g, i):
        combine(g, i, [(ry4.at[g, 1], ry4_s.at[g, 1])])
        send(g, r0.at[g, i], rn.at[g], rn_s.at[g], (b, fz1))

    def own_last(g, i):
        combine(g, i, [(ry3.at[g, 0], ry3_s.at[g, 0])] + [(rz.at[g, k], rz_s.at[g, k]) for k in range(3)])
        send(g, r0.at[g, i], rt.at[g, 0], rt_s.at[g, 0], X)

    def other_last(g, i):
        combine(g, i, [(ry4.at[g, 0], ry4_s.at[g, 0]), (rn.at[g], rn_s.at[g])])
        send(g, r0.at[g, i], rt.at[g, 1], rt_s.at[g, 1], X)

    finals = []

    def final(g):
        if finals:
            for cp in finals[-2:]:
                cp[0].wait()
                cp[1].wait_send()
        for q, (i, slot, j) in enumerate(((14, 1, b), (15, 0, bx))):
            wait_on(rt.at[g, slot], rt_s.at[g, slot])
            add(fin.at[q], [r0.at[g, i], rt.at[g, slot]])
            loc = start(fin.at[q], O[g].at[j], o_loc.at[g, q])
            rc = pltpu.make_async_remote_copy(
                src_ref=fin.at[q], dst_ref=O[g].at[j], send_sem=o_send.at[g, q], recv_sem=o_recv.at[g, q],
                device_id=(bc, f), device_id_type=MESH,
            )
            rc.start()
            finals.append((loc, rc))

    def steps_of(g):
        return [
            (lambda: to_x4(g, 0, 0), 0), (lambda: to_y4(g, 4, 1), 4), (lambda: to_x4(g, 1, 1), 1), (lambda: to_y4(g, 5, 0), 5),
            (lambda: to_x2(g, 2, 0), 2), (lambda: to_x2(g, 3, 1), 3), (lambda: to_y3(g, 6, 3, 0), 6), (lambda: to_y3(g, 7, 2, 1), 7),
            (lambda: to_y3(g, 8, 1, None), 8), (lambda: to_y3(g, 9, 0, None), 9), (lambda: to_near(g, 12), 12),
            (lambda: to_z(g, 10, z3, s3, 0, 3), 10), (lambda: other_last(g, 15), 15), (lambda: to_z(g, 11, z2, s2, 1, 2), 11),
            (lambda: to_z(g, 13, z1, 0, None, 1), 13), (lambda: own_last(g, 14), 14), (lambda: final(g), None),
        ]

    rows = res.shape[0]
    tiles = rows // TILE

    def tile(i):
        return pl.ds(pl.multiple_of(i * TILE, TILE), TILE)

    def row(i):
        return vec[i : i + 1, :]

    def load_mat(k, src):
        return start(src, mats.at[k], m_sem.at[k])

    def load_fl(k, src):
        return start(src, fl.at[k], f_sem.at[k])

    w_list = []
    for j in range(4):
        w_list += [wc_ref.at[j], wb_ref.at[j]]
    w_list += [wa_ref.at[3], wa_ref.at[0], wa_ref.at[1], wa_ref.at[2]] + [wc_ref.at[j] for j in range(4)]
    w_at = [0]

    def fetch(k):
        if k < len(w_list):
            start(w_list[k], wbuf.at[k % 2], w_sem.at[k % 2])

    def with_weight(body):
        k = w_at[0]
        w_at[0] += 1
        wait_on(wbuf.at[k % 2], w_sem.at[k % 2])
        body(wbuf.at[k % 2])
        fetch(k + 2)

    def colsum(i, v):
        sums8[i] += v[:8] + v[8:]

    p_cnt = [0]
    part = pst.shape[1]
    steps = WID // part

    def outer(left, right, dst, many=1):
        n = p_cnt[0]
        p_cnt[0] += many

        @pl.loop(0, steps * many)
        def _(i):
            k = n * steps + i
            slot = lax.rem(k, 2)

            @pl.when(k >= 2)
            def _():
                wait_on(pst.at[slot], p_sem.at[slot])
            at = pl.multiple_of(lax.rem(i, steps) * part, part)
            other = right[...] if many == 1 else right[i // steps]
            pst[slot] = dense_tn(left[:, pl.ds(at, part)], other).astype(bf16)
            to = dst if many == 1 else dst.at[i // steps]
            start(pst.at[slot], to.at[pl.ds(at, part)], p_sem.at[slot])

    def drain():
        for slot in range(2):
            wait_on(pst.at[slot], p_sem.at[slot])
        p_cnt[0] = 0

    GO, H2, GP, Q = 0, 1, 2, 3
    ATT, GB, GA, H1 = 0, 1, 2, 0

    def slope_load(j, i):
        at = tile(i)
        start(slope_ref.at[at, pl.ds(j * WID, WID)], fl.at[2, at], sl_sem.at[i])

    def mlp_back(j):
        def body(w):
            @pl.loop(0, tiles)
            def _(i):
                sl = fl.at[2, tile(i)]
                fl[3, :TILE, :] = dense_nt(mats[GO, tile(i), :], w[...])
                wait_on(sl, sl_sem.at[i])

                def strip(r):
                    v = (fl[3, r, :] * sl[r, :]).astype(bf16)
                    mats[GP, pl.ds(pl.multiple_of(i * TILE + r.start, STRIP), STRIP), :] = v
                    colsum(9 + j, v.astype(f32))

                strip_loop(TILE, strip, 2)
                if j < 3:
                    slope_load(j + 1, i)
        with_weight(body)

    def hidden_in(dst, j, left):
        def body(w):
            @pl.loop(0, tiles)
            def _(i):
                v = dense_nt(mats[left, tile(i), :], w[...])
                if j == 0:
                    fl[dst, tile(i), :] = v
                else:
                    fl[dst, tile(i), :] += v
        with_weight(body)

    def first_sums():
        def strip(r):
            colsum(13, mats[GO, r, :].astype(f32))
        strip_loop(rows, strip, UN)

    def norm_two():
        wait_on(fl.at[1], f_sem.at[1])
        wait_on(fl.at[2], f_sem.at[2])

        def strip(r):
            n = fl[1, r, :]
            inv = inv2[r, 0:1]
            g = fl[0, r, :]
            colsum(4, g * n)
            colsum(3, g)
            dn = g * (1.0 + row(4))
            pull = dn - jnp.mean(dn, axis=-1, keepdims=True) - n * jnp.mean(dn * n, axis=-1, keepdims=True)
            gm = res[r, :].astype(f32) + inv * pull
            colsum(2, gm * fl[2, r, :])
            gb = (row(2) * gm).astype(bf16)
            colsum(8, gb.astype(f32))
            fl[1, r, :] = gm
            mats[GB, r, :] = gb

        strip_loop(rows, strip, UN)

    def att_in():
        def body(w):
            @pl.loop(0, tiles)
            def _(i):
                mats[GA, tile(i), :] = dense_nt(mats[GB, tile(i), :], w[...]).astype(bf16)
        with_weight(body)

    def clear():
        def strip(r):
            for k in (0, 2, 3):
                fl[k, r, :] = jnp.zeros((STRIP, WID), f32)
        strip_loop(rows, strip, UN)

    def att_back(heads):
        @pl.loop(0, tiles)
        def _(i):
            for h in heads:
                low, width, off = head_window(h)
                cols = slice(low, low + width)
                mask = head_mask(off, width)

                def pick(k):
                    v = mats[k, tile(i), cols]
                    return v, jnp.where(mask, v, jnp.zeros_like(v))

                _, q = pick(Q)
                k_all, k_own = pick(Q + 1)
                v_all = mats[Q + 2, tile(i), cols]
                _, g = pick(GA)
                scores = dense_nt(k_all, q) * HEAD_DIM ** (-0.5)
                probs = jnp.exp(scores - lse[i, h : h + 1, :])
                grad_probs = dense_nt(v_all, g)
                total = jnp.sum(probs * grad_probs, axis=0, keepdims=True)
                gs = (probs * (grad_probs - total)).astype(bf16)
                fl[3, tile(i), cols] += dense(probs.astype(bf16), g)
                fl[2, tile(i), cols] += dense(gs, q) * HEAD_DIM ** (-0.5)
                fl[0, tile(i), cols] += dense_tn(gs, k_own) * HEAD_DIM ** (-0.5)

    def att_done():
        def strip(r):
            for k, a in enumerate((0, 2, 3)):
                v = fl[a, r, :].astype(bf16)
                mats[Q + k, r, :] = v
                if k != 1:
                    colsum(6 + k // 2, v.astype(f32))
        strip_loop(rows, strip, UN)

    def norm_one():
        wait_on(mats.at[0], m_sem.at[0])

        def strip(r):
            n, inv = center_rows(mats[0, r, :].astype(f32))
            g = fl[0, r, :]
            colsum(1, g * n)
            colsum(0, g)
            dn = g * (1.0 + row(1))
            pull = dn - jnp.mean(dn, axis=-1, keepdims=True) - n * jnp.mean(dn * n, axis=-1, keepdims=True)
            fl[0, r, :] = fl[1, r, :] + inv * pull

        strip_loop(rows, strip, UN)
        start(fl.at[0], lat_out, out_sem.at[0])

    def mlp_out(j):
        k = 1 + j
        wait_on(mats.at[k], m_sem.at[k])

        def body(w):
            @pl.loop(0, tiles)
            def _(i):
                v = dense(mats[k, tile(i), :], w[...])
                if j == 0:
                    fl[2, tile(i), :] = v
                else:
                    fl[2, tile(i), :] += v
        with_weight(body)

    def block_end():
        wait_on(fl.at[3], f_sem.at[3])
        for i in range(tiles):
            m = mask_ref[i]

            def strip(r):
                at = pl.ds(pl.multiple_of(i * TILE + r.start, STRIP), STRIP)
                v = fl[2, at, :] + row(13)
                colsum(5, v * res[at, :].astype(f32))
                mats[5, at, :] = ((fl[3, at, :] + row(5) * v) * m).astype(bf16)

            strip_loop(TILE, strip, UN)
        start(mats.at[5], block_out, out_sem.at[1])

    def small_send(k, src, dst, dev):
        cp = pltpu.make_async_remote_copy(
            src_ref=src, dst_ref=dst, send_sem=sm_send.at[k], recv_sem=sm_recv.at[k], device_id=dev, device_id_type=MESH
        )
        cp.start()
        pend.append((cp, None))

    partners = [(b, fy), (b, fz1), (b, zb * 2 + y)]

    def small_first():
        for i in range(16):
            smine[0, i : i + 1, :] = jnp.sum(sums8[i], axis=0, keepdims=True)
        small_send(0, smine.at[0], srecv.at[0], partners[0])

    def small_step(k):
        wait_on(srecv.at[k], sm_recv.at[k])
        if k < 2:
            smine[k + 1] = smine[k] + srecv[k]
            small_send(k + 1, smine.at[k + 1], srecv.at[k + 1], partners[k + 1])
        else:
            sall[b] = smine[k] + srecv[k]
            sall[b, 14:15, :] = row(14).astype(bf16).astype(f32)
            small_send(3, sall.at[b], sall.at[b], X)
            small_send(4, sall.at[b], sall.at[b], (bc, f))

    def cond_first():
        at = 3 * f // 4
        for k in range(4):
            @pl.when(lax.rem(3 * f, 4) == k)
            def _(k=k):
                both = jnp.concatenate([sall[b, pl.ds(at, 1), :], sall[b, pl.ds(at + 1, 1), :]], axis=1)
                gvec[...] = both[:, 288 * k : 288 * k + gvec.shape[1]]
        wait_on(ada, ada_sem)
        v = gvec[...]
        high = v.astype(bf16)
        v = v - high.astype(f32)
        middle = v.astype(bf16)
        low = (v - middle.astype(f32)).astype(bf16)
        left = jnp.concatenate([high, middle, low, jnp.zeros((13, gvec.shape[1]), bf16)], axis=0)
        part_sum = dense(left, ada[...])
        cmine[0] = jnp.broadcast_to(jnp.sum(part_sum[:8], axis=0, keepdims=True), cmine.shape[1:])
        small_send(6, cmine.at[0], crecv.at[0], partners[0])

    def cond_step(k):
        wait_on(crecv.at[k], sm_recv.at[6 + k])
        cmine[k + 1] = cmine[k] + crecv[k]
        if k < 2:
            small_send(7 + k, cmine.at[k + 1], crecv.at[k + 1], partners[k + 1])
        else:
            start(cmine.at[3], cond_out, out_sem.at[5])

    def small_x():
        wait_on(sall.at[bx], sm_recv.at[3])
        small_send(5, sall.at[bx], sall.at[bx], (bc, f))

    def small_core():
        wait_on(sall.at[bc], sm_recv.at[4])
        wait_on(sall.at[bxc], sm_recv.at[5])
        start(sall, sums_out, out_sem.at[2])

    A, B, C = 0, 1, 2
    pieces1 = []
    for j in range(4):
        pieces1 += [
            functools.partial(mlp_back, j),
            functools.partial(outer, mats.at[H2], mats.at[GP], pb_ref.at[j]),
            functools.partial(hidden_in, 0, j, GP),
        ]

    def after_one():
        drain()
        open_group(B)
        load_mat(ATT, att_ref)
        load_fl(1, norm_ref)
        load_fl(2, branch_ref)

    def proj_outer():
        wait_on(mats.at[ATT], m_sem.at[ATT])
        outer(mats.at[ATT], mats.at[GB], pa_ref.at[3])

    def before_att():
        load_mat(H1, h1_ref)
        for k in range(3):
            wait_on(mats.at[Q + k], m_sem.at[Q + k])
        clear()

    heads = WID // HEAD_DIM
    pieces2 = [norm_two, proj_outer, att_in, before_att]
    pieces2 += [functools.partial(att_back, range(k, k + 4)) for k in range(0, heads, 4)] + [att_done]

    def a_outer():
        wait_on(mats.at[H1], m_sem.at[H1])
        outer(mats.at[H1], mats.at[pl.ds(Q, 3)], pa_ref, 3)

    pieces2 += [a_outer]

    def after_two():
        drain()
        open_group(A)
        load_mat(0, x_ref)
        load_fl(3, mid_ref)
        for j in range(2):
            load_mat(1 + j, hid_ref.at[:, pl.ds(j * WID, WID)])

    def h1_in(k):
        hidden_in(0, k, Q + k)
        if k < 2:
            load_mat(Q + k, hid_ref.at[:, pl.ds((2 + k) * WID, WID)])

    pieces3 = [functools.partial(h1_in, k) for k in range(3)] + [norm_one]
    pieces3 += [functools.partial(mlp_out, j) for j in range(4)] + [block_end]
    tail = [small_first] + [functools.partial(small_step, k) for k in range(3)] + [cond_first, small_x] + [functools.partial(cond_step, k) for k in range(3)] + [small_core]

    pieces = pieces1 + [after_one] + pieces2 + [after_two] + pieces3 + tail
    groups = [steps_of(g) for g in range(NG)]
    size = len(groups[0])
    seq = []
    for code in PROGRAM:
        if code < 0:
            seq.append((pieces.pop(0), None))
        else:
            g, n = divmod(code, size)
            fn, i = groups[g][n]
            seq.append((fn, None if i is None else (g, i)))
    assert not pieces
    plan = [t for _, t in seq if t is not None]

    open_group(C)
    start(vec_ref, vec, out_sem.at[3])
    start(ada_ref, ada, ada_sem)
    start(lse_ref, lse, lse_sem)
    start(inv_ref, inv2, inv_sem)
    load_mat(GO, go_ref)
    fetch(0)
    for i in range(tiles):
        slope_load(0, i)
    load_mat(H2, h2_ref)
    fetch(1)
    for k in range(3):
        load_mat(Q + k, qkv_ref.at[k])
    start(res_ref, res, out_sem.at[4])
    sums8[...] = jnp.zeros_like(sums8)
    wait_on(vec, out_sem.at[3])
    wait_on(mats.at[GO], m_sem.at[GO])
    wait_on(mats.at[H2], m_sem.at[H2])
    wait_on(res, out_sem.at[4])
    wait_on(lse, lse_sem)
    wait_on(inv2, inv_sem)
    first_sums()
    for fn, _ in seq:
        fn()
    for loc, rc in finals[-2:]:
        loc.wait()
        rc.wait_send()
    for g in range(NG):
        for q, j in enumerate((bc, bxc)):
            wait_on(O[g].at[j], o_recv.at[g, q])
    for cp, _ in pend:
        cp.wait_send()
    wait_on(lat_out, out_sem.at[0])
    wait_on(block_out, out_sem.at[1])
    wait_on(sums_out, out_sem.at[2])
    wait_on(cond_out, out_sem.at[5])


def backward(mask, vec, wa, wb, wc, x, res, h1, qkv, att, branch, mid, h2, slope, hid, go, pc, w_ada, lse, norm, inv):
    any_space = pl.BlockSpec(memory_space=pl.ANY)
    f32, bf16 = jnp.float32, jnp.bfloat16
    rows = x.shape[0]
    sds = jax.ShapeDtypeStruct
    sem = pltpu.SemaphoreType.DMA
    mat = (rows, WID)
    blkshape = (ROWS, WID)
    outs = (
        sds((4, 16, WID), f32), sds((8, WID), f32), sds((4,) + blkshape, f32), sds((4,) + blkshape, f32), sds((4,) + blkshape, f32),
        sds(mat, bf16), sds(mat, f32), sds((4, WID, WID), bf16), sds((4, WID, WID), bf16),
    )

    def vm(*shape, dt=bf16):
        return pltpu.VMEM(shape, dt)

    return pl.pallas_call(
        backward_kernel,
        out_shape=outs,
        in_specs=[pl.BlockSpec(memory_space=pltpu.SMEM)] + [any_space] * 20,
        out_specs=(any_space,) * len(outs),
        scratch_shapes=[
            vm(NG, 16, *blkshape), vm(4, *blkshape), vm(NG, 2, *blkshape), vm(NG, 2, *blkshape), vm(NG, 4, *blkshape), vm(NG, 2, *blkshape),
            vm(NG, *blkshape), vm(NG, 3, *blkshape), vm(NG, 2, *blkshape), vm(2, *blkshape, dt=f32),
            vm(16, WID, dt=f32), vm(2, WID, WID), vm(2, 384, WID), vm(6, *mat), vm(*mat), vm(4, *mat, dt=f32),
            vm(16, 8, WID, dt=f32), vm(3, 16, WID, dt=f32), vm(3, 16, WID, dt=f32), vm(4, 16, WID, dt=f32),
            vm(*w_ada.shape), vm(1, w_ada.shape[0], dt=f32), vm(4, 8, WID, dt=f32), vm(3, 8, WID, dt=f32), vm(*lse.shape, dt=f32), vm(rows, 128, dt=f32),
            sem((4,)), sem((NG, 16)), sem((NG, 16)), sem((NG, 24)), sem((NG, 2)), sem((NG, 2)), sem((NG, 4)), sem((NG, 2)), sem((NG,)),
            sem((NG, 3)), sem((NG, 2)), sem((NG, 2)), sem((NG, 2)), sem((NG, 2)),
            sem((2,)), sem((2,)), sem((6,)), sem((4,)), sem((2,)), sem((6,)), sem((9,)), sem((9,)), sem, sem, sem,
        ],
        compiler_params=pltpu.CompilerParams(collective_id=2, has_side_effects=True, vmem_limit_bytes=64 << 20),
        name="backward",
    )(mask, vec, wa, wb, wc, x, res, h1, qkv, att, branch, mid, h2, slope, hid, go, pc, w_ada, lse, norm, inv)


def on_device_fast(
    latents, cond, live, w_ada, b_ada, w_qkv, b_qv, w_proj, b_proj, w_fc1, b_fc1, w_fc2, b_fc2, cotangent
):
    images, length, width = latents.shape[1:]
    rows = images * length
    f32 = jnp.float32
    scaled = jax.nn.silu(cond[0]).astype(jnp.bfloat16)
    mod_part = jnp.dot(scaled, w_ada, preferred_element_type=f32) + b_ada.astype(f32)
    at = lax.axis_index("fsdp")

    def place(part, total):
        return lax.dynamic_update_slice(jnp.zeros((total,), f32), part, (at * part.shape[0],))

    parts = (mod_part, b_qv.astype(f32), b_proj.astype(f32), b_fc1.astype(f32), b_fc2.astype(f32))
    vec = jnp.concatenate([place(p, 8 * p.shape[0]) for p in parts] + [jnp.where(at == 0, scaled.astype(f32), 0.0), jnp.zeros((width,), f32)]).reshape(16, width)
    la = jnp.concatenate([jnp.transpose(w_qkv.reshape(ROWS, 3, WID), (1, 0, 2)), w_proj[None]])
    lc = w_fc2.reshape(4, ROWS, WID)
    live_mask = (lax.iota(jnp.int32, images) < live[0, 0]).astype(f32)
    row_mask = jnp.repeat(live_mask, length)[:, None]
    x_rows = latents[0].reshape(rows, width)
    res = cotangent[0].reshape(rows, width) * row_mask.astype(jnp.bfloat16)
    vec, wa, wb, wc, h_first, qkv, attended, branch, middle, h_second, slope, hidden, grad_out, grad_fc2, lse, norm, inv = forward(vec, la, w_fc1, lc, x_rows, res)
    sums, cond_sum, oa, ob, oc, block_out, grad_rows, _, _ = backward(
        live_mask, vec, wa, wb, wc.reshape(4, width, width), x_rows, res, h_first, qkv, attended, branch, middle, h_second, slope, hidden,
        grad_out, grad_fc2.reshape(8, 4, ROWS, width), jnp.transpose(w_ada), lse, norm, inv,
    )
    flat = sums.reshape(4, 16 * width)
    total = jnp.sum(flat, axis=0)

    def mine(v, begin, size):
        return lax.dynamic_slice_in_dim(v, begin + at * size, size, axis=-1)

    mod_bins = mine(flat, 0, 6 * width // 8)
    high = lax.reduce_precision(mod_bins, 8, 7)
    middle = lax.reduce_precision(mod_bins - high, 8, 7)
    low = lax.reduce_precision(mod_bins - high - middle, 8, 7)
    split = jnp.concatenate([high, middle, low]).astype(jnp.bfloat16)
    scaled_bins = jnp.tile(sums[:, 14].astype(jnp.bfloat16), (3, 1))
    grad_wada = jnp.einsum("bd,be->de", scaled_bins, split, preferred_element_type=f32)
    silu_pull = jax.vjp(jax.nn.silu, cond[0])[1]
    grad_cond = silu_pull(cond_sum[0])[0][None, :]
    return (
        block_out.reshape(latents.shape),
        grad_rows.reshape(latents.shape),
        grad_cond,
        grad_wada,
        mine(total, 0, 6 * width // 8),
        jnp.transpose(oa[:3], (1, 0, 2)).reshape(ROWS, 3 * width),
        mine(total, 6 * width, 2 * width // 8),
        oa[3],
        mine(total, 8 * width, width // 8),
        jnp.transpose(ob, (1, 0, 2)).reshape(ROWS, 4 * width),
        mine(total, 9 * width, 4 * width // 8),
        oc.reshape(4 * ROWS, width),
        mine(total, 13 * width, width // 8),
    )


def solution(mesh):
    fast = mesh.shape["bin"] == 4 and mesh.shape["fsdp"] == 8
    return jax.shard_map(
        on_device_fast if fast else on_device_generic,
        mesh=mesh,
        in_specs=(
            P("bin", "fsdp", None, None),
            P("bin", None),
            P("bin", "fsdp"),
            P(None, "fsdp"),
            P("fsdp"),
            P("fsdp", None),
            P("fsdp"),
            P("fsdp", None),
            P("fsdp"),
            P("fsdp", None),
            P("fsdp"),
            P("fsdp", None),
            P("fsdp"),
            P("bin", "fsdp", None, None),
        ),
        out_specs=(
            P("bin", "fsdp", None, None),
            P("bin", "fsdp", None, None),
            P("bin", None),
            P(None, "fsdp"),
            P("fsdp"),
            P("fsdp", None),
            P("fsdp"),
            P("fsdp", None),
            P("fsdp"),
            P("fsdp", None),
            P("fsdp"),
            P("fsdp", None),
            P("fsdp"),
        ),
        check_vma=False,
    )
```
